32 devices in a mesh: shard: 16 (over z, y, x), rep: 2 (over core).
Axes of the slice: x: 2, y: 2, z: 4, core: 2. Of those that a mesh axis runs over, the one named last changes fastest.
Arguments:
- tokens: bfloat16 [32768, 1536], P(('shard', 'rep')), may hold values from -6 to 6
- seg_ids: int32 [32, 1024], P(('shard', 'rep')), may hold values from 0 to 5, never falling along the last dimension, each value on 1 to 800 neighbouring positions
- gain_in: bfloat16 [1536], P('shard'), may hold values from 0.5 to 1.5
- w_in: bfloat16 [1536, 6448], P('shard'), may hold values from -0.15625 to 0.15625
- conv_weight: bfloat16 [4, 3328], P(None, 'shard'), may hold values from -3 to 3
- conv_bias: bfloat16 [3328], P('shard'), may hold values from -3 to 3
- dt_bias: float32 [48], replicated, may hold values from -6 to -2
- a_log: float32 [48], replicated, may hold values from 0 to 2.77
- d_skip: float32 [48], replicated, may hold values from 0.5 to 1.5
- gain_out: bfloat16 [3072], P('shard'), may hold values from 0.5 to 1.5
- w_out: bfloat16 [3072, 1536], P('shard'), may hold values from -0.109375 to 0.109375
- cotangent: bfloat16 [32768, 1536], P(('shard', 'rep')), may hold values from -6 to 6
Outputs:
- output: bfloat16 [32768, 1536], P(('shard', 'rep'))
- grad_tokens: bfloat16 [32768, 1536], P(('shard', 'rep'))
- grad_gain_in: float32 [1536], P('shard')
- grad_w_in: float32 [1536, 6448], P('shard')
- grad_conv_weight: float32 [4, 3328], P(None, 'shard')
- grad_conv_bias: float32 [3328], P('shard')
- grad_dt_bias: float32 [48], replicated
- grad_a_log: float32 [48], replicated
- grad_d_skip: float32 [48], replicated
- grad_gain_out: float32 [3072], P('shard')
- grad_w_out: float32 [3072, 1536], P('shard')
The draws below stay inside these ranges and needn't reach their ends.
Inputs may be any that keep to these rules, and one draw needn't show every extreme that they name: `seg_ids`: within each packed sequence of 1024 tokens the document numbers never fall; each document has 1 to 800 tokens and one has exactly 800.
All inputs are finite; a program needn't handle non-finite values.
Results may differ from the reference program's by a relative error of at most 0.0068.
Values may be sent and summed in bfloat16 or wider, within the bound.
No kernel may reach another device: no remote copies, remote signals or barrier semaphores. Data moves between devices by JAX's collectives and lax.ppermute only.
A program may use at most 384 MiB of HBM per device.

```python
import math
import jax
import jax.numpy as jnp
import numpy as np
from jax import lax

D = 1536
H = 48
P_SIZE = 64
N = 128
CONV = 4
SPAN = 256
SEQ_LEN = 1024
DOCS = 6
DOC_MOST = 800
DI = 3072
CONVDIM = 3328
PROJ = 6448
SEQS = 32
TOKENS = 32768


def raised(drawn, stream_key, source, target, shards_of, factor):
    owner, partner = [(jnp.arange(drawn.shape[axis_at]) // (drawn.shape[axis_at] // shards_of)).reshape([-1 if axis == axis_at else 1 for axis in range(drawn.ndim)]) for axis_at in (source, target)]
    chosen = jax.random.permutation(stream_key, shards_of)[partner]
    strong = (owner == chosen) | (owner == (partner + shards_of // 2) % shards_of)
    return jnp.where(strong, factor * drawn, drawn)


def shard_levels(rng, shape, shards, smallest, largest):
    def one(axis_at, shards_of):
        draws = jax.random.uniform(jax.random.fold_in(jax.random.fold_in(rng, 6), axis_at), (shards_of,), jnp.float32, smallest / len(shards), largest / len(shards))
        return jnp.repeat(jnp.exp(draws), shape[axis_at] // shards_of).reshape((-1,) + (1,) * (len(shape) - axis_at - 1))

    level = one(*shards[0])
    for cut in shards[1:]:
        level = level * one(*cut)
    return level


def split_up(count, total, most, lean):
    weights = [(1 << 20) // math.isqrt(grade ** lean) + 1 for grade in range(2, count + 1)]
    rest, given = total - most - (count - 1), [1] * (count - 1)
    while rest > 0:
        candidates = [i for i in range(count - 1) if given[i] < most]
        whole, remaining = sum([weights[i] for i in candidates]), rest
        for i in candidates:
            addition = min(most - given[i], max(1, remaining * weights[i] // whole), rest)
            given[i] = given[i] + addition
            rest = rest - addition
    return np.array([most] + given)


def ragged_sizes(key, number_of, total, most, skew):
    if number_of == 2:
        one = jax.random.randint(key, (), max(1, total - most), min(most, total - 1) + 1)
        return jnp.stack([one, total - one])
    lengths = jnp.asarray(split_up(number_of, total, most, skew), jnp.int32)
    pairs = (number_of - 1) // 2
    giver, taker = lengths[1:1 + 2 * pairs:2], lengths[2:2 + 2 * pairs:2]
    room = jnp.minimum(giver - 1, most - taker)
    moved = jax.random.randint(jax.random.fold_in(key, 1), (pairs,), 0, 1 << 20) % (room + 1)
    lengths = lengths.at[1:1 + 2 * pairs:2].set(giver - moved).at[2:2 + 2 * pairs:2].set(taker + moved)
    return lengths[jax.random.permutation(jax.random.fold_in(key, 2), number_of)]


def centred(rng, shape, width, most, cuts=(), kind=jnp.bfloat16):
    values = jax.random.normal(rng, shape, jnp.float32) * width
    if len(cuts) > 0:
        values = shard_levels(rng, shape, cuts, -0.22, 0.18) * values
    return jnp.clip(values, min=-most, max=most).astype(kind)


def gaussian_with(rng, shape, spread, most, split, heavy, held_as=jnp.bfloat16):
    entries = spread * jax.random.normal(rng, shape, jnp.float32)
    if split:
        entries = entries * shard_levels(rng, shape, split, -0.22, 0.18)
    return jnp.clip(raised(entries, jax.random.fold_in(rng, 3), *heavy), -most, most).astype(held_as)


def setup_inputs(seed: int = 0) -> dict:
    seeds = jax.random.split(jax.random.key(seed), 13)
    return {
        "tokens": gaussian_with(seeds[0], (TOKENS, D), 1.0, 6.0, ((0, 32),), (0, 1, 32, 2.75)),
        "seg_ids": jax.vmap(lambda own: jnp.searchsorted(jnp.cumsum(ragged_sizes(own, DOCS, SEQ_LEN, DOC_MOST, 1)), jnp.arange(SEQ_LEN), side="right"))(jax.random.split(seeds[1], SEQS)).reshape((SEQS, SEQ_LEN)).astype(jnp.int32),
        "gain_in": jnp.clip(1.0 + 0.1 * jax.random.normal(seeds[2], (D,), jnp.float32), 0.5, 1.5).astype(jnp.bfloat16),
        "w_in": centred(seeds[3], (D, PROJ), D ** -0.5, 0.15625, ((0, 16),)),
        "conv_weight": centred(seeds[4], (CONV, CONVDIM), CONV ** -0.5, 3.0, ((1, 16),)),
        "conv_bias": centred(seeds[5], (CONVDIM,), 0.5, 3.0, ((0, 16),)),
        "dt_bias": jnp.clip(jax.random.uniform(seeds[6], (H,), jnp.float32, -6.0, -2.0), -6.0, -2.0),
        "a_log": jnp.clip(jax.random.uniform(seeds[7], (H,), jnp.float32, 0.0, 2.77), 0.0, 2.77),
        "d_skip": jnp.clip(jax.random.uniform(seeds[8], (H,), jnp.float32, 0.5, 1.5), 0.5, 1.5),
        "gain_out": jnp.clip(1.0 + 0.1 * jax.random.normal(seeds[9], (DI,), jnp.float32), 0.5, 1.5).astype(jnp.bfloat16),
        "w_out": centred(seeds[10], (DI, D), DI ** -0.5, 0.109375, ((0, 16),)),
        "cotangent": centred(seeds[11], (TOKENS, D), 1.0, 6.0, ((0, 32),)),
    }


EPSILON = 1e-05
HIGHEST = lax.Precision.HIGHEST

@jax.custom_vjp
def low(v):
    return lax.optimization_barrier(v.astype(jnp.bfloat16)).astype(jnp.float32)

@jax.custom_vjp
def low_back(v):
    return v

def low_keep(v):
    return (low(v), None)

def low_pass(kept, grad):
    return (grad,)

def back_keep(v):
    return (v, None)

def back_low(kept, grad):
    return (low(grad),)
low.defvjp(low_keep, low_pass)
low_back.defvjp(back_keep, back_low)

def rms_rows(values):
    return values * lax.rsqrt(lax.optimization_barrier(jnp.mean(values * values, axis=-1, keepdims=True)) + EPSILON)

def conv_silu(signal, conv_kernel, conv_shift, seg_row):
    kernel_len = conv_kernel.shape[0]
    summed = conv_shift[None, :] + conv_kernel[kernel_len - 1][None, :] * signal
    for offset in range(1, kernel_len):
        shifted = jnp.concatenate([jnp.zeros((offset, signal.shape[1]), jnp.float32), signal[:-offset]], axis=0)
        seg_moved = jnp.concatenate([jnp.full((offset,), -1, jnp.int32), seg_row[:-offset].astype(jnp.int32)])
        same_doc = (seg_moved == seg_row.astype(jnp.int32)).astype(jnp.float32)
        summed = summed + conv_kernel[kernel_len - 1 - offset][None, :] * shifted * same_doc[:, None]
    return jax.nn.silu(summed)

def ssd_scan(values, keys_b, query_c, steps, rates, seg_row):
    length = values.shape[0]
    blocks = length // SPAN
    seg_row = seg_row.astype(jnp.int32)
    seg_last = seg_row[SPAN - 1::SPAN]
    seg_before = jnp.concatenate([seg_row[:1], seg_last[:-1]])
    position = jnp.arange(SPAN, dtype=jnp.int32)
    causal = position[:, None] >= position[None, :]

    def span_step(state, pieces):
        block_x, block_b, block_c, block_dt, block_seg, seg_prior = pieces
        cumul = jnp.cumsum(block_dt * rates[None, :], axis=0).T
        linked = causal & (block_seg[:, None] == block_seg[None, :])
        gaps = jnp.where(linked[None], cumul[:, :, None] - cumul[:, None, :], 0.0)
        decay = jnp.where(linked[None], jnp.exp(gaps), 0.0)
        scores = jnp.dot(block_c, block_b.T, precision=HIGHEST)
        mixing = decay * scores[None] * block_dt.T[:, None, :]
        inner = jnp.einsum('hij,jhp->ihp', mixing, block_x, precision=HIGHEST)
        entry = jnp.exp(cumul) * (block_seg == seg_prior).astype(jnp.float32)[None, :]
        carried = jnp.einsum('in,hpn->ihp', block_c, state, precision=HIGHEST) * entry.T[:, :, None]
        tail = (block_seg == block_seg[-1]).astype(jnp.float32)
        weights_tail = jnp.exp(cumul[:, -1:] - cumul) * block_dt.T * tail[None, :]
        retain = jnp.exp(cumul[:, -1]) * (block_seg[-1] == seg_prior).astype(jnp.float32)
        fresh = jnp.einsum('hj,jhp,jn->hpn', weights_tail, block_x, block_b, precision=HIGHEST)
        return (state * retain[:, None, None] + fresh, inner + carried)
    pieces = (values.reshape(blocks, SPAN, H, P_SIZE), keys_b.reshape(blocks, SPAN, N), query_c.reshape(blocks, SPAN, N), steps.reshape(blocks, SPAN, H), seg_row.reshape(blocks, SPAN), seg_before)
    start = jnp.zeros((H, P_SIZE, N), jnp.float32)
    ending, result = lax.scan(jax.checkpoint(span_step), start, pieces)
    return result.reshape(length, H, P_SIZE)

def mixer_front(projected, conv_kernel, conv_shift, seg_row):
    inner_dim = conv_kernel.shape[1] - 2 * N
    signal = projected[:, inner_dim:inner_dim + conv_kernel.shape[1]]
    return conv_silu(signal, conv_kernel, conv_shift, seg_row)

def mixer_back(conved, projected, bias_dt, log_rate, skip_gain, norm_gain, seg_row):
    inner_dim = norm_gain.shape[0]
    length = conved.shape[0]
    gate = projected[:, :inner_dim]
    raw_step = projected[:, projected.shape[1] - H:]
    values = conved[:, :inner_dim].reshape(length, H, P_SIZE)
    keys_b = conved[:, inner_dim:inner_dim + N]
    query_c = conved[:, inner_dim + N:]
    steps = jax.nn.softplus(raw_step + bias_dt[None, :])
    rates = -jnp.exp(log_rate)
    mixed = ssd_scan(values, keys_b, query_c, steps, rates, seg_row) + values * skip_gain[None, :, None]
    gated = mixed.reshape(length, inner_dim) * jax.nn.silu(gate)
    return rms_rows(gated) * norm_gain[None, :]

def sequence_out(params, sequence, seg_row):
    gain_in, w_in, conv_weight, conv_bias, dt_bias, a_log, d_skip, gain_out, w_out = params
    normed = low(rms_rows(sequence) * gain_in[None, :])
    projected = low_back(jnp.dot(normed, w_in, precision=HIGHEST))
    conved = low(mixer_front(projected, conv_weight, conv_bias, seg_row))
    ynorm = low(mixer_back(conved, projected, dt_bias, a_log, d_skip, gain_out, seg_row))
    return sequence + jnp.dot(ynorm, w_out, precision=HIGHEST)

def reference(tokens, seg_ids, gain_in, w_in, conv_weight, conv_bias, dt_bias, a_log, d_skip, gain_out, w_out, cotangent):
    params = tuple((weight_item.astype(jnp.float32) for weight_item in (gain_in, w_in, conv_weight, conv_bias, dt_bias, a_log, d_skip, gain_out, w_out)))
    inputs = tokens.astype(jnp.float32).reshape(SEQS, SEQ_LEN, D)

    def whole_layer(params, inputs):

        def one_sequence(counter, pieces):
            return (counter, sequence_out(params, pieces[0], pieces[1]))
        counter_end, outputs = lax.scan(jax.checkpoint(one_sequence), jnp.zeros((), jnp.float32), (inputs, seg_ids))
        return outputs
    outputs, pullback = jax.vjp(whole_layer, params, inputs)
    grad_params, grad_inputs = pullback(cotangent.astype(jnp.float32).reshape(SEQS, SEQ_LEN, D))
    return (outputs.reshape(TOKENS, D).astype(jnp.bfloat16), grad_inputs.reshape(TOKENS, D).astype(jnp.bfloat16), grad_params[0], grad_params[1], grad_params[2], grad_params[3], grad_params[4], grad_params[5], grad_params[6], grad_params[7], grad_params[8])
```

```python
import jax
import jax.numpy as jnp
from jax import lax
from jax.experimental import pallas as pl
from jax.experimental.pallas import tpu as pltpu
from jax.sharding import PartitionSpec as P

H = 48
P_SIZE = 64
N = 128
SPAN = 256
HALF = 128
GROUP = 8
TILE = 128
EPSILON = 1e-05
HIGHEST = lax.Precision.HIGHEST
LOG2E = 1.4426950408889634
NEG = -1e30
F32 = jnp.float32
BF16 = jnp.bfloat16


def dot_f32(a, b, contract, precision=None):
    return lax.dot_general(
        a, b, ((contract[0], contract[1]), ((), ())), preferred_element_type=F32, precision=precision
    )


def mm(a, b):
    return dot_f32(a, b, ((1,), (0,)))


def mm_nt(a, b):
    return dot_f32(a, b, ((1,), (1,)))


def lanes_of(column, rows):
    return jnp.broadcast_to(column, (rows, TILE))


def step_sizes(raw, heads):
    shifted = raw + heads[0:1]
    return jnp.maximum(shifted, 0.0) + jnp.log1p(jnp.exp(-jnp.abs(shifted)))


def conv_taps(ext, same, start, width, rows=SPAN):
    out = [ext[8 : 8 + rows, start : start + width]]
    for offset in (1, 2, 3):
        moved = ext[8 - offset : 8 - offset + rows, start : start + width]
        mask = same[offset - 1]
        if width > TILE:
            mask = jnp.concatenate([mask] * (width // TILE), axis=1)
        out.append(moved * mask)
    return out


def conv_sum(taps, weights):
    total = weights[4:5] + weights[3:4] * taps[0]
    for offset in (1, 2, 3):
        total = total + weights[3 - offset : 4 - offset] * taps[offset]
    return total


def prepare(raw_ref, heads_ref, aux_ref, pack_a, pack_b, cum_rows, same):
    aux = aux_ref[...]
    heads = heads_ref[...]
    step = step_sizes(raw_ref[...], heads)
    row = lax.broadcasted_iota(jnp.int32, (SPAN, SPAN), 0)
    col = lax.broadcasted_iota(jnp.int32, (SPAN, SPAN), 1)
    tri = (row >= col).astype(F32)
    cum = dot_f32(tri, step * heads[1:2], ((1,), (0,)), HIGHEST)
    last = cum[SPAN - 1 : SPAN]
    entry = jnp.exp2(cum) * lanes_of(aux[:, 3:4], SPAN)
    tail = jnp.exp2(last - cum) * lanes_of(aux[:, 4:5], SPAN)
    lane = lax.broadcasted_iota(jnp.int32, (SPAN, TILE), 1)
    low = lane < 64
    pack_a[...] = jnp.where(low, cum, pltpu.roll(step, 64, 1))
    pack_b[...] = jnp.where(low, entry, pltpu.roll(tail, 64, 1))
    cum_rows[...] = cum.T
    for offset in (1, 2, 3):
        same[offset - 1] = lanes_of(aux[:, offset - 1 : offset], SPAN)


def forward_kernel(
    pc_ref, halo_ref, bc_ref, bc_halo_ref, raw_ref, cw_ref, bcw_ref, aux_ref, seg_ref, heads_ref, skip_ref,
    x_out, bc_out, y_out, st_out,
    state, scores, block, same, pack_a, pack_b, cum_rows, b_t, ext, ext_bc, halo_bf,
):
    span = pl.program_id(0)
    group = pl.program_id(1)

    @pl.when((span == 0) & (group == 0))
    def _():
        state[...] = jnp.zeros_like(state)

    @pl.when(group == 0)
    def _():
        prepare(raw_ref, heads_ref, aux_ref, pack_a, pack_b, cum_rows, same)
        ext_bc[0:8] = bc_halo_ref[...]
        ext_bc[8:] = bc_ref[...]
        total = conv_sum(conv_taps(ext_bc, same, 0, 2 * N), bcw_ref[...])
        both = (total * jax.nn.sigmoid(total)).astype(BF16)
        bc_out[...] = both
        keys, query = both[:, :N], both[:, N:]
        row = lax.broadcasted_iota(jnp.int32, (SPAN, SPAN), 0)
        col = lax.broadcasted_iota(jnp.int32, (SPAN, SPAN), 1)
        linked = (row >= col) & (aux_ref[:, 5:6] == seg_ref[...])
        block[...] = jnp.where(linked, 0.0, NEG)
        scores[...] = mm_nt(query, keys)
        b_t[...] = keys.T

    ext[0:8] = halo_ref[...]
    ext[8:] = pc_ref[...]
    shift = (TILE - GROUP * group) % TILE
    cols_a = pltpu.roll(pack_a[...], shift, 1)
    cols_b = pltpu.roll(pack_b[...], shift, 1)
    retain = cols_b[SPAN - 1 : SPAN]
    lane = lax.broadcasted_iota(jnp.int32, (SPAN, TILE), 1)
    first = lane < P_SIZE
    query = bc_out[:, N:]
    for pair in range(GROUP // 2):
        at = pair * TILE
        total = conv_sum(conv_taps(ext, same, at, TILE), cw_ref[:, at : at + TILE])
        x = total * jax.nn.sigmoid(total)
        xb = x.astype(BF16)
        x_out[:, at : at + TILE] = xb
        here = group * (GROUP // 2) * TILE + at
        tile = pl.ds(pl.multiple_of(here, TILE), TILE)
        old = state[:, tile]
        old_b = old.astype(BF16)
        st_out[:, at : at + TILE] = old_b
        parts = []
        for head in (2 * pair, 2 * pair + 1):
            cum_col = lanes_of(cols_a[:, head : head + 1], SPAN)
            cum_row = cum_rows[pl.ds(group * GROUP + head, 1), :]
            step_row = None
            blocks = []
            for i, j in ((0, 0), (1, 0), (1, 1)):
                rows = slice(i * HALF, (i + 1) * HALF)
                cols = slice(j * HALF, (j + 1) * HALF)
                gap = cum_col[rows] - cum_row[:, cols] + block[rows, cols]
                blocks.append((jnp.exp2(gap) * scores[rows, cols]).astype(BF16))
            parts.append(blocks)
        step_pair = jnp.where(
            first,
            lanes_of(cols_a[:, 64 + 2 * pair : 65 + 2 * pair], SPAN),
            lanes_of(cols_a[:, 65 + 2 * pair : 66 + 2 * pair], SPAN),
        )
        xs = x * step_pair
        xs = xb.astype(F32) * step_pair
        xsb = xs.astype(BF16)
        outs = []
        for blocks in parts:
            top = mm(blocks[0], xsb[:HALF])
            bottom = mm(jnp.concatenate(blocks[1:], axis=1), xsb)
            outs.append(jnp.concatenate([top, bottom], axis=0))
        entry_pair = jnp.where(
            first,
            lanes_of(cols_b[:, 2 * pair : 2 * pair + 1], SPAN),
            lanes_of(cols_b[:, 2 * pair + 1 : 2 * pair + 2], SPAN),
        )
        tail_pair = jnp.where(
            first,
            lanes_of(cols_b[:, 64 + 2 * pair : 65 + 2 * pair], SPAN),
            lanes_of(cols_b[:, 65 + 2 * pair : 66 + 2 * pair], SPAN),
        )
        carried = mm(query, old_b)
        y_out[:, at : at + TILE] = (
            jnp.where(first, outs[0], outs[1])
            + entry_pair * carried
            + skip_ref[:, at : at + TILE] * xb.astype(F32)
        )
        retain_pair = jnp.where(
            first[:N],
            jnp.broadcast_to(retain[:, 2 * pair : 2 * pair + 1], (N, TILE)),
            jnp.broadcast_to(retain[:, 2 * pair + 1 : 2 * pair + 2], (N, TILE)),
        )
        state[:, tile] = old * retain_pair + mm(b_t[...], (xs * tail_pair).astype(BF16))


def run_forward(pc, raw, conv_all, aux, seg_row, heads, skip):
    tokens = pc.shape[0]
    spans = tokens // SPAN
    di = pc.shape[1] - 2 * N
    width = GROUP * P_SIZE
    groups = di // width
    last_block = di // (2 * N)
    grid_spec = pltpu.PrefetchScalarGridSpec(
        num_scalar_prefetch=0,
        grid=(spans, groups),
        in_specs=[
            pl.BlockSpec((SPAN, width), lambda s, g: (s, g)),
            pl.BlockSpec((8, width), lambda s, g: (jnp.maximum(s * (SPAN // 8) - 1, 0), g)),
            pl.BlockSpec((SPAN, 2 * N), lambda s, g: (s, last_block)),
            pl.BlockSpec((8, 2 * N), lambda s, g: (jnp.maximum(s * (SPAN // 8) - 1, 0), last_block)),
            pl.BlockSpec((SPAN, TILE), lambda s, g: (s, 0)),
            pl.BlockSpec((8, width), lambda s, g: (0, g)),
            pl.BlockSpec((8, 2 * N), lambda s, g: (0, last_block)),
            pl.BlockSpec((SPAN, 8), lambda s, g: (s, 0)),
            pl.BlockSpec((1, SPAN), lambda s, g: (0, s)),
            pl.BlockSpec((8, TILE), lambda s, g: (0, 0)),
            pl.BlockSpec((1, width), lambda s, g: (0, g)),
        ],
        out_specs=[
            pl.BlockSpec((SPAN, width), lambda s, g: (s, g)),
            pl.BlockSpec((SPAN, 2 * N), lambda s, g: (s, 0)),
            pl.BlockSpec((SPAN, width), lambda s, g: (s, g)),
            pl.BlockSpec((N, width), lambda s, g: (s, g)),
        ],
        scratch_shapes=[
            pltpu.VMEM((N, di), F32),
            pltpu.VMEM((SPAN, SPAN), F32),
            pltpu.VMEM((SPAN, SPAN), F32),
            pltpu.VMEM((3, SPAN, TILE), F32),
            pltpu.VMEM((SPAN, TILE), F32),
            pltpu.VMEM((SPAN, TILE), F32),
            pltpu.VMEM((TILE, SPAN), F32),
            pltpu.VMEM((N, SPAN), BF16),
            pltpu.VMEM((SPAN + 8, width), F32),
            pltpu.VMEM((SPAN + 8, 2 * N), F32),
            pltpu.VMEM((8, TILE), F32),
        ],
    )
    return pl.pallas_call(
        forward_kernel,
        grid_spec=grid_spec,
        out_shape=[
            jax.ShapeDtypeStruct((tokens, di), BF16),
            jax.ShapeDtypeStruct((tokens, 2 * N), BF16),
            jax.ShapeDtypeStruct((tokens, di), F32),
            jax.ShapeDtypeStruct((spans * N, di), BF16),
        ],
        compiler_params=pltpu.CompilerParams(dimension_semantics=("arbitrary", "arbitrary")),
        name="scan_forward",
    )(pc, pc, pc, pc, raw, conv_all, conv_all, aux, seg_row, heads, skip)


def conv_back(grad, ext, same, weights, carry, start, width):
    taps = conv_taps(ext, same, start, width)
    total = conv_sum(taps, weights)
    gate = jax.nn.sigmoid(total)
    du = grad * (gate * (1.0 + total * (1.0 - gate)))
    row_index = lax.broadcasted_iota(jnp.int32, (SPAN, width), 0)
    out = weights[3:4] * du
    sums = [jnp.sum(du.reshape(SPAN // 8, 8, width), axis=0)]
    sums.append(jnp.sum((du * taps[0]).reshape(SPAN // 8, 8, width), axis=0))
    for offset in (1, 2, 3):
        mask = same[offset - 1]
        if width > TILE:
            mask = jnp.concatenate([mask] * (width // TILE), axis=1)
        masked = du * mask
        after = carry[offset - 1]
        moved = jnp.concatenate([masked, after], axis=0)[offset : offset + SPAN]
        carry[offset - 1] = masked[0:8]
        out = out + weights[3 - offset : 4 - offset] * moved
        sums.append(jnp.sum((du * taps[offset]).reshape(SPAN // 8, 8, width), axis=0))
    return out, sums


def backward_kernel(
    dy_ref, x_ref, bcv_ref, st_ref, pc_ref, halo_ref, bc_ref, bc_halo_ref, raw_ref, cw_ref, bcw_ref,
    aux_ref, seg_ref, heads_ref, skip_ref,
    dpc_out, dbc_out, draw_out, dcw_out, dbcw_out, dskip_out, dhead_out,
    dstate, scores, block, dscores, same, pack_a, pack_b, cum_rows, c_t, ext, ext_bc,
    carry, carry_bc, d_b, d_c, per_row, dcum_rows, dlast, dcw_acc, dskip_acc,
):
    back = pl.program_id(0)
    group = pl.program_id(1)
    spans = pl.num_programs(0)
    groups = pl.num_programs(1)
    width = GROUP * P_SIZE

    @pl.when((back == 0) & (group == 0))
    def _():
        dstate[...] = jnp.zeros_like(dstate)
        carry[...] = jnp.zeros_like(carry)
        carry_bc[...] = jnp.zeros_like(carry_bc)
        dbcw_out[...] = jnp.zeros_like(dbcw_out)
        dhead_out[...] = jnp.zeros_like(dhead_out)
        dcw_acc[...] = jnp.zeros_like(dcw_acc)
        dskip_acc[...] = jnp.zeros_like(dskip_acc)

    keys = bcv_ref[:, :N]
    query = bcv_ref[:, N:]

    @pl.when(group == 0)
    def _():
        prepare(raw_ref, heads_ref, aux_ref, pack_a, pack_b, cum_rows, same)
        row = lax.broadcasted_iota(jnp.int32, (SPAN, SPAN), 0)
        col = lax.broadcasted_iota(jnp.int32, (SPAN, SPAN), 1)
        linked = (row <= col) & (aux_ref[:, 5:6] == seg_ref[...])
        block[...] = jnp.where(linked, 0.0, NEG)
        scores[...] = mm_nt(keys, query)
        c_t[...] = query.T
        dscores[...] = jnp.zeros_like(dscores)
        d_b[...] = jnp.zeros_like(d_b)
        d_c[...] = jnp.zeros_like(d_c)
        per_row[...] = jnp.zeros_like(per_row)
        dlast[...] = jnp.zeros_like(dlast)

    ext[0:8] = halo_ref[...]
    ext[8:] = pc_ref[...]
    shift = (TILE - GROUP * group) % TILE
    cols_a = pltpu.roll(pack_a[...], shift, 1)
    cols_b = pltpu.roll(pack_b[...], shift, 1)
    retain = cols_b[SPAN - 1 : SPAN]
    lane = lax.broadcasted_iota(jnp.int32, (SPAN, TILE), 1)
    first = lane < P_SIZE
    lane_row = lax.broadcasted_iota(jnp.int32, (TILE, TILE), 0)
    lane_col = lax.broadcasted_iota(jnp.int32, (TILE, TILE), 1)
    sums = jnp.zeros((SPAN, TILE), F32)
    last_sum = jnp.zeros((1, TILE), F32)
    group_at = group * width
    for pair in range(GROUP // 2):
        at = pair * TILE
        tile = pl.ds(pl.multiple_of(group_at + at, TILE), TILE)
        dy = dy_ref[:, at : at + TILE]
        dyf = dy.astype(F32)
        xf = x_ref[:, at : at + TILE].astype(F32)
        step_pair = jnp.where(
            first,
            lanes_of(cols_a[:, 64 + 2 * pair : 65 + 2 * pair], SPAN),
            lanes_of(cols_a[:, 65 + 2 * pair : 66 + 2 * pair], SPAN),
        )
        entry_pair = jnp.where(
            first,
            lanes_of(cols_b[:, 2 * pair : 2 * pair + 1], SPAN),
            lanes_of(cols_b[:, 2 * pair + 1 : 2 * pair + 2], SPAN),
        )
        tail_pair = jnp.where(
            first,
            lanes_of(cols_b[:, 64 + 2 * pair : 65 + 2 * pair], SPAN),
            lanes_of(cols_b[:, 65 + 2 * pair : 66 + 2 * pair], SPAN),
        )
        xs = xf * step_pair
        inner = []
        for which in (0, 1):
            head = 2 * pair + which
            mine = first if which == 0 else ~first
            xh = jnp.where(mine, xs, 0.0).astype(BF16)
            cum_col = lanes_of(cols_a[:, head : head + 1], SPAN)
            cum_row = cum_rows[pl.ds(group * GROUP + head, 1), :]
            g_top = mm_nt(xh[:HALF], dy)
            g_bottom = mm_nt(xh[HALF:], dy[HALF:])
            mixes = []
            across = []
            down = []
            for j, i in ((0, 0), (0, 1), (1, 1)):
                rows = slice(j * HALF, (j + 1) * HALF)
                cols = slice(i * HALF, (i + 1) * HALF)
                decay = jnp.exp2(cum_row[:, cols] - cum_col[rows] + block[rows, cols])
                mix = decay * scores[rows, cols]
                g = g_bottom if j == 1 else g_top[:, cols]
                dscores[rows, cols] += decay * g
                w = mix * g
                mixes.append(mix.astype(BF16))
                across.append(w)
                down.append(jnp.sum(w, axis=0, keepdims=True))
            row_sum = jnp.concatenate(
                [
                    jnp.sum(across[0] + across[1], axis=1, keepdims=True),
                    jnp.sum(across[2], axis=1, keepdims=True),
                ],
                axis=0,
            )
            sums = sums + jnp.where(lane == 24 + head, row_sum, 0.0)
            dcum_rows[pl.ds(group * GROUP + head, 1), :] = jnp.concatenate([down[0], down[1] + down[2]], axis=1)
            top = mm(jnp.concatenate(mixes[:2], axis=1), dy)
            bottom = mm(mixes[2], dy[HALF:])
            inner.append(jnp.concatenate([top, bottom], axis=0))
        stb = st_ref[:, at : at + TILE]
        stf = stb.astype(F32)
        ds = dstate[:, tile]
        dsb = ds.astype(BF16)
        dye = (dyf * entry_pair).astype(BF16)
        fresh = mm(keys, dsb)
        fresh = fresh * tail_pair
        total = jnp.where(first, inner[0], inner[1]) + fresh
        carried = mm(query, stb)
        d_c[...] += mm_nt(dye, stb)
        d_b[...] += mm_nt((xs * tail_pair).astype(BF16), dsb)

        def spread(kind):
            return (lane_col == kind * GROUP + 2 * pair + (lane_row >= P_SIZE).astype(jnp.int32)).astype(BF16)

        def head_sum(values, kind):
            high = values.astype(BF16)
            rest = (values - high.astype(F32)).astype(BF16)
            return mm(high, spread(kind)) + mm(rest, spread(kind))

        sums = sums + head_sum(xf * total, 0) + head_sum(xs * fresh, 1) + head_sum(dyf * entry_pair * carried, 2)
        retain_pair = jnp.where(
            first[:N],
            jnp.broadcast_to(retain[:, 2 * pair : 2 * pair + 1], (N, TILE)),
            jnp.broadcast_to(retain[:, 2 * pair + 1 : 2 * pair + 2], (N, TILE)),
        )
        kept = ds * retain_pair
        kept_sum = jnp.sum(kept * stf, axis=0, keepdims=True)
        low_sum = jnp.sum(jnp.where(first[0:1], kept_sum, 0.0), axis=1, keepdims=True)
        high_sum = jnp.sum(jnp.where(first[0:1], 0.0, kept_sum), axis=1, keepdims=True)
        last_sum = last_sum + jnp.where(lane[0:1] == 2 * pair, low_sum, 0.0)
        last_sum = last_sum + jnp.where(lane[0:1] == 2 * pair + 1, high_sum, 0.0)
        dstate[:, tile] = kept + mm(c_t[...], dye)
        dx = total * step_pair + skip_ref[:, at : at + TILE] * dyf
        dskip_acc[:, tile] += jnp.sum((dyf * xf).reshape(SPAN // 8, 8, TILE), axis=0)
        out, conv_sums = conv_back(
            dx, ext, same, cw_ref[:, at : at + TILE], carry.at[:, :, tile], at, TILE
        )
        dpc_out[:, at : at + TILE] = out.astype(BF16)
        for k, value in enumerate(conv_sums):
            dcw_acc[k, :, tile] += value

    back_shift = GROUP * group
    in_place = (lane >= back_shift) & (lane < back_shift + GROUP)
    for kind in range(4):
        moved = pltpu.roll(sums, (back_shift + TILE - GROUP * kind) % TILE, 1)
        per_row[kind] += jnp.where(in_place, moved, 0.0)
    moved = pltpu.roll(jnp.broadcast_to(last_sum, (8, TILE)), back_shift, 1)
    dlast[...] += jnp.where(in_place[0:8], moved, 0.0)

    @pl.when(group == groups - 1)
    def _():
        ds_b = dscores[...].astype(BF16)
        grad_b = d_b[...] + mm(ds_b, query)
        grad_c = d_c[...] + mm(dscores[...].T.astype(BF16), keys)
        ext_bc[0:8] = bc_halo_ref[...]
        ext_bc[8:] = bc_ref[...]
        grad = jnp.concatenate([grad_b, grad_c], axis=1)
        out, conv_sums = conv_back(grad, ext_bc, same, bcw_ref[...], carry_bc, 0, 2 * N)
        dbc_out[...] = out.astype(BF16)
        for k, value in enumerate(conv_sums):
            dbcw_out[k] += value
        heads = heads_ref[...]
        raw = raw_ref[...]
        step = step_sizes(raw, heads)
        state_part = step * 0.0 + per_row[1]
        dcum = dcum_rows[...].T - per_row[3] + per_row[2] - state_part
        dlast_all = dlast[0:1] + jnp.sum(state_part, axis=0, keepdims=True)
        row = lax.broadcasted_iota(jnp.int32, (SPAN, SPAN), 0)
        col = lax.broadcasted_iota(jnp.int32, (SPAN, SPAN), 1)
        tri = (row <= col).astype(F32)
        da = dot_f32(tri, dcum, ((1,), (0,)), HIGHEST) + dlast_all
        dstep = per_row[0] + da * heads[2:3]
        draw = dstep * jax.nn.sigmoid(raw + heads[0:1])
        live = lane < H
        draw = jnp.where(live, draw, 0.0)
        draw_out[...] = draw.astype(BF16)
        dhead_out[0] += jnp.sum(draw.reshape(SPAN // 8, 8, TILE), axis=0)
        dhead_out[1] += jnp.sum(jnp.where(live, da * step, 0.0).reshape(SPAN // 8, 8, TILE), axis=0)

    @pl.when((group == groups - 1) & (back == spans - 1))
    def _():
        dcw_out[...] = dcw_acc[...]
        dskip_out[...] = dskip_acc[...]


def run_backward(dy, x, bcv, states, pc, raw, conv_all, aux, seg_row, heads, skip):
    tokens, di = dy.shape
    spans = tokens // SPAN
    width = GROUP * P_SIZE
    groups = di // width
    last_block = di // (2 * N)
    turn = lambda s: spans - 1 - s
    halo = lambda s: jnp.maximum(turn(s) * (SPAN // 8) - 1, 0)
    grid_spec = pltpu.PrefetchScalarGridSpec(
        num_scalar_prefetch=0,
        grid=(spans, groups),
        in_specs=[
            pl.BlockSpec((SPAN, width), lambda s, g: (turn(s), g)),
            pl.BlockSpec((SPAN, width), lambda s, g: (turn(s), g)),
            pl.BlockSpec((SPAN, 2 * N), lambda s, g: (turn(s), 0)),
            pl.BlockSpec((N, width), lambda s, g: (turn(s), g)),
            pl.BlockSpec((SPAN, width), lambda s, g: (turn(s), g)),
            pl.BlockSpec((8, width), lambda s, g: (halo(s), g)),
            pl.BlockSpec((SPAN, 2 * N), lambda s, g: (turn(s), last_block)),
            pl.BlockSpec((8, 2 * N), lambda s, g: (halo(s), last_block)),
            pl.BlockSpec((SPAN, TILE), lambda s, g: (turn(s), 0)),
            pl.BlockSpec((8, width), lambda s, g: (0, g)),
            pl.BlockSpec((8, 2 * N), lambda s, g: (0, last_block)),
            pl.BlockSpec((SPAN, 8), lambda s, g: (turn(s), 0)),
            pl.BlockSpec((1, SPAN), lambda s, g: (0, turn(s))),
            pl.BlockSpec((8, TILE), lambda s, g: (0, 0)),
            pl.BlockSpec((1, width), lambda s, g: (0, g)),
        ],
        out_specs=[
            pl.BlockSpec((SPAN, width), lambda s, g: (turn(s), g)),
            pl.BlockSpec((SPAN, 2 * N), lambda s, g: (turn(s), 0)),
            pl.BlockSpec((SPAN, TILE), lambda s, g: (turn(s), 0)),
            pl.BlockSpec((5, 8, di), lambda s, g: (0, 0, 0)),
            pl.BlockSpec((5, 8, 2 * N), lambda s, g: (0, 0, 0)),
            pl.BlockSpec((8, di), lambda s, g: (0, 0)),
            pl.BlockSpec((2, 8, TILE), lambda s, g: (0, 0, 0)),
        ],
        scratch_shapes=[
            pltpu.VMEM((N, di), F32),
            pltpu.VMEM((SPAN, SPAN), F32),
            pltpu.VMEM((SPAN, SPAN), F32),
            pltpu.VMEM((SPAN, SPAN), F32),
            pltpu.VMEM((3, SPAN, TILE), F32),
            pltpu.VMEM((SPAN, TILE), F32),
            pltpu.VMEM((SPAN, TILE), F32),
            pltpu.VMEM((TILE, SPAN), F32),
            pltpu.VMEM((N, SPAN), BF16),
            pltpu.VMEM((SPAN + 8, width), F32),
            pltpu.VMEM((SPAN + 8, 2 * N), F32),
            pltpu.VMEM((3, 8, di), F32),
            pltpu.VMEM((3, 8, 2 * N), F32),
            pltpu.VMEM((SPAN, N), F32),
            pltpu.VMEM((SPAN, N), F32),
            pltpu.VMEM((4, SPAN, TILE), F32),
            pltpu.VMEM((TILE, SPAN), F32),
            pltpu.VMEM((8, TILE), F32),
            pltpu.VMEM((5, 8, di), F32),
            pltpu.VMEM((8, di), F32),
        ],
    )
    return pl.pallas_call(
        backward_kernel,
        grid_spec=grid_spec,
        out_shape=[
            jax.ShapeDtypeStruct((tokens, di), BF16),
            jax.ShapeDtypeStruct((tokens, 2 * N), BF16),
            jax.ShapeDtypeStruct((tokens, TILE), BF16),
            jax.ShapeDtypeStruct((5, 8, di), F32),
            jax.ShapeDtypeStruct((5, 8, 2 * N), F32),
            jax.ShapeDtypeStruct((8, di), F32),
            jax.ShapeDtypeStruct((2, 8, TILE), F32),
        ],
        compiler_params=pltpu.CompilerParams(dimension_semantics=("arbitrary", "arbitrary")),
        name="scan_backward",
    )(dy, x, bcv, states, pc, pc, pc, pc, raw, conv_all, conv_all, aux, seg_row, heads, skip)


def seg_facts(seg):
    length = seg.shape[0]
    cols = []
    for offset in (1, 2, 3):
        moved = jnp.concatenate([jnp.full((offset,), -1, jnp.int32), seg[:-offset]])
        cols.append((moved == seg).astype(F32))
    spans = length // SPAN
    ends = seg[SPAN - 1 :: SPAN]
    before = jnp.concatenate([seg[:1], ends[:-1]])
    cols.append((seg == jnp.repeat(before, SPAN)).astype(F32))
    cols.append((seg == jnp.repeat(ends, SPAN)).astype(F32))
    value = seg.astype(F32)
    cols.append(value)
    cols.append(value)
    cols.append(value)
    return jnp.stack(cols, axis=1), value[None, :]


def head_rows(dt_bias, a_log):
    rate = -jnp.exp(a_log)
    rows = jnp.stack([dt_bias, rate * LOG2E, rate] + [jnp.zeros_like(rate)] * 5, axis=0)
    return jnp.pad(rows, ((0, 0), (0, TILE - H)))


def pad_lanes(values, width):
    return jnp.pad(values, ((0, 0), (0, width - values.shape[1])))


def on_device(
    tokens,
    seg_ids,
    gain_in,
    w_in,
    conv_weight,
    conv_bias,
    dt_bias,
    a_log,
    d_skip,
    gain_out,
    w_out,
    cotangent,
):
    shards = lax.psum(1, "shard")
    conv_local = conv_bias.shape[0]
    small = jnp.concatenate([conv_weight.reshape(-1), conv_bias, gain_in, gain_out])
    small_all = lax.all_gather(small, "shard", axis=0, tiled=False)
    full_w_in = lax.all_gather(w_in, "shard", axis=0, tiled=True)
    full_w_out = lax.all_gather(w_out, "shard", axis=0, tiled=True)
    taps = conv_weight.shape[0]
    cut = taps * conv_local
    conv_w = small_all[:, :cut].reshape(shards, taps, conv_local).transpose(1, 0, 2).reshape(taps, -1)
    conv_b = small_all[:, cut : cut + conv_local].reshape(1, -1)
    cut += conv_local
    full_gain_in = small_all[:, cut : cut + gain_in.shape[0]].reshape(-1).astype(F32)
    full_gain_out = small_all[:, cut + gain_in.shape[0] :].reshape(-1).astype(F32)
    conv_all = jnp.concatenate(
        [conv_w.astype(F32), conv_b.astype(F32), jnp.zeros((3, conv_w.shape[1]), F32)], axis=0
    )
    di = full_gain_out.shape[0]
    conv_dim = conv_w.shape[1]
    inputs = tokens.astype(F32)
    rscale = lax.rsqrt(jnp.mean(inputs * inputs, axis=1, keepdims=True) + EPSILON)
    unit = inputs * rscale
    normed = (unit * full_gain_in[None]).astype(BF16)
    seg = seg_ids[0]
    aux, seg_row = seg_facts(seg)
    heads = head_rows(dt_bias, a_log)
    skip = jnp.repeat(d_skip, P_SIZE)[None]

    w_gate = full_w_in[:, :di]
    w_conv = full_w_in[:, di : di + conv_dim]
    w_step = pad_lanes(full_w_in[:, di + conv_dim :], TILE)
    pc = mm(normed, w_conv)
    raw = mm(normed, w_step)
    gate = mm(normed, w_gate)
    x, bcv, y, states = run_forward(pc, raw, conv_all, aux, seg_row, heads, skip)
    gated = y * (gate * jax.nn.sigmoid(gate))
    inverse = lax.rsqrt(jnp.mean(gated * gated, axis=1, keepdims=True) + EPSILON)
    ynorm = (gated * inverse * full_gain_out[None]).astype(BF16)
    projected = mm(ynorm, full_w_out)
    output = (inputs + projected).astype(BF16)
    cot = cotangent.astype(F32)
    dots = jnp.sum(cot * projected, axis=1, keepdims=True)
    grad_ynorm = mm_nt(cotangent, full_w_out)
    grad_w_out = dot_f32(ynorm, cotangent, ((0,), (0,)))
    dz = inverse * (full_gain_out[None] * grad_ynorm) - gated * (inverse * inverse * dots / di)
    sig = jax.nn.sigmoid(gate)
    dy = (dz * (gate * sig)).astype(BF16)
    dgate = (dz * y * (sig * (1.0 + gate * (1.0 - sig)))).astype(BF16)
    dpc, dbc, draw, dcw, dbcw, dskip, dhead = run_backward(
        dy, x, bcv, states, pc, raw, conv_all, aux, seg_row, heads, skip
    )
    grad_projected = jnp.concatenate([dgate, dpc, dbc, draw[:, :H]], axis=1)
    grad_w_in = dot_f32(normed, grad_projected, ((0,), (0,)))
    grad_normed = mm_nt(grad_projected, full_w_in)
    scaled = grad_normed * full_gain_in[None]
    inner = jnp.mean(unit * scaled, axis=1, keepdims=True)
    grad_tokens = (cot + rscale * (scaled - unit * inner)).astype(BF16)

    conv_sums = jnp.concatenate([dcw, dbcw], axis=2).sum(1)
    conv_sums = jnp.concatenate([conv_sums[4:5], conv_sums[3:4], conv_sums[2:3], conv_sums[1:2], conv_sums[0:1]])
    per_head = jnp.concatenate(
        [
            dhead[0].sum(0)[:H],
            dhead[1].sum(0)[:H] * -jnp.exp(a_log),
            dskip.sum(0).reshape(H, P_SIZE).sum(1),
        ]
    )
    conv_part = conv_sums.reshape(taps + 1, shards, conv_local).transpose(1, 0, 2).reshape(shards, -1)
    small_grad = jnp.concatenate([conv_part, jnp.broadcast_to(per_head[None], (shards, 3 * H))], axis=1)
    small_sum = lax.psum(lax.psum_scatter(small_grad, "shard", scatter_dimension=0, tiled=True), "rep")[0]
    sum_w_in = lax.psum_scatter(grad_w_in.astype(BF16), "shard", scatter_dimension=0, tiled=True)
    sum_w_out = lax.psum_scatter(grad_w_out.astype(BF16), "shard", scatter_dimension=0, tiled=True)
    sum_w_in, sum_w_out = lax.psum((sum_w_in.astype(F32), sum_w_out.astype(F32)), "rep")
    grad_gain_in = jnp.sum(sum_w_in * w_in.astype(F32), axis=1) / gain_in.astype(F32)
    grad_gain_out = jnp.sum(sum_w_out * w_out.astype(F32), axis=1) / gain_out.astype(F32)
    cut = taps * conv_local
    head_at = cut + conv_local
    return (
        output,
        grad_tokens,
        grad_gain_in,
        sum_w_in,
        small_sum[:cut].reshape(taps, conv_local),
        small_sum[cut:head_at],
        small_sum[head_at : head_at + H],
        small_sum[head_at + H : head_at + 2 * H],
        small_sum[head_at + 2 * H :],
        grad_gain_out,
        sum_w_out,
    )


def solution(mesh):
    rows = P(("shard", "rep"), None)
    in_specs = (
        rows, rows, P("shard"), P("shard", None), P(None, "shard"), P("shard"), P(), P(), P(), P("shard"),
        P("shard", None), rows,
    )
    out_specs = (
        rows, rows, P("shard"), P("shard", None), P(None, "shard"), P("shard"), P(), P(), P(), P("shard"),
        P("shard", None),
    )
    return jax.shard_map(
        on_device, mesh=mesh, in_specs=in_specs, out_specs=out_specs, check_vma=False
    )
```

```python
import functools

import jax
import jax.numpy as jnp
from jax import lax
from jax.experimental import pallas as pl
from jax.experimental.pallas import tpu as pltpu
from jax.sharding import PartitionSpec as P

H = 48
P_SIZE = 64
N = 128
SPAN = 256
HALF = 128
GROUP = 8
TILE = 128
EPSILON = 1e-05
HIGHEST = lax.Precision.HIGHEST
LOG2E = 1.4426950408889634
NEG = -1e30
F32 = jnp.float32
BF16 = jnp.bfloat16


def dot_f32(a, b, contract, precision=None):
    return lax.dot_general(
        a, b, ((contract[0], contract[1]), ((), ())), preferred_element_type=F32, precision=precision
    )


def mm(a, b):
    return dot_f32(a, b, ((1,), (0,)))


def mm_nt(a, b):
    return dot_f32(a, b, ((1,), (1,)))


def lanes_of(column, rows):
    return jnp.broadcast_to(column, (rows, TILE))


def step_sizes(raw, heads):
    shifted = raw + heads[0:1]
    return jnp.maximum(shifted, 0.0) + jnp.log1p(jnp.exp(-jnp.abs(shifted)))


def conv_taps(ext, same, start, width, rows=SPAN):
    out = [ext[8 : 8 + rows, start : start + width]]
    for offset in (1, 2, 3):
        moved = ext[8 - offset : 8 - offset + rows, start : start + width]
        mask = same[offset - 1]
        if width > TILE:
            mask = jnp.concatenate([mask] * (width // TILE), axis=1)
        out.append(moved * mask)
    return out


def conv_sum(taps, weights):
    total = weights[4:5] + weights[3:4] * taps[0]
    for offset in (1, 2, 3):
        total = total + weights[3 - offset : 4 - offset] * taps[offset]
    return total


def prepare(raw_ref, heads_ref, aux_ref, pack_a, pack_b, cum_rows, same):
    aux = aux_ref[...]
    heads = heads_ref[...]
    step = step_sizes(raw_ref[...], heads)
    row = lax.broadcasted_iota(jnp.int32, (SPAN, SPAN), 0)
    col = lax.broadcasted_iota(jnp.int32, (SPAN, SPAN), 1)
    tri = (row >= col).astype(F32)
    cum = dot_f32(tri, step * heads[1:2], ((1,), (0,)), HIGHEST)
    last = cum[SPAN - 1 : SPAN]
    entry = jnp.exp2(cum) * lanes_of(aux[:, 3:4], SPAN)
    tail = jnp.exp2(last - cum) * lanes_of(aux[:, 4:5], SPAN)
    lane = lax.broadcasted_iota(jnp.int32, (SPAN, TILE), 1)
    low = lane < 64
    pack_a[...] = jnp.where(low, cum, pltpu.roll(step, 64, 1))
    pack_b[...] = jnp.where(low, entry, pltpu.roll(tail, 64, 1))
    cum_rows[...] = cum.T
    for offset in (1, 2, 3):
        same[offset - 1] = lanes_of(aux[:, offset - 1 : offset], SPAN)


def forward_kernel(
    pc_ref, halo_ref, bc_ref, bc_halo_ref, raw_ref, cw_ref, bcw_ref, aux_ref, seg_ref, heads_ref, skip_ref,
    x_out, bc_out, y_out, st_out,
    state, scores, block, same, pack_a, pack_b, cum_rows, b_t, ext, ext_bc, halo_bf,
):
    span = pl.program_id(0)
    group = pl.program_id(1)

    @pl.when((span == 0) & (group == 0))
    def _():
        state[...] = jnp.zeros_like(state)

    @pl.when(group == 0)
    def _():
        prepare(raw_ref, heads_ref, aux_ref, pack_a, pack_b, cum_rows, same)
        ext_bc[0:8] = bc_halo_ref[...]
        ext_bc[8:] = bc_ref[...]
        total = conv_sum(conv_taps(ext_bc, same, 0, 2 * N), bcw_ref[...])
        both = (total * jax.nn.sigmoid(total)).astype(BF16)
        bc_out[...] = both
        keys, query = both[:, :N], both[:, N:]
        row = lax.broadcasted_iota(jnp.int32, (SPAN, SPAN), 0)
        col = lax.broadcasted_iota(jnp.int32, (SPAN, SPAN), 1)
        linked = (row >= col) & (aux_ref[:, 5:6] == seg_ref[...])
        block[...] = jnp.where(linked, 0.0, NEG)
        scores[...] = mm_nt(query, keys)
        b_t[...] = keys.T

    ext[0:8] = halo_ref[...]
    ext[8:] = pc_ref[...]
    shift = (TILE - GROUP * group) % TILE
    cols_a = pltpu.roll(pack_a[...], shift, 1)
    cols_b = pltpu.roll(pack_b[...], shift, 1)
    retain = cols_b[SPAN - 1 : SPAN]
    lane = lax.broadcasted_iota(jnp.int32, (SPAN, TILE), 1)
    first = lane < P_SIZE
    query = bc_out[:, N:]
    for pair in range(GROUP // 2):
        at = pair * TILE
        total = conv_sum(conv_taps(ext, same, at, TILE), cw_ref[:, at : at + TILE])
        x = total * jax.nn.sigmoid(total)
        xb = x.astype(BF16)
        x_out[:, at : at + TILE] = xb
        here = group * (GROUP // 2) * TILE + at
        tile = pl.ds(pl.multiple_of(here, TILE), TILE)
        old = state[:, tile]
        old_b = old.astype(BF16)
        st_out[:, at : at + TILE] = old_b
        parts = []
        for head in (2 * pair, 2 * pair + 1):
            cum_col = lanes_of(cols_a[:, head : head + 1], SPAN)
            cum_row = cum_rows[pl.ds(group * GROUP + head, 1), :]
            blocks = []
            for i, j in ((0, 0), (1, 0), (1, 1)):
                rows = slice(i * HALF, (i + 1) * HALF)
                cols = slice(j * HALF, (j + 1) * HALF)
                gap = cum_col[rows] - cum_row[:, cols] + block[rows, cols]
                blocks.append((jnp.exp2(gap) * scores[rows, cols]).astype(BF16))
            parts.append(blocks)
        step_pair = jnp.where(
            first,
            lanes_of(cols_a[:, 64 + 2 * pair : 65 + 2 * pair], SPAN),
            lanes_of(cols_a[:, 65 + 2 * pair : 66 + 2 * pair], SPAN),
        )
        xs = xb.astype(F32) * step_pair
        xsb = xs.astype(BF16)
        outs = []
        for blocks in parts:
            top = mm(blocks[0], xsb[:HALF])
            bottom = mm(jnp.concatenate(blocks[1:], axis=1), xsb)
            outs.append(jnp.concatenate([top, bottom], axis=0))
        entry_pair = jnp.where(
            first,
            lanes_of(cols_b[:, 2 * pair : 2 * pair + 1], SPAN),
            lanes_of(cols_b[:, 2 * pair + 1 : 2 * pair + 2], SPAN),
        )
        tail_pair = jnp.where(
            first,
            lanes_of(cols_b[:, 64 + 2 * pair : 65 + 2 * pair], SPAN),
            lanes_of(cols_b[:, 65 + 2 * pair : 66 + 2 * pair], SPAN),
        )
        carried = mm(query, old_b)
        y_out[:, at : at + TILE] = (
            jnp.where(first, outs[0], outs[1])
            + entry_pair * carried
            + skip_ref[:, at : at + TILE] * xb.astype(F32)
        )
        retain_pair = jnp.where(
            first[:N],
            jnp.broadcast_to(retain[:, 2 * pair : 2 * pair + 1], (N, TILE)),
            jnp.broadcast_to(retain[:, 2 * pair + 1 : 2 * pair + 2], (N, TILE)),
        )
        state[:, tile] = old * retain_pair + mm(b_t[...], (xs * tail_pair).astype(BF16))


def run_forward(pc, conv_all, aux, seg_row, heads, skip):
    tokens = pc.shape[0]
    spans = tokens // SPAN
    di = skip.shape[1]
    raw_block = (di + 2 * N) // TILE
    width = GROUP * P_SIZE
    groups = di // width
    last_block = di // (2 * N)
    grid_spec = pltpu.PrefetchScalarGridSpec(
        num_scalar_prefetch=0,
        grid=(spans, groups),
        in_specs=[
            pl.BlockSpec((SPAN, width), lambda s, g: (s, g)),
            pl.BlockSpec((8, width), lambda s, g: (jnp.maximum(s * (SPAN // 8) - 1, 0), g)),
            pl.BlockSpec((SPAN, 2 * N), lambda s, g: (s, last_block)),
            pl.BlockSpec((8, 2 * N), lambda s, g: (jnp.maximum(s * (SPAN // 8) - 1, 0), last_block)),
            pl.BlockSpec((SPAN, TILE), lambda s, g: (s, raw_block)),
            pl.BlockSpec((8, width), lambda s, g: (0, g)),
            pl.BlockSpec((8, 2 * N), lambda s, g: (0, last_block)),
            pl.BlockSpec((SPAN, 8), lambda s, g: (s, 0)),
            pl.BlockSpec((1, SPAN), lambda s, g: (0, s)),
            pl.BlockSpec((8, TILE), lambda s, g: (0, 0)),
            pl.BlockSpec((1, width), lambda s, g: (0, g)),
        ],
        out_specs=[
            pl.BlockSpec((SPAN, width), lambda s, g: (s, g)),
            pl.BlockSpec((SPAN, 2 * N), lambda s, g: (s, 0)),
            pl.BlockSpec((SPAN, width), lambda s, g: (s, g)),
            pl.BlockSpec((N, width), lambda s, g: (s, g)),
        ],
        scratch_shapes=[
            pltpu.VMEM((N, di), F32),
            pltpu.VMEM((SPAN, SPAN), F32),
            pltpu.VMEM((SPAN, SPAN), F32),
            pltpu.VMEM((3, SPAN, TILE), F32),
            pltpu.VMEM((SPAN, TILE), F32),
            pltpu.VMEM((SPAN, TILE), F32),
            pltpu.VMEM((TILE, SPAN), F32),
            pltpu.VMEM((N, SPAN), BF16),
            pltpu.VMEM((SPAN + 8, width), F32),
            pltpu.VMEM((SPAN + 8, 2 * N), F32),
            pltpu.VMEM((8, TILE), F32),
        ],
    )
    return pl.pallas_call(
        forward_kernel,
        grid_spec=grid_spec,
        out_shape=[
            jax.ShapeDtypeStruct((tokens, di), BF16),
            jax.ShapeDtypeStruct((tokens, 2 * N), BF16),
            jax.ShapeDtypeStruct((tokens, di), F32),
            jax.ShapeDtypeStruct((spans * N, di), BF16),
        ],
        compiler_params=pltpu.CompilerParams(dimension_semantics=("arbitrary", "arbitrary")),
        name="scan_forward",
    )(pc, pc, pc, pc, pc, conv_all, conv_all, aux, seg_row, heads, skip)


def conv_back(grad, ext, same, weights, carry, start, width):
    taps = conv_taps(ext, same, start, width)
    total = conv_sum(taps, weights)
    gate = jax.nn.sigmoid(total)
    du = grad * (gate * (1.0 + total * (1.0 - gate)))
    row_index = lax.broadcasted_iota(jnp.int32, (SPAN, width), 0)
    out = weights[3:4] * du
    sums = [jnp.sum(du.reshape(SPAN // 8, 8, width), axis=0)]
    sums.append(jnp.sum((du * taps[0]).reshape(SPAN // 8, 8, width), axis=0))
    for offset in (1, 2, 3):
        mask = same[offset - 1]
        if width > TILE:
            mask = jnp.concatenate([mask] * (width // TILE), axis=1)
        masked = du * mask
        after = carry[offset - 1]
        moved = jnp.concatenate([masked, after], axis=0)[offset : offset + SPAN]
        carry[offset - 1] = masked[0:8]
        out = out + weights[3 - offset : 4 - offset] * moved
        sums.append(jnp.sum((du * taps[offset]).reshape(SPAN // 8, 8, width), axis=0))
    return out, sums


def backward_kernel(
    dy_ref, x_ref, bcv_ref, st_ref, pc_ref, halo_ref, bc_ref, bc_halo_ref, raw_ref, cw_ref, bcw_ref,
    aux_ref, seg_ref, heads_ref, skip_ref,
    dproj_out, dcw_out, dbcw_out, dskip_out, dhead_out,
    dstate, scores, block, dscores, same, pack_a, pack_b, cum_rows, c_t, ext, ext_bc,
    carry, carry_bc, d_b, d_c, per_row, dcum_rows, dlast, dcw_acc, dskip_acc,
):
    back = pl.program_id(0)
    group = pl.program_id(1)
    spans = pl.num_programs(0)
    groups = pl.num_programs(1)
    width = GROUP * P_SIZE

    @pl.when((back == 0) & (group == 0))
    def _():
        dstate[...] = jnp.zeros_like(dstate)
        carry[...] = jnp.zeros_like(carry)
        carry_bc[...] = jnp.zeros_like(carry_bc)
        dbcw_out[...] = jnp.zeros_like(dbcw_out)
        dhead_out[...] = jnp.zeros_like(dhead_out)
        dcw_acc[...] = jnp.zeros_like(dcw_acc)
        dskip_acc[...] = jnp.zeros_like(dskip_acc)

    keys = bcv_ref[:, :N]
    query = bcv_ref[:, N:]

    @pl.when(group == 0)
    def _():
        prepare(raw_ref, heads_ref, aux_ref, pack_a, pack_b, cum_rows, same)
        row = lax.broadcasted_iota(jnp.int32, (SPAN, SPAN), 0)
        col = lax.broadcasted_iota(jnp.int32, (SPAN, SPAN), 1)
        linked = (row <= col) & (aux_ref[:, 5:6] == seg_ref[...])
        block[...] = jnp.where(linked, 0.0, NEG)
        scores[...] = mm_nt(keys, query)
        c_t[...] = query.T
        dscores[...] = jnp.zeros_like(dscores)
        d_b[...] = jnp.zeros_like(d_b)
        d_c[...] = jnp.zeros_like(d_c)
        per_row[...] = jnp.zeros_like(per_row)
        dlast[...] = jnp.zeros_like(dlast)

    ext[0:8] = halo_ref[...]
    ext[8:] = pc_ref[...]
    shift = (TILE - GROUP * group) % TILE
    cols_a = pltpu.roll(pack_a[...], shift, 1)
    cols_b = pltpu.roll(pack_b[...], shift, 1)
    retain = cols_b[SPAN - 1 : SPAN]
    lane = lax.broadcasted_iota(jnp.int32, (SPAN, TILE), 1)
    first = lane < P_SIZE
    lane_row = lax.broadcasted_iota(jnp.int32, (TILE, TILE), 0)
    lane_col = lax.broadcasted_iota(jnp.int32, (TILE, TILE), 1)
    sums = jnp.zeros((SPAN, TILE), F32)
    last_sum = jnp.zeros((1, TILE), F32)
    group_at = group * width
    for pair in range(GROUP // 2):
        at = pair * TILE
        tile = pl.ds(pl.multiple_of(group_at + at, TILE), TILE)
        dy = dy_ref[:, at : at + TILE]
        dyf = dy.astype(F32)
        xf = x_ref[:, at : at + TILE].astype(F32)
        step_pair = jnp.where(
            first,
            lanes_of(cols_a[:, 64 + 2 * pair : 65 + 2 * pair], SPAN),
            lanes_of(cols_a[:, 65 + 2 * pair : 66 + 2 * pair], SPAN),
        )
        entry_pair = jnp.where(
            first,
            lanes_of(cols_b[:, 2 * pair : 2 * pair + 1], SPAN),
            lanes_of(cols_b[:, 2 * pair + 1 : 2 * pair + 2], SPAN),
        )
        tail_pair = jnp.where(
            first,
            lanes_of(cols_b[:, 64 + 2 * pair : 65 + 2 * pair], SPAN),
            lanes_of(cols_b[:, 65 + 2 * pair : 66 + 2 * pair], SPAN),
        )
        xs = xf * step_pair
        inner = []
        for which in (0, 1):
            head = 2 * pair + which
            mine = first if which == 0 else ~first
            xh = jnp.where(mine, xs, 0.0).astype(BF16)
            cum_col = lanes_of(cols_a[:, head : head + 1], SPAN)
            cum_row = cum_rows[pl.ds(group * GROUP + head, 1), :]
            g_top = mm_nt(xh[:HALF], dy)
            g_bottom = mm_nt(xh[HALF:], dy[HALF:])
            mixes = []
            across = []
            down = []
            for j, i in ((0, 0), (0, 1), (1, 1)):
                rows = slice(j * HALF, (j + 1) * HALF)
                cols = slice(i * HALF, (i + 1) * HALF)
                decay = jnp.exp2(cum_row[:, cols] - cum_col[rows] + block[rows, cols])
                mix = decay * scores[rows, cols]
                g = g_bottom if j == 1 else g_top[:, cols]
                dscores[rows, cols] += decay * g
                w = mix * g
                mixes.append(mix.astype(BF16))
                across.append(w)
                down.append(jnp.sum(w, axis=0, keepdims=True))
            row_sum = jnp.concatenate(
                [
                    jnp.sum(across[0] + across[1], axis=1, keepdims=True),
                    jnp.sum(across[2], axis=1, keepdims=True),
                ],
                axis=0,
            )
            sums = sums + jnp.where(lane == 24 + head, row_sum, 0.0)
            dcum_rows[pl.ds(group * GROUP + head, 1), :] = jnp.concatenate([down[0], down[1] + down[2]], axis=1)
            top = mm(jnp.concatenate(mixes[:2], axis=1), dy)
            bottom = mm(mixes[2], dy[HALF:])
            inner.append(jnp.concatenate([top, bottom], axis=0))
        stb = st_ref[:, at : at + TILE]
        stf = stb.astype(F32)
        ds = dstate[:, tile]
        dsb = ds.astype(BF16)
        dye = (dyf * entry_pair).astype(BF16)
        fresh = mm(keys, dsb)
        fresh = fresh * tail_pair
        total = jnp.where(first, inner[0], inner[1]) + fresh
        carried = mm(query, stb)
        d_c[...] += mm_nt(dye, stb)
        d_b[...] += mm_nt((xs * tail_pair).astype(BF16), dsb)

        def spread(kind):
            return (lane_col == kind * GROUP + 2 * pair + (lane_row >= P_SIZE).astype(jnp.int32)).astype(BF16)

        def head_sum(values, kind):
            high = values.astype(BF16)
            rest = (values - high.astype(F32)).astype(BF16)
            return mm(high, spread(kind)) + mm(rest, spread(kind))

        sums = sums + head_sum(xf * total, 0) + head_sum(xs * fresh, 1) + head_sum(dyf * entry_pair * carried, 2)
        retain_pair = jnp.where(
            first[:N],
            jnp.broadcast_to(retain[:, 2 * pair : 2 * pair + 1], (N, TILE)),
            jnp.broadcast_to(retain[:, 2 * pair + 1 : 2 * pair + 2], (N, TILE)),
        )
        kept = ds * retain_pair
        kept_sum = jnp.sum(kept * stf, axis=0, keepdims=True)
        low_sum = jnp.sum(jnp.where(first[0:1], kept_sum, 0.0), axis=1, keepdims=True)
        high_sum = jnp.sum(jnp.where(first[0:1], 0.0, kept_sum), axis=1, keepdims=True)
        last_sum = last_sum + jnp.where(lane[0:1] == 2 * pair, low_sum, 0.0)
        last_sum = last_sum + jnp.where(lane[0:1] == 2 * pair + 1, high_sum, 0.0)
        dstate[:, tile] = kept + mm(c_t[...], dye)
        dx = total * step_pair + skip_ref[:, at : at + TILE] * dyf
        dskip_acc[:, tile] += jnp.sum((dyf * xf).reshape(SPAN // 8, 8, TILE), axis=0)
        out, conv_sums = conv_back(
            dx, ext, same, cw_ref[:, at : at + TILE], carry.at[:, :, tile], at, TILE
        )
        dproj_out[:, tile] = out.astype(BF16)
        for k, value in enumerate(conv_sums):
            dcw_acc[k, :, tile] += value

    back_shift = GROUP * group
    in_place = (lane >= back_shift) & (lane < back_shift + GROUP)
    for kind in range(4):
        moved = pltpu.roll(sums, (back_shift + TILE - GROUP * kind) % TILE, 1)
        per_row[kind] += jnp.where(in_place, moved, 0.0)
    moved = pltpu.roll(jnp.broadcast_to(last_sum, (8, TILE)), back_shift, 1)
    dlast[...] += jnp.where(in_place[0:8], moved, 0.0)

    @pl.when(group == groups - 1)
    def _():
        ds_b = dscores[...].astype(BF16)
        grad_b = d_b[...] + mm(ds_b, query)
        grad_c = d_c[...] + mm(dscores[...].T.astype(BF16), keys)
        ext_bc[0:8] = bc_halo_ref[...]
        ext_bc[8:] = bc_ref[...]
        grad = jnp.concatenate([grad_b, grad_c], axis=1)
        out, conv_sums = conv_back(grad, ext_bc, same, bcw_ref[...], carry_bc, 0, 2 * N)
        di = dstate.shape[1]
        dproj_out[:, di : di + 2 * N] = out.astype(BF16)
        for k, value in enumerate(conv_sums):
            dbcw_out[k] += value
        heads = heads_ref[...]
        raw = raw_ref[...]
        step = step_sizes(raw, heads)
        state_part = per_row[1]
        dcum = dcum_rows[...].T - per_row[3] + per_row[2] - state_part
        dlast_all = dlast[0:1] + jnp.sum(state_part, axis=0, keepdims=True)
        row = lax.broadcasted_iota(jnp.int32, (SPAN, SPAN), 0)
        col = lax.broadcasted_iota(jnp.int32, (SPAN, SPAN), 1)
        tri = (row <= col).astype(F32)
        da = dot_f32(tri, dcum, ((1,), (0,)), HIGHEST) + dlast_all
        dstep = per_row[0] + da * heads[2:3]
        draw = dstep * jax.nn.sigmoid(raw + heads[0:1])
        live = lane < H
        draw = jnp.where(live, draw, 0.0)
        dproj_out[:, di + 2 * N : di + 2 * N + TILE] = draw.astype(BF16)
        dproj_out[:, di + 2 * N + TILE :] = jnp.zeros_like(dproj_out[:, di + 2 * N + TILE :])
        dhead_out[0] += jnp.sum(draw.reshape(SPAN // 8, 8, TILE), axis=0)
        dhead_out[1] += jnp.sum(jnp.where(live, da * step, 0.0).reshape(SPAN // 8, 8, TILE), axis=0)

    @pl.when((group == groups - 1) & (back == spans - 1))
    def _():
        dcw_out[...] = dcw_acc[...]
        dskip_out[...] = dskip_acc[...]


def run_backward(dy, x, bcv, states, pc, conv_all, aux, seg_row, heads, skip):
    tokens, di = dy.shape
    full = pc.shape[1]
    raw_block = (di + 2 * N) // TILE
    spans = tokens // SPAN
    width = GROUP * P_SIZE
    groups = di // width
    last_block = di // (2 * N)
    turn = lambda s: spans - 1 - s
    halo = lambda s: jnp.maximum(turn(s) * (SPAN // 8) - 1, 0)
    grid_spec = pltpu.PrefetchScalarGridSpec(
        num_scalar_prefetch=0,
        grid=(spans, groups),
        in_specs=[
            pl.BlockSpec((SPAN, width), lambda s, g: (turn(s), g)),
            pl.BlockSpec((SPAN, width), lambda s, g: (turn(s), g)),
            pl.BlockSpec((SPAN, 2 * N), lambda s, g: (turn(s), 0)),
            pl.BlockSpec((N, width), lambda s, g: (turn(s), g)),
            pl.BlockSpec((SPAN, width), lambda s, g: (turn(s), g)),
            pl.BlockSpec((8, width), lambda s, g: (halo(s), g)),
            pl.BlockSpec((SPAN, 2 * N), lambda s, g: (turn(s), last_block)),
            pl.BlockSpec((8, 2 * N), lambda s, g: (halo(s), last_block)),
            pl.BlockSpec((SPAN, TILE), lambda s, g: (turn(s), raw_block)),
            pl.BlockSpec((8, width), lambda s, g: (0, g)),
            pl.BlockSpec((8, 2 * N), lambda s, g: (0, last_block)),
            pl.BlockSpec((SPAN, 8), lambda s, g: (turn(s), 0)),
            pl.BlockSpec((1, SPAN), lambda s, g: (0, turn(s))),
            pl.BlockSpec((8, TILE), lambda s, g: (0, 0)),
            pl.BlockSpec((1, width), lambda s, g: (0, g)),
        ],
        out_specs=[
            pl.BlockSpec((SPAN, full), lambda s, g: (turn(s), 0)),
            pl.BlockSpec((5, 8, di), lambda s, g: (0, 0, 0)),
            pl.BlockSpec((5, 8, 2 * N), lambda s, g: (0, 0, 0)),
            pl.BlockSpec((8, di), lambda s, g: (0, 0)),
            pl.BlockSpec((2, 8, TILE), lambda s, g: (0, 0, 0)),
        ],
        scratch_shapes=[
            pltpu.VMEM((N, di), F32),
            pltpu.VMEM((SPAN, SPAN), F32),
            pltpu.VMEM((SPAN, SPAN), F32),
            pltpu.VMEM((SPAN, SPAN), F32),
            pltpu.VMEM((3, SPAN, TILE), F32),
            pltpu.VMEM((SPAN, TILE), F32),
            pltpu.VMEM((SPAN, TILE), F32),
            pltpu.VMEM((TILE, SPAN), F32),
            pltpu.VMEM((N, SPAN), BF16),
            pltpu.VMEM((SPAN + 8, width), F32),
            pltpu.VMEM((SPAN + 8, 2 * N), F32),
            pltpu.VMEM((3, 8, di), F32),
            pltpu.VMEM((3, 8, 2 * N), F32),
            pltpu.VMEM((SPAN, N), F32),
            pltpu.VMEM((SPAN, N), F32),
            pltpu.VMEM((4, SPAN, TILE), F32),
            pltpu.VMEM((TILE, SPAN), F32),
            pltpu.VMEM((8, TILE), F32),
            pltpu.VMEM((5, 8, di), F32),
            pltpu.VMEM((8, di), F32),
        ],
    )
    return pl.pallas_call(
        backward_kernel,
        grid_spec=grid_spec,
        out_shape=[
            jax.ShapeDtypeStruct((tokens, full), BF16),
            jax.ShapeDtypeStruct((5, 8, di), F32),
            jax.ShapeDtypeStruct((5, 8, 2 * N), F32),
            jax.ShapeDtypeStruct((8, di), F32),
            jax.ShapeDtypeStruct((2, 8, TILE), F32),
        ],
        compiler_params=pltpu.CompilerParams(dimension_semantics=("arbitrary", "arbitrary")),
        name="scan_backward",
    )(dy, x, bcv, states, pc, pc, pc, pc, pc, conv_all, conv_all, aux, seg_row, heads, skip)


def seg_facts(seg):
    length = seg.shape[0]
    cols = []
    for offset in (1, 2, 3):
        moved = jnp.concatenate([jnp.full((offset,), -1, jnp.int32), seg[:-offset]])
        cols.append((moved == seg).astype(F32))
    spans = length // SPAN
    ends = seg[SPAN - 1 :: SPAN]
    before = jnp.concatenate([seg[:1], ends[:-1]])
    cols.append((seg == jnp.repeat(before, SPAN)).astype(F32))
    cols.append((seg == jnp.repeat(ends, SPAN)).astype(F32))
    value = seg.astype(F32)
    cols.append(value)
    cols.append(value)
    cols.append(value)
    return jnp.stack(cols, axis=1), value[None, :]


def head_rows(dt_bias, a_log):
    rate = -jnp.exp(a_log)
    rows = jnp.stack([dt_bias, rate * LOG2E, rate] + [jnp.zeros_like(rate)] * 5, axis=0)
    return jnp.pad(rows, ((0, 0), (0, TILE - H)))


BLOCKS = 32
ORDERS = ((8, 1, 4, 2), (8, 2, 4, 1))


def reach(masks):
    out = [0]
    for mask in masks:
        out = out + [mask ^ place for place in out]
    return out


def exchange(values, stage):
    pairs = []
    for shard in range(16):
        for core in range(2):
            pairs.append((shard * 2 + core, (shard ^ ORDERS[core][stage]) * 2 + core))
    return lax.ppermute(values, ("shard", "rep"), pairs)


def swap_cores(values):
    return lax.ppermute(values, "rep", [(0, 1), (1, 0)])


def gather_pieces(local):
    held = local
    arrived = None
    for stage in range(4):
        arrived = exchange(held, stage)
        if stage < 3:
            held = jnp.concatenate([held, arrived], axis=0)
    return held, arrived, swap_cores(held), swap_cores(arrived)


def gather_small(local):
    held = local[None]
    for stage in range(4):
        held = jnp.concatenate([held, exchange(held, stage)], axis=0)
    core = lax.axis_index("rep")
    places = jnp.asarray([reach(order) for order in ORDERS], jnp.int32)[core] ^ lax.axis_index("shard")
    hot = (places[None, :] == jnp.arange(16, dtype=jnp.int32)[:, None]).astype(local.dtype)
    return dot_f32(hot, held, ((1,), (0,)), HIGHEST).astype(local.dtype)


def scatter_sum(mine, other, block):
    arrived = swap_cores(other)
    total = mine.astype(F32) + arrived.astype(F32)
    for stage in (3, 2, 1, 0):
        cut = block << stage
        total = total[:cut] + exchange(total[cut:].astype(BF16), stage).astype(F32)
    return total


def block_order():
    shard = lax.axis_index("shard")
    core = lax.axis_index("rep")
    tables = jnp.asarray([reach(order) for order in ORDERS], jnp.int32)
    inverse = jnp.asarray(
        [[reach(order).index(mask) for mask in range(16)] for order in ORDERS], jnp.int32
    )
    own = 2 * (tables[core] ^ shard) + core
    partner = 2 * (tables[1 - core] ^ shard) + (1 - core)
    order = jnp.concatenate([own, partner])
    natural = jnp.arange(BLOCKS, dtype=jnp.int32)
    which = natural % 2
    place = inverse[which, (natural // 2) ^ shard] + 16 * (which != core).astype(jnp.int32)
    return order, place


def fetch_tile(order_ref, pieces, buffer, sems, tile, slot, block, width):
    for q in range(BLOCKS):
        pltpu.make_async_copy(
            pieces[q // 8].at[pl.ds((q % 8) * block, block), pl.ds(pl.multiple_of(tile * width, width), width)],
            buffer.at[slot, pl.ds(pl.multiple_of(order_ref[q] * block, block), block), :],
            sems.at[slot],
        ).start()


def next_tile(order_ref, pieces, buffer, sems, block, width):
    tile = pl.program_id(0)
    slot = lax.rem(tile, 2)

    @pl.when(tile == 0)
    def _():
        fetch_tile(order_ref, pieces, buffer, sems, tile, slot, block, width)

    @pl.when(tile + 1 < pl.num_programs(0))
    def _():
        fetch_tile(order_ref, pieces, buffer, sems, tile + 1, 1 - slot, block, width)

    pltpu.make_async_copy(buffer.at[slot], buffer.at[slot], sems.at[slot]).wait()
    return slot


def project_kernel(block, width, order_ref, x_ref, p0, p1, p2, p3, *rest):
    out_ref, w_ref, buffer, sems = rest[-4:]
    slot = next_tile(order_ref, (p0, p1, p2, p3), buffer, sems, block, width)
    w = buffer[slot]
    w_ref[...] = w
    for i in range(x_ref.shape[0] // SPAN):
        rows = slice(i * SPAN, (i + 1) * SPAN)
        out_ref[rows] = mm(x_ref[rows], w)


def project(x, pieces, order, so_far, start, full, width=512):
    tokens, depth = x.shape
    columns = pieces[0].shape[1]
    block = depth // BLOCKS
    at = start // width
    any_spec = pl.BlockSpec(memory_space=pl.ANY)
    extra = [] if so_far is None else list(so_far)
    return pl.pallas_call(
        functools.partial(project_kernel, block, width),
        grid_spec=pltpu.PrefetchScalarGridSpec(
            num_scalar_prefetch=1,
            grid=(columns // width,),
            in_specs=[pl.BlockSpec((tokens, depth), lambda j, o: (0, 0))] + [any_spec] * (4 + len(extra)),
            out_specs=[
                pl.BlockSpec((tokens, width), lambda j, o: (0, at + j)),
                pl.BlockSpec((depth, width), lambda j, o: (0, at + j)),
            ],
            scratch_shapes=[pltpu.VMEM((2, depth, width), BF16), pltpu.SemaphoreType.DMA((2,))],
        ),
        out_shape=[jax.ShapeDtypeStruct((tokens, full), F32), jax.ShapeDtypeStruct((depth, full), BF16)],
        input_output_aliases={} if so_far is None else {6: 0, 7: 1},
        cost_estimate=pl.CostEstimate(
            flops=2 * tokens * depth * columns,
            bytes_accessed=4 * depth * columns + 4 * tokens * columns + 2 * tokens * depth,
            transcendentals=0,
        ),
        name="project",
    )(order, x, *pieces, *extra)


def gate_kernel(block, width, order_ref, x_ref, p0, p1, p2, p3, y_ref, gain_ref, *rest):
    gate_ref, w_ref, zg_ref, square_ref, buffer, sems = rest[-6:]
    slot = next_tile(order_ref, (p0, p1, p2, p3), buffer, sems, block, width)
    w = buffer[slot]
    w_ref[...] = w

    @pl.when(pl.program_id(0) == 0)
    def _():
        square_ref[...] = jnp.zeros_like(square_ref)

    for i in range(x_ref.shape[0] // SPAN):
        rows = slice(i * SPAN, (i + 1) * SPAN)
        gate = mm(x_ref[rows], w)
        gate_ref[rows] = gate
        gated = y_ref[rows] * (gate * jax.nn.sigmoid(gate))
        zg_ref[rows] = (gated * gain_ref[...]).astype(BF16)
        square = gated * gated
        total = square[:, :TILE]
        for k in range(1, width // TILE):
            total = total + square[:, k * TILE : (k + 1) * TILE]
        square_ref[rows] += total


def gate_project(x, pieces, order, y, gain, so_far, start, full, width=512):
    tokens, depth = x.shape
    columns = pieces[0].shape[1]
    block = depth // BLOCKS
    at = start // width
    any_spec = pl.BlockSpec(memory_space=pl.ANY)
    extra = [] if so_far is None else list(so_far)
    wide = pl.BlockSpec((tokens, width), lambda j, o: (0, at + j))
    return pl.pallas_call(
        functools.partial(gate_kernel, block, width),
        grid_spec=pltpu.PrefetchScalarGridSpec(
            num_scalar_prefetch=1,
            grid=(columns // width,),
            in_specs=[pl.BlockSpec((tokens, depth), lambda j, o: (0, 0))]
            + [any_spec] * 4
            + [wide, pl.BlockSpec((1, width), lambda j, o: (0, at + j))]
            + [any_spec] * len(extra),
            out_specs=[
                wide,
                pl.BlockSpec((depth, width), lambda j, o: (0, at + j)),
                wide,
                pl.BlockSpec((tokens, TILE), lambda j, o: (0, 0)),
            ],
            scratch_shapes=[pltpu.VMEM((2, depth, width), BF16), pltpu.SemaphoreType.DMA((2,))],
        ),
        out_shape=[
            jax.ShapeDtypeStruct((tokens, full), F32),
            jax.ShapeDtypeStruct((depth, full), BF16),
            jax.ShapeDtypeStruct((tokens, full), BF16),
            jax.ShapeDtypeStruct((tokens, TILE), F32),
        ],
        input_output_aliases={} if so_far is None else {8: 0, 9: 1, 10: 2},
        cost_estimate=pl.CostEstimate(
            flops=2 * tokens * depth * columns,
            bytes_accessed=4 * depth * columns + 10 * tokens * columns + 2 * tokens * depth,
            transcendentals=tokens * columns,
        ),
        name="project_gate",
    )(order, x, *pieces, y, gain, *extra)


def restore_kernel(block, width, order_ref, p0, p1, p2, p3, *rest):
    w_ref, buffer, sems = rest[-3:]
    slot = next_tile(order_ref, (p0, p1, p2, p3), buffer, sems, block, width)
    w_ref[...] = buffer[slot]


def restore(pieces, order, so_far, start, full, width=256):
    columns = pieces[0].shape[1]
    block = pieces[0].shape[0] // 8
    depth = block * BLOCKS
    at = start // width
    any_spec = pl.BlockSpec(memory_space=pl.ANY)
    extra = [] if so_far is None else [so_far]
    return pl.pallas_call(
        functools.partial(restore_kernel, block, width),
        grid_spec=pltpu.PrefetchScalarGridSpec(
            num_scalar_prefetch=1,
            grid=(columns // width,),
            in_specs=[any_spec] * (4 + len(extra)),
            out_specs=pl.BlockSpec((depth, width), lambda j, o: (0, at + j)),
            scratch_shapes=[pltpu.VMEM((2, depth, width), BF16), pltpu.SemaphoreType.DMA((2,))],
        ),
        out_shape=jax.ShapeDtypeStruct((depth, full), BF16),
        input_output_aliases={} if so_far is None else {5: 0},
        cost_estimate=pl.CostEstimate(flops=0, bytes_accessed=4 * depth * columns, transcendentals=0),
        name="restore",
    )(order, *pieces, *extra)


def weight_grad_kernel(block, place_ref, lhs_ref, rhs_ref, mine, other, buffer, sems):
    step = pl.program_id(0)
    slot = lax.rem(step, 2)

    def settle(which):
        pltpu.make_async_copy(buffer.at[which], buffer.at[which], sems.at[which]).wait()

    @pl.when(step >= 2)
    def _():
        settle(slot)

    buffer[slot] = dot_f32(lhs_ref[...], rhs_ref[...], ((0,), (0,))).astype(BF16)
    for t in range(8):
        q = place_ref[step * 8 + t]
        source = buffer.at[slot, pl.ds(t * block, block), :]

        @pl.when(q < 16)
        def _():
            pltpu.make_async_copy(
                source, mine.at[pl.ds(pl.multiple_of(q * block, block), block), :], sems.at[slot]
            ).start()

        @pl.when(q >= 16)
        def _():
            pltpu.make_async_copy(
                source, other.at[pl.ds(pl.multiple_of((q - 16) * block, block), block), :], sems.at[slot]
            ).start()

    @pl.when(step == pl.num_programs(0) - 1)
    def _():
        settle(1 - slot)
        settle(slot)


def weight_grad(lhs, rhs, place, column, columns):
    tokens, rows = lhs.shape
    block = rows // BLOCKS
    any_spec = pl.BlockSpec(memory_space=pl.ANY)
    out = jax.ShapeDtypeStruct((16 * block, columns), BF16)
    return pl.pallas_call(
        functools.partial(weight_grad_kernel, block),
        grid_spec=pltpu.PrefetchScalarGridSpec(
            num_scalar_prefetch=1,
            grid=(4,),
            in_specs=[
                pl.BlockSpec((tokens, 8 * block), lambda i, o: (0, i)),
                pl.BlockSpec((tokens, columns), lambda i, o: (0, column)),
            ],
            out_specs=[any_spec, any_spec],
            scratch_shapes=[pltpu.VMEM((2, 8 * block, columns), BF16), pltpu.SemaphoreType.DMA((2,))],
        ),
        out_shape=[out, out],
        cost_estimate=pl.CostEstimate(
            flops=2 * tokens * rows * columns,
            bytes_accessed=2 * (tokens * rows + tokens * columns + rows * columns),
            transcendentals=0,
        ),
        name="weight_grad",
    )(place, lhs, rhs)


def rows_of(packed, start, count):
    return packed[:, start : start + count]


def on_device(
    hypercube,
    tokens,
    seg_ids,
    gain_in,
    w_in,
    conv_weight,
    conv_bias,
    dt_bias,
    a_log,
    d_skip,
    gain_out,
    w_out,
    cotangent,
):
    shards = lax.psum(1, "shard")
    taps, conv_local = conv_weight.shape
    model = tokens.shape[1]
    di = gain_out.shape[0] * shards
    conv_dim = conv_local * shards
    wide = -(-(conv_dim + TILE) // 512) * 512
    cuts = ((0, 1024), (1024, 1024), (2048, wide - 2048))
    halves = ((0, di // 2), (di // 2, di // 2))
    thirds = ((0, model // 2), (model // 2, model // 2))

    small = jnp.concatenate([conv_weight.reshape(-1), conv_bias, gain_in, gain_out])
    if hypercube:
        core = lax.axis_index("rep")
        order, place = block_order()
        small_all = gather_small(small)
        w_half = lax.dynamic_slice_in_dim(w_in, core * (w_in.shape[0] // 2), w_in.shape[0] // 2, 0)
        o_half = lax.dynamic_slice_in_dim(w_out, core * (w_out.shape[0] // 2), w_out.shape[0] // 2, 0)
        rest = jnp.pad(w_half[:, di:], ((0, 0), (0, wide - (w_in.shape[1] - di))))
        conv_pieces = [gather_pieces(rest[:, a : a + n]) for a, n in cuts]
        gate_pieces = [gather_pieces(w_half[:, a : a + n]) for a, n in halves]
        out_pieces = [gather_pieces(o_half[:, a : a + n]) for a, n in thirds]
    else:
        small_all = lax.all_gather(small, "shard", axis=0, tiled=False)
        full_w_in = lax.all_gather(w_in, "shard", axis=0, tiled=True)
        full_w_out = lax.all_gather(w_out, "shard", axis=0, tiled=True)
    cut = taps * conv_local
    conv_w = small_all[:, :cut].reshape(shards, taps, conv_local).transpose(1, 0, 2).reshape(taps, -1)
    conv_b = rows_of(small_all, cut, conv_local).reshape(1, -1)
    cut += conv_local
    full_gain_in = rows_of(small_all, cut, gain_in.shape[0]).reshape(1, -1).astype(F32)
    full_gain_out = rows_of(small_all, cut + gain_in.shape[0], gain_out.shape[0]).reshape(1, -1).astype(F32)
    conv_all = jnp.concatenate(
        [conv_w.astype(F32), conv_b.astype(F32), jnp.zeros((3, conv_dim), F32)], axis=0
    )
    inputs = tokens.astype(F32)
    rscale = lax.rsqrt(jnp.mean(inputs * inputs, axis=1, keepdims=True) + EPSILON)
    unit = inputs * rscale
    normed = (unit * full_gain_in).astype(BF16)
    aux, seg_row = seg_facts(seg_ids[0])
    heads = head_rows(dt_bias, a_log)
    skip = jnp.repeat(d_skip, P_SIZE)[None]

    if hypercube:
        front = None
        for (a, n), pieces in zip(cuts, conv_pieces):
            front = project(normed, pieces, order, front, a, wide)
        pc, w_rest = front
    else:
        w_gate = full_w_in[:, :di]
        w_rest = jnp.pad(full_w_in[:, di:], ((0, 0), (0, wide - (w_in.shape[1] - di))))
        pc = mm(normed, w_rest)
    x, bcv, y, states = run_forward(pc, conv_all, aux, seg_row, heads, skip)
    if hypercube:
        part = None
        squares = 0.0
        for (a, n), pieces in zip(halves, gate_pieces):
            *part, square = gate_project(normed, pieces, order, y, full_gain_out, part, a, di)
            squares = squares + square
        gate, w_gate, zg = part
        full_w_out = None
        for (a, n), pieces in zip(thirds, out_pieces):
            full_w_out = restore(pieces, order, full_w_out, a, model)
        gated = y * (gate * jax.nn.sigmoid(gate))
    else:
        gate = mm(normed, w_gate)
        gated = y * (gate * jax.nn.sigmoid(gate))
        squares = gated * gated
        zg = (gated * full_gain_out).astype(BF16)
    inverse = lax.rsqrt(jnp.sum(squares, axis=1, keepdims=True) / di + EPSILON)
    projected = inverse * mm(zg, full_w_out)
    output = (inputs + projected).astype(BF16)
    cot = cotangent.astype(F32)
    dots = jnp.sum(cot * projected, axis=1, keepdims=True)
    cot_scaled = (inverse * cot).astype(BF16)
    grad_ynorm = mm_nt(cotangent, full_w_out)
    dz = inverse * (full_gain_out * grad_ynorm) - gated * (inverse * inverse * dots / di)
    sig = jax.nn.sigmoid(gate)
    dy = (dz * (gate * sig)).astype(BF16)
    dgate = (dz * y * (sig * (1.0 + gate * (1.0 - sig)))).astype(BF16)
    if hypercube:
        out_sum = scatter_sum(*weight_grad(zg, cot_scaled, place, 0, model), w_out.shape[0] // 2)
        gate_sums = [
            scatter_sum(*weight_grad(normed, dgate, place, k, n), w_in.shape[0] // 2)
            for k, (a, n) in enumerate(halves)
        ]
    dproj, dcw, dbcw, dskip, dhead = run_backward(
        dy, x, bcv, states, pc, conv_all, aux, seg_row, heads, skip
    )
    scaled = (mm_nt(dgate, w_gate) + mm_nt(dproj, w_rest)) * full_gain_in
    inner = jnp.mean(unit * scaled, axis=1, keepdims=True)
    grad_tokens = (cot + rscale * (scaled - unit * inner)).astype(BF16)

    conv_sums = jnp.concatenate([dcw, dbcw], axis=2).sum(1)
    conv_sums = jnp.concatenate([conv_sums[4:5], conv_sums[3:4], conv_sums[2:3], conv_sums[1:2], conv_sums[0:1]])
    per_head = jnp.concatenate(
        [
            dhead[0].sum(0)[:H],
            dhead[1].sum(0)[:H] * -jnp.exp(a_log),
            dskip.sum(0).reshape(H, P_SIZE).sum(1),
        ]
    )
    conv_part = conv_sums.reshape(taps + 1, shards, conv_local).transpose(1, 0, 2).reshape(shards, -1)
    small_grad = jnp.concatenate([conv_part, jnp.broadcast_to(per_head[None], (shards, 3 * H))], axis=1)
    real = w_in.shape[1] - di
    if hypercube:
        small_sum = reduce_small(small_grad)[0]
        rest_sums = []
        for k, (a, n) in enumerate(cuts):
            part = (dproj, k) if a == k * n else (dproj[:, a : a + n], 0)
            rest_sums.append(scatter_sum(*weight_grad(normed, part[0], place, part[1], n), w_in.shape[0] // 2))
        rest_sums[-1] = rest_sums[-1][:, : real - cuts[-1][0]]
        own = jnp.concatenate(gate_sums + rest_sums, axis=1)
        sum_w_in = both_cores(own)
        sum_w_out = both_cores(out_sum)
    else:
        grad_w_out = dot_f32(zg, cot_scaled, ((0,), (0,)))
        grads = jnp.concatenate([dgate, dproj[:, :real]], axis=1)
        grad_w_in = dot_f32(normed, grads, ((0,), (0,)))
        small_sum = lax.psum(
            lax.psum_scatter(small_grad, "shard", scatter_dimension=0, tiled=True), "rep"
        )[0]
        sum_w_in = lax.psum_scatter(grad_w_in, "shard", scatter_dimension=0, tiled=True)
        sum_w_out = lax.psum_scatter(grad_w_out, "shard", scatter_dimension=0, tiled=True)
        sum_w_in, sum_w_out = lax.psum((sum_w_in, sum_w_out), "rep")
    grad_gain_in = jnp.sum(sum_w_in * w_in.astype(F32), axis=1) / gain_in.astype(F32)
    grad_gain_out = jnp.sum(sum_w_out * w_out.astype(F32), axis=1) / gain_out.astype(F32)
    cut = taps * conv_local
    head_at = cut + conv_local
    return (
        output,
        grad_tokens,
        grad_gain_in,
        sum_w_in,
        small_sum[:cut].reshape(taps, conv_local),
        small_sum[cut:head_at],
        small_sum[head_at : head_at + H],
        small_sum[head_at + H : head_at + 2 * H],
        small_sum[head_at + 2 * H :],
        grad_gain_out,
        sum_w_out,
    )


def both_cores(own):
    partner = swap_cores(own)
    first = lax.axis_index("rep") == 0
    return jnp.concatenate([jnp.where(first, own, partner), jnp.where(first, partner, own)], axis=0)


def reduce_small(rows):
    core = lax.axis_index("rep")
    places = jnp.asarray([reach(order) for order in ORDERS], jnp.int32)[core] ^ lax.axis_index("shard")
    hot = (places[:, None] == jnp.arange(16, dtype=jnp.int32)[None, :]).astype(F32)
    total = dot_f32(hot, rows, ((1,), (0,)), HIGHEST)
    for stage in (3, 2, 1, 0):
        cut = 1 << stage
        total = total[:cut] + exchange(total[cut:], stage)
    return total + swap_cores(total)


def solution(mesh):
    rows = P(("shard", "rep"), None)
    in_specs = (
        rows, rows, P("shard"), P("shard", None), P(None, "shard"), P("shard"), P(), P(), P(), P("shard"),
        P("shard", None), rows,
    )
    out_specs = (
        rows, rows, P("shard"), P("shard", None), P(None, "shard"), P("shard"), P(), P(), P(), P("shard"),
        P("shard", None),
    )
    hypercube = mesh.shape["shard"] == 16 and mesh.shape["rep"] == 2
    return jax.shard_map(
        functools.partial(on_device, hypercube),
        mesh=mesh,
        in_specs=in_specs,
        out_specs=out_specs,
        check_vma=False,
    )
```

```python
import functools

import jax
import jax.numpy as jnp
from jax import lax
from jax.experimental import pallas as pl
from jax.experimental.pallas import tpu as pltpu
from jax.sharding import PartitionSpec as P

H = 48
P_SIZE = 64
N = 128
SPAN = 256
HALF = 128
GROUP = 8
TILE = 128
EPSILON = 1e-05
HIGHEST = lax.Precision.HIGHEST
LOG2E = 1.4426950408889634
NEG = -1e30
F32 = jnp.float32
BF16 = jnp.bfloat16


def dot_f32(a, b, contract, precision=None):
    return lax.dot_general(
        a, b, ((contract[0], contract[1]), ((), ())), preferred_element_type=F32, precision=precision
    )


def mm(a, b):
    return dot_f32(a, b, ((1,), (0,)))


def mm_nt(a, b):
    return dot_f32(a, b, ((1,), (1,)))


def lanes_of(column, rows):
    return jnp.broadcast_to(column, (rows, TILE))


def step_sizes(raw, heads):
    shifted = raw + heads[0:1]
    return jnp.maximum(shifted, 0.0) + jnp.log1p(jnp.exp(-jnp.abs(shifted)))


def conv_taps(ext, same, start, width, rows=SPAN):
    out = [ext[8 : 8 + rows, start : start + width]]
    for offset in (1, 2, 3):
        moved = ext[8 - offset : 8 - offset + rows, start : start + width]
        mask = same[offset - 1]
        if width > TILE:
            mask = jnp.concatenate([mask] * (width // TILE), axis=1)
        out.append(moved * mask)
    return out


def conv_sum(taps, weights):
    total = weights[4:5] + weights[3:4] * taps[0]
    for offset in (1, 2, 3):
        total = total + weights[3 - offset : 4 - offset] * taps[offset]
    return total


def prepare(raw_ref, heads_ref, aux_ref, pack_a, pack_b, cum_rows, same):
    aux = aux_ref[...]
    heads = heads_ref[...]
    step = step_sizes(raw_ref[...], heads)
    row = lax.broadcasted_iota(jnp.int32, (SPAN, SPAN), 0)
    col = lax.broadcasted_iota(jnp.int32, (SPAN, SPAN), 1)
    tri = (row >= col).astype(F32)
    cum = dot_f32(tri, step * heads[1:2], ((1,), (0,)), HIGHEST)
    last = cum[SPAN - 1 : SPAN]
    entry = jnp.exp2(cum) * lanes_of(aux[:, 3:4], SPAN)
    tail = jnp.exp2(last - cum) * lanes_of(aux[:, 4:5], SPAN)
    lane = lax.broadcasted_iota(jnp.int32, (SPAN, TILE), 1)
    low = lane < 64
    pack_a[...] = jnp.where(low, cum, pltpu.roll(step, 64, 1))
    pack_b[...] = jnp.where(low, entry, pltpu.roll(tail, 64, 1))
    cum_rows[...] = cum.T
    for offset in (1, 2, 3):
        same[offset - 1] = lanes_of(aux[:, offset - 1 : offset], SPAN)


def forward_kernel(
    pc_ref, halo_ref, bc_ref, bc_halo_ref, raw_ref, cw_ref, bcw_ref, aux_ref, seg_ref, heads_ref, skip_ref,
    x_out, bc_out, y_out, st_out,
    state, scores, block, same, pack_a, pack_b, cum_rows, b_t, ext, ext_bc, halo_bf,
):
    span = pl.program_id(0)
    group = pl.program_id(1)

    @pl.when((span == 0) & (group == 0))
    def _():
        state[...] = jnp.zeros_like(state)

    @pl.when(group == 0)
    def _():
        prepare(raw_ref, heads_ref, aux_ref, pack_a, pack_b, cum_rows, same)
        ext_bc[0:8] = bc_halo_ref[...]
        ext_bc[8:] = bc_ref[...]
        total = conv_sum(conv_taps(ext_bc, same, 0, 2 * N), bcw_ref[...])
        both = (total * jax.nn.sigmoid(total)).astype(BF16)
        bc_out[...] = both
        keys, query = both[:, :N], both[:, N:]
        row = lax.broadcasted_iota(jnp.int32, (SPAN, SPAN), 0)
        col = lax.broadcasted_iota(jnp.int32, (SPAN, SPAN), 1)
        linked = (row >= col) & (aux_ref[:, 5:6] == seg_ref[...])
        block[...] = jnp.where(linked, 0.0, NEG)
        scores[...] = mm_nt(query, keys)
        b_t[...] = keys.T

    ext[0:8] = halo_ref[...]
    ext[8:] = pc_ref[...]
    shift = (TILE - GROUP * group) % TILE
    cols_a = pltpu.roll(pack_a[...], shift, 1)
    cols_b = pltpu.roll(pack_b[...], shift, 1)
    retain = cols_b[SPAN - 1 : SPAN]
    lane = lax.broadcasted_iota(jnp.int32, (SPAN, TILE), 1)
    first = lane < P_SIZE
    query = bc_out[:, N:]
    for pair in range(GROUP // 2):
        at = pair * TILE
        total = conv_sum(conv_taps(ext, same, at, TILE), cw_ref[:, at : at + TILE])
        x = total * jax.nn.sigmoid(total)
        xb = x.astype(BF16)
        x_out[:, at : at + TILE] = xb
        here = group * (GROUP // 2) * TILE + at
        tile = pl.ds(pl.multiple_of(here, TILE), TILE)
        old = state[:, tile]
        old_b = old.astype(BF16)
        st_out[:, at : at + TILE] = old_b
        parts = []
        for head in (2 * pair, 2 * pair + 1):
            cum_col = lanes_of(cols_a[:, head : head + 1], SPAN)
            cum_row = cum_rows[pl.ds(group * GROUP + head, 1), :]
            blocks = []
            for i, j in ((0, 0), (1, 0), (1, 1)):
                rows = slice(i * HALF, (i + 1) * HALF)
                cols = slice(j * HALF, (j + 1) * HALF)
                gap = cum_col[rows] - cum_row[:, cols] + block[rows, cols]
                blocks.append((jnp.exp2(gap) * scores[rows, cols]).astype(BF16))
            parts.append(blocks)
        step_pair = jnp.where(
            first,
            lanes_of(cols_a[:, 64 + 2 * pair : 65 + 2 * pair], SPAN),
            lanes_of(cols_a[:, 65 + 2 * pair : 66 + 2 * pair], SPAN),
        )
        xs = xb.astype(F32) * step_pair
        xsb = xs.astype(BF16)
        outs = []
        for blocks in parts:
            top = mm(blocks[0], xsb[:HALF])
            bottom = mm(jnp.concatenate(blocks[1:], axis=1), xsb)
            outs.append(jnp.concatenate([top, bottom], axis=0))
        entry_pair = jnp.where(
            first,
            lanes_of(cols_b[:, 2 * pair : 2 * pair + 1], SPAN),
            lanes_of(cols_b[:, 2 * pair + 1 : 2 * pair + 2], SPAN),
        )
        tail_pair = jnp.where(
            first,
            lanes_of(cols_b[:, 64 + 2 * pair : 65 + 2 * pair], SPAN),
            lanes_of(cols_b[:, 65 + 2 * pair : 66 + 2 * pair], SPAN),
        )
        carried = mm(query, old_b)
        y_out[:, at : at + TILE] = (
            jnp.where(first, outs[0], outs[1])
            + entry_pair * carried
            + skip_ref[:, at : at + TILE] * xb.astype(F32)
        )
        retain_pair = jnp.where(
            first[:N],
            jnp.broadcast_to(retain[:, 2 * pair : 2 * pair + 1], (N, TILE)),
            jnp.broadcast_to(retain[:, 2 * pair + 1 : 2 * pair + 2], (N, TILE)),
        )
        state[:, tile] = old * retain_pair + mm(b_t[...], (xs * tail_pair).astype(BF16))


def run_forward(pc, conv_all, aux, seg_row, heads, skip):
    tokens = pc.shape[0]
    spans = tokens // SPAN
    di = skip.shape[1]
    raw_block = (di + 2 * N) // TILE
    width = GROUP * P_SIZE
    groups = di // width
    last_block = di // (2 * N)
    grid_spec = pltpu.PrefetchScalarGridSpec(
        num_scalar_prefetch=0,
        grid=(spans, groups),
        in_specs=[
            pl.BlockSpec((SPAN, width), lambda s, g: (s, g)),
            pl.BlockSpec((8, width), lambda s, g: (jnp.maximum(s * (SPAN // 8) - 1, 0), g)),
            pl.BlockSpec((SPAN, 2 * N), lambda s, g: (s, last_block)),
            pl.BlockSpec((8, 2 * N), lambda s, g: (jnp.maximum(s * (SPAN // 8) - 1, 0), last_block)),
            pl.BlockSpec((SPAN, TILE), lambda s, g: (s, raw_block)),
            pl.BlockSpec((8, width), lambda s, g: (0, g)),
            pl.BlockSpec((8, 2 * N), lambda s, g: (0, last_block)),
            pl.BlockSpec((SPAN, 8), lambda s, g: (s, 0)),
            pl.BlockSpec((1, SPAN), lambda s, g: (0, s)),
            pl.BlockSpec((8, TILE), lambda s, g: (0, 0)),
            pl.BlockSpec((1, width), lambda s, g: (0, g)),
        ],
        out_specs=[
            pl.BlockSpec((SPAN, width), lambda s, g: (s, g)),
            pl.BlockSpec((SPAN, 2 * N), lambda s, g: (s, 0)),
            pl.BlockSpec((SPAN, width), lambda s, g: (s, g)),
            pl.BlockSpec((N, width), lambda s, g: (s, g)),
        ],
        scratch_shapes=[
            pltpu.VMEM((N, di), F32),
            pltpu.VMEM((SPAN, SPAN), F32),
            pltpu.VMEM((SPAN, SPAN), F32),
            pltpu.VMEM((3, SPAN, TILE), F32),
            pltpu.VMEM((SPAN, TILE), F32),
            pltpu.VMEM((SPAN, TILE), F32),
            pltpu.VMEM((TILE, SPAN), F32),
            pltpu.VMEM((N, SPAN), BF16),
            pltpu.VMEM((SPAN + 8, width), F32),
            pltpu.VMEM((SPAN + 8, 2 * N), F32),
            pltpu.VMEM((8, TILE), F32),
        ],
    )
    return pl.pallas_call(
        forward_kernel,
        grid_spec=grid_spec,
        out_shape=[
            jax.ShapeDtypeStruct((tokens, di), BF16),
            jax.ShapeDtypeStruct((tokens, 2 * N), BF16),
            jax.ShapeDtypeStruct((tokens, di), F32),
            jax.ShapeDtypeStruct((spans * N, di), BF16),
        ],
        compiler_params=pltpu.CompilerParams(dimension_semantics=("arbitrary", "arbitrary")),
        cost_estimate=pl.CostEstimate(flops=int(3.5e10), bytes_accessed=40 * tokens * di, transcendentals=0),
        name="scan_forward",
    )(pc, pc, pc, pc, pc, conv_all, conv_all, aux, seg_row, heads, skip)


def conv_back(grad, ext, same, weights, carry, start, width):
    taps = conv_taps(ext, same, start, width)
    total = conv_sum(taps, weights)
    gate = jax.nn.sigmoid(total)
    du = grad * (gate * (1.0 + total * (1.0 - gate)))
    row_index = lax.broadcasted_iota(jnp.int32, (SPAN, width), 0)
    out = weights[3:4] * du
    sums = [jnp.sum(du.reshape(SPAN // 8, 8, width), axis=0)]
    sums.append(jnp.sum((du * taps[0]).reshape(SPAN // 8, 8, width), axis=0))
    for offset in (1, 2, 3):
        mask = same[offset - 1]
        if width > TILE:
            mask = jnp.concatenate([mask] * (width // TILE), axis=1)
        masked = du * mask
        after = carry[offset - 1]
        moved = jnp.concatenate([masked, after], axis=0)[offset : offset + SPAN]
        carry[offset - 1] = masked[0:8]
        out = out + weights[3 - offset : 4 - offset] * moved
        sums.append(jnp.sum((du * taps[offset]).reshape(SPAN // 8, 8, width), axis=0))
    return out, sums


def backward_kernel(
    first_call, last_call,
    dy_ref, x_ref, bcv_ref, st_ref, pc_ref, halo_ref, bc_ref, bc_halo_ref, raw_ref, cw_ref, bcw_ref,
    aux_ref, seg_ref, heads_ref, skip_ref, *rest,
):
    rest = list(rest)
    before = None if first_call else [rest.pop(0) for _ in range(4)]
    dproj_out, dcw_out, dskip_out = [rest.pop(0) for _ in range(3)]
    if last_call:
        dbcw_out, dhead_out = [rest.pop(0) for _ in range(2)]
        after = None
    else:
        after = [rest.pop(0) for _ in range(4)]
    (
        dstate, scores, block, dscores, same, pack_a, pack_b, cum_rows, c_t, ext, ext_bc,
        carry, carry_bc, d_bc, per_row, dcum_rows, dlast, base,
    ) = rest
    back = pl.program_id(0)
    group = pl.program_id(1)
    spans = pl.num_programs(0)
    groups = pl.num_programs(1)
    width = GROUP * P_SIZE
    group_head = base[0] + GROUP * group

    @pl.when((back == 0) & (group == 0))
    def _():
        dstate[...] = jnp.zeros_like(dstate)
        carry[...] = jnp.zeros_like(carry)
        dcw_out[...] = jnp.zeros_like(dcw_out)
        dskip_out[...] = jnp.zeros_like(dskip_out)
        dcum_rows[...] = jnp.zeros_like(dcum_rows)
        if last_call:
            carry_bc[...] = jnp.zeros_like(carry_bc)
            dbcw_out[...] = jnp.zeros_like(dbcw_out)
            dhead_out[...] = jnp.zeros_like(dhead_out)

    keys = bcv_ref[:, :N]
    query = bcv_ref[:, N:]

    @pl.when(group == 0)
    def _():
        prepare(raw_ref, heads_ref, aux_ref, pack_a, pack_b, cum_rows, same)
        row = lax.broadcasted_iota(jnp.int32, (SPAN, SPAN), 0)
        col = lax.broadcasted_iota(jnp.int32, (SPAN, SPAN), 1)
        linked = (row <= col) & (aux_ref[:, 5:6] == seg_ref[...])
        block[...] = jnp.where(linked, 0.0, NEG)
        scores[...] = mm_nt(keys, query)
        c_t[...] = query.T
        per_row[...] = jnp.zeros_like(per_row)
        if first_call:
            dscores[...] = jnp.zeros_like(dscores)
            d_bc[...] = jnp.zeros_like(d_bc)
            dlast[...] = jnp.zeros_like(dlast)
        else:
            dscores[...] = before[0][...]
            d_bc[...] = before[1][...]
            per_row[0] = before[2][:, :TILE]
            per_row[2] = before[2][:, TILE:]
            dlast[...] = before[3][...]

    ext[0:8] = halo_ref[...]
    ext[8:] = pc_ref[...]
    shift = lax.rem(TILE - group_head, TILE)
    cols_a = pltpu.roll(pack_a[...], shift, 1)
    cols_b = pltpu.roll(pack_b[...], shift, 1)
    retain = cols_b[SPAN - 1 : SPAN]
    lane = lax.broadcasted_iota(jnp.int32, (SPAN, TILE), 1)
    first = lane < P_SIZE
    lane_row = lax.broadcasted_iota(jnp.int32, (TILE, TILE), 0)
    lane_col = lax.broadcasted_iota(jnp.int32, (TILE, TILE), 1)
    sums = jnp.zeros((SPAN, TILE), F32)
    last_sum = jnp.zeros((1, TILE), F32)
    group_at = group * width
    for pair in range(GROUP // 2):
        at = pair * TILE
        tile = pl.ds(pl.multiple_of(group_at + at, TILE), TILE)
        dy = dy_ref[:, at : at + TILE]
        dyf = dy.astype(F32)
        xf = x_ref[:, at : at + TILE].astype(F32)
        step_pair = jnp.where(
            first,
            lanes_of(cols_a[:, 64 + 2 * pair : 65 + 2 * pair], SPAN),
            lanes_of(cols_a[:, 65 + 2 * pair : 66 + 2 * pair], SPAN),
        )
        entry_pair = jnp.where(
            first,
            lanes_of(cols_b[:, 2 * pair : 2 * pair + 1], SPAN),
            lanes_of(cols_b[:, 2 * pair + 1 : 2 * pair + 2], SPAN),
        )
        tail_pair = jnp.where(
            first,
            lanes_of(cols_b[:, 64 + 2 * pair : 65 + 2 * pair], SPAN),
            lanes_of(cols_b[:, 65 + 2 * pair : 66 + 2 * pair], SPAN),
        )
        xs = xf * step_pair
        inner = []
        for which in (0, 1):
            head = 2 * pair + which
            mine = first if which == 0 else ~first
            xh = jnp.where(mine, xs, 0.0).astype(BF16)
            cum_col = lanes_of(cols_a[:, head : head + 1], SPAN)
            cum_row = cum_rows[pl.ds(group_head + head, 1), :]
            g_top = mm_nt(xh[:HALF], dy)
            g_bottom = mm_nt(xh[HALF:], dy[HALF:])
            mixes = []
            across = []
            down = []
            for j, i in ((0, 0), (0, 1), (1, 1)):
                rows = slice(j * HALF, (j + 1) * HALF)
                cols = slice(i * HALF, (i + 1) * HALF)
                decay = jnp.exp2(cum_row[:, cols] - cum_col[rows] + block[rows, cols])
                mix = decay * scores[rows, cols]
                g = g_bottom if j == 1 else g_top[:, cols]
                dscores[rows, cols] += decay * g
                w = mix * g
                mixes.append(mix.astype(BF16))
                across.append(w)
                down.append(jnp.sum(w, axis=0, keepdims=True))
            row_sum = jnp.concatenate(
                [
                    jnp.sum(across[0] + across[1], axis=1, keepdims=True),
                    jnp.sum(across[2], axis=1, keepdims=True),
                ],
                axis=0,
            )
            sums = sums - jnp.where(lane == 2 * GROUP + head, row_sum, 0.0)
            dcum_rows[pl.ds(group_head + head, 1), :] = jnp.concatenate([down[0], down[1] + down[2]], axis=1)
            top = mm(jnp.concatenate(mixes[:2], axis=1), dy)
            bottom = mm(mixes[2], dy[HALF:])
            inner.append(jnp.concatenate([top, bottom], axis=0))
        stb = st_ref[:, at : at + TILE]
        stf = stb.astype(F32)
        ds = dstate[:, tile]
        dsb = ds.astype(BF16)
        dye_f = dyf * entry_pair
        dye = dye_f.astype(BF16)
        fresh = mm(keys, dsb) * tail_pair
        total = jnp.where(first, inner[0], inner[1]) + fresh
        carried = mm(query, stb)
        d_bc[:, N:] += mm_nt(dye, stb)
        d_bc[:, :N] += mm_nt((xs * tail_pair).astype(BF16), dsb)

        def head_sum(values, kind):
            spread = (lane_col == kind * GROUP + 2 * pair + (lane_row >= P_SIZE).astype(jnp.int32)).astype(BF16)
            high = values.astype(BF16)
            rest = (values - high.astype(F32)).astype(BF16)
            return mm(high, spread) + mm(rest, spread)

        sums = sums + head_sum(xf * total, 0) + head_sum(xs * fresh, 1) + head_sum(dye_f * carried, 2)
        retain_pair = jnp.where(
            first[:N],
            jnp.broadcast_to(retain[:, 2 * pair : 2 * pair + 1], (N, TILE)),
            jnp.broadcast_to(retain[:, 2 * pair + 1 : 2 * pair + 2], (N, TILE)),
        )
        kept = ds * retain_pair
        kept_sum = jnp.sum(kept * stf, axis=0, keepdims=True)
        low_sum = jnp.sum(jnp.where(first[0:1], kept_sum, 0.0), axis=1, keepdims=True)
        high_sum = jnp.sum(jnp.where(first[0:1], 0.0, kept_sum), axis=1, keepdims=True)
        last_sum = last_sum + jnp.where(lane[0:1] == 2 * pair, low_sum, 0.0)
        last_sum = last_sum + jnp.where(lane[0:1] == 2 * pair + 1, high_sum, 0.0)
        dstate[:, tile] = kept + mm(c_t[...], dye)
        dx = total * step_pair + skip_ref[:, at : at + TILE] * dyf
        dskip_out[:, tile] += jnp.sum((dyf * xf).reshape(SPAN // 8, 8, TILE), axis=0)
        out, conv_sums = conv_back(
            dx, ext, same, cw_ref[:, at : at + TILE], carry.at[:, :, tile], at, TILE
        )
        dproj_out[:, tile] = out.astype(BF16)
        for k, value in enumerate(conv_sums):
            dcw_out[k, :, tile] += value

    in_place = (lane >= group_head) & (lane < group_head + GROUP)
    for kind in range(3):
        moved = pltpu.roll(sums, lax.rem(group_head + TILE - GROUP * kind, TILE), 1)
        per_row[kind] += jnp.where(in_place, moved, 0.0)
    moved = pltpu.roll(jnp.broadcast_to(last_sum, (8, TILE)), group_head, 1)
    dlast[...] += jnp.where(in_place[0:8], moved, 0.0)

    @pl.when(group == groups - 1)
    def _():
        state_part = per_row[1]
        dcum = dcum_rows[...].T + per_row[2] - state_part
        dlast_all = dlast[0:1] + jnp.sum(state_part, axis=0, keepdims=True)
        if not last_call:
            after[0][...] = dscores[...]
            after[1][...] = d_bc[...]
            after[2][:, :TILE] = per_row[0]
            after[2][:, TILE:] = dcum
            after[3][...] = jnp.broadcast_to(dlast_all, (8, TILE))
            return
        start = groups * width
        ds_b = dscores[...].astype(BF16)
        grad_b = d_bc[:, :N] + mm(ds_b, query)
        grad_c = d_bc[:, N:] + mm(dscores[...].T.astype(BF16), keys)
        ext_bc[0:8] = bc_halo_ref[...]
        ext_bc[8:] = bc_ref[...]
        grad = jnp.concatenate([grad_b, grad_c], axis=1)
        out, conv_sums = conv_back(grad, ext_bc, same, bcw_ref[...], carry_bc, 0, 2 * N)
        dproj_out[:, start : start + 2 * N] = out.astype(BF16)
        for k, value in enumerate(conv_sums):
            dbcw_out[k] += value
        heads = heads_ref[...]
        raw = raw_ref[...]
        step = step_sizes(raw, heads)
        row = lax.broadcasted_iota(jnp.int32, (SPAN, SPAN), 0)
        col = lax.broadcasted_iota(jnp.int32, (SPAN, SPAN), 1)
        tri = (row <= col).astype(F32)
        da = dot_f32(tri, dcum, ((1,), (0,)), HIGHEST) + dlast_all
        dstep = per_row[0] + da * heads[2:3]
        draw = dstep * jax.nn.sigmoid(raw + heads[0:1])
        live = lane < H
        draw = jnp.where(live, draw, 0.0)
        dproj_out[:, start + 2 * N : start + 2 * N + TILE] = draw.astype(BF16)
        dproj_out[:, start + 2 * N + TILE :] = jnp.zeros_like(dproj_out[:, start + 2 * N + TILE :])
        dhead_out[0] += jnp.sum(draw.reshape(SPAN // 8, 8, TILE), axis=0)
        dhead_out[1] += jnp.sum(jnp.where(live, da * step, 0.0).reshape(SPAN // 8, 8, TILE), axis=0)


def run_backward(dy, x, bcv, states, pc, conv_all, aux, seg_row, heads, skip, start, count, last, before):
    tokens, di = dy.shape
    full = pc.shape[1]
    raw_block = (di + 2 * N) // TILE
    spans = tokens // SPAN
    width = GROUP * P_SIZE
    last_block = di // (2 * N)
    turn = lambda s: spans - 1 - s
    halo = lambda s: jnp.maximum(turn(s) * (SPAN // 8) - 1, 0)
    own = count * width
    out_width = own + (full - di if last else 0)
    sums_specs = [
        pl.BlockSpec((SPAN, SPAN), lambda s, g: (turn(s), 0)),
        pl.BlockSpec((SPAN, 2 * N), lambda s, g: (turn(s), 0)),
        pl.BlockSpec((SPAN, 2 * TILE), lambda s, g: (turn(s), 0)),
        pl.BlockSpec((8, TILE), lambda s, g: (turn(s), 0)),
    ]
    sums_shapes = [
        jax.ShapeDtypeStruct((tokens, SPAN), F32),
        jax.ShapeDtypeStruct((tokens, 2 * N), F32),
        jax.ShapeDtypeStruct((tokens, 2 * TILE), F32),
        jax.ShapeDtypeStruct((spans * 8, TILE), F32),
    ]
    out_specs = [
        pl.BlockSpec((SPAN, out_width), lambda s, g: (turn(s), 0)),
        pl.BlockSpec((5, 8, own), lambda s, g: (0, 0, 0)),
        pl.BlockSpec((8, own), lambda s, g: (0, 0)),
    ]
    out_shape = [
        jax.ShapeDtypeStruct((tokens, out_width), BF16),
        jax.ShapeDtypeStruct((5, 8, own), F32),
        jax.ShapeDtypeStruct((8, own), F32),
    ]
    if last:
        out_specs += [
            pl.BlockSpec((5, 8, 2 * N), lambda s, g: (0, 0, 0)),
            pl.BlockSpec((2, 8, TILE), lambda s, g: (0, 0, 0)),
        ]
        out_shape += [
            jax.ShapeDtypeStruct((5, 8, 2 * N), F32),
            jax.ShapeDtypeStruct((2, 8, TILE), F32),
        ]
    else:
        out_specs += sums_specs
        out_shape += sums_shapes
    wide = pl.BlockSpec((SPAN, width), lambda s, g: (turn(s), start + g))
    grid_spec = pltpu.PrefetchScalarGridSpec(
        num_scalar_prefetch=0,
        grid=(spans, count),
        in_specs=[
            wide,
            wide,
            pl.BlockSpec((SPAN, 2 * N), lambda s, g: (turn(s), 0)),
            pl.BlockSpec((N, width), lambda s, g: (turn(s), start + g)),
            wide,
            pl.BlockSpec((8, width), lambda s, g: (halo(s), start + g)),
            pl.BlockSpec((SPAN, 2 * N), lambda s, g: (turn(s), last_block)),
            pl.BlockSpec((8, 2 * N), lambda s, g: (halo(s), last_block)),
            pl.BlockSpec((SPAN, TILE), lambda s, g: (turn(s), raw_block)),
            pl.BlockSpec((8, width), lambda s, g: (0, start + g)),
            pl.BlockSpec((8, 2 * N), lambda s, g: (0, last_block)),
            pl.BlockSpec((SPAN, 8), lambda s, g: (turn(s), 0)),
            pl.BlockSpec((1, SPAN), lambda s, g: (0, turn(s))),
            pl.BlockSpec((8, TILE), lambda s, g: (0, 0)),
            pl.BlockSpec((1, width), lambda s, g: (0, start + g)),
        ]
        + ([] if before is None else sums_specs),
        out_specs=out_specs,
        scratch_shapes=[
            pltpu.VMEM((N, own), F32),
            pltpu.VMEM((SPAN, SPAN), F32),
            pltpu.VMEM((SPAN, SPAN), F32),
            pltpu.VMEM((SPAN, SPAN), F32),
            pltpu.VMEM((3, SPAN, TILE), F32),
            pltpu.VMEM((SPAN, TILE), F32),
            pltpu.VMEM((SPAN, TILE), F32),
            pltpu.VMEM((TILE, SPAN), F32),
            pltpu.VMEM((N, SPAN), BF16),
            pltpu.VMEM((SPAN + 8, width), F32),
            pltpu.VMEM((SPAN + 8, 2 * N), F32),
            pltpu.VMEM((3, 8, own), F32),
            pltpu.VMEM((3, 8, 2 * N), F32),
            pltpu.VMEM((SPAN, 2 * N), F32),
            pltpu.VMEM((3, SPAN, TILE), F32),
            pltpu.VMEM((TILE, SPAN), F32),
            pltpu.VMEM((8, TILE), F32),
        ],
    )
    call = functools.partial(with_base, functools.partial(backward_kernel, before is None, last), start * GROUP)
    return pl.pallas_call(
        call,
        grid_spec=grid_spec,
        out_shape=out_shape,
        compiler_params=pltpu.CompilerParams(dimension_semantics=("arbitrary", "arbitrary")),
        cost_estimate=pl.CostEstimate(
            flops=int(1.5e10 * count), bytes_accessed=12 * tokens * own, transcendentals=0
        ),
        name="scan_backward",
    )(
        dy, x, bcv, states, pc, pc, pc, pc, pc, conv_all, conv_all, aux, seg_row, heads, skip,
        *([] if before is None else before),
    )


def with_base(kernel, base, *refs):
    kernel(*refs, (base,))


def seg_facts(seg):
    length = seg.shape[0]
    cols = []
    for offset in (1, 2, 3):
        moved = jnp.concatenate([jnp.full((offset,), -1, jnp.int32), seg[:-offset]])
        cols.append((moved == seg).astype(F32))
    spans = length // SPAN
    ends = seg[SPAN - 1 :: SPAN]
    before = jnp.concatenate([seg[:1], ends[:-1]])
    cols.append((seg == jnp.repeat(before, SPAN)).astype(F32))
    cols.append((seg == jnp.repeat(ends, SPAN)).astype(F32))
    value = seg.astype(F32)
    cols.append(value)
    cols.append(value)
    cols.append(value)
    return jnp.stack(cols, axis=1), value[None, :]


def head_rows(dt_bias, a_log):
    rate = -jnp.exp(a_log)
    rows = jnp.stack([dt_bias, rate * LOG2E, rate] + [jnp.zeros_like(rate)] * 5, axis=0)
    return jnp.pad(rows, ((0, 0), (0, TILE - H)))


BLOCKS = 32
ORDERS = ((8, 1, 4, 2), (8, 2, 4, 1))


def reach(masks):
    out = [0]
    for mask in masks:
        out = out + [mask ^ place for place in out]
    return out


def exchange(values, stage):
    pairs = []
    for shard in range(16):
        for core in range(2):
            pairs.append((shard * 2 + core, (shard ^ ORDERS[core][stage]) * 2 + core))
    return lax.ppermute(values, ("shard", "rep"), pairs)


def swap_cores(values):
    return lax.ppermute(values, "rep", [(0, 1), (1, 0)])


def after(values, *others):
    return lax.optimization_barrier((values, *others))[0]


def gather_pieces(local, ahead=None):
    held = local
    seen = []
    for stage in range(4):
        send = held if ahead is None else after(held, ahead[stage])
        seen.append(exchange(send, stage))
        if stage < 3:
            held = jnp.concatenate([held, seen[-1]], axis=0)
    return (held, seen[3], swap_cores(held), swap_cores(seen[3])), seen


def gather_small(local):
    held = local[None]
    for stage in range(4):
        held = jnp.concatenate([held, exchange(held, stage)], axis=0)
    core = lax.axis_index("rep")
    places = jnp.asarray([reach(order) for order in ORDERS], jnp.int32)[core] ^ lax.axis_index("shard")
    hot = (places[None, :] == jnp.arange(16, dtype=jnp.int32)[:, None]).astype(local.dtype)
    return dot_f32(hot, held, ((1,), (0,)), HIGHEST).astype(local.dtype)


class Scatter:
    def __init__(self, partial, block):
        self.mine, self.other = partial
        self.block = block
        self.left = [3, 2, 1, 0]
        self.total = None

    def step(self):
        if self.total is None:
            self.total = self.mine.astype(F32) + swap_cores(self.other).astype(F32)
        elif self.left:
            stage = self.left.pop(0)
            cut = self.block << stage
            self.total = self.total[:cut] + exchange(self.total[cut:].astype(BF16), stage).astype(F32)
        return self.total

    def finish(self):
        while self.left:
            self.step()
        return self.total


def block_order():
    shard = lax.axis_index("shard")
    core = lax.axis_index("rep")
    tables = jnp.asarray([reach(order) for order in ORDERS], jnp.int32)
    inverse = jnp.asarray(
        [[reach(order).index(mask) for mask in range(16)] for order in ORDERS], jnp.int32
    )
    own = 2 * (tables[core] ^ shard) + core
    partner = 2 * (tables[1 - core] ^ shard) + (1 - core)
    order = jnp.concatenate([own, partner])
    natural = jnp.arange(BLOCKS, dtype=jnp.int32)
    which = natural % 2
    place = inverse[which, (natural // 2) ^ shard] + 16 * (which != core).astype(jnp.int32)
    return order, place


def fetch_tile(order_ref, pieces, buffer, sems, tile, slot, block, width):
    for q in range(BLOCKS):
        pltpu.make_async_copy(
            pieces[q // 8].at[pl.ds((q % 8) * block, block), pl.ds(pl.multiple_of(tile * width, width), width)],
            buffer.at[slot, pl.ds(pl.multiple_of(order_ref[q] * block, block), block), :],
            sems.at[slot],
        ).start()


def next_tile(order_ref, pieces, buffer, sems, block, width):
    tile = pl.program_id(0)
    slot = lax.rem(tile, 2)

    @pl.when(tile == 0)
    def _():
        fetch_tile(order_ref, pieces, buffer, sems, tile, slot, block, width)

    @pl.when(tile + 1 < pl.num_programs(0))
    def _():
        fetch_tile(order_ref, pieces, buffer, sems, tile + 1, 1 - slot, block, width)

    pltpu.make_async_copy(buffer.at[slot], buffer.at[slot], sems.at[slot]).wait()
    return slot


def project_kernel(block, width, order_ref, x_ref, p0, p1, p2, p3, *rest):
    out_ref, w_ref, buffer, sems = rest[-4:]
    slot = next_tile(order_ref, (p0, p1, p2, p3), buffer, sems, block, width)
    w = buffer[slot]
    w_ref[...] = w
    for i in range(x_ref.shape[0] // SPAN):
        rows = slice(i * SPAN, (i + 1) * SPAN)
        out_ref[rows] = mm(x_ref[rows], w)


def project(x, pieces, order, so_far, start, full, width=512):
    tokens, depth = x.shape
    columns = pieces[0].shape[1]
    block = depth // BLOCKS
    at = start // width
    any_spec = pl.BlockSpec(memory_space=pl.ANY)
    extra = [] if so_far is None else list(so_far)
    return pl.pallas_call(
        functools.partial(project_kernel, block, width),
        grid_spec=pltpu.PrefetchScalarGridSpec(
            num_scalar_prefetch=1,
            grid=(columns // width,),
            in_specs=[pl.BlockSpec((tokens, depth), lambda j, o: (0, 0))] + [any_spec] * (4 + len(extra)),
            out_specs=[
                pl.BlockSpec((tokens, width), lambda j, o: (0, at + j)),
                pl.BlockSpec((depth, width), lambda j, o: (0, at + j)),
            ],
            scratch_shapes=[pltpu.VMEM((2, depth, width), BF16), pltpu.SemaphoreType.DMA((2,))],
        ),
        out_shape=[jax.ShapeDtypeStruct((tokens, full), F32), jax.ShapeDtypeStruct((depth, full), BF16)],
        input_output_aliases={} if so_far is None else {6: 0, 7: 1},
        cost_estimate=pl.CostEstimate(
            flops=2 * tokens * depth * columns,
            bytes_accessed=4 * depth * columns + 4 * tokens * columns + 2 * tokens * depth,
            transcendentals=0,
        ),
        name="project",
    )(order, x, *pieces, *extra)


def gate_kernel(block, width, order_ref, x_ref, p0, p1, p2, p3, y_ref, gain_ref, *rest):
    gate_ref, w_ref, zg_ref, square_ref, buffer, sems = rest[-6:]
    slot = next_tile(order_ref, (p0, p1, p2, p3), buffer, sems, block, width)
    w = buffer[slot]
    w_ref[...] = w

    @pl.when(pl.program_id(0) == 0)
    def _():
        square_ref[...] = jnp.zeros_like(square_ref)

    for i in range(x_ref.shape[0] // SPAN):
        rows = slice(i * SPAN, (i + 1) * SPAN)
        gate = mm(x_ref[rows], w)
        gate_ref[rows] = gate
        gated = y_ref[rows] * (gate * jax.nn.sigmoid(gate))
        zg_ref[rows] = (gated * gain_ref[...]).astype(BF16)
        square = gated * gated
        total = square[:, :TILE]
        for k in range(1, width // TILE):
            total = total + square[:, k * TILE : (k + 1) * TILE]
        square_ref[rows] += total


def gate_project(x, pieces, order, y, gain, so_far, start, full, width=512):
    tokens, depth = x.shape
    columns = pieces[0].shape[1]
    block = depth // BLOCKS
    at = start // width
    any_spec = pl.BlockSpec(memory_space=pl.ANY)
    extra = [] if so_far is None else list(so_far)
    wide = pl.BlockSpec((tokens, width), lambda j, o: (0, at + j))
    return pl.pallas_call(
        functools.partial(gate_kernel, block, width),
        grid_spec=pltpu.PrefetchScalarGridSpec(
            num_scalar_prefetch=1,
            grid=(columns // width,),
            in_specs=[pl.BlockSpec((tokens, depth), lambda j, o: (0, 0))]
            + [any_spec] * 4
            + [wide, pl.BlockSpec((1, width), lambda j, o: (0, at + j))]
            + [any_spec] * len(extra),
            out_specs=[
                wide,
                pl.BlockSpec((depth, width), lambda j, o: (0, at + j)),
                wide,
                pl.BlockSpec((tokens, TILE), lambda j, o: (0, 0)),
            ],
            scratch_shapes=[pltpu.VMEM((2, depth, width), BF16), pltpu.SemaphoreType.DMA((2,))],
        ),
        out_shape=[
            jax.ShapeDtypeStruct((tokens, full), F32),
            jax.ShapeDtypeStruct((depth, full), BF16),
            jax.ShapeDtypeStruct((tokens, full), BF16),
            jax.ShapeDtypeStruct((tokens, TILE), F32),
        ],
        input_output_aliases={} if so_far is None else {8: 0, 9: 1, 10: 2},
        cost_estimate=pl.CostEstimate(
            flops=2 * tokens * depth * columns,
            bytes_accessed=4 * depth * columns + 10 * tokens * columns + 2 * tokens * depth,
            transcendentals=tokens * columns,
        ),
        name="project_gate",
    )(order, x, *pieces, y, gain, *extra)


def restore_kernel(block, width, order_ref, p0, p1, p2, p3, *rest):
    w_ref, buffer, sems = rest[-3:]
    slot = next_tile(order_ref, (p0, p1, p2, p3), buffer, sems, block, width)
    w_ref[...] = buffer[slot]


def restore(pieces, order, so_far, start, full, width=256):
    columns = pieces[0].shape[1]
    block = pieces[0].shape[0] // 8
    depth = block * BLOCKS
    at = start // width
    any_spec = pl.BlockSpec(memory_space=pl.ANY)
    extra = [] if so_far is None else [so_far]
    return pl.pallas_call(
        functools.partial(restore_kernel, block, width),
        grid_spec=pltpu.PrefetchScalarGridSpec(
            num_scalar_prefetch=1,
            grid=(columns // width,),
            in_specs=[any_spec] * (4 + len(extra)),
            out_specs=pl.BlockSpec((depth, width), lambda j, o: (0, at + j)),
            scratch_shapes=[pltpu.VMEM((2, depth, width), BF16), pltpu.SemaphoreType.DMA((2,))],
        ),
        out_shape=jax.ShapeDtypeStruct((depth, full), BF16),
        input_output_aliases={} if so_far is None else {5: 0},
        cost_estimate=pl.CostEstimate(flops=0, bytes_accessed=4 * depth * columns, transcendentals=0),
        name="restore",
    )(order, *pieces, *extra)


def weight_grad_kernel(block, place_ref, lhs_ref, rhs_ref, mine, other, buffer, sems):
    step = pl.program_id(0)
    slot = lax.rem(step, 2)

    def settle(which):
        pltpu.make_async_copy(buffer.at[which], buffer.at[which], sems.at[which]).wait()

    @pl.when(step >= 2)
    def _():
        settle(slot)

    buffer[slot] = dot_f32(lhs_ref[...], rhs_ref[...], ((0,), (0,))).astype(BF16)
    for t in range(8):
        q = place_ref[step * 8 + t]
        source = buffer.at[slot, pl.ds(t * block, block), :]

        @pl.when(q < 16)
        def _():
            pltpu.make_async_copy(
                source, mine.at[pl.ds(pl.multiple_of(q * block, block), block), :], sems.at[slot]
            ).start()

        @pl.when(q >= 16)
        def _():
            pltpu.make_async_copy(
                source, other.at[pl.ds(pl.multiple_of((q - 16) * block, block), block), :], sems.at[slot]
            ).start()

    @pl.when(step == pl.num_programs(0) - 1)
    def _():
        settle(1 - slot)
        settle(slot)


def weight_grad(lhs, rhs, place, column, columns):
    tokens, rows = lhs.shape
    block = rows // BLOCKS
    any_spec = pl.BlockSpec(memory_space=pl.ANY)
    out = jax.ShapeDtypeStruct((16 * block, columns), BF16)
    return pl.pallas_call(
        functools.partial(weight_grad_kernel, block),
        grid_spec=pltpu.PrefetchScalarGridSpec(
            num_scalar_prefetch=1,
            grid=(4,),
            in_specs=[
                pl.BlockSpec((tokens, 8 * block), lambda i, o: (0, i)),
                pl.BlockSpec((tokens, columns), lambda i, o: (0, column)),
            ],
            out_specs=[any_spec, any_spec],
            scratch_shapes=[pltpu.VMEM((2, 8 * block, columns), BF16), pltpu.SemaphoreType.DMA((2,))],
        ),
        out_shape=[out, out],
        cost_estimate=pl.CostEstimate(
            flops=2 * tokens * rows * columns,
            bytes_accessed=2 * (tokens * rows + tokens * columns + rows * columns),
            transcendentals=0,
        ),
        name="weight_grad",
    )(place, lhs, rhs)


def rows_of(packed, start, count):
    return packed[:, start : start + count]


def on_device(
    hypercube,
    tokens,
    seg_ids,
    gain_in,
    w_in,
    conv_weight,
    conv_bias,
    dt_bias,
    a_log,
    d_skip,
    gain_out,
    w_out,
    cotangent,
):
    shards = lax.psum(1, "shard")
    taps, conv_local = conv_weight.shape
    model = tokens.shape[1]
    di = gain_out.shape[0] * shards
    conv_dim = conv_local * shards
    wide = -(-(conv_dim + TILE) // 512) * 512
    cuts = ((0, 1024), (1024, 1024), (2048, wide - 2048))
    halves = ((0, di),)
    thirds = ((0, model),)
    per_call = (0, 2), (2, 2), (4, 2)

    small = jnp.concatenate([conv_weight.reshape(-1), conv_bias, gain_in, gain_out])
    if hypercube:
        core = lax.axis_index("rep")
        order, place = block_order()
        small_all = gather_small(small)
        w_half = lax.dynamic_slice_in_dim(w_in, core * (w_in.shape[0] // 2), w_in.shape[0] // 2, 0)
        o_half = lax.dynamic_slice_in_dim(w_out, core * (w_out.shape[0] // 2), w_out.shape[0] // 2, 0)
        rest = jnp.pad(w_half[:, di:], ((0, 0), (0, wide - (w_in.shape[1] - di))))
        seen = None
        conv_pieces, gate_pieces, out_pieces = [], [], []
        for source, parts, into in (
            (rest, cuts, conv_pieces),
            (w_half, halves, gate_pieces),
            (o_half, thirds, out_pieces),
        ):
            for a, n in parts:
                pieces, seen = gather_pieces(source[:, a : a + n], seen)
                into.append(pieces)
    else:
        small_all = lax.all_gather(small, "shard", axis=0, tiled=False)
        full_w_in = lax.all_gather(w_in, "shard", axis=0, tiled=True)
        full_w_out = lax.all_gather(w_out, "shard", axis=0, tiled=True)
    cut = taps * conv_local
    conv_w = small_all[:, :cut].reshape(shards, taps, conv_local).transpose(1, 0, 2).reshape(taps, -1)
    conv_b = rows_of(small_all, cut, conv_local).reshape(1, -1)
    cut += conv_local
    full_gain_in = rows_of(small_all, cut, gain_in.shape[0]).reshape(1, -1).astype(F32)
    full_gain_out = rows_of(small_all, cut + gain_in.shape[0], gain_out.shape[0]).reshape(1, -1).astype(F32)
    conv_all = jnp.concatenate(
        [conv_w.astype(F32), conv_b.astype(F32), jnp.zeros((3, conv_dim), F32)], axis=0
    )
    inputs = tokens.astype(F32)
    rscale = lax.rsqrt(jnp.mean(inputs * inputs, axis=1, keepdims=True) + EPSILON)
    unit = inputs * rscale
    normed = (unit * full_gain_in).astype(BF16)
    aux, seg_row = seg_facts(seg_ids[0])
    heads = head_rows(dt_bias, a_log)
    skip = jnp.repeat(d_skip, P_SIZE)[None]

    if hypercube:
        front = None
        for (a, n), pieces in zip(cuts, conv_pieces):
            front = project(normed, pieces, order, front, a, wide)
        pc, w_rest = front
    else:
        w_gate = full_w_in[:, :di]
        w_rest = jnp.pad(full_w_in[:, di:], ((0, 0), (0, wide - (w_in.shape[1] - di))))
        pc = mm(normed, w_rest)
    x, bcv, y, states = run_forward(pc, conv_all, aux, seg_row, heads, skip)
    if hypercube:
        part = None
        squares = 0.0
        for (a, n), pieces in zip(halves, gate_pieces):
            *part, square = gate_project(normed, pieces, order, y, full_gain_out, part, a, di)
            squares = squares + square
        gate, w_gate, zg = part
        full_w_out = None
        for (a, n), pieces in zip(thirds, out_pieces):
            full_w_out = restore(pieces, order, full_w_out, a, model)
        gated = y * (gate * jax.nn.sigmoid(gate))
    else:
        gate = mm(normed, w_gate)
        gated = y * (gate * jax.nn.sigmoid(gate))
        squares = gated * gated
        zg = (gated * full_gain_out).astype(BF16)
    inverse = lax.rsqrt(jnp.sum(squares, axis=1, keepdims=True) / di + EPSILON)
    projected = inverse * mm(zg, full_w_out)
    output = (inputs + projected).astype(BF16)
    cot = cotangent.astype(F32)
    dots = jnp.sum(cot * projected, axis=1, keepdims=True)
    cot_scaled = (inverse * cot).astype(BF16)
    grad_ynorm = mm_nt(cotangent, full_w_out)
    dz = inverse * (full_gain_out * grad_ynorm) - gated * (inverse * inverse * dots / di)
    sig = jax.nn.sigmoid(gate)
    dy = (dz * (gate * sig)).astype(BF16)
    dgate = (dz * y * (sig * (1.0 + gate * (1.0 - sig)))).astype(BF16)
    backward_args = (x, bcv, states, pc, conv_all, aux, seg_row, heads, skip)
    if hypercube:
        in_block = w_in.shape[0] // 2
        out_sum = Scatter(weight_grad(zg, cot_scaled, place, 0, model), w_out.shape[0] // 2)
        out_sum.step()
        gate_grad = weight_grad(normed, dgate, place, 0, di)
        gate_sum = Scatter(gate_grad, in_block)
        gate_sum.step()
        flow = [out_sum, gate_sum]
        dy = after(dy, *gate_grad, out_sum.total)
    else:
        flow = []
    sums = None
    dprojs, dcws, dskips = [], [], []
    for index, (start, count) in enumerate(per_call):
        last = index == len(per_call) - 1
        dpart, dcw, dskip, *sums = run_backward(dy, *backward_args, start, count, last, sums)
        dprojs.append(dpart)
        dcws.append(dcw)
        dskips.append(dskip)
        if hypercube:
            steps = [each.step() for each in flow]
            grad = weight_grad(normed, dpart, place, 0, dpart.shape[1])
            flow.append(Scatter(grad, in_block))
            flow[-1].step()
            if not last:
                dy = after(dy, dpart, *grad, *steps)
    dbcw, dhead = sums
    dcw = jnp.concatenate(dcws, axis=2)
    dskip = jnp.concatenate(dskips, axis=1)
    scaled = mm_nt(dgate, w_gate)
    column = 0
    for dpart in dprojs:
        scaled = scaled + mm_nt(dpart, w_rest[:, column : column + dpart.shape[1]])
        column += dpart.shape[1]
    scaled = scaled * full_gain_in
    inner = jnp.mean(unit * scaled, axis=1, keepdims=True)
    grad_tokens = (cot + rscale * (scaled - unit * inner)).astype(BF16)

    conv_sums = jnp.concatenate([dcw, dbcw], axis=2).sum(1)
    conv_sums = jnp.concatenate([conv_sums[4:5], conv_sums[3:4], conv_sums[2:3], conv_sums[1:2], conv_sums[0:1]])
    per_head = jnp.concatenate(
        [
            dhead[0].sum(0)[:H],
            dhead[1].sum(0)[:H] * -jnp.exp(a_log),
            dskip.sum(0).reshape(H, P_SIZE).sum(1),
        ]
    )
    conv_part = conv_sums.reshape(taps + 1, shards, conv_local).transpose(1, 0, 2).reshape(shards, -1)
    small_grad = jnp.concatenate([conv_part, jnp.broadcast_to(per_head[None], (shards, 3 * H))], axis=1)
    real = w_in.shape[1] - di
    if hypercube:
        small_sum = reduce_small(small_grad)[0]
        while any(each.left for each in flow):
            for each in flow:
                each.step()
        own = [each.total for each in flow[1:]]
        own[-1] = own[-1][:, : real - cuts[-1][0]]
        own = jnp.concatenate(own, axis=1)
        sum_w_in = both_cores(own)
        sum_w_out = both_cores(out_sum.total)
    else:
        grad_w_out = dot_f32(zg, cot_scaled, ((0,), (0,)))
        grads = jnp.concatenate([dgate, *dprojs], axis=1)[:, : w_in.shape[1]]
        grad_w_in = dot_f32(normed, grads, ((0,), (0,)))
        small_sum = lax.psum(
            lax.psum_scatter(small_grad, "shard", scatter_dimension=0, tiled=True), "rep"
        )[0]
        sum_w_in = lax.psum_scatter(grad_w_in, "shard", scatter_dimension=0, tiled=True)
        sum_w_out = lax.psum_scatter(grad_w_out, "shard", scatter_dimension=0, tiled=True)
        sum_w_in, sum_w_out = lax.psum((sum_w_in, sum_w_out), "rep")
    grad_gain_in = jnp.sum(sum_w_in * w_in.astype(F32), axis=1) / gain_in.astype(F32)
    grad_gain_out = jnp.sum(sum_w_out * w_out.astype(F32), axis=1) / gain_out.astype(F32)
    cut = taps * conv_local
    head_at = cut + conv_local
    return (
        output,
        grad_tokens,
        grad_gain_in,
        sum_w_in,
        small_sum[:cut].reshape(taps, conv_local),
        small_sum[cut:head_at],
        small_sum[head_at : head_at + H],
        small_sum[head_at + H : head_at + 2 * H],
        small_sum[head_at + 2 * H :],
        grad_gain_out,
        sum_w_out,
    )


def both_cores(own):
    partner = swap_cores(own)
    first = lax.axis_index("rep") == 0
    return jnp.concatenate([jnp.where(first, own, partner), jnp.where(first, partner, own)], axis=0)


def reduce_small(rows):
    core = lax.axis_index("rep")
    places = jnp.asarray([reach(order) for order in ORDERS], jnp.int32)[core] ^ lax.axis_index("shard")
    hot = (places[:, None] == jnp.arange(16, dtype=jnp.int32)[None, :]).astype(F32)
    total = dot_f32(hot, rows, ((1,), (0,)), HIGHEST)
    for stage in (3, 2, 1, 0):
        cut = 1 << stage
        total = total[:cut] + exchange(total[cut:], stage)
    return total + swap_cores(total)


def solution(mesh):
    rows = P(("shard", "rep"), None)
    in_specs = (
        rows, rows, P("shard"), P("shard", None), P(None, "shard"), P("shard"), P(), P(), P(), P("shard"),
        P("shard", None), rows,
    )
    out_specs = (
        rows, rows, P("shard"), P("shard", None), P(None, "shard"), P("shard"), P(), P(), P(), P("shard"),
        P("shard", None),
    )
    hypercube = mesh.shape["shard"] == 16 and mesh.shape["rep"] == 2
    return jax.shard_map(
        functools.partial(on_device, hypercube),
        mesh=mesh,
        in_specs=in_specs,
        out_specs=out_specs,
        check_vma=False,
    )
```

```python
import functools

import jax
import jax.numpy as jnp
from jax import lax
from jax.experimental import pallas as pl
from jax.experimental.pallas import tpu as pltpu
from jax.sharding import PartitionSpec as P
from jax.sharding import PartitionSpec as P

H = 48
P_SIZE = 64
N = 128
SPAN = 256
HALF = 128
GROUP = 8
TILE = 128
EPSILON = 1e-05
HIGHEST = lax.Precision.HIGHEST
LOG2E = 1.4426950408889634
NEG = -1e30
F32 = jnp.float32
BF16 = jnp.bfloat16


def dot_f32(a, b, contract, precision=None):
    return lax.dot_general(
        a, b, ((contract[0], contract[1]), ((), ())), preferred_element_type=F32, precision=precision
    )


def mm(a, b):
    return dot_f32(a, b, ((1,), (0,)))


def mm_nt(a, b):
    return dot_f32(a, b, ((1,), (1,)))


def lanes_of(column, rows):
    return jnp.broadcast_to(column, (rows, TILE))


def step_sizes(raw, heads):
    shifted = raw + heads[0:1]
    return jnp.maximum(shifted, 0.0) + jnp.log1p(jnp.exp(-jnp.abs(shifted)))


def conv_taps(ext, same, start, width, rows=SPAN):
    out = [ext[8 : 8 + rows, start : start + width]]
    for offset in (1, 2, 3):
        moved = ext[8 - offset : 8 - offset + rows, start : start + width]
        mask = same[offset - 1]
        if width > TILE:
            mask = jnp.concatenate([mask] * (width // TILE), axis=1)
        out.append(moved * mask)
    return out


def conv_sum(taps, weights):
    total = weights[4:5] + weights[3:4] * taps[0]
    for offset in (1, 2, 3):
        total = total + weights[3 - offset : 4 - offset] * taps[offset]
    return total


def prepare(raw_ref, heads_ref, aux_ref, same):
    aux = aux_ref[...]
    heads = heads_ref[...]
    step = step_sizes(raw_ref[...], heads)
    row = lax.broadcasted_iota(jnp.int32, (SPAN, SPAN), 0)
    col = lax.broadcasted_iota(jnp.int32, (SPAN, SPAN), 1)
    tri = (row >= col).astype(F32)
    cum = dot_f32(tri, step * heads[1:2], ((1,), (0,)), HIGHEST)
    for place in range(5):
        same[place] = lanes_of(aux[:, place : place + 1], SPAN)
    return step, cum, cum - jnp.log2(step)


def pick(first, columns, at):
    return jnp.where(first, lanes_of(columns[:, at : at + 1], first.shape[0]), lanes_of(columns[:, at + 1 : at + 2], first.shape[0]))


def forward_kernel(first_call, base, pc_ref, halo_ref, raw_ref, cw_ref, aux_ref, seg_ref, heads_ref, skip_ref, *rest):
    rest = list(rest)
    if first_call:
        bc_ref, bc_halo_ref, bcw_ref = [rest.pop(0) for _ in range(3)]
        x_out, y_out, st_out, slope_out, mark, bc_out, bc_slope_out = [rest.pop(0) for _ in range(7)]
    else:
        bc_out = rest.pop(0)
        mark_ref = rest[4]
        rest = rest[5:]
        x_out, y_out, st_out, slope_out, mark = [rest.pop(0) for _ in range(5)]
    state, scores, block, same, pack, cum_rows, w_rows, keep_row, b_t, ext, ext_bc = rest
    span = pl.program_id(0)
    group = pl.program_id(1)
    group_head = base + GROUP * group

    @pl.when((span == 0) & (group == 0))
    def _():
        state[...] = jnp.zeros_like(state)
        mark[...] = jnp.zeros_like(mark) if first_call else mark_ref[...]

    @pl.when(group == 0)
    def _():
        step, cum, shifted = prepare(raw_ref, heads_ref, aux_ref, same)
        last = cum[SPAN - 1 : SPAN]
        pack[...] = cum
        cum_rows[...] = shifted.T
        w_rows[...] = (jnp.exp2(last - shifted) * same[4]).T
        keep_row[...] = jnp.broadcast_to(jnp.exp2(last) * same[3, SPAN - 1 : SPAN], (8, TILE))
        if first_call:
            ext_bc[0:8] = bc_halo_ref[...]
            ext_bc[8:] = bc_ref[...]
            total = conv_sum(conv_taps(ext_bc, same, 0, 2 * N), bcw_ref[...])
            gate = jax.nn.sigmoid(total)
            both = total * gate
            bc_out[...] = both.astype(BF16)
            bc_slope_out[...] = (gate + both * (1.0 - gate)).astype(BF16)
        row = lax.broadcasted_iota(jnp.int32, (SPAN, SPAN), 0)
        col = lax.broadcasted_iota(jnp.int32, (SPAN, SPAN), 1)
        linked = (row >= col) & (aux_ref[:, 5:6] == seg_ref[...])
        block[...] = jnp.where(linked, 0.0, NEG)
        scores[...] = mm_nt(bc_out[:, N:], bc_out[:, :N])
        b_t[...] = bc_out[:, :N].astype(F32).T

    ext[0:8] = halo_ref[...]
    ext[8:] = pc_ref[...]
    shift = lax.rem(TILE - group_head, TILE)
    cums = pltpu.roll(pack[...], shift, 1)
    keep = jnp.broadcast_to(pltpu.roll(keep_row[...], shift, 1)[0:1], (N, TILE))
    first = lax.broadcasted_iota(jnp.int32, (SPAN, TILE), 1) < P_SIZE
    query = bc_out[:, N:]
    empty = jnp.zeros((HALF, HALF), BF16)
    wide = lambda parts: jnp.concatenate(parts, axis=1)
    for quad in range(GROUP // 4):
        xbs, outs, entries, keeps, fresh = [], [], [], [], []
        for pair in (2 * quad, 2 * quad + 1):
            at = pair * TILE
            total = conv_sum(conv_taps(ext, same, at, TILE), cw_ref[:, at : at + TILE])
            gate = jax.nn.sigmoid(total)
            x = total * gate
            xb = x.astype(BF16)
            x_out[:, at : at + TILE] = xb
            slope_out[:, at : at + TILE] = (gate + x * (1.0 - gate)).astype(BF16)
            mixes, weighted, cum_cols = [], [], []
            for head in (2 * pair, 2 * pair + 1):
                cum_col = lanes_of(cums[:, head : head + 1], SPAN)
                cum_cols.append(cum_col)
                cum_row = cum_rows[pl.ds(group_head + head, 1), :]
                blocks = []
                for i, j in ((0, 0), (1, 0), (1, 1)):
                    rows = slice(i * HALF, (i + 1) * HALF)
                    cols = slice(j * HALF, (j + 1) * HALF)
                    gap = cum_col[rows] - cum_row[:, cols] + block[rows, cols]
                    blocks.append((jnp.exp2(gap) * scores[rows, cols]).astype(BF16))
                mixes.append(wide([blocks[0], empty]))
                mixes.append(wide(blocks[1:]))
                weighted.append((b_t[...] * w_rows[pl.ds(group_head + head, 1), :]).astype(BF16))
            inner = mm(jnp.concatenate(mixes + weighted, axis=0), xb)
            outs.append(jnp.where(first, inner[:SPAN], inner[SPAN : 2 * SPAN]))
            fresh.append(jnp.where(first[:N], inner[2 * SPAN : 2 * SPAN + N], inner[2 * SPAN + N :]))
            xbs.append(xb)
            entries.append(jnp.exp2(jnp.where(first, cum_cols[0], cum_cols[1])) * same[3])
            keeps.append(pick(first[:N], keep, 2 * pair))
        both = slice(quad * 2 * TILE, (quad + 1) * 2 * TILE)
        tile = pl.ds(pl.multiple_of(group * GROUP * P_SIZE + quad * 2 * TILE, 2 * TILE), 2 * TILE)
        old = state[:, tile]
        old_b = old.astype(BF16)
        st_out[:, both] = old_b
        carried = mm(query, old_b)
        y_out[:, both] = wide(outs) + wide(entries) * carried + skip_ref[:, both] * wide(xbs).astype(F32)
        state[:, tile] = old * wide(keeps) + wide(fresh)


def run_forward(pc, first_x, pc_bc, conv_x, conv_bc, aux, seg_row, heads, skip, start, count, bcv, before):
    tokens = pc.shape[0]
    spans = tokens // SPAN
    di = skip.shape[1]
    width = GROUP * P_SIZE
    own = count * width
    first_call = before is None
    any_spec = pl.BlockSpec(memory_space=pl.ANY)
    halo = lambda s: jnp.maximum(s * (SPAN // 8) - 1, 0)
    wide = pl.BlockSpec((SPAN, width), lambda s, g: (s, start + g))
    bcv_spec = pl.BlockSpec((SPAN, 2 * N), lambda s, g: (s, 0))
    in_specs = [
        pl.BlockSpec((SPAN, width), lambda s, g: (s, first_x + g)),
        pl.BlockSpec((8, width), lambda s, g: (halo(s), first_x + g)),
        pl.BlockSpec((SPAN, TILE), lambda s, g: (s, 2)),
        pl.BlockSpec((8, width), lambda s, g: (0, start + g)),
        pl.BlockSpec((SPAN, 8), lambda s, g: (s, 0)),
        pl.BlockSpec((1, SPAN), lambda s, g: (0, s)),
        pl.BlockSpec((8, TILE), lambda s, g: (0, 0)),
        pl.BlockSpec((1, width), lambda s, g: (0, start + g)),
    ]
    args = [pc, pc, pc_bc, conv_x, aux, seg_row, heads, skip]
    mark_spec = pl.BlockSpec((8, TILE), lambda s, g: (0, 0))
    out_specs = [wide, wide, pl.BlockSpec((N, width), lambda s, g: (s, start + g)), wide, mark_spec]
    out_shape = [
        jax.ShapeDtypeStruct((tokens, di), BF16),
        jax.ShapeDtypeStruct((tokens, di), F32),
        jax.ShapeDtypeStruct((spans * N, di), BF16),
        jax.ShapeDtypeStruct((tokens, di), BF16),
        jax.ShapeDtypeStruct((8, TILE), F32),
    ]
    if first_call:
        in_specs += [
            pl.BlockSpec((SPAN, 2 * N), lambda s, g: (s, 0)),
            pl.BlockSpec((8, 2 * N), lambda s, g: (halo(s), 0)),
            pl.BlockSpec((8, 2 * N), lambda s, g: (0, 0)),
        ]
        args += [pc_bc, pc_bc, conv_bc]
        out_specs += [bcv_spec, bcv_spec]
        out_shape += [jax.ShapeDtypeStruct((tokens, 2 * N), BF16)] * 2
        aliases = {}
    else:
        in_specs += [bcv_spec, any_spec, any_spec, any_spec, any_spec, mark_spec]
        args += [bcv, *before]
        aliases = {9: 0, 10: 1, 11: 2, 12: 3}
    return pl.pallas_call(
        functools.partial(forward_kernel, first_call, start * GROUP),
        grid_spec=pltpu.PrefetchScalarGridSpec(
            num_scalar_prefetch=0,
            grid=(spans, count),
            in_specs=in_specs,
            out_specs=out_specs,
            scratch_shapes=[
                pltpu.VMEM((N, own), F32),
                pltpu.VMEM((SPAN, SPAN), F32),
                pltpu.VMEM((SPAN, SPAN), F32),
                pltpu.VMEM((5, SPAN, TILE), F32),
                pltpu.VMEM((SPAN, TILE), F32),
                pltpu.VMEM((TILE, SPAN), F32),
                pltpu.VMEM((TILE, SPAN), F32),
                pltpu.VMEM((8, TILE), F32),
                pltpu.VMEM((N, SPAN), F32),
                pltpu.VMEM((SPAN + 8, width), F32),
                pltpu.VMEM((SPAN + 8, 2 * N), F32),
            ],
        ),
        out_shape=out_shape,
        input_output_aliases=aliases,
        compiler_params=pltpu.CompilerParams(dimension_semantics=("arbitrary", "arbitrary")),
        cost_estimate=pl.CostEstimate(flops=int(5e9 * count), bytes_accessed=14 * tokens * own, transcendentals=0),
        name="scan_forward",
    )(*args)


def conv_back(grad, slope, signal, same, weights, carry):
    width = grad.shape[1]
    du = grad * slope.astype(F32)

    def add_rows(values):
        return jnp.sum(values.reshape(SPAN // 8, 8, width), axis=0)

    out = weights[3:4] * du
    sums = [add_rows(du), add_rows(du * signal)]
    for offset in (1, 2, 3):
        mask = same[offset - 1]
        if width > TILE:
            mask = jnp.concatenate([mask] * (width // TILE), axis=1)
        masked = du * mask
        moved = jnp.concatenate([masked, carry[offset - 1]], axis=0)[offset : offset + SPAN]
        carry[offset - 1] = masked[0:8]
        out = out + weights[3 - offset : 4 - offset] * moved
        sums.append(add_rows(moved * signal))
    return out, sums


def backward_kernel(
    first_call, last_call, base,
    dy_ref, x_ref, bcv_ref, st_ref, slope_ref, pc_ref, raw_ref, cw_ref, aux_ref, seg_ref, heads_ref, skip_ref, *rest,
):
    rest = list(rest)
    before = None if first_call else [rest.pop(0) for _ in range(4)]
    if last_call:
        bc_ref, bc_slope_ref, bcw_ref = [rest.pop(0) for _ in range(3)]
    dproj_out, dcw_out, dskip_out = [rest.pop(0) for _ in range(3)]
    if last_call:
        dbcw_out, dhead_out = [rest.pop(0) for _ in range(2)]
    else:
        after_out = [rest.pop(0) for _ in range(4)]
    (
        dstate, scores, block, dscores, same, pack, last_row, cum_rows, c_t,
        carry, carry_bc, d_bc, per_row, dcum_rows, dlast,
    ) = rest
    back = pl.program_id(0)
    group = pl.program_id(1)
    groups = pl.num_programs(1)
    width = GROUP * P_SIZE
    group_head = base + GROUP * group
    first_x = 4 * N if last_call else 0

    @pl.when((back == 0) & (group == 0))
    def _():
        dstate[...] = jnp.zeros_like(dstate)
        carry[...] = jnp.zeros_like(carry)
        dcw_out[...] = jnp.zeros_like(dcw_out)
        dskip_out[...] = jnp.zeros_like(dskip_out)
        dcum_rows[...] = jnp.zeros_like(dcum_rows)
        if last_call:
            carry_bc[...] = jnp.zeros_like(carry_bc)
            dbcw_out[...] = jnp.zeros_like(dbcw_out)
            dhead_out[...] = jnp.zeros_like(dhead_out)

    keys = bcv_ref[:, :N]
    query = bcv_ref[:, N:]
    lane = lax.broadcasted_iota(jnp.int32, (SPAN, TILE), 1)

    @pl.when(group == 0)
    def _():
        step, cum, shifted = prepare(raw_ref, heads_ref, aux_ref, same)
        entry = jnp.exp2(cum) * same[3]
        pack[...] = jnp.where(lane < 64, shifted, pltpu.roll(entry, 64, 1))
        last_row[...] = jnp.broadcast_to(cum[SPAN - 1 : SPAN], (8, TILE))
        cum_rows[...] = cum.T
        row = lax.broadcasted_iota(jnp.int32, (SPAN, SPAN), 0)
        col = lax.broadcasted_iota(jnp.int32, (SPAN, SPAN), 1)
        linked = (row <= col) & (aux_ref[:, 5:6] == seg_ref[...])
        block[...] = jnp.where(linked, 0.0, NEG)
        scores[...] = mm_nt(keys, query)
        c_t[...] = query.T
        per_row[...] = jnp.zeros_like(per_row)
        if first_call:
            dscores[...] = jnp.zeros_like(dscores)
            d_bc[...] = jnp.zeros_like(d_bc)
            dlast[...] = jnp.zeros_like(dlast)
        else:
            dscores[...] = before[0][...]
            d_bc[...] = before[1][...]
            per_row[0] = before[2][:, :TILE]
            per_row[2] = before[2][:, TILE:]
            dlast[...] = before[3][...]

    shift = lax.rem(TILE - group_head, TILE)
    cols = pltpu.roll(pack[...], shift, 1)
    last_cum = pltpu.roll(last_row[...], shift, 1)[0:1]
    keep_mask = same[3, SPAN - 1 : SPAN]
    first = lane < P_SIZE
    lane_row = lax.broadcasted_iota(jnp.int32, (2 * TILE, TILE), 0) // P_SIZE
    lane_col = lax.broadcasted_iota(jnp.int32, (2 * TILE, TILE), 1)
    sums = jnp.zeros((SPAN, TILE), F32)
    last_sum = jnp.zeros((1, TILE), F32)
    group_at = group * width
    empty = jnp.zeros((HALF, HALF), BF16)
    wide = lambda parts: jnp.concatenate(parts, axis=1)
    for quad in range(GROUP // 4):
        both = slice(quad * 2 * TILE, (quad + 1) * 2 * TILE)
        tile = pl.ds(pl.multiple_of(group_at + quad * 2 * TILE, 2 * TILE), 2 * TILE)
        entries, tails, keeps, inners = [], [], [], []
        for pair in (2 * quad, 2 * quad + 1):
            at = pair * TILE
            heads = (2 * pair, 2 * pair + 1)
            dy_pair = dy_ref[:, at : at + TILE]
            xb = x_ref[:, at : at + TILE]
            nothing = jnp.zeros_like(xb)
            split = jnp.concatenate([jnp.where(first, xb, nothing), jnp.where(first, nothing, xb)], axis=0)
            g_both = mm_nt(split, dy_pair)
            cum_cols = [lanes_of(cols[:, head : head + 1], SPAN) for head in heads]
            cum_lines = [cum_rows[pl.ds(group_head + head, 1), :] for head in heads]
            mixes = [[], []]
            across = [[], []]
            down = [[], []]
            for j, i in ((0, 0), (0, 1), (1, 1)):
                rows = slice(j * HALF, (j + 1) * HALF)
                cells = slice(i * HALF, (i + 1) * HALF)
                spread = jnp.zeros((HALF, HALF), F32)
                for which in (0, 1):
                    decay = jnp.exp2(cum_lines[which][:, cells] - cum_cols[which][rows] + block[rows, cells])
                    mix = decay * scores[rows, cells]
                    g = g_both[which * SPAN + j * HALF : which * SPAN + (j + 1) * HALF, cells]
                    spread = spread + decay * g
                    w = mix * g
                    mixes[which].append(mix.astype(BF16))
                    across[which].append(w)
                    down[which].append(jnp.sum(w, axis=0, keepdims=True))
                dscores[rows, cells] += spread
            lefts = []
            for which in (0, 1):
                row_sum = jnp.concatenate(
                    [
                        jnp.sum(across[which][0] + across[which][1], axis=1, keepdims=True),
                        jnp.sum(across[which][2], axis=1, keepdims=True),
                    ],
                    axis=0,
                )
                sums = sums - jnp.where(lane == 2 * GROUP + heads[which], row_sum, 0.0)
                dcum_rows[pl.ds(group_head + heads[which], 1), :] = wide(
                    [down[which][0], down[which][1] + down[which][2]]
                )
                lefts += [wide(mixes[which][:2]), wide([empty, mixes[which][2]])]
            inner = mm(jnp.concatenate(lefts, axis=0), dy_pair)
            inners.append(jnp.where(first, inner[:SPAN], inner[SPAN:]))
            last_pair = jnp.where(
                first[0:1],
                jnp.broadcast_to(last_cum[:, heads[0] : heads[0] + 1], (1, TILE)),
                jnp.broadcast_to(last_cum[:, heads[1] : heads[1] + 1], (1, TILE)),
            )
            tails.append(jnp.exp2(last_pair - jnp.where(first, cum_cols[0], cum_cols[1])) * same[4])
            keeps.append(jnp.exp2(last_pair) * keep_mask)
            entries.append(pick(first, cols, 64 + 2 * pair))
        dyf = dy_ref[:, both].astype(F32)
        xf = x_ref[:, both].astype(F32)
        tail = wide(tails)
        stb = st_ref[:, both]
        ds = dstate[:, tile]
        dsb = ds.astype(BF16)
        dye_f = dyf * wide(entries)
        dye = dye_f.astype(BF16)
        fresh = mm(keys, dsb) * tail
        total = wide(inners) + fresh
        d_bc[:, N:] += mm_nt(dye, stb)
        d_bc[:, :N] += mm_nt((xf * tail).astype(BF16), dsb)

        def head_sum(values, kind):
            spread = (lane_col == kind * GROUP + 4 * quad + lane_row).astype(BF16)
            return mm(values.astype(BF16), spread)

        sums = sums + head_sum(xf * total, 0) + head_sum(xf * fresh, 1) + head_sum(dye_f * mm(query, stb), 2)
        kept = ds * wide(keeps)
        kept_sum = jnp.sum(kept * stb.astype(F32), axis=0, keepdims=True)
        lane_pair = lax.broadcasted_iota(jnp.int32, (1, 2 * TILE), 1) // P_SIZE
        for head in range(4):
            one = jnp.sum(jnp.where(lane_pair == head, kept_sum, 0.0), axis=1, keepdims=True)
            last_sum = last_sum + jnp.where(lane[0:1] == 4 * quad + head, one, 0.0)
        dstate[:, tile] = kept + mm(c_t[...], dye)
        dskip_out[:, tile] += jnp.sum((dyf * xf).reshape(SPAN // 8, 8, 2 * TILE), axis=0)
        dx = total + skip_ref[:, both] * dyf
        for part in (0, 1):
            at = (2 * quad + part) * TILE
            one = pl.ds(pl.multiple_of(group_at + at, TILE), TILE)
            out, conv_sums = conv_back(
                dx[:, part * TILE : (part + 1) * TILE], slope_ref[:, at : at + TILE], pc_ref[:, at : at + TILE],
                same, cw_ref[:, at : at + TILE], carry.at[:, :, one],
            )
            dproj_out[:, pl.ds(pl.multiple_of(first_x + group_at + at, TILE), TILE)] = out.astype(BF16)
            for k, value in enumerate(conv_sums):
                dcw_out[k, :, one] += value

    in_place = (lane >= group_head) & (lane < group_head + GROUP)
    for kind in range(3):
        moved = pltpu.roll(sums, lax.rem(group_head + TILE - GROUP * kind, TILE), 1)
        per_row[kind] += jnp.where(in_place, moved, 0.0)
    moved = pltpu.roll(jnp.broadcast_to(last_sum, (8, TILE)), group_head, 1)
    dlast[...] += jnp.where(in_place[0:8], moved, 0.0)

    @pl.when(group == groups - 1)
    def _():
        state_part = per_row[1]
        dcum = dcum_rows[...].T + per_row[2] - state_part
        dlast_all = dlast[0:1] + jnp.sum(state_part, axis=0, keepdims=True)
        if not last_call:
            after_out[0][...] = dscores[...]
            after_out[1][...] = d_bc[...]
            after_out[2][:, :TILE] = per_row[0]
            after_out[2][:, TILE:] = dcum
            after_out[3][...] = jnp.broadcast_to(dlast_all, (8, TILE))
            return
        ds_b = dscores[...].astype(BF16)
        grad_b = d_bc[:, :N] + mm(ds_b, query)
        grad_c = d_bc[:, N:] + mm(dscores[...].T.astype(BF16), keys)
        out, conv_sums = conv_back(
            wide([grad_b, grad_c]), bc_slope_ref[...], bc_ref[...], same, bcw_ref[...], carry_bc
        )
        dproj_out[:, : 2 * N] = out.astype(BF16)
        for k, value in enumerate(conv_sums):
            dbcw_out[k] += value
        heads = heads_ref[...]
        shifted = raw_ref[...] + heads[0:1]
        step = step_sizes(raw_ref[...], heads)
        slope = jax.nn.sigmoid(shifted)
        row = lax.broadcasted_iota(jnp.int32, (SPAN, SPAN), 0)
        col = lax.broadcasted_iota(jnp.int32, (SPAN, SPAN), 1)
        tri = (row <= col).astype(F32)
        da = dot_f32(tri, dcum, ((1,), (0,)), HIGHEST) + dlast_all
        small = shifted < -16.0
        ratio = jnp.where(small, 1.0, slope / jnp.where(small, 1.0, step))
        live = lane < H
        draw = jnp.where(live, per_row[0] * ratio + da * heads[2:3] * slope, 0.0)
        dproj_out[:, 2 * N : 3 * N] = draw.astype(BF16)
        dproj_out[:, 3 * N : 4 * N] = jnp.zeros((SPAN, N), BF16)
        dhead_out[0] += jnp.sum(draw.reshape(SPAN // 8, 8, TILE), axis=0)
        dhead_out[1] += jnp.sum(jnp.where(live, da * step, 0.0).reshape(SPAN // 8, 8, TILE), axis=0)


def run_backward(
    dy, x, bcv, states, slope, bc_slope, pc, first_x, pc_bc, conv_x, conv_bc, aux, seg_row, heads, skip, start, count, last, before
):
    tokens, di = dy.shape
    spans = tokens // SPAN
    width = GROUP * P_SIZE
    turn = lambda s: spans - 1 - s
    own = count * width
    out_width = own + (4 * N if last else 0)
    sums_specs = [
        pl.BlockSpec((SPAN, SPAN), lambda s, g: (turn(s), 0)),
        pl.BlockSpec((SPAN, 2 * N), lambda s, g: (turn(s), 0)),
        pl.BlockSpec((SPAN, 2 * TILE), lambda s, g: (turn(s), 0)),
        pl.BlockSpec((8, TILE), lambda s, g: (turn(s), 0)),
    ]
    sums_shapes = [
        jax.ShapeDtypeStruct((tokens, SPAN), F32),
        jax.ShapeDtypeStruct((tokens, 2 * N), F32),
        jax.ShapeDtypeStruct((tokens, 2 * TILE), F32),
        jax.ShapeDtypeStruct((spans * 8, TILE), F32),
    ]
    out_specs = [
        pl.BlockSpec((SPAN, out_width), lambda s, g: (turn(s), 0)),
        pl.BlockSpec((5, 8, own), lambda s, g: (0, 0, 0)),
        pl.BlockSpec((8, own), lambda s, g: (0, 0)),
    ]
    out_shape = [
        jax.ShapeDtypeStruct((tokens, out_width), BF16),
        jax.ShapeDtypeStruct((5, 8, own), F32),
        jax.ShapeDtypeStruct((8, own), F32),
    ]
    wide = pl.BlockSpec((SPAN, width), lambda s, g: (turn(s), start + g))
    in_specs = [
        wide,
        wide,
        pl.BlockSpec((SPAN, 2 * N), lambda s, g: (turn(s), 0)),
        pl.BlockSpec((N, width), lambda s, g: (turn(s), start + g)),
        wide,
        pl.BlockSpec((SPAN, width), lambda s, g: (turn(s), first_x + g)),
        pl.BlockSpec((SPAN, TILE), lambda s, g: (turn(s), 2)),
        pl.BlockSpec((8, width), lambda s, g: (0, start + g)),
        pl.BlockSpec((SPAN, 8), lambda s, g: (turn(s), 0)),
        pl.BlockSpec((1, SPAN), lambda s, g: (0, turn(s))),
        pl.BlockSpec((8, TILE), lambda s, g: (0, 0)),
        pl.BlockSpec((1, width), lambda s, g: (0, start + g)),
    ]
    args = [dy, x, bcv, states, slope, pc, pc_bc, conv_x, aux, seg_row, heads, skip]
    if before is not None:
        in_specs += sums_specs
        args += before
    if last:
        in_specs += [
            pl.BlockSpec((SPAN, 2 * N), lambda s, g: (turn(s), 0)),
            pl.BlockSpec((SPAN, 2 * N), lambda s, g: (turn(s), 0)),
            pl.BlockSpec((8, 2 * N), lambda s, g: (0, 0)),
        ]
        args += [pc_bc, bc_slope, conv_bc]
        out_specs += [
            pl.BlockSpec((5, 8, 2 * N), lambda s, g: (0, 0, 0)),
            pl.BlockSpec((2, 8, TILE), lambda s, g: (0, 0, 0)),
        ]
        out_shape += [
            jax.ShapeDtypeStruct((5, 8, 2 * N), F32),
            jax.ShapeDtypeStruct((2, 8, TILE), F32),
        ]
    else:
        out_specs += sums_specs
        out_shape += sums_shapes
    return pl.pallas_call(
        functools.partial(backward_kernel, before is None, last, start * GROUP),
        grid_spec=pltpu.PrefetchScalarGridSpec(
            num_scalar_prefetch=0,
            grid=(spans, count),
            in_specs=in_specs,
            out_specs=out_specs,
            scratch_shapes=[
                pltpu.VMEM((N, own), F32),
                pltpu.VMEM((SPAN, SPAN), F32),
                pltpu.VMEM((SPAN, SPAN), F32),
                pltpu.VMEM((SPAN, SPAN), F32),
                pltpu.VMEM((5, SPAN, TILE), F32),
                pltpu.VMEM((SPAN, TILE), F32),
                pltpu.VMEM((8, TILE), F32),
                pltpu.VMEM((TILE, SPAN), F32),
                pltpu.VMEM((N, SPAN), BF16),
                pltpu.VMEM((3, 8, own), F32),
                pltpu.VMEM((3, 8, 2 * N), F32),
                pltpu.VMEM((SPAN, 2 * N), F32),
                pltpu.VMEM((3, SPAN, TILE), F32),
                pltpu.VMEM((TILE, SPAN), F32),
                pltpu.VMEM((8, TILE), F32),
            ],
        ),
        out_shape=out_shape,
        compiler_params=pltpu.CompilerParams(dimension_semantics=("arbitrary", "arbitrary")),
        cost_estimate=pl.CostEstimate(
            flops=int(1.2e10 * count), bytes_accessed=12 * tokens * own, transcendentals=0
        ),
        name="scan_backward",
    )(*args)


def seg_facts(seg):
    length = seg.shape[0]
    cols = []
    for offset in (1, 2, 3):
        moved = jnp.concatenate([jnp.full((offset,), -1, jnp.int32), seg[:-offset]])
        cols.append((moved == seg).astype(F32))
    spans = length // SPAN
    ends = seg[SPAN - 1 :: SPAN]
    before = jnp.concatenate([seg[:1], ends[:-1]])
    cols.append((seg == jnp.repeat(before, SPAN)).astype(F32))
    cols.append((seg == jnp.repeat(ends, SPAN)).astype(F32))
    value = seg.astype(F32)
    cols.append(value)
    cols.append(value)
    cols.append(value)
    return jnp.stack(cols, axis=1), value[None, :]


def head_rows(dt_bias, a_log):
    rate = -jnp.exp(a_log)
    rows = jnp.stack([dt_bias, rate * LOG2E, rate] + [jnp.zeros_like(rate)] * 5, axis=0)
    return jnp.pad(rows, ((0, 0), (0, TILE - H)))


BLOCKS = 32
ORDERS = ((8, 1, 4, 2), (8, 2, 4, 1))


def reach(masks):
    out = [0]
    for mask in masks:
        out = out + [mask ^ place for place in out]
    return out


def exchange(values, stage):
    pairs = []
    for shard in range(16):
        for core in range(2):
            pairs.append((shard * 2 + core, (shard ^ ORDERS[core][stage]) * 2 + core))
    return lax.ppermute(values, ("shard", "rep"), pairs)


def swap_cores(values):
    return lax.ppermute(values, "rep", [(0, 1), (1, 0)])


def after(values, *others):
    return lax.optimization_barrier((values, *others))[0]


class Gather:
    def __init__(self, local):
        self.held = local
        self.seen = []
        self.swapped = []

    def step(self, *ahead):
        stage = len(self.seen)
        send = after(self.held, *ahead)
        got = exchange(send, stage)
        self.seen.append(got)
        if stage < 3:
            self.held = jnp.concatenate([send, got], axis=0)
        return send, got

    def swap(self, *ahead):
        send = after(self.held if not self.swapped else self.seen[3], *ahead)
        self.swapped.append(swap_cores(send))
        return send, self.swapped[-1]

    def pieces(self):
        return self.held, self.seen[3], *self.swapped


def gather_small(local):
    held = local[None]
    ahead = yield None
    for stage in range(4):
        send = after(held, *ahead)
        got = exchange(send, stage)
        ahead = yield send, got
        held = jnp.concatenate([send, got], axis=0)
    core = lax.axis_index("rep")
    places = jnp.asarray([reach(order) for order in ORDERS], jnp.int32)[core] ^ lax.axis_index("shard")
    hot = (places[None, :] == jnp.arange(16, dtype=jnp.int32)[:, None]).astype(local.dtype)
    yield dot_f32(hot, held, ((1,), (0,)), HIGHEST).astype(local.dtype)


class Scatter:
    def __init__(self, partial, block):
        mine, self.other = partial
        self.terms = [mine]
        self.block = block
        self.left = [3, 2, 1, 0]

    def rows(self, start, stop):
        total = self.terms[0][start:stop].astype(F32)
        for term in self.terms[1:]:
            total = total + term[start:stop].astype(F32)
        return total

    def step(self, *ahead):
        if len(self.terms) == 1:
            send = after(self.other, *ahead)
            self.terms.append(swap_cores(send))
            return send, self.terms[-1]
        if self.left:
            stage = self.left.pop(0)
            cut = self.block << stage
            send = after(self.rows(cut, 2 * cut).astype(BF16), *ahead)
            self.terms.append(exchange(send, stage))
            return send, self.terms[-1]
        return self.terms[-1], self.terms[-1]

    def finish(self):
        while self.left:
            self.step()
        return self.rows(0, self.block)


def block_order(core):
    shard = lax.axis_index("shard")
    tables = jnp.asarray([reach(order) for order in ORDERS], jnp.int32)
    inverse = jnp.asarray(
        [[reach(order).index(mask) for mask in range(16)] for order in ORDERS], jnp.int32
    )
    own = 2 * (tables[core] ^ shard) + core
    partner = 2 * (tables[1 - core] ^ shard) + (1 - core)
    order = jnp.concatenate([own, partner])
    natural = jnp.arange(BLOCKS, dtype=jnp.int32)
    which = natural % 2
    place = inverse[which, (natural // 2) ^ shard] + 16 * (which != core).astype(jnp.int32)
    return order, place


def fetch_tile(order_ref, pieces, buffer, sems, tile, slot, block, width):
    for q in range(BLOCKS):
        pltpu.make_async_copy(
            pieces[q // 8].at[pl.ds((q % 8) * block, block), pl.ds(pl.multiple_of(tile * width, width), width)],
            buffer.at[slot, pl.ds(pl.multiple_of(order_ref[q] * block, block), block), :],
            sems.at[slot],
        ).start()


def next_tile(order_ref, pieces, buffer, sems, block, width):
    tile = pl.program_id(0)
    slot = lax.rem(tile, 2)

    @pl.when(tile == 0)
    def _():
        fetch_tile(order_ref, pieces, buffer, sems, tile, slot, block, width)

    @pl.when(tile + 1 < pl.num_programs(0))
    def _():
        fetch_tile(order_ref, pieces, buffer, sems, tile + 1, 1 - slot, block, width)

    pltpu.make_async_copy(buffer.at[slot], buffer.at[slot], sems.at[slot]).wait()
    return slot


def project_kernel(block, width, order_ref, x_ref, p0, p1, p2, p3, *rest):
    out_ref, w_ref, buffer, sems = rest[-4:]
    slot = next_tile(order_ref, (p0, p1, p2, p3), buffer, sems, block, width)
    w = buffer[slot]
    w_ref[...] = w
    for i in range(x_ref.shape[0] // SPAN):
        rows = slice(i * SPAN, (i + 1) * SPAN)
        out_ref[rows] = mm(x_ref[rows], w)


def project(x, pieces, order, so_far, start, full, width=512):
    tokens, depth = x.shape
    columns = pieces[0].shape[1]
    block = depth // BLOCKS
    at = start // width
    any_spec = pl.BlockSpec(memory_space=pl.ANY)
    extra = [] if so_far is None else list(so_far)
    return pl.pallas_call(
        functools.partial(project_kernel, block, width),
        grid_spec=pltpu.PrefetchScalarGridSpec(
            num_scalar_prefetch=1,
            grid=(columns // width,),
            in_specs=[pl.BlockSpec((tokens, depth), lambda j, o: (0, 0))] + [any_spec] * (4 + len(extra)),
            out_specs=[
                pl.BlockSpec((tokens, width), lambda j, o: (0, at + j)),
                pl.BlockSpec((depth, width), lambda j, o: (0, at + j)),
            ],
            scratch_shapes=[pltpu.VMEM((2, depth, width), BF16), pltpu.SemaphoreType.DMA((2,))],
        ),
        out_shape=[jax.ShapeDtypeStruct((tokens, full), F32), jax.ShapeDtypeStruct((depth, full), BF16)],
        input_output_aliases={} if so_far is None else {6: 0, 7: 1},
        cost_estimate=pl.CostEstimate(
            flops=2 * tokens * depth * columns,
            bytes_accessed=4 * depth * columns + 4 * tokens * columns + 2 * tokens * depth,
            transcendentals=0,
        ),
        name="project",
    )(order, x, *pieces, *extra)


def gate_kernel(block, width, order_ref, x_ref, p0, p1, p2, p3, y_ref, gain_ref, *rest):
    gate_ref, w_ref, zg_ref, square_ref, buffer, sems = rest[-6:]
    slot = next_tile(order_ref, (p0, p1, p2, p3), buffer, sems, block, width)
    w = buffer[slot]
    w_ref[...] = w

    @pl.when(pl.program_id(0) == 0)
    def _():
        square_ref[...] = jnp.zeros_like(square_ref)

    for i in range(x_ref.shape[0] // SPAN):
        rows = slice(i * SPAN, (i + 1) * SPAN)
        gate = mm(x_ref[rows], w)
        gate_ref[rows] = gate
        gated = y_ref[rows] * (gate * jax.nn.sigmoid(gate))
        zg_ref[rows] = (gated * gain_ref[...]).astype(BF16)
        square = gated * gated
        total = square[:, :TILE]
        for k in range(1, width // TILE):
            total = total + square[:, k * TILE : (k + 1) * TILE]
        square_ref[rows] += total


def gate_project(x, pieces, order, y, gain, so_far, start, full, width=512):
    tokens, depth = x.shape
    columns = pieces[0].shape[1]
    block = depth // BLOCKS
    at = start // width
    any_spec = pl.BlockSpec(memory_space=pl.ANY)
    extra = [] if so_far is None else list(so_far)
    wide = pl.BlockSpec((tokens, width), lambda j, o: (0, at + j))
    return pl.pallas_call(
        functools.partial(gate_kernel, block, width),
        grid_spec=pltpu.PrefetchScalarGridSpec(
            num_scalar_prefetch=1,
            grid=(columns // width,),
            in_specs=[pl.BlockSpec((tokens, depth), lambda j, o: (0, 0))]
            + [any_spec] * 4
            + [wide, pl.BlockSpec((1, width), lambda j, o: (0, at + j))]
            + [any_spec] * len(extra),
            out_specs=[
                wide,
                pl.BlockSpec((depth, width), lambda j, o: (0, at + j)),
                wide,
                pl.BlockSpec((tokens, TILE), lambda j, o: (0, 0)),
            ],
            scratch_shapes=[pltpu.VMEM((2, depth, width), BF16), pltpu.SemaphoreType.DMA((2,))],
        ),
        out_shape=[
            jax.ShapeDtypeStruct((tokens, full), F32),
            jax.ShapeDtypeStruct((depth, full), BF16),
            jax.ShapeDtypeStruct((tokens, full), BF16),
            jax.ShapeDtypeStruct((tokens, TILE), F32),
        ],
        input_output_aliases={} if so_far is None else {8: 0, 9: 1, 10: 2},
        cost_estimate=pl.CostEstimate(
            flops=2 * tokens * depth * columns,
            bytes_accessed=4 * depth * columns + 10 * tokens * columns + 2 * tokens * depth,
            transcendentals=tokens * columns,
        ),
        name="project_gate",
    )(order, x, *pieces, y, gain, *extra)


def restore_kernel(block, width, order_ref, p0, p1, p2, p3, *rest):
    w_ref, buffer, sems = rest[-3:]
    slot = next_tile(order_ref, (p0, p1, p2, p3), buffer, sems, block, width)
    w_ref[...] = buffer[slot]


def restore(pieces, order, so_far, start, full, width=256):
    columns = pieces[0].shape[1]
    block = pieces[0].shape[0] // 8
    depth = block * BLOCKS
    at = start // width
    any_spec = pl.BlockSpec(memory_space=pl.ANY)
    extra = [] if so_far is None else [so_far]
    return pl.pallas_call(
        functools.partial(restore_kernel, block, width),
        grid_spec=pltpu.PrefetchScalarGridSpec(
            num_scalar_prefetch=1,
            grid=(columns // width,),
            in_specs=[any_spec] * (4 + len(extra)),
            out_specs=pl.BlockSpec((depth, width), lambda j, o: (0, at + j)),
            scratch_shapes=[pltpu.VMEM((2, depth, width), BF16), pltpu.SemaphoreType.DMA((2,))],
        ),
        out_shape=jax.ShapeDtypeStruct((depth, full), BF16),
        input_output_aliases={} if so_far is None else {5: 0},
        cost_estimate=pl.CostEstimate(flops=0, bytes_accessed=4 * depth * columns, transcendentals=0),
        name="restore",
    )(order, *pieces, *extra)


def weight_grad_kernel(block, place_ref, lhs_ref, rhs_ref, mine, other, buffer, sems):
    step = pl.program_id(0)
    slot = lax.rem(step, 2)

    def settle(which):
        pltpu.make_async_copy(buffer.at[which], buffer.at[which], sems.at[which]).wait()

    @pl.when(step >= 2)
    def _():
        settle(slot)

    buffer[slot] = dot_f32(lhs_ref[...], rhs_ref[...], ((0,), (0,))).astype(BF16)
    for t in range(8):
        q = place_ref[step * 8 + t]
        source = buffer.at[slot, pl.ds(t * block, block), :]

        @pl.when(q < 16)
        def _():
            pltpu.make_async_copy(
                source, mine.at[pl.ds(pl.multiple_of(q * block, block), block), :], sems.at[slot]
            ).start()

        @pl.when(q >= 16)
        def _():
            pltpu.make_async_copy(
                source, other.at[pl.ds(pl.multiple_of((q - 16) * block, block), block), :], sems.at[slot]
            ).start()

    @pl.when(step == pl.num_programs(0) - 1)
    def _():
        settle(1 - slot)
        settle(slot)


def weight_grad(lhs, rhs, place, column, columns):
    tokens, rows = lhs.shape
    block = rows // BLOCKS
    any_spec = pl.BlockSpec(memory_space=pl.ANY)
    out = jax.ShapeDtypeStruct((16 * block, columns), BF16)
    return pl.pallas_call(
        functools.partial(weight_grad_kernel, block),
        grid_spec=pltpu.PrefetchScalarGridSpec(
            num_scalar_prefetch=1,
            grid=(4,),
            in_specs=[
                pl.BlockSpec((tokens, 8 * block), lambda i, o: (0, i)),
                pl.BlockSpec((tokens, columns), lambda i, o: (0, column)),
            ],
            out_specs=[any_spec, any_spec],
            scratch_shapes=[pltpu.VMEM((2, 8 * block, columns), BF16), pltpu.SemaphoreType.DMA((2,))],
        ),
        out_shape=[out, out],
        cost_estimate=pl.CostEstimate(
            flops=2 * tokens * rows * columns,
            bytes_accessed=2 * (tokens * rows + tokens * columns + rows * columns),
            transcendentals=0,
        ),
        name="weight_grad",
    )(place, lhs, rhs)


def rows_of(packed, start, count):
    return packed[:, start : start + count]


def on_device(
    hypercube,
    tokens,
    seg_ids,
    gain_in,
    w_in,
    conv_weight,
    conv_bias,
    dt_bias,
    a_log,
    d_skip,
    gain_out,
    w_out,
    cotangent,
):
    shards = lax.psum(1, "shard")
    taps, conv_local = conv_weight.shape
    model = tokens.shape[1]
    di = gain_out.shape[0] * shards
    conv_dim = conv_local * shards
    calls = ((0, 1), (1, 2), (3, 3))
    width = GROUP * P_SIZE

    def columns(w, call):
        start, count = call
        own = w[:, di + start * width : di + (start + count) * width]
        if start > 0:
            return own
        head = w[:, 2 * di :]
        return jnp.concatenate([jnp.pad(head, ((0, 0), (0, 4 * N - head.shape[1]))), own], axis=1)

    small = jnp.concatenate([conv_weight.reshape(-1), conv_bias, gain_in, gain_out])
    if hypercube:
        core = lax.axis_index("rep")
        w_half = lax.dynamic_slice_in_dim(w_in, core * (w_in.shape[0] // 2), w_in.shape[0] // 2, 0)
        o_half = lax.dynamic_slice_in_dim(w_out, core * (w_out.shape[0] // 2), w_out.shape[0] // 2, 0)
        near, middle, far = [Gather(columns(w_half, call)) for call in calls]
        gate_gather, out_gather = Gather(w_half[:, :di]), Gather(o_half)
        small_flow = gather_small(small)
        next(small_flow)
        got = []
        for starts in ((near,), (near, middle), (near, middle, far), (near, middle, far)):
            pairs = [each.step(*got) for each in starts] + [small_flow.send(got)]
            got = [pair[1] for pair in pairs]
            if len(starts) == 1:
                later = (far.held, gate_gather.held, out_gather.held), (tokens, seg_ids, dt_bias, a_log, d_skip, core)
                helds, (tokens, seg_ids, dt_bias, a_log, d_skip, core) = after(later, *got)
                far.held, gate_gather.held, out_gather.held = helds
        small_all = small_flow.send(got)
        order, place = block_order(core)
        sent, got = zip(middle.step(*got), far.step(*got), near.swap(*got), near.swap(*got))
        normed_tie = sent + got[2:]
        last_pair = got[:2]
    else:
        small_all = lax.all_gather(small, "shard", axis=0, tiled=False)
        full_w_in = lax.all_gather(w_in, "shard", axis=0, tiled=True)
        full_w_out = lax.all_gather(w_out, "shard", axis=0, tiled=True)
    cut = taps * conv_local
    conv_w = small_all[:, :cut].reshape(shards, taps, conv_local).transpose(1, 0, 2).reshape(taps, -1)
    conv_b = rows_of(small_all, cut, conv_local).reshape(1, -1)
    cut += conv_local
    full_gain_in = rows_of(small_all, cut, gain_in.shape[0]).reshape(1, -1).astype(F32)
    full_gain_out = rows_of(small_all, cut + gain_in.shape[0], gain_out.shape[0]).reshape(1, -1).astype(F32)
    conv_all = jnp.concatenate(
        [conv_w.astype(F32), conv_b.astype(F32), jnp.zeros((3, conv_dim), F32)], axis=0
    )
    conv_x, conv_bc = conv_all[:, :di], conv_all[:, di:]
    inputs = tokens.astype(F32)
    rscale = lax.rsqrt(jnp.mean(inputs * inputs, axis=1, keepdims=True) + EPSILON)
    unit = inputs * rscale
    normed = (unit * full_gain_in).astype(BF16)
    if hypercube:
        normed = after(normed, *normed_tie)
    aux, seg_row = seg_facts(seg_ids[0])
    heads = head_rows(dt_bias, a_log)
    skip = jnp.repeat(d_skip, P_SIZE)[None]

    pcs, w_parts = [], []
    bcv = written = mark = None
    if hypercube:
        sent, got = zip(
            far.step(*last_pair), middle.swap(*last_pair), middle.swap(*last_pair), gate_gather.step(*last_pair)
        )
        pending = {"project": sent, "scan": got[1:3]}
    for index, call in enumerate(calls):
        if hypercube:
            flow = (near, middle, far)[index]
            pieces = flow.pieces()
            pc, w_part = project(
                after(normed, *pending["project"]), pieces, order, None, 0, pieces[0].shape[1]
            )
        else:
            w_part = columns(full_w_in, call)
            pc = mm(normed, w_part)
        if hypercube and index == 0:
            done = far.seen[3], gate_gather.seen[0], pc
            sent, got = zip(far.swap(*done), far.swap(*done), gate_gather.step(*done))
            pc = after(pc, *sent, *done)
        if hypercube and index == 2:
            done = out_gather.seen[1], pc
            sent, got = out_gather.step(*done)
            pc = after(pc, sent, out_gather.seen[1])
        pcs.append((pc, 1 if index == 0 else 0))
        w_parts.append(w_part)
        written = run_forward(
            pc, pcs[-1][1], pcs[0][0], conv_x, conv_bc, aux, seg_row, heads, skip, *call, bcv, written
        )
        mark = written[4]
        if index == 0:
            bcv, bc_slope = written[5:]
        written = written[:5]
        if hypercube and index == 0:
            done = gate_gather.seen[1], mark
            sent, got = zip(gate_gather.step(*done), out_gather.step(*done))
            pending["project"] = (*sent, *far.swapped, done[0])
        if hypercube and index == 1:
            done = gate_gather.seen[2], out_gather.seen[0], mark
            sent, got = zip(gate_gather.step(*done), gate_gather.swap(*done), out_gather.step(*done))
            pending["project"] = sent + done[:2]
    if hypercube:
        done = gate_gather.seen[3], gate_gather.swapped[0], out_gather.seen[2], mark
        sent, got = zip(gate_gather.swap(*done), out_gather.step(*done), out_gather.swap(*done))
        gate_tie = sent + done
    x, y, states, slope, mark = written
    if hypercube:
        gate, w_gate, zg, squares = gate_project(
            after(normed, *gate_tie), gate_gather.pieces(), order, y, full_gain_out + mark[0, 0], None, 0, di
        )
        out_gather.swap(out_gather.seen[3], squares)
        full_w_out = restore(out_gather.pieces(), order, None, 0, model)
    else:
        w_gate = full_w_in[:, :di]
        gate = mm(normed, w_gate)
        gated = y * (gate * jax.nn.sigmoid(gate))
        squares = gated * gated
        zg = (gated * full_gain_out).astype(BF16)
    inverse = lax.rsqrt(jnp.sum(squares, axis=1, keepdims=True) / di + EPSILON)
    projected = inverse * mm(zg, full_w_out)
    output = (inputs + projected).astype(BF16)
    cot = cotangent.astype(F32)
    dots = jnp.sum(cot * projected, axis=1, keepdims=True)
    cot_scaled = (inverse * cot).astype(BF16)
    sig = jax.nn.sigmoid(gate)
    sums = None
    parts = {}
    if hypercube:
        in_block = w_in.shape[0] // 2
        out_sum = Scatter(weight_grad(zg, cot_scaled, place, 0, model), w_out.shape[0] // 2)
        sent, got_out = out_sum.step()
        grad_ynorm = mm_nt(after(cotangent, sent), full_w_out)
    else:
        grad_ynorm = mm_nt(cotangent, full_w_out)
    dz = inverse * (full_gain_out * grad_ynorm) - (y * (gate * sig)) * (inverse * inverse * dots / di)
    dy = (dz * (gate * sig)).astype(BF16)
    dgate = (dz * y * (sig * (1.0 + gate * (1.0 - sig)))).astype(BF16)
    if hypercube:
        sent, got_out = out_sum.step(dgate)
        gate_grad = weight_grad(normed, after(dgate, sent), place, 0, di)
        gate_sum = Scatter(gate_grad, in_block)
        sent, got_gate = gate_sum.step()
        scaled = mm_nt(after(dgate, sent), w_gate)
        done = got_out, got_gate, scaled
        sent, got = zip(out_sum.step(*done), gate_sum.step(*done))
        dy = after(dy, *sent, *done)
    else:
        scaled = mm_nt(dgate, w_gate)
    grad_sums = {}
    for index, call in reversed(list(enumerate(calls))):
        pc, first_x = pcs[index]
        dpart, dcw, dskip, *sums = run_backward(
            dy, x, bcv, states, slope, bc_slope, pc, first_x, pcs[0][0], conv_x, conv_bc, aux, seg_row, heads, skip, *call,
            index == 0, sums,
        )
        parts[index] = (dpart, dcw, dskip)
        if not hypercube:
            scaled = scaled + mm_nt(dpart, w_parts[index])
            continue
        done = *got, dpart
        if index == 2:
            moves = [out_sum, gate_sum]
        elif index == 1:
            moves = [gate_sum, grad_sums[2]]
        else:
            moves = [grad_sums[2], grad_sums[1]]
        sent, got = zip(*[each.step(*done) for each in moves])
        grad = weight_grad(normed, after(dpart, *sent, *done), place, 0, dpart.shape[1])
        grad_sums[index] = Scatter(grad, in_block)
        swap_sent, swap_got = grad_sums[index].step()
        scaled = scaled + mm_nt(after(dpart, swap_sent), w_parts[index])
        if index == 2:
            done = got[0], swap_got, scaled
            sent, late = zip(out_sum.step(*done), grad_sums[2].step(*done))
            got = late + got[1:]
            dy = after(dy, *sent, *done)
        elif index == 1:
            done = *got, swap_got, scaled
            sent, got = zip(gate_sum.step(*done), grad_sums[2].step(*done), grad_sums[1].step(*done))
            dy = after(dy, *sent, *done)
        else:
            last_got = got
    dbcw, dhead = sums
    dcw = jnp.concatenate([parts[index][1] for index in range(len(calls))] + [dbcw], axis=2)
    dskip = jnp.concatenate([parts[index][2] for index in range(len(calls))], axis=1)
    scaled = scaled * full_gain_in
    inner = jnp.mean(unit * scaled, axis=1, keepdims=True)
    grad_tokens = (cot + rscale * (scaled - unit * inner)).astype(BF16)

    conv_sums = dcw.sum(1)
    conv_sums = jnp.concatenate([conv_sums[4:5], conv_sums[3:4], conv_sums[2:3], conv_sums[1:2], conv_sums[0:1]])
    per_head = jnp.concatenate(
        [
            dhead[0].sum(0)[:H],
            dhead[1].sum(0)[:H] * -jnp.exp(a_log),
            dskip.sum(0).reshape(H, P_SIZE).sum(1),
        ]
    )
    conv_part = conv_sums.reshape(taps + 1, shards, conv_local).transpose(1, 0, 2).reshape(shards, -1)
    small_grad = jnp.concatenate([conv_part, jnp.broadcast_to(per_head[None], (shards, 3 * H))], axis=1)
    real = w_in.shape[1] - 2 * di
    if hypercube:
        small_sum = reduce_small(small_grad)[0]
        _, got = grad_sums[0].step(swap_got, *last_got)
        _, late = grad_sums[1].step(swap_got, *last_got)
        _, got = grad_sums[0].step(got, late, grad_tokens)
        grad_sums[1].step(late)
        gate_part, *rest = [each.finish() for each in (gate_sum, grad_sums[2], grad_sums[1], grad_sums[0])]
        rest = rest[::-1]
        own = jnp.concatenate([gate_part, rest[0][:, 4 * N :], *rest[1:], rest[0][:, :real]], axis=1)
        sum_w_in = both_cores(own)
        sum_w_out = both_cores(out_sum.finish())
    else:
        grad_w_out = dot_f32(zg, cot_scaled, ((0,), (0,)))
        rest = [parts[index][0] for index in range(len(calls))]
        grads = jnp.concatenate([dgate, rest[0][:, 4 * N :], *rest[1:], rest[0][:, :real]], axis=1)
        grad_w_in = dot_f32(normed, grads, ((0,), (0,)))
        small_sum = lax.psum(
            lax.psum_scatter(small_grad, "shard", scatter_dimension=0, tiled=True), "rep"
        )[0]
        sum_w_in = lax.psum_scatter(grad_w_in, "shard", scatter_dimension=0, tiled=True)
        sum_w_out = lax.psum_scatter(grad_w_out, "shard", scatter_dimension=0, tiled=True)
        sum_w_in, sum_w_out = lax.psum((sum_w_in, sum_w_out), "rep")
    grad_gain_in = jnp.sum(sum_w_in * w_in.astype(F32), axis=1) / gain_in.astype(F32)
    grad_gain_out = jnp.sum(sum_w_out * w_out.astype(F32), axis=1) / gain_out.astype(F32)
    cut = taps * conv_local
    head_at = cut + conv_local
    return (
        output,
        grad_tokens,
        grad_gain_in,
        sum_w_in,
        small_sum[:cut].reshape(taps, conv_local),
        small_sum[cut:head_at],
        small_sum[head_at : head_at + H],
        small_sum[head_at + H : head_at + 2 * H],
        small_sum[head_at + 2 * H :],
        grad_gain_out,
        sum_w_out,
    )


def both_cores(own):
    partner = swap_cores(own)
    first = lax.axis_index("rep") == 0
    return jnp.concatenate([jnp.where(first, own, partner), jnp.where(first, partner, own)], axis=0)


def reduce_small(rows):
    core = lax.axis_index("rep")
    places = jnp.asarray([reach(order) for order in ORDERS], jnp.int32)[core] ^ lax.axis_index("shard")
    hot = (places[:, None] == jnp.arange(16, dtype=jnp.int32)[None, :]).astype(F32)
    total = dot_f32(hot, rows, ((1,), (0,)), HIGHEST)
    for stage in (3, 2, 1, 0):
        cut = 1 << stage
        total = total[:cut] + exchange(total[cut:], stage)
    return total + swap_cores(total)


def solution(mesh):
    rows = P(("shard", "rep"), None)
    in_specs = (
        rows, rows, P("shard"), P("shard", None), P(None, "shard"), P("shard"), P(), P(), P(), P("shard"),
        P("shard", None), rows,
    )
    out_specs = (
        rows, rows, P("shard"), P("shard", None), P(None, "shard"), P("shard"), P(), P(), P(), P("shard"),
        P("shard", None),
    )
    hypercube = mesh.shape["shard"] == 16 and mesh.shape["rep"] == 2
    return jax.shard_map(
        functools.partial(on_device, hypercube),
        mesh=mesh,
        in_specs=in_specs,
        out_specs=out_specs,
        check_vma=False,
    )
```

```python
import functools

import jax
import jax.numpy as jnp
from jax import lax
from jax.experimental import pallas as pl
from jax.experimental.pallas import tpu as pltpu
from jax.sharding import PartitionSpec as P
from jax.sharding import PartitionSpec as P

H = 48
P_SIZE = 64
N = 128
SPAN = 256
HALF = 128
GROUP = 8
TILE = 128
EPSILON = 1e-05
HIGHEST = lax.Precision.HIGHEST
LOG2E = 1.4426950408889634
NEG = -1e30
F32 = jnp.float32
BF16 = jnp.bfloat16


def dot_f32(a, b, contract, precision=None):
    return lax.dot_general(
        a, b, ((contract[0], contract[1]), ((), ())), preferred_element_type=F32, precision=precision
    )


def mm(a, b):
    return dot_f32(a, b, ((1,), (0,)))


def mm_nt(a, b):
    return dot_f32(a, b, ((1,), (1,)))


def lanes_of(column, rows):
    return jnp.broadcast_to(column, (rows, TILE))


def step_sizes(raw, heads):
    shifted = raw + heads[0:1]
    return jnp.maximum(shifted, 0.0) + jnp.log1p(jnp.exp(-jnp.abs(shifted)))


def conv_taps(ext, same, start, width, rows=SPAN):
    out = [ext[8 : 8 + rows, start : start + width]]
    for offset in (1, 2, 3):
        moved = ext[8 - offset : 8 - offset + rows, start : start + width]
        mask = same[offset - 1]
        if width > TILE:
            mask = jnp.concatenate([mask] * (width // TILE), axis=1)
        out.append(moved * mask)
    return out


def conv_sum(taps, weights):
    total = weights[4:5] + weights[3:4] * taps[0]
    for offset in (1, 2, 3):
        total = total + weights[3 - offset : 4 - offset] * taps[offset]
    return total


def prepare(raw_ref, heads_ref, aux_ref, same):
    aux = aux_ref[...]
    heads = heads_ref[...]
    step = step_sizes(raw_ref[...], heads)
    row = lax.broadcasted_iota(jnp.int32, (SPAN, SPAN), 0)
    col = lax.broadcasted_iota(jnp.int32, (SPAN, SPAN), 1)
    tri = (row >= col).astype(F32)
    cum = dot_f32(tri, step * heads[1:2], ((1,), (0,)), HIGHEST)
    for place in range(5):
        same[place] = lanes_of(aux[:, place : place + 1], SPAN)
    return step, cum, cum - jnp.log2(step)


def pick(first, columns, at):
    return jnp.where(first, lanes_of(columns[:, at : at + 1], first.shape[0]), lanes_of(columns[:, at + 1 : at + 2], first.shape[0]))


def forward_kernel(first_call, base, pc_ref, halo_ref, raw_ref, cw_ref, aux_ref, seg_ref, heads_ref, skip_ref, *rest):
    rest = list(rest)
    if first_call:
        bc_ref, bc_halo_ref, bcw_ref = [rest.pop(0) for _ in range(3)]
        x_out, y_out, st_out, slope_out, mark, bc_out, bc_slope_out = [rest.pop(0) for _ in range(7)]
    else:
        bc_out = rest.pop(0)
        mark_ref = rest[4]
        rest = rest[5:]
        x_out, y_out, st_out, slope_out, mark = [rest.pop(0) for _ in range(5)]
    state, scores, block, same, pack, cum_rows, w_rows, keep_row, b_t, ext, ext_bc = rest
    span = pl.program_id(0)
    group = pl.program_id(1)
    group_head = base + GROUP * group

    @pl.when((span == 0) & (group == 0))
    def _():
        state[...] = jnp.zeros_like(state)
        mark[...] = jnp.zeros_like(mark) if first_call else mark_ref[...]

    @pl.when(group == 0)
    def _():
        step, cum, shifted = prepare(raw_ref, heads_ref, aux_ref, same)
        last = cum[SPAN - 1 : SPAN]
        pack[...] = cum
        cum_rows[...] = shifted.T
        w_rows[...] = (jnp.exp2(last - shifted) * same[4]).T
        keep_row[...] = jnp.broadcast_to(jnp.exp2(last) * same[3, SPAN - 1 : SPAN], (8, TILE))
        if first_call:
            ext_bc[0:8] = bc_halo_ref[...]
            ext_bc[8:] = bc_ref[...]
            total = conv_sum(conv_taps(ext_bc, same, 0, 2 * N), bcw_ref[...])
            gate = jax.nn.sigmoid(total)
            both = total * gate
            bc_out[...] = both.astype(BF16)
            bc_slope_out[...] = (gate + both * (1.0 - gate)).astype(BF16)
        row = lax.broadcasted_iota(jnp.int32, (SPAN, SPAN), 0)
        col = lax.broadcasted_iota(jnp.int32, (SPAN, SPAN), 1)
        linked = (row >= col) & (aux_ref[:, 5:6] == seg_ref[...])
        block[...] = jnp.where(linked, 0.0, NEG)
        scores[...] = mm_nt(bc_out[:, N:], bc_out[:, :N])
        b_t[...] = bc_out[:, :N].astype(F32).T

    ext[0:8] = halo_ref[...]
    ext[8:] = pc_ref[...]
    shift = lax.rem(TILE - group_head, TILE)
    cums = pltpu.roll(pack[...], shift, 1)
    keep = jnp.broadcast_to(pltpu.roll(keep_row[...], shift, 1)[0:1], (N, TILE))
    first = lax.broadcasted_iota(jnp.int32, (SPAN, TILE), 1) < P_SIZE
    query = bc_out[:, N:]
    empty = jnp.zeros((HALF, HALF), BF16)
    wide = lambda parts: jnp.concatenate(parts, axis=1)
    for quad in range(GROUP // 4):
        xbs, outs, entries, keeps, fresh = [], [], [], [], []
        for pair in (2 * quad, 2 * quad + 1):
            at = pair * TILE
            total = conv_sum(conv_taps(ext, same, at, TILE), cw_ref[:, at : at + TILE])
            gate = jax.nn.sigmoid(total)
            x = total * gate
            xb = x.astype(BF16)
            x_out[:, at : at + TILE] = xb
            slope_out[:, at : at + TILE] = (gate + x * (1.0 - gate)).astype(BF16)
            mixes, weighted, cum_cols = [], [], []
            for head in (2 * pair, 2 * pair + 1):
                cum_col = lanes_of(cums[:, head : head + 1], SPAN)
                cum_cols.append(cum_col)
                cum_row = cum_rows[pl.ds(group_head + head, 1), :]
                blocks = []
                for i, j in ((0, 0), (1, 0), (1, 1)):
                    rows = slice(i * HALF, (i + 1) * HALF)
                    cols = slice(j * HALF, (j + 1) * HALF)
                    gap = cum_col[rows] - cum_row[:, cols] + block[rows, cols]
                    blocks.append((jnp.exp2(gap) * scores[rows, cols]).astype(BF16))
                mixes.append(wide([blocks[0], empty]))
                mixes.append(wide(blocks[1:]))
                weighted.append((b_t[...] * w_rows[pl.ds(group_head + head, 1), :]).astype(BF16))
            inner = mm(jnp.concatenate(mixes + weighted, axis=0), xb)
            outs.append(jnp.where(first, inner[:SPAN], inner[SPAN : 2 * SPAN]))
            fresh.append(jnp.where(first[:N], inner[2 * SPAN : 2 * SPAN + N], inner[2 * SPAN + N :]))
            xbs.append(xb)
            entries.append(jnp.exp2(jnp.where(first, cum_cols[0], cum_cols[1])) * same[3])
            keeps.append(pick(first[:N], keep, 2 * pair))
        both = slice(quad * 2 * TILE, (quad + 1) * 2 * TILE)
        tile = pl.ds(pl.multiple_of(group * GROUP * P_SIZE + quad * 2 * TILE, 2 * TILE), 2 * TILE)
        old = state[:, tile]
        old_b = old.astype(BF16)
        st_out[:, both] = old_b
        carried = mm(query, old_b)
        y = wide(outs) + wide(entries) * carried + skip_ref[:, both] * wide(xbs).astype(F32)
        y_out[:, both] = y.astype(BF16)
        state[:, tile] = old * wide(keeps) + wide(fresh)


def run_forward(pc, first_x, pc_bc, conv_x, conv_bc, aux, seg_row, heads, skip, start, count, bcv, before):
    tokens = pc.shape[0]
    spans = tokens // SPAN
    di = skip.shape[1]
    width = GROUP * P_SIZE
    own = count * width
    first_call = before is None
    any_spec = pl.BlockSpec(memory_space=pl.ANY)
    halo = lambda s: jnp.maximum(s * (SPAN // 8) - 1, 0)
    wide = pl.BlockSpec((SPAN, width), lambda s, g: (s, start + g))
    bcv_spec = pl.BlockSpec((SPAN, 2 * N), lambda s, g: (s, 0))
    in_specs = [
        pl.BlockSpec((SPAN, width), lambda s, g: (s, first_x + g)),
        pl.BlockSpec((8, width), lambda s, g: (halo(s), first_x + g)),
        pl.BlockSpec((SPAN, TILE), lambda s, g: (s, 2)),
        pl.BlockSpec((8, width), lambda s, g: (0, start + g)),
        pl.BlockSpec((SPAN, 8), lambda s, g: (s, 0)),
        pl.BlockSpec((1, SPAN), lambda s, g: (0, s)),
        pl.BlockSpec((8, TILE), lambda s, g: (0, 0)),
        pl.BlockSpec((1, width), lambda s, g: (0, start + g)),
    ]
    args = [pc, pc, pc_bc, conv_x, aux, seg_row, heads, skip]
    mark_spec = pl.BlockSpec((8, TILE), lambda s, g: (0, 0))
    out_specs = [wide, wide, pl.BlockSpec((N, width), lambda s, g: (s, start + g)), wide, mark_spec]
    out_shape = [
        jax.ShapeDtypeStruct((tokens, di), BF16),
        jax.ShapeDtypeStruct((tokens, di), BF16),
        jax.ShapeDtypeStruct((spans * N, di), BF16),
        jax.ShapeDtypeStruct((tokens, di), BF16),
        jax.ShapeDtypeStruct((8, TILE), F32),
    ]
    if first_call:
        in_specs += [
            pl.BlockSpec((SPAN, 2 * N), lambda s, g: (s, 0)),
            pl.BlockSpec((8, 2 * N), lambda s, g: (halo(s), 0)),
            pl.BlockSpec((8, 2 * N), lambda s, g: (0, 0)),
        ]
        args += [pc_bc, pc_bc, conv_bc]
        out_specs += [bcv_spec, bcv_spec]
        out_shape += [jax.ShapeDtypeStruct((tokens, 2 * N), BF16)] * 2
        aliases = {}
    else:
        in_specs += [bcv_spec, any_spec, any_spec, any_spec, any_spec, mark_spec]
        args += [bcv, *before]
        aliases = {9: 0, 10: 1, 11: 2, 12: 3}
    return pl.pallas_call(
        functools.partial(forward_kernel, first_call, start * GROUP),
        grid_spec=pltpu.PrefetchScalarGridSpec(
            num_scalar_prefetch=0,
            grid=(spans, count),
            in_specs=in_specs,
            out_specs=out_specs,
            scratch_shapes=[
                pltpu.VMEM((N, own), F32),
                pltpu.VMEM((SPAN, SPAN), F32),
                pltpu.VMEM((SPAN, SPAN), F32),
                pltpu.VMEM((5, SPAN, TILE), F32),
                pltpu.VMEM((SPAN, TILE), F32),
                pltpu.VMEM((TILE, SPAN), F32),
                pltpu.VMEM((TILE, SPAN), F32),
                pltpu.VMEM((8, TILE), F32),
                pltpu.VMEM((N, SPAN), F32),
                pltpu.VMEM((SPAN + 8, width), F32),
                pltpu.VMEM((SPAN + 8, 2 * N), F32),
            ],
        ),
        out_shape=out_shape,
        input_output_aliases=aliases,
        compiler_params=pltpu.CompilerParams(dimension_semantics=("arbitrary", "arbitrary")),
        cost_estimate=pl.CostEstimate(flops=int(5e9 * count), bytes_accessed=14 * tokens * own, transcendentals=0),
        name="scan_forward",
    )(*args)


def conv_back(grad, slope, signal, same, weights, carry):
    width = grad.shape[1]
    du = grad * slope.astype(F32)

    def add_rows(values):
        return jnp.sum(values.reshape(SPAN // 8, 8, width), axis=0)

    out = weights[3:4] * du
    sums = [add_rows(du), add_rows(du * signal)]
    for offset in (1, 2, 3):
        mask = same[offset - 1]
        if width > TILE:
            mask = jnp.concatenate([mask] * (width // TILE), axis=1)
        masked = du * mask
        moved = jnp.concatenate([masked, carry[offset - 1]], axis=0)[offset : offset + SPAN]
        carry[offset - 1] = masked[0:8]
        out = out + weights[3 - offset : 4 - offset] * moved
        sums.append(add_rows(moved * signal))
    return out, sums


def backward_kernel(
    first_call, last_call, base,
    dy_ref, x_ref, bcv_ref, st_ref, slope_ref, pc_ref, raw_ref, cw_ref, aux_ref, seg_ref, heads_ref, skip_ref, *rest,
):
    rest = list(rest)
    before = None if first_call else [rest.pop(0) for _ in range(4)]
    if last_call:
        bc_ref, bc_slope_ref, bcw_ref = [rest.pop(0) for _ in range(3)]
    dproj_out, dcw_out, dskip_out = [rest.pop(0) for _ in range(3)]
    if last_call:
        dbcw_out, dhead_out = [rest.pop(0) for _ in range(2)]
    else:
        after_out = [rest.pop(0) for _ in range(4)]
    (
        dstate, scores, block, dscores, same, pack, last_row, cum_rows, c_t,
        carry, carry_bc, d_bc, per_row, dcum_rows, dlast,
    ) = rest
    back = pl.program_id(0)
    group = pl.program_id(1)
    groups = pl.num_programs(1)
    width = GROUP * P_SIZE
    group_head = base + GROUP * group
    first_x = 4 * N if last_call else 0

    @pl.when((back == 0) & (group == 0))
    def _():
        dstate[...] = jnp.zeros_like(dstate)
        carry[...] = jnp.zeros_like(carry)
        dcw_out[...] = jnp.zeros_like(dcw_out)
        dskip_out[...] = jnp.zeros_like(dskip_out)
        dcum_rows[...] = jnp.zeros_like(dcum_rows)
        if last_call:
            carry_bc[...] = jnp.zeros_like(carry_bc)
            dbcw_out[...] = jnp.zeros_like(dbcw_out)
            dhead_out[...] = jnp.zeros_like(dhead_out)

    keys = bcv_ref[:, :N]
    query = bcv_ref[:, N:]
    lane = lax.broadcasted_iota(jnp.int32, (SPAN, TILE), 1)

    @pl.when(group == 0)
    def _():
        step, cum, shifted = prepare(raw_ref, heads_ref, aux_ref, same)
        entry = jnp.exp2(cum) * same[3]
        pack[...] = jnp.where(lane < 64, shifted, pltpu.roll(entry, 64, 1))
        last_row[...] = jnp.broadcast_to(cum[SPAN - 1 : SPAN], (8, TILE))
        cum_rows[...] = cum.T
        row = lax.broadcasted_iota(jnp.int32, (SPAN, SPAN), 0)
        col = lax.broadcasted_iota(jnp.int32, (SPAN, SPAN), 1)
        linked = (row <= col) & (aux_ref[:, 5:6] == seg_ref[...])
        block[...] = jnp.where(linked, 0.0, NEG)
        scores[...] = mm_nt(keys, query)
        c_t[...] = query.T
        per_row[...] = jnp.zeros_like(per_row)
        if first_call:
            dscores[...] = jnp.zeros_like(dscores)
            d_bc[...] = jnp.zeros_like(d_bc)
            dlast[...] = jnp.zeros_like(dlast)
        else:
            dscores[...] = before[0][...]
            d_bc[...] = before[1][...]
            per_row[0] = before[2][:, :TILE]
            per_row[2] = before[2][:, TILE:]
            dlast[...] = before[3][...]

    shift = lax.rem(TILE - group_head, TILE)
    cols = pltpu.roll(pack[...], shift, 1)
    last_cum = pltpu.roll(last_row[...], shift, 1)[0:1]
    keep_mask = same[3, SPAN - 1 : SPAN]
    first = lane < P_SIZE
    lane_row = lax.broadcasted_iota(jnp.int32, (2 * TILE, TILE), 0) // P_SIZE
    lane_col = lax.broadcasted_iota(jnp.int32, (2 * TILE, TILE), 1)
    sums = jnp.zeros((SPAN, TILE), F32)
    last_sum = jnp.zeros((1, TILE), F32)
    group_at = group * width
    empty = jnp.zeros((HALF, HALF), BF16)
    wide = lambda parts: jnp.concatenate(parts, axis=1)
    for quad in range(GROUP // 4):
        both = slice(quad * 2 * TILE, (quad + 1) * 2 * TILE)
        tile = pl.ds(pl.multiple_of(group_at + quad * 2 * TILE, 2 * TILE), 2 * TILE)
        entries, tails, keeps, inners = [], [], [], []
        for pair in (2 * quad, 2 * quad + 1):
            at = pair * TILE
            heads = (2 * pair, 2 * pair + 1)
            dy_pair = dy_ref[:, at : at + TILE]
            xb = x_ref[:, at : at + TILE]
            nothing = jnp.zeros_like(xb)
            split = jnp.concatenate([jnp.where(first, xb, nothing), jnp.where(first, nothing, xb)], axis=0)
            g_both = mm_nt(split, dy_pair)
            cum_cols = [lanes_of(cols[:, head : head + 1], SPAN) for head in heads]
            cum_lines = [cum_rows[pl.ds(group_head + head, 1), :] for head in heads]
            mixes = [[], []]
            across = [[], []]
            down = [[], []]
            for j, i in ((0, 0), (0, 1), (1, 1)):
                rows = slice(j * HALF, (j + 1) * HALF)
                cells = slice(i * HALF, (i + 1) * HALF)
                spread = jnp.zeros((HALF, HALF), F32)
                for which in (0, 1):
                    decay = jnp.exp2(cum_lines[which][:, cells] - cum_cols[which][rows] + block[rows, cells])
                    mix = decay * scores[rows, cells]
                    g = g_both[which * SPAN + j * HALF : which * SPAN + (j + 1) * HALF, cells]
                    spread = spread + decay * g
                    w = mix * g
                    mixes[which].append(mix.astype(BF16))
                    across[which].append(w)
                    down[which].append(jnp.sum(w, axis=0, keepdims=True))
                dscores[rows, cells] += spread
            lefts = []
            for which in (0, 1):
                row_sum = jnp.concatenate(
                    [
                        jnp.sum(across[which][0] + across[which][1], axis=1, keepdims=True),
                        jnp.sum(across[which][2], axis=1, keepdims=True),
                    ],
                    axis=0,
                )
                sums = sums - jnp.where(lane == 2 * GROUP + heads[which], row_sum, 0.0)
                dcum_rows[pl.ds(group_head + heads[which], 1), :] = wide(
                    [down[which][0], down[which][1] + down[which][2]]
                )
                lefts += [wide(mixes[which][:2]), wide([empty, mixes[which][2]])]
            inner = mm(jnp.concatenate(lefts, axis=0), dy_pair)
            inners.append(jnp.where(first, inner[:SPAN], inner[SPAN:]))
            last_pair = jnp.where(
                first[0:1],
                jnp.broadcast_to(last_cum[:, heads[0] : heads[0] + 1], (1, TILE)),
                jnp.broadcast_to(last_cum[:, heads[1] : heads[1] + 1], (1, TILE)),
            )
            tails.append(jnp.exp2(last_pair - jnp.where(first, cum_cols[0], cum_cols[1])) * same[4])
            keeps.append(jnp.exp2(last_pair) * keep_mask)
            entries.append(pick(first, cols, 64 + 2 * pair))
        dyf = dy_ref[:, both].astype(F32)
        xf = x_ref[:, both].astype(F32)
        tail = wide(tails)
        stb = st_ref[:, both]
        ds = dstate[:, tile]
        dsb = ds.astype(BF16)
        dye_f = dyf * wide(entries)
        dye = dye_f.astype(BF16)
        fresh = mm(keys, dsb) * tail
        total = wide(inners) + fresh
        d_bc[:, N:] += mm_nt(dye, stb)
        d_bc[:, :N] += mm_nt((xf * tail).astype(BF16), dsb)

        def head_sum(values, kind):
            spread = (lane_col == kind * GROUP + 4 * quad + lane_row).astype(BF16)
            return mm(values.astype(BF16), spread)

        sums = sums + head_sum(xf * total, 0) + head_sum(xf * fresh, 1) + head_sum(dye_f * mm(query, stb), 2)
        kept = ds * wide(keeps)
        kept_sum = jnp.sum(kept * stb.astype(F32), axis=0, keepdims=True)
        lane_pair = lax.broadcasted_iota(jnp.int32, (1, 2 * TILE), 1) // P_SIZE
        for head in range(4):
            one = jnp.sum(jnp.where(lane_pair == head, kept_sum, 0.0), axis=1, keepdims=True)
            last_sum = last_sum + jnp.where(lane[0:1] == 4 * quad + head, one, 0.0)
        dstate[:, tile] = kept + mm(c_t[...], dye)
        dskip_out[:, tile] += jnp.sum((dyf * xf).reshape(SPAN // 8, 8, 2 * TILE), axis=0)
        dx = total + skip_ref[:, both] * dyf
        for part in (0, 1):
            at = (2 * quad + part) * TILE
            one = pl.ds(pl.multiple_of(group_at + at, TILE), TILE)
            out, conv_sums = conv_back(
                dx[:, part * TILE : (part + 1) * TILE], slope_ref[:, at : at + TILE], pc_ref[:, at : at + TILE],
                same, cw_ref[:, at : at + TILE], carry.at[:, :, one],
            )
            dproj_out[:, pl.ds(pl.multiple_of(first_x + group_at + at, TILE), TILE)] = out.astype(BF16)
            for k, value in enumerate(conv_sums):
                dcw_out[k, :, one] += value

    in_place = (lane >= group_head) & (lane < group_head + GROUP)
    for kind in range(3):
        moved = pltpu.roll(sums, lax.rem(group_head + TILE - GROUP * kind, TILE), 1)
        per_row[kind] += jnp.where(in_place, moved, 0.0)
    moved = pltpu.roll(jnp.broadcast_to(last_sum, (8, TILE)), group_head, 1)
    dlast[...] += jnp.where(in_place[0:8], moved, 0.0)

    @pl.when(group == groups - 1)
    def _():
        state_part = per_row[1]
        dcum = dcum_rows[...].T + per_row[2] - state_part
        dlast_all = dlast[0:1] + jnp.sum(state_part, axis=0, keepdims=True)
        if not last_call:
            after_out[0][...] = dscores[...]
            after_out[1][...] = d_bc[...]
            after_out[2][:, :TILE] = per_row[0]
            after_out[2][:, TILE:] = dcum
            after_out[3][...] = jnp.broadcast_to(dlast_all, (8, TILE))
            return
        ds_b = dscores[...].astype(BF16)
        grad_b = d_bc[:, :N] + mm(ds_b, query)
        grad_c = d_bc[:, N:] + mm(dscores[...].T.astype(BF16), keys)
        out, conv_sums = conv_back(
            wide([grad_b, grad_c]), bc_slope_ref[...], bc_ref[...], same, bcw_ref[...], carry_bc
        )
        dproj_out[:, : 2 * N] = out.astype(BF16)
        for k, value in enumerate(conv_sums):
            dbcw_out[k] += value
        heads = heads_ref[...]
        shifted = raw_ref[...] + heads[0:1]
        step = step_sizes(raw_ref[...], heads)
        slope = jax.nn.sigmoid(shifted)
        row = lax.broadcasted_iota(jnp.int32, (SPAN, SPAN), 0)
        col = lax.broadcasted_iota(jnp.int32, (SPAN, SPAN), 1)
        tri = (row <= col).astype(F32)
        da = dot_f32(tri, dcum, ((1,), (0,)), HIGHEST) + dlast_all
        small = shifted < -16.0
        ratio = jnp.where(small, 1.0, slope / jnp.where(small, 1.0, step))
        live = lane < H
        draw = jnp.where(live, per_row[0] * ratio + da * heads[2:3] * slope, 0.0)
        dproj_out[:, 2 * N : 3 * N] = draw.astype(BF16)
        dproj_out[:, 3 * N : 4 * N] = jnp.zeros((SPAN, N), BF16)
        dhead_out[0] += jnp.sum(draw.reshape(SPAN // 8, 8, TILE), axis=0)
        dhead_out[1] += jnp.sum(jnp.where(live, da * step, 0.0).reshape(SPAN // 8, 8, TILE), axis=0)


def run_backward(
    dy, x, bcv, states, slope, bc_slope, pc, first_x, pc_bc, conv_x, conv_bc, aux, seg_row, heads, skip, start, count, last, before
):
    tokens, di = dy.shape
    spans = tokens // SPAN
    width = GROUP * P_SIZE
    turn = lambda s: spans - 1 - s
    own = count * width
    out_width = own + (4 * N if last else 0)
    sums_specs = [
        pl.BlockSpec((SPAN, SPAN), lambda s, g: (turn(s), 0)),
        pl.BlockSpec((SPAN, 2 * N), lambda s, g: (turn(s), 0)),
        pl.BlockSpec((SPAN, 2 * TILE), lambda s, g: (turn(s), 0)),
        pl.BlockSpec((8, TILE), lambda s, g: (turn(s), 0)),
    ]
    sums_shapes = [
        jax.ShapeDtypeStruct((tokens, SPAN), F32),
        jax.ShapeDtypeStruct((tokens, 2 * N), F32),
        jax.ShapeDtypeStruct((tokens, 2 * TILE), F32),
        jax.ShapeDtypeStruct((spans * 8, TILE), F32),
    ]
    out_specs = [
        pl.BlockSpec((SPAN, out_width), lambda s, g: (turn(s), 0)),
        pl.BlockSpec((5, 8, own), lambda s, g: (0, 0, 0)),
        pl.BlockSpec((8, own), lambda s, g: (0, 0)),
    ]
    out_shape = [
        jax.ShapeDtypeStruct((tokens, out_width), BF16),
        jax.ShapeDtypeStruct((5, 8, own), F32),
        jax.ShapeDtypeStruct((8, own), F32),
    ]
    wide = pl.BlockSpec((SPAN, width), lambda s, g: (turn(s), start + g))
    in_specs = [
        wide,
        wide,
        pl.BlockSpec((SPAN, 2 * N), lambda s, g: (turn(s), 0)),
        pl.BlockSpec((N, width), lambda s, g: (turn(s), start + g)),
        wide,
        pl.BlockSpec((SPAN, width), lambda s, g: (turn(s), first_x + g)),
        pl.BlockSpec((SPAN, TILE), lambda s, g: (turn(s), 2)),
        pl.BlockSpec((8, width), lambda s, g: (0, start + g)),
        pl.BlockSpec((SPAN, 8), lambda s, g: (turn(s), 0)),
        pl.BlockSpec((1, SPAN), lambda s, g: (0, turn(s))),
        pl.BlockSpec((8, TILE), lambda s, g: (0, 0)),
        pl.BlockSpec((1, width), lambda s, g: (0, start + g)),
    ]
    args = [dy, x, bcv, states, slope, pc, pc_bc, conv_x, aux, seg_row, heads, skip]
    if before is not None:
        in_specs += sums_specs
        args += before
    if last:
        in_specs += [
            pl.BlockSpec((SPAN, 2 * N), lambda s, g: (turn(s), 0)),
            pl.BlockSpec((SPAN, 2 * N), lambda s, g: (turn(s), 0)),
            pl.BlockSpec((8, 2 * N), lambda s, g: (0, 0)),
        ]
        args += [pc_bc, bc_slope, conv_bc]
        out_specs += [
            pl.BlockSpec((5, 8, 2 * N), lambda s, g: (0, 0, 0)),
            pl.BlockSpec((2, 8, TILE), lambda s, g: (0, 0, 0)),
        ]
        out_shape += [
            jax.ShapeDtypeStruct((5, 8, 2 * N), F32),
            jax.ShapeDtypeStruct((2, 8, TILE), F32),
        ]
    else:
        out_specs += sums_specs
        out_shape += sums_shapes
    return pl.pallas_call(
        functools.partial(backward_kernel, before is None, last, start * GROUP),
        grid_spec=pltpu.PrefetchScalarGridSpec(
            num_scalar_prefetch=0,
            grid=(spans, count),
            in_specs=in_specs,
            out_specs=out_specs,
            scratch_shapes=[
                pltpu.VMEM((N, own), F32),
                pltpu.VMEM((SPAN, SPAN), F32),
                pltpu.VMEM((SPAN, SPAN), F32),
                pltpu.VMEM((SPAN, SPAN), F32),
                pltpu.VMEM((5, SPAN, TILE), F32),
                pltpu.VMEM((SPAN, TILE), F32),
                pltpu.VMEM((8, TILE), F32),
                pltpu.VMEM((TILE, SPAN), F32),
                pltpu.VMEM((N, SPAN), BF16),
                pltpu.VMEM((3, 8, own), F32),
                pltpu.VMEM((3, 8, 2 * N), F32),
                pltpu.VMEM((SPAN, 2 * N), F32),
                pltpu.VMEM((3, SPAN, TILE), F32),
                pltpu.VMEM((TILE, SPAN), F32),
                pltpu.VMEM((8, TILE), F32),
            ],
        ),
        out_shape=out_shape,
        compiler_params=pltpu.CompilerParams(dimension_semantics=("arbitrary", "arbitrary")),
        cost_estimate=pl.CostEstimate(
            flops=int(1.2e10 * count), bytes_accessed=12 * tokens * own, transcendentals=0
        ),
        name="scan_backward",
    )(*args)


def seg_facts(seg):
    length = seg.shape[0]
    cols = []
    for offset in (1, 2, 3):
        moved = jnp.concatenate([jnp.full((offset,), -1, jnp.int32), seg[:-offset]])
        cols.append((moved == seg).astype(F32))
    spans = length // SPAN
    ends = seg[SPAN - 1 :: SPAN]
    before = jnp.concatenate([seg[:1], ends[:-1]])
    cols.append((seg == jnp.repeat(before, SPAN)).astype(F32))
    cols.append((seg == jnp.repeat(ends, SPAN)).astype(F32))
    value = seg.astype(F32)
    cols.append(value)
    cols.append(value)
    cols.append(value)
    return jnp.stack(cols, axis=1), value[None, :]


def head_rows(dt_bias, a_log):
    rate = -jnp.exp(a_log)
    rows = jnp.stack([dt_bias, rate * LOG2E, rate] + [jnp.zeros_like(rate)] * 5, axis=0)
    return jnp.pad(rows, ((0, 0), (0, TILE - H)))


BLOCKS = 32
ORDERS = ((8, 1, 4, 2), (8, 2, 4, 1))


def reach(masks):
    out = [0]
    for mask in masks:
        out = out + [mask ^ place for place in out]
    return out


def exchange(values, stage):
    pairs = []
    for shard in range(16):
        for core in range(2):
            pairs.append((shard * 2 + core, (shard ^ ORDERS[core][stage]) * 2 + core))
    return lax.ppermute(values, ("shard", "rep"), pairs)


def swap_cores(values):
    return lax.ppermute(values, "rep", [(0, 1), (1, 0)])


def after(values, *others):
    return lax.optimization_barrier((values, *others))[0]


class Gather:
    def __init__(self, local):
        self.held = local
        self.seen = []
        self.swapped = []

    def step(self, *ahead):
        stage = len(self.seen)
        if stage > 0:
            self.held = jnp.concatenate([self.held, after(self.seen[-1], *ahead)], axis=0)
        elif ahead:
            self.held = after(self.held, *ahead)
        got = exchange(self.held, stage)
        self.seen.append(got)
        return self.held, got

    def swap(self, *ahead):
        send = after(self.held if not self.swapped else self.seen[3], *ahead)
        self.swapped.append(swap_cores(send))
        return send, self.swapped[-1]

    def pieces(self):
        return self.held, self.seen[3], *self.swapped


def gather_small(local):
    held = local[None]
    ahead = yield None
    for stage in range(4):
        send = after(held, *ahead)
        got = exchange(send, stage)
        ahead = yield send, got
        held = jnp.concatenate([send, got], axis=0)
    core = lax.axis_index("rep")
    places = jnp.asarray([reach(order) for order in ORDERS], jnp.int32)[core] ^ lax.axis_index("shard")
    hot = (places[None, :] == jnp.arange(16, dtype=jnp.int32)[:, None]).astype(local.dtype)
    yield dot_f32(hot, held, ((1,), (0,)), HIGHEST).astype(local.dtype)


class Scatter:
    def __init__(self, partial, block):
        mine, self.other = partial
        self.terms = [mine]
        self.block = block
        self.left = [3, 2, 1, 0]

    def rows(self, start, stop):
        total = self.terms[0][start:stop].astype(F32)
        for term in self.terms[1:]:
            total = total + term[start:stop].astype(F32)
        return total

    def step(self, *ahead):
        if len(self.terms) == 1:
            self.other = after(self.other, *ahead)
            self.terms.append(swap_cores(self.other))
            return self.other, self.terms[-1]
        if self.left:
            stage = self.left.pop(0)
            cut = self.block << stage
            self.terms[-1] = after(self.terms[-1], *ahead)
            send = self.rows(cut, 2 * cut).astype(BF16)
            self.terms.append(exchange(send, stage))
            return send, self.terms[-1]
        return self.terms[-1], self.terms[-1]

    def finish(self):
        while self.left:
            self.step()
        return self.rows(0, self.block)


def block_order(core):
    shard = lax.axis_index("shard")
    tables = jnp.asarray([reach(order) for order in ORDERS], jnp.int32)
    inverse = jnp.asarray(
        [[reach(order).index(mask) for mask in range(16)] for order in ORDERS], jnp.int32
    )
    own = 2 * (tables[core] ^ shard) + core
    partner = 2 * (tables[1 - core] ^ shard) + (1 - core)
    order = jnp.concatenate([own, partner])
    natural = jnp.arange(BLOCKS, dtype=jnp.int32)
    which = natural % 2
    place = inverse[which, (natural // 2) ^ shard] + 16 * (which != core).astype(jnp.int32)
    return order, place


def fetch_tile(order_ref, pieces, buffer, sems, tile, slot, block, width):
    for q in range(BLOCKS):
        pltpu.make_async_copy(
            pieces[q // 8].at[pl.ds((q % 8) * block, block), pl.ds(pl.multiple_of(tile * width, width), width)],
            buffer.at[slot, pl.ds(pl.multiple_of(order_ref[q] * block, block), block), :],
            sems.at[slot],
        ).start()


def next_tile(order_ref, pieces, buffer, sems, block, width):
    tile = pl.program_id(0)
    slot = lax.rem(tile, 2)

    @pl.when(tile == 0)
    def _():
        fetch_tile(order_ref, pieces, buffer, sems, tile, slot, block, width)

    @pl.when(tile + 1 < pl.num_programs(0))
    def _():
        fetch_tile(order_ref, pieces, buffer, sems, tile + 1, 1 - slot, block, width)

    pltpu.make_async_copy(buffer.at[slot], buffer.at[slot], sems.at[slot]).wait()
    return slot


def project_kernel(block, width, order_ref, x_ref, p0, p1, p2, p3, *rest):
    out_ref, w_ref, buffer, sems = rest[-4:]
    slot = next_tile(order_ref, (p0, p1, p2, p3), buffer, sems, block, width)
    w = buffer[slot]
    w_ref[...] = w
    for i in range(x_ref.shape[0] // SPAN):
        rows = slice(i * SPAN, (i + 1) * SPAN)
        out_ref[rows] = mm(x_ref[rows], w)


def project(x, pieces, order, so_far, start, full, width=512):
    tokens, depth = x.shape
    columns = pieces[0].shape[1]
    block = depth // BLOCKS
    at = start // width
    any_spec = pl.BlockSpec(memory_space=pl.ANY)
    extra = [] if so_far is None else list(so_far)
    return pl.pallas_call(
        functools.partial(project_kernel, block, width),
        grid_spec=pltpu.PrefetchScalarGridSpec(
            num_scalar_prefetch=1,
            grid=(columns // width,),
            in_specs=[pl.BlockSpec((tokens, depth), lambda j, o: (0, 0))] + [any_spec] * (4 + len(extra)),
            out_specs=[
                pl.BlockSpec((tokens, width), lambda j, o: (0, at + j)),
                pl.BlockSpec((depth, width), lambda j, o: (0, at + j)),
            ],
            scratch_shapes=[pltpu.VMEM((2, depth, width), BF16), pltpu.SemaphoreType.DMA((2,))],
        ),
        out_shape=[jax.ShapeDtypeStruct((tokens, full), F32), jax.ShapeDtypeStruct((depth, full), BF16)],
        input_output_aliases={} if so_far is None else {6: 0, 7: 1},
        cost_estimate=pl.CostEstimate(
            flops=2 * tokens * depth * columns,
            bytes_accessed=4 * depth * columns + 4 * tokens * columns + 2 * tokens * depth,
            transcendentals=0,
        ),
        name="project",
    )(order, x, *pieces, *extra)


def gate_kernel(block, width, order_ref, x_ref, p0, p1, p2, p3, y_ref, gain_ref, *rest):
    gate_ref, w_ref, zg_ref, square_ref, buffer, sems = rest[-6:]
    slot = next_tile(order_ref, (p0, p1, p2, p3), buffer, sems, block, width)
    w = buffer[slot]
    w_ref[...] = w

    @pl.when(pl.program_id(0) == 0)
    def _():
        square_ref[...] = jnp.zeros_like(square_ref)

    for i in range(x_ref.shape[0] // SPAN):
        rows = slice(i * SPAN, (i + 1) * SPAN)
        gate = mm(x_ref[rows], w)
        gate_ref[rows] = gate.astype(BF16)
        gated = y_ref[rows].astype(F32) * (gate * jax.nn.sigmoid(gate))
        zg_ref[rows] = (gated * gain_ref[...]).astype(BF16)
        square = gated * gated
        total = square[:, :TILE]
        for k in range(1, width // TILE):
            total = total + square[:, k * TILE : (k + 1) * TILE]
        square_ref[rows] += total


def gate_project(x, pieces, order, y, gain, so_far, start, full, width=512):
    tokens, depth = x.shape
    columns = pieces[0].shape[1]
    block = depth // BLOCKS
    at = start // width
    any_spec = pl.BlockSpec(memory_space=pl.ANY)
    extra = [] if so_far is None else list(so_far)
    wide = pl.BlockSpec((tokens, width), lambda j, o: (0, at + j))
    return pl.pallas_call(
        functools.partial(gate_kernel, block, width),
        grid_spec=pltpu.PrefetchScalarGridSpec(
            num_scalar_prefetch=1,
            grid=(columns // width,),
            in_specs=[pl.BlockSpec((tokens, depth), lambda j, o: (0, 0))]
            + [any_spec] * 4
            + [wide, pl.BlockSpec((1, width), lambda j, o: (0, at + j))]
            + [any_spec] * len(extra),
            out_specs=[
                wide,
                pl.BlockSpec((depth, width), lambda j, o: (0, at + j)),
                wide,
                pl.BlockSpec((tokens, TILE), lambda j, o: (0, 0)),
            ],
            scratch_shapes=[pltpu.VMEM((2, depth, width), BF16), pltpu.SemaphoreType.DMA((2,))],
        ),
        out_shape=[
            jax.ShapeDtypeStruct((tokens, full), BF16),
            jax.ShapeDtypeStruct((depth, full), BF16),
            jax.ShapeDtypeStruct((tokens, full), BF16),
            jax.ShapeDtypeStruct((tokens, TILE), F32),
        ],
        input_output_aliases={} if so_far is None else {8: 0, 9: 1, 10: 2},
        cost_estimate=pl.CostEstimate(
            flops=2 * tokens * depth * columns,
            bytes_accessed=4 * depth * columns + 10 * tokens * columns + 2 * tokens * depth,
            transcendentals=tokens * columns,
        ),
        name="project_gate",
    )(order, x, *pieces, y, gain, *extra)


def restore_kernel(block, width, order_ref, p0, p1, p2, p3, *rest):
    w_ref, buffer, sems = rest[-3:]
    slot = next_tile(order_ref, (p0, p1, p2, p3), buffer, sems, block, width)
    w_ref[...] = buffer[slot]


def restore(pieces, order, so_far, start, full, width=256):
    columns = pieces[0].shape[1]
    block = pieces[0].shape[0] // 8
    depth = block * BLOCKS
    at = start // width
    any_spec = pl.BlockSpec(memory_space=pl.ANY)
    extra = [] if so_far is None else [so_far]
    return pl.pallas_call(
        functools.partial(restore_kernel, block, width),
        grid_spec=pltpu.PrefetchScalarGridSpec(
            num_scalar_prefetch=1,
            grid=(columns // width,),
            in_specs=[any_spec] * (4 + len(extra)),
            out_specs=pl.BlockSpec((depth, width), lambda j, o: (0, at + j)),
            scratch_shapes=[pltpu.VMEM((2, depth, width), BF16), pltpu.SemaphoreType.DMA((2,))],
        ),
        out_shape=jax.ShapeDtypeStruct((depth, full), BF16),
        input_output_aliases={} if so_far is None else {5: 0},
        cost_estimate=pl.CostEstimate(flops=0, bytes_accessed=4 * depth * columns, transcendentals=0),
        name="restore",
    )(order, *pieces, *extra)


def output_kernel(block, width, order_ref, zg_ref, inverse_ref, tokens_ref, cot_ref, p0, p1, p2, p3, w_ref, out_ref, dots_ref, buffer, sems):
    slot = next_tile(order_ref, (p0, p1, p2, p3), buffer, sems, block, width)
    w = buffer[slot]
    w_ref[...] = w

    @pl.when(pl.program_id(0) == 0)
    def _():
        dots_ref[...] = jnp.zeros_like(dots_ref)

    for i in range(zg_ref.shape[0] // SPAN):
        rows = slice(i * SPAN, (i + 1) * SPAN)
        projected = inverse_ref[rows] * mm(zg_ref[rows], w)
        out_ref[rows] = (tokens_ref[rows].astype(F32) + projected).astype(BF16)
        dots_ref[rows] += jnp.sum(cot_ref[rows].astype(F32) * projected, axis=1, keepdims=True)


def output_project(zg, inverse, tokens, cot, pieces, order, width=512):
    count, depth = zg.shape
    model = tokens.shape[1]
    block = depth // BLOCKS
    any_spec = pl.BlockSpec(memory_space=pl.ANY)
    whole = lambda i, o: (0, 0)
    part = pl.BlockSpec((count, width), lambda i, o: (0, i))
    return pl.pallas_call(
        functools.partial(output_kernel, block, width),
        grid_spec=pltpu.PrefetchScalarGridSpec(
            num_scalar_prefetch=1,
            grid=(model // width,),
            in_specs=[pl.BlockSpec((count, depth), whole), pl.BlockSpec((count, 1), whole), part, part]
            + [any_spec] * 4,
            out_specs=[
                pl.BlockSpec((depth, width), lambda i, o: (0, i)),
                part,
                pl.BlockSpec((count, 1), whole),
            ],
            scratch_shapes=[pltpu.VMEM((2, depth, width), BF16), pltpu.SemaphoreType.DMA((2,))],
        ),
        out_shape=[
            jax.ShapeDtypeStruct((depth, model), BF16),
            jax.ShapeDtypeStruct((count, model), BF16),
            jax.ShapeDtypeStruct((count, 1), F32),
        ],
        cost_estimate=pl.CostEstimate(
            flops=2 * count * depth * model,
            bytes_accessed=4 * depth * model + 2 * count * (depth + 3 * model),
            transcendentals=0,
        ),
        name="project_out",
    )(order, zg, inverse, tokens, cot, *pieces)


def weight_grad_kernel(block, place_ref, lhs_ref, rhs_ref, mine, other, buffer, sems):
    step = pl.program_id(0)
    slot = lax.rem(step, 2)

    def settle(which):
        pltpu.make_async_copy(buffer.at[which], buffer.at[which], sems.at[which]).wait()

    @pl.when(step >= 2)
    def _():
        settle(slot)

    buffer[slot] = dot_f32(lhs_ref[...], rhs_ref[...], ((0,), (0,))).astype(BF16)
    for t in range(8):
        q = place_ref[step * 8 + t]
        source = buffer.at[slot, pl.ds(t * block, block), :]

        @pl.when(q < 16)
        def _():
            pltpu.make_async_copy(
                source, mine.at[pl.ds(pl.multiple_of(q * block, block), block), :], sems.at[slot]
            ).start()

        @pl.when(q >= 16)
        def _():
            pltpu.make_async_copy(
                source, other.at[pl.ds(pl.multiple_of((q - 16) * block, block), block), :], sems.at[slot]
            ).start()

    @pl.when(step == pl.num_programs(0) - 1)
    def _():
        settle(1 - slot)
        settle(slot)


def weight_grad(lhs, rhs, place, column, columns):
    tokens, rows = lhs.shape
    block = rows // BLOCKS
    any_spec = pl.BlockSpec(memory_space=pl.ANY)
    out = jax.ShapeDtypeStruct((16 * block, columns), BF16)
    return pl.pallas_call(
        functools.partial(weight_grad_kernel, block),
        grid_spec=pltpu.PrefetchScalarGridSpec(
            num_scalar_prefetch=1,
            grid=(4,),
            in_specs=[
                pl.BlockSpec((tokens, 8 * block), lambda i, o: (0, i)),
                pl.BlockSpec((tokens, columns), lambda i, o: (0, column)),
            ],
            out_specs=[any_spec, any_spec],
            scratch_shapes=[pltpu.VMEM((2, 8 * block, columns), BF16), pltpu.SemaphoreType.DMA((2,))],
        ),
        out_shape=[out, out],
        cost_estimate=pl.CostEstimate(
            flops=2 * tokens * rows * columns,
            bytes_accessed=2 * (tokens * rows + tokens * columns + rows * columns),
            transcendentals=0,
        ),
        name="weight_grad",
    )(place, lhs, rhs)


def rows_of(packed, start, count):
    return packed[:, start : start + count]


def on_device(
    hypercube,
    tokens,
    seg_ids,
    gain_in,
    w_in,
    conv_weight,
    conv_bias,
    dt_bias,
    a_log,
    d_skip,
    gain_out,
    w_out,
    cotangent,
):
    shards = lax.psum(1, "shard")
    taps, conv_local = conv_weight.shape
    model = tokens.shape[1]
    di = gain_out.shape[0] * shards
    conv_dim = conv_local * shards
    calls = ((0, 1), (1, 2), (3, 3))
    width = GROUP * P_SIZE

    def columns(w, call):
        start, count = call
        own = w[:, di + start * width : di + (start + count) * width]
        if start > 0:
            return own
        head = w[:, 2 * di :]
        return jnp.concatenate([jnp.pad(head, ((0, 0), (0, 4 * N - head.shape[1]))), own], axis=1)

    small = jnp.concatenate([conv_weight.reshape(-1), conv_bias, gain_in, gain_out])
    if hypercube:
        core = lax.axis_index("rep")
        w_half = lax.dynamic_slice_in_dim(w_in, core * (w_in.shape[0] // 2), w_in.shape[0] // 2, 0)
        o_half = lax.dynamic_slice_in_dim(w_out, core * (w_out.shape[0] // 2), w_out.shape[0] // 2, 0)
        near, middle, far = [Gather(columns(w_half, call)) for call in calls]
        gate_gather, out_gather = Gather(w_half[:, :di]), Gather(o_half)
        small_flow = gather_small(small)
        next(small_flow)
        got = []
        for starts in ((near,), (near, middle), (near, middle, far), (near, middle, far)):
            pairs = [each.step(*got) for each in starts] + [small_flow.send(got)]
            got = [pair[1] for pair in pairs]
            if len(starts) == 1:
                later = (far.held, gate_gather.held, out_gather.held), (tokens, seg_ids, dt_bias, a_log, d_skip, core)
                helds, (tokens, seg_ids, dt_bias, a_log, d_skip, core) = after(later, *got)
                far.held, gate_gather.held, out_gather.held = helds
        small_all = small_flow.send(got)
        order, place = block_order(core)
        sent, got = zip(
            middle.step(*got), far.step(*got), near.swap(*got), near.swap(*got), gate_gather.step(*got)
        )
        normed_tie = sent
        conv_tie = sent
        last_pair = got[0], got[1], got[4]
    else:
        small_all = lax.all_gather(small, "shard", axis=0, tiled=False)
        full_w_in = lax.all_gather(w_in, "shard", axis=0, tiled=True)
        full_w_out = lax.all_gather(w_out, "shard", axis=0, tiled=True)
    cut = taps * conv_local
    small_conv = after(small_all, *conv_tie) if hypercube else small_all
    conv_w = small_conv[:, :cut].reshape(shards, taps, conv_local).transpose(1, 0, 2).reshape(taps, -1)
    conv_b = rows_of(small_conv, cut, conv_local).reshape(1, -1)
    cut += conv_local
    full_gain_in = rows_of(small_all, cut, gain_in.shape[0]).reshape(1, -1).astype(F32)
    full_gain_out = rows_of(small_conv, cut + gain_in.shape[0], gain_out.shape[0]).reshape(1, -1).astype(F32)
    conv_all = jnp.concatenate(
        [conv_w.astype(F32), conv_b.astype(F32), jnp.zeros((3, conv_dim), F32)], axis=0
    )
    conv_x, conv_bc = conv_all[:, :di], conv_all[:, di:]
    inputs = tokens.astype(F32)
    rscale = lax.rsqrt(jnp.mean(inputs * inputs, axis=1, keepdims=True) + EPSILON)
    unit = inputs * rscale
    normed = (unit * full_gain_in).astype(BF16)
    if hypercube:
        normed = after(normed, *normed_tie)
    aux, seg_row = seg_facts(seg_ids[0])
    heads = head_rows(dt_bias, a_log)
    skip = jnp.repeat(d_skip, P_SIZE)[None]

    pcs, w_parts = [], []
    bcv = written = mark = None
    project_tie = ()
    for index, call in enumerate(calls):
        if hypercube:
            pieces = (near, middle, far)[index].pieces()
            pc, w_part = project(after(normed, *project_tie), pieces, order, None, 0, pieces[0].shape[1])
            if index == 0:
                done = last_pair[0], last_pair[2], pc
                sent, got = zip(
                    middle.swap(*done), middle.swap(*done), gate_gather.step(*done), out_gather.step(*done)
                )
                pc = after(pc, *sent)
            if index == 1:
                done = got[0], pc
                sent, _ = zip(far.swap(*done), far.swap(*done))
                pc = after(pc, *sent)
        else:
            w_part = columns(full_w_in, call)
            pc = mm(normed, w_part)
        pcs.append((pc, 1 if index == 0 else 0))
        w_parts.append(w_part)
        written = run_forward(
            pc, pcs[-1][1], pcs[0][0], conv_x, conv_bc, aux, seg_row, heads, skip, *call, bcv, written
        )
        mark = written[4]
        if index == 0:
            bcv, bc_slope = written[5:]
        written = written[:5]
        if hypercube and index == 0:
            done = last_pair[1], got[2], got[3], mark
            sent, got = zip(far.step(*done), gate_gather.step(*done), out_gather.step(*done))
            project_tie = sent
        if hypercube and index == 1:
            done = got[1], got[2], mark
            sent, got = zip(gate_gather.step(*done), gate_gather.swap(*done), out_gather.step(*done))
            project_tie = sent
    if hypercube:
        done = got[0], got[1], got[2], mark
        sent, got = zip(gate_gather.swap(*done), out_gather.step(*done), out_gather.swap(*done))
        gate_tie = sent
    x, y, states, slope, mark = written
    if hypercube:
        gate, w_gate, zg, squares = gate_project(
            after(normed, *gate_tie), gate_gather.pieces(), order, y, full_gain_out + mark[0, 0], None, 0, di
        )
    else:
        w_gate = full_w_in[:, :di]
        gate = mm(normed, w_gate)
        gated = y.astype(F32) * (gate * jax.nn.sigmoid(gate))
        squares = gated * gated
        zg = (gated * full_gain_out).astype(BF16)
    inverse = lax.rsqrt(jnp.sum(squares, axis=1, keepdims=True) / di + EPSILON)
    cot = cotangent.astype(F32)
    cot_scaled = (inverse * cot).astype(BF16)
    y, gate = y.astype(F32), gate.astype(F32)
    sig = jax.nn.sigmoid(gate)
    sums = None
    parts = {}
    if hypercube:
        in_block = w_in.shape[0] // 2
        out_tie, out_got = out_gather.swap(out_gather.seen[3], zg)
        out_grad = weight_grad(zg, after(cot_scaled, out_tie), place, 0, model)
        out_sum = Scatter(out_grad, w_out.shape[0] // 2)
        sent, got = out_sum.step(*out_gather.swapped)
        full_w_out, output, dots = output_project(
            after(zg, sent), inverse, tokens, cotangent, out_gather.pieces(), order
        )
        sent, got = out_sum.step(got, dots)
        grad_ynorm = mm_nt(after(cotangent, sent), full_w_out)
    else:
        projected = inverse * mm(zg, full_w_out)
        output = (inputs + projected).astype(BF16)
        dots = jnp.sum(cot * projected, axis=1, keepdims=True)
        grad_ynorm = mm_nt(cotangent, full_w_out)
    dz = inverse * (full_gain_out * grad_ynorm) - (y * (gate * sig)) * (inverse * inverse * dots / di)
    dy = (dz * (gate * sig)).astype(BF16)
    dgate = (dz * y * (sig * (1.0 + gate * (1.0 - sig)))).astype(BF16)
    if hypercube:
        gate_grad = weight_grad(normed, after(dgate, got), place, 0, di)
        gate_sum = Scatter(gate_grad, in_block)
        sent, gate_got = gate_sum.step()
        scaled = mm_nt(after(dgate, sent), w_gate)
        sent, got = zip(out_sum.step(got, scaled), gate_sum.step(gate_got, scaled))
        dy = after(dy, *sent, gate_got, scaled)
    else:
        scaled = mm_nt(dgate, w_gate)
    grad_sums = {}
    for index, call in reversed(list(enumerate(calls))):
        pc, first_x = pcs[index]
        dpart, dcw, dskip, *sums = run_backward(
            dy, x, bcv, states, slope, bc_slope, pc, first_x, pcs[0][0], conv_x, conv_bc, aux, seg_row, heads, skip, *call,
            index == 0, sums,
        )
        parts[index] = (dpart, dcw, dskip)
        if not hypercube:
            scaled = scaled + mm_nt(dpart, w_parts[index])
            continue
        done = *got, dpart
        if index == 2:
            sent, out_got = out_sum.step(*done)
            early = (sent,)
        elif index == 1:
            sent, gate_got = gate_sum.step(*done)
            early = (sent,)
        else:
            early, late = zip(grad_sums[2].step(*done), grad_sums[1].step(*done))
        grad = weight_grad(normed, after(dpart, *early, *done), place, 0, dpart.shape[1])
        grad_sums[index] = Scatter(grad, in_block)
        swap_sent, swap_got = grad_sums[index].step()
        if index == 2:
            scaled = scaled + mm_nt(after(dpart, swap_sent), w_parts[index])
            done = swap_got, scaled
            sent, got = zip(out_sum.step(out_got, *done), gate_sum.step(got[1], *done), grad_sums[2].step(*done))
            dy = after(dy, *sent, *done)
        elif index == 1:
            scaled = scaled + mm_nt(after(dpart, swap_sent), w_parts[index])
            done = swap_got, scaled
            sent, got = zip(gate_sum.step(gate_got, *done), grad_sums[2].step(got[2], *done), grad_sums[1].step(*done))
            dy = after(dy, *sent, *done)
        else:
            sent, late = zip(grad_sums[2].step(*late, grad[0]), grad_sums[1].step(*late, grad[0]))
            scaled = scaled + mm_nt(after(dpart, swap_sent, *sent), w_parts[index])
            sent, got = grad_sums[0].step(swap_got, *late, scaled)
            grad_sums[1].step(*late, scaled)
            scaled = after(scaled, sent)
    dbcw, dhead = sums
    dcw = jnp.concatenate([parts[index][1] for index in range(len(calls))] + [dbcw], axis=2)
    dskip = jnp.concatenate([parts[index][2] for index in range(len(calls))], axis=1)
    scaled = scaled * full_gain_in
    inner = jnp.mean(unit * scaled, axis=1, keepdims=True)
    grad_tokens = (cot + rscale * (scaled - unit * inner)).astype(BF16)

    conv_sums = dcw.sum(1)
    conv_sums = jnp.concatenate([conv_sums[4:5], conv_sums[3:4], conv_sums[2:3], conv_sums[1:2], conv_sums[0:1]])
    per_head = jnp.concatenate(
        [
            dhead[0].sum(0)[:H],
            dhead[1].sum(0)[:H] * -jnp.exp(a_log),
            dskip.sum(0).reshape(H, P_SIZE).sum(1),
        ]
    )
    conv_part = conv_sums.reshape(taps + 1, shards, conv_local).transpose(1, 0, 2).reshape(shards, -1)
    small_grad = jnp.concatenate([conv_part, jnp.broadcast_to(per_head[None], (shards, 3 * H))], axis=1)
    real = w_in.shape[1] - 2 * di
    if hypercube:
        small_sum = reduce_small(small_grad, (grad[0], swap_got, got, grad_tokens))[0]
        sent, got = grad_sums[0].step(got, grad_tokens)
        grad_sums[1].step(sent)
        _, got = grad_sums[0].step(got)
        grad_sums[0].step(got)
        gate_part, *rest = [each.finish() for each in (gate_sum, grad_sums[2], grad_sums[1], grad_sums[0])]
        rest = rest[::-1]
        own = jnp.concatenate([gate_part, rest[0][:, 4 * N :], *rest[1:], rest[0][:, :real]], axis=1)
        sum_w_in = both_cores(own)
        sum_w_out = both_cores(out_sum.finish())
    else:
        grad_w_out = dot_f32(zg, cot_scaled, ((0,), (0,)))
        rest = [parts[index][0] for index in range(len(calls))]
        grads = jnp.concatenate([dgate, rest[0][:, 4 * N :], *rest[1:], rest[0][:, :real]], axis=1)
        grad_w_in = dot_f32(normed, grads, ((0,), (0,)))
        small_sum = lax.psum(
            lax.psum_scatter(small_grad, "shard", scatter_dimension=0, tiled=True), "rep"
        )[0]
        sum_w_in = lax.psum_scatter(grad_w_in, "shard", scatter_dimension=0, tiled=True)
        sum_w_out = lax.psum_scatter(grad_w_out, "shard", scatter_dimension=0, tiled=True)
        sum_w_in, sum_w_out = lax.psum((sum_w_in, sum_w_out), "rep")
    grad_gain_in = jnp.sum(sum_w_in * w_in.astype(F32), axis=1) / gain_in.astype(F32)
    grad_gain_out = jnp.sum(sum_w_out * w_out.astype(F32), axis=1) / gain_out.astype(F32)
    cut = taps * conv_local
    head_at = cut + conv_local
    return (
        output,
        grad_tokens,
        grad_gain_in,
        sum_w_in,
        small_sum[:cut].reshape(taps, conv_local),
        small_sum[cut:head_at],
        small_sum[head_at : head_at + H],
        small_sum[head_at + H : head_at + 2 * H],
        small_sum[head_at + 2 * H :],
        grad_gain_out,
        sum_w_out,
    )


def both_cores(own):
    partner = swap_cores(own)
    first = lax.axis_index("rep") == 0
    return jnp.concatenate([jnp.where(first, own, partner), jnp.where(first, partner, own)], axis=0)


def reduce_small(rows, ties):
    core = lax.axis_index("rep")
    places = jnp.asarray([reach(order) for order in ORDERS], jnp.int32)[core] ^ lax.axis_index("shard")
    hot = (places[:, None] == jnp.arange(16, dtype=jnp.int32)[None, :]).astype(F32)
    total = dot_f32(hot, rows, ((1,), (0,)), HIGHEST)
    for stage, tie in zip((3, 2, 1, 0), ties):
        cut = 1 << stage
        total = after(total, tie)
        total = total[:cut] + exchange(total[cut:], stage)
    return total + swap_cores(total)


def solution(mesh):
    rows = P(("shard", "rep"), None)
    in_specs = (
        rows, rows, P("shard"), P("shard", None), P(None, "shard"), P("shard"), P(), P(), P(), P("shard"),
        P("shard", None), rows,
    )
    out_specs = (
        rows, rows, P("shard"), P("shard", None), P(None, "shard"), P("shard"), P(), P(), P(), P("shard"),
        P("shard", None),
    )
    hypercube = mesh.shape["shard"] == 16 and mesh.shape["rep"] == 2
    return jax.shard_map(
        functools.partial(on_device, hypercube),
        mesh=mesh,
        in_specs=in_specs,
        out_specs=out_specs,
        check_vma=False,
    )
```

```python
import functools

import jax
import jax.numpy as jnp
from jax import lax
from jax.experimental import pallas as pl
from jax.experimental.pallas import tpu as pltpu
from jax.sharding import PartitionSpec as P
from jax.sharding import PartitionSpec as P

H = 48
P_SIZE = 64
N = 128
SPAN = 256
HALF = 128
GROUP = 8
TILE = 128
EPSILON = 1e-05
HIGHEST = lax.Precision.HIGHEST
LOG2E = 1.4426950408889634
NEG = -1e30
F32 = jnp.float32
BF16 = jnp.bfloat16


def dot_f32(a, b, contract, precision=None):
    return lax.dot_general(
        a, b, ((contract[0], contract[1]), ((), ())), preferred_element_type=F32, precision=precision
    )


def mm(a, b):
    return dot_f32(a, b, ((1,), (0,)))


def mm_nt(a, b):
    return dot_f32(a, b, ((1,), (1,)))


def lanes_of(column, rows):
    return jnp.broadcast_to(column, (rows, TILE))


def step_sizes(raw, heads):
    shifted = raw + heads[0:1]
    return jnp.maximum(shifted, 0.0) + jnp.log1p(jnp.exp(-jnp.abs(shifted)))


def conv_taps(ext, same, start, width, rows=SPAN):
    out = [ext[8 : 8 + rows, start : start + width]]
    for offset in (1, 2, 3):
        moved = ext[8 - offset : 8 - offset + rows, start : start + width]
        mask = same[offset - 1]
        if width > TILE:
            mask = jnp.concatenate([mask] * (width // TILE), axis=1)
        out.append(moved * mask)
    return out


def conv_sum(taps, weights):
    total = weights[4:5] + weights[3:4] * taps[0]
    for offset in (1, 2, 3):
        total = total + weights[3 - offset : 4 - offset] * taps[offset]
    return total


def prepare(raw_ref, heads_ref):
    heads = heads_ref[...]
    step = step_sizes(raw_ref[...], heads)
    row = lax.broadcasted_iota(jnp.int32, (SPAN, SPAN), 0)
    col = lax.broadcasted_iota(jnp.int32, (SPAN, SPAN), 1)
    tri = (row >= col).astype(F32)
    cum = dot_f32(tri, step * heads[1:2], ((1,), (0,)), HIGHEST)
    return cum, cum - jnp.log2(step)


def pick(first, columns, at):
    return jnp.where(first, lanes_of(columns[:, at : at + 1], first.shape[0]), lanes_of(columns[:, at + 1 : at + 2], first.shape[0]))


def forward_kernel(first_call, base, pc_ref, halo_ref, cw_ref, same, seg_col_ref, seg_ref, skip_ref, *rest):
    rest = list(rest)
    if first_call:
        raw_ref, heads_ref, bc_ref, bc_halo_ref, bcw_ref = [rest.pop(0) for _ in range(5)]
        x_out, y_out, st_out, slope_out, mark, bc_out, bc_slope_out = [rest.pop(0) for _ in range(7)]
        pack, shifted_out, cum_out, cum_rows, w_rows = [rest.pop(0) for _ in range(5)]
    else:
        bc_out, pack, cum_rows, w_rows = [rest.pop(0) for _ in range(4)]
        mark_ref = rest[4]
        rest = rest[5:]
        x_out, y_out, st_out, slope_out, mark = [rest.pop(0) for _ in range(5)]
    state, scores, block, keep_row, b_t, ext, ext_bc = rest
    span = pl.program_id(0)
    group = pl.program_id(1)
    group_head = base + GROUP * group

    @pl.when((span == 0) & (group == 0))
    def _():
        state[...] = jnp.zeros_like(state)
        mark[...] = jnp.zeros_like(mark) if first_call else mark_ref[...]

    @pl.when(group == 0)
    def _():
        if first_call:
            cum, shifted = prepare(raw_ref, heads_ref)
            pack[...] = cum
            shifted_out[...] = shifted
            cum_out[...] = cum.T
            cum_rows[...] = shifted.T
            w_rows[...] = (jnp.exp2(cum[SPAN - 1 : SPAN] - shifted) * same[4]).T
        last = pack[SPAN - 1 : SPAN]
        keep_row[...] = jnp.broadcast_to(jnp.exp2(last) * same[3, SPAN - 1 : SPAN], (8, TILE))
        if first_call:
            ext_bc[0:8] = bc_halo_ref[...]
            ext_bc[8:] = bc_ref[...]
            total = conv_sum(conv_taps(ext_bc, same, 0, 2 * N), bcw_ref[...])
            gate = jax.nn.sigmoid(total)
            both = total * gate
            bc_out[...] = both.astype(BF16)
            bc_slope_out[...] = (gate + both * (1.0 - gate)).astype(BF16)
        row = lax.broadcasted_iota(jnp.int32, (SPAN, SPAN), 0)
        col = lax.broadcasted_iota(jnp.int32, (SPAN, SPAN), 1)
        linked = (row >= col) & (seg_col_ref[...] == seg_ref[...])
        block[...] = jnp.where(linked, 0.0, NEG)
        scores[...] = mm_nt(bc_out[:, N:], bc_out[:, :N])
        b_t[...] = bc_out[:, :N].astype(F32).T

    ext[0:8] = halo_ref[...]
    ext[8:] = pc_ref[...]
    shift = lax.rem(TILE - group_head, TILE)
    cums = pltpu.roll(pack[...], shift, 1)
    keep = jnp.broadcast_to(pltpu.roll(keep_row[...], shift, 1)[0:1], (N, TILE))
    first = lax.broadcasted_iota(jnp.int32, (SPAN, TILE), 1) < P_SIZE
    query = bc_out[:, N:]
    empty = jnp.zeros((HALF, HALF), BF16)
    wide = lambda parts: jnp.concatenate(parts, axis=1)
    for quad in range(GROUP // 4):
        xbs, outs, entries, keeps, fresh = [], [], [], [], []
        for pair in (2 * quad, 2 * quad + 1):
            at = pair * TILE
            total = conv_sum(conv_taps(ext, same, at, TILE), cw_ref[:, at : at + TILE])
            gate = jax.nn.sigmoid(total)
            x = total * gate
            xb = x.astype(BF16)
            x_out[:, at : at + TILE] = xb
            slope_out[:, at : at + TILE] = (gate + x * (1.0 - gate)).astype(BF16)
            mixes, weighted, cum_cols = [], [], []
            for head in (2 * pair, 2 * pair + 1):
                cum_col = lanes_of(cums[:, head : head + 1], SPAN)
                cum_cols.append(cum_col)
                cum_row = cum_rows[pl.ds(group_head + head, 1), :]
                blocks = []
                for i, j in ((0, 0), (1, 0), (1, 1)):
                    rows = slice(i * HALF, (i + 1) * HALF)
                    cols = slice(j * HALF, (j + 1) * HALF)
                    gap = cum_col[rows] - cum_row[:, cols] + block[rows, cols]
                    blocks.append((jnp.exp2(gap) * scores[rows, cols]).astype(BF16))
                mixes.append(wide([blocks[0], empty]))
                mixes.append(wide(blocks[1:]))
                weighted.append((b_t[...] * w_rows[pl.ds(group_head + head, 1), :]).astype(BF16))
            inner = mm(jnp.concatenate(mixes + weighted, axis=0), xb)
            outs.append(jnp.where(first, inner[:SPAN], inner[SPAN : 2 * SPAN]))
            fresh.append(jnp.where(first[:N], inner[2 * SPAN : 2 * SPAN + N], inner[2 * SPAN + N :]))
            xbs.append(xb)
            entries.append(jnp.exp2(jnp.where(first, cum_cols[0], cum_cols[1])) * same[3])
            keeps.append(pick(first[:N], keep, 2 * pair))
        both = slice(quad * 2 * TILE, (quad + 1) * 2 * TILE)
        tile = pl.ds(pl.multiple_of(group * GROUP * P_SIZE + quad * 2 * TILE, 2 * TILE), 2 * TILE)
        old = state[:, tile]
        old_b = old.astype(BF16)
        st_out[:, both] = old_b
        carried = mm(query, old_b)
        y = wide(outs) + wide(entries) * carried + skip_ref[:, both] * wide(xbs).astype(F32)
        y_out[:, both] = y.astype(BF16)
        state[:, tile] = old * wide(keeps) + wide(fresh)


def run_forward(pc, first_x, pc_bc, conv_x, conv_bc, same, seg_col, seg_row, heads, skip, start, count, shared, before):
    tokens = pc.shape[0]
    spans = tokens // SPAN
    di = skip.shape[1]
    width = GROUP * P_SIZE
    own = count * width
    first_call = before is None
    any_spec = pl.BlockSpec(memory_space=pl.ANY)
    halo = lambda s: jnp.maximum(s * (SPAN // 8) - 1, 0)
    wide = pl.BlockSpec((SPAN, width), lambda s, g: (s, start + g))
    bcv_spec = pl.BlockSpec((SPAN, 2 * N), lambda s, g: (s, 0))
    in_specs = [
        pl.BlockSpec((SPAN, width), lambda s, g: (s, first_x + g)),
        pl.BlockSpec((8, width), lambda s, g: (halo(s), first_x + g)),
        pl.BlockSpec((8, width), lambda s, g: (0, start + g)),
        pl.BlockSpec((5, SPAN, TILE), lambda s, g: (0, s, 0)),
        pl.BlockSpec((SPAN, 1), lambda s, g: (s, 0)),
        pl.BlockSpec((1, SPAN), lambda s, g: (0, s)),
        pl.BlockSpec((1, width), lambda s, g: (0, start + g)),
    ]
    args = [pc, pc, conv_x, same, seg_col, seg_row, skip]
    column_spec = pl.BlockSpec((SPAN, TILE), lambda s, g: (s, 0))
    row_spec = pl.BlockSpec((TILE, SPAN), lambda s, g: (s, 0))
    columns_shape = jax.ShapeDtypeStruct((tokens, TILE), F32)
    rows_shape = jax.ShapeDtypeStruct((spans * TILE, SPAN), F32)
    mark_spec = pl.BlockSpec((8, TILE), lambda s, g: (0, 0))
    out_specs = [wide, wide, pl.BlockSpec((N, width), lambda s, g: (s, start + g)), wide, mark_spec]
    out_shape = [
        jax.ShapeDtypeStruct((tokens, di), BF16),
        jax.ShapeDtypeStruct((tokens, di), BF16),
        jax.ShapeDtypeStruct((spans * N, di), BF16),
        jax.ShapeDtypeStruct((tokens, di), BF16),
        jax.ShapeDtypeStruct((8, TILE), F32),
    ]
    if first_call:
        in_specs += [
            pl.BlockSpec((SPAN, TILE), lambda s, g: (s, 2)),
            pl.BlockSpec((8, TILE), lambda s, g: (0, 0)),
            pl.BlockSpec((SPAN, 2 * N), lambda s, g: (s, 0)),
            pl.BlockSpec((8, 2 * N), lambda s, g: (halo(s), 0)),
            pl.BlockSpec((8, 2 * N), lambda s, g: (0, 0)),
        ]
        args += [pc_bc, heads, pc_bc, pc_bc, conv_bc]
        out_specs += [bcv_spec, bcv_spec, column_spec, column_spec, row_spec, row_spec, row_spec]
        out_shape += [jax.ShapeDtypeStruct((tokens, 2 * N), BF16)] * 2
        out_shape += [columns_shape] * 2 + [rows_shape] * 3
        aliases = {}
    else:
        in_specs += [bcv_spec, column_spec, row_spec, row_spec, any_spec, any_spec, any_spec, any_spec, mark_spec]
        args += [*shared, *before]
        aliases = {11: 0, 12: 1, 13: 2, 14: 3}
    return pl.pallas_call(
        functools.partial(forward_kernel, first_call, start * GROUP),
        grid_spec=pltpu.PrefetchScalarGridSpec(
            num_scalar_prefetch=0,
            grid=(spans, count),
            in_specs=in_specs,
            out_specs=out_specs,
            scratch_shapes=[
                pltpu.VMEM((N, own), F32),
                pltpu.VMEM((SPAN, SPAN), F32),
                pltpu.VMEM((SPAN, SPAN), F32),
                pltpu.VMEM((8, TILE), F32),
                pltpu.VMEM((N, SPAN), F32),
                pltpu.VMEM((SPAN + 8, width), F32),
                pltpu.VMEM((SPAN + 8, 2 * N), F32),
            ],
        ),
        out_shape=out_shape,
        input_output_aliases=aliases,
        compiler_params=pltpu.CompilerParams(dimension_semantics=("arbitrary", "arbitrary")),
        cost_estimate=pl.CostEstimate(flops=int(5e9 * count), bytes_accessed=14 * tokens * own, transcendentals=0),
        name="scan_forward",
    )(*args)


def conv_back(grad, slope, signal, same, weights, carry):
    width = grad.shape[1]
    du = grad * slope.astype(F32)

    def add_rows(values):
        return jnp.sum(values.reshape(SPAN // 8, 8, width), axis=0)

    out = weights[3:4] * du
    sums = [add_rows(du), add_rows(du * signal)]
    for offset in (1, 2, 3):
        mask = same[offset - 1]
        if width > TILE:
            mask = jnp.concatenate([mask] * (width // TILE), axis=1)
        masked = du * mask
        moved = jnp.concatenate([masked, carry[offset - 1]], axis=0)[offset : offset + SPAN]
        carry[offset - 1] = masked[0:8]
        out = out + weights[3 - offset : 4 - offset] * moved
        sums.append(add_rows(moved * signal))
    return out, sums


def backward_kernel(
    first_call, last_call, base,
    dy_ref, x_ref, bcv_ref, st_ref, slope_ref, pc_ref, cw_ref, same, seg_col_ref, seg_ref, skip_ref,
    cum_ref, shifted_ref, cum_rows, *rest,
):
    rest = list(rest)
    before = None if first_call else [rest.pop(0) for _ in range(4)]
    if last_call:
        raw_ref, heads_ref, bc_ref, bc_slope_ref, bcw_ref = [rest.pop(0) for _ in range(5)]
    dproj_out, dcw_out, dskip_out = [rest.pop(0) for _ in range(3)]
    if last_call:
        dbcw_out, dhead_out = [rest.pop(0) for _ in range(2)]
    else:
        after_out = [rest.pop(0) for _ in range(4)]
    (
        dstate, scores, block, dscores, pack, c_t,
        carry, carry_bc, d_bc, per_row, dcum_rows, dlast,
    ) = rest
    back = pl.program_id(0)
    group = pl.program_id(1)
    groups = pl.num_programs(1)
    width = GROUP * P_SIZE
    group_head = base + GROUP * group
    first_x = 4 * N if last_call else 0

    @pl.when((back == 0) & (group == 0))
    def _():
        dstate[...] = jnp.zeros_like(dstate)
        carry[...] = jnp.zeros_like(carry)
        dcw_out[...] = jnp.zeros_like(dcw_out)
        dskip_out[...] = jnp.zeros_like(dskip_out)
        dcum_rows[...] = jnp.zeros_like(dcum_rows)
        if last_call:
            carry_bc[...] = jnp.zeros_like(carry_bc)
            dbcw_out[...] = jnp.zeros_like(dbcw_out)
            dhead_out[...] = jnp.zeros_like(dhead_out)

    keys = bcv_ref[:, :N]
    query = bcv_ref[:, N:]
    lane = lax.broadcasted_iota(jnp.int32, (SPAN, TILE), 1)

    @pl.when(group == 0)
    def _():
        entry = jnp.exp2(cum_ref[...]) * same[3]
        pack[...] = jnp.where(lane < 64, shifted_ref[...], pltpu.roll(entry, 64, 1))
        row = lax.broadcasted_iota(jnp.int32, (SPAN, SPAN), 0)
        col = lax.broadcasted_iota(jnp.int32, (SPAN, SPAN), 1)
        linked = (row <= col) & (seg_col_ref[...] == seg_ref[...])
        block[...] = jnp.where(linked, 0.0, NEG)
        scores[...] = mm_nt(keys, query)
        c_t[...] = query.T
        per_row[...] = jnp.zeros_like(per_row)
        if first_call:
            dscores[...] = jnp.zeros_like(dscores)
            d_bc[...] = jnp.zeros_like(d_bc)
            dlast[...] = jnp.zeros_like(dlast)
        else:
            dscores[...] = before[0][...]
            d_bc[...] = before[1][...]
            per_row[0] = before[2][:, :TILE]
            per_row[2] = before[2][:, TILE:]
            dlast[...] = before[3][...]

    shift = lax.rem(TILE - group_head, TILE)
    cols = pltpu.roll(pack[...], shift, 1)
    last_cum = pltpu.roll(jnp.broadcast_to(cum_ref[SPAN - 1 : SPAN], (8, TILE)), shift, 1)[0:1]
    keep_mask = same[3, SPAN - 1 : SPAN]
    first = lane < P_SIZE
    lane_row = lax.broadcasted_iota(jnp.int32, (2 * TILE, TILE), 0) // P_SIZE
    lane_col = lax.broadcasted_iota(jnp.int32, (2 * TILE, TILE), 1)
    sums = jnp.zeros((SPAN, TILE), F32)
    last_sum = jnp.zeros((1, TILE), F32)
    group_at = group * width
    empty = jnp.zeros((HALF, HALF), BF16)
    wide = lambda parts: jnp.concatenate(parts, axis=1)
    for quad in range(GROUP // 4):
        both = slice(quad * 2 * TILE, (quad + 1) * 2 * TILE)
        tile = pl.ds(pl.multiple_of(group_at + quad * 2 * TILE, 2 * TILE), 2 * TILE)
        entries, tails, keeps, inners = [], [], [], []
        for pair in (2 * quad, 2 * quad + 1):
            at = pair * TILE
            heads = (2 * pair, 2 * pair + 1)
            dy_pair = dy_ref[:, at : at + TILE]
            xb = x_ref[:, at : at + TILE]
            nothing = jnp.zeros_like(xb)
            split = jnp.concatenate([jnp.where(first, xb, nothing), jnp.where(first, nothing, xb)], axis=0)
            g_both = mm_nt(split, dy_pair)
            cum_cols = [lanes_of(cols[:, head : head + 1], SPAN) for head in heads]
            cum_lines = [cum_rows[pl.ds(group_head + head, 1), :] for head in heads]
            mixes = [[], []]
            across = [[], []]
            down = [[], []]
            for j, i in ((0, 0), (0, 1), (1, 1)):
                rows = slice(j * HALF, (j + 1) * HALF)
                cells = slice(i * HALF, (i + 1) * HALF)
                spread = jnp.zeros((HALF, HALF), F32)
                for which in (0, 1):
                    decay = jnp.exp2(cum_lines[which][:, cells] - cum_cols[which][rows] + block[rows, cells])
                    mix = decay * scores[rows, cells]
                    g = g_both[which * SPAN + j * HALF : which * SPAN + (j + 1) * HALF, cells]
                    spread = spread + decay * g
                    w = mix * g
                    mixes[which].append(mix.astype(BF16))
                    across[which].append(w)
                    down[which].append(jnp.sum(w, axis=0, keepdims=True))
                dscores[rows, cells] += spread
            lefts = []
            for which in (0, 1):
                row_sum = jnp.concatenate(
                    [
                        jnp.sum(across[which][0] + across[which][1], axis=1, keepdims=True),
                        jnp.sum(across[which][2], axis=1, keepdims=True),
                    ],
                    axis=0,
                )
                sums = sums - jnp.where(lane == 2 * GROUP + heads[which], row_sum, 0.0)
                dcum_rows[pl.ds(group_head + heads[which], 1), :] = wide(
                    [down[which][0], down[which][1] + down[which][2]]
                )
                lefts += [wide(mixes[which][:2]), wide([empty, mixes[which][2]])]
            inner = mm(jnp.concatenate(lefts, axis=0), dy_pair)
            inners.append(jnp.where(first, inner[:SPAN], inner[SPAN:]))
            last_pair = jnp.where(
                first[0:1],
                jnp.broadcast_to(last_cum[:, heads[0] : heads[0] + 1], (1, TILE)),
                jnp.broadcast_to(last_cum[:, heads[1] : heads[1] + 1], (1, TILE)),
            )
            tails.append(jnp.exp2(last_pair - jnp.where(first, cum_cols[0], cum_cols[1])) * same[4])
            keeps.append(jnp.exp2(last_pair) * keep_mask)
            entries.append(pick(first, cols, 64 + 2 * pair))
        dyf = dy_ref[:, both].astype(F32)
        xf = x_ref[:, both].astype(F32)
        tail = wide(tails)
        stb = st_ref[:, both]
        ds = dstate[:, tile]
        dsb = ds.astype(BF16)
        dye_f = dyf * wide(entries)
        dye = dye_f.astype(BF16)
        fresh = mm(keys, dsb) * tail
        total = wide(inners) + fresh
        d_bc[:, N:] += mm_nt(dye, stb)
        d_bc[:, :N] += mm_nt((xf * tail).astype(BF16), dsb)

        def head_sum(values, kind):
            spread = (lane_col == kind * GROUP + 4 * quad + lane_row).astype(BF16)
            return mm(values.astype(BF16), spread)

        sums = sums + head_sum(xf * total, 0) + head_sum(xf * fresh, 1) + head_sum(dye_f * mm(query, stb), 2)
        kept = ds * wide(keeps)
        kept_sum = jnp.sum(kept * stb.astype(F32), axis=0, keepdims=True)
        lane_pair = lax.broadcasted_iota(jnp.int32, (1, 2 * TILE), 1) // P_SIZE
        for head in range(4):
            one = jnp.sum(jnp.where(lane_pair == head, kept_sum, 0.0), axis=1, keepdims=True)
            last_sum = last_sum + jnp.where(lane[0:1] == 4 * quad + head, one, 0.0)
        dstate[:, tile] = kept + mm(c_t[...], dye)
        dskip_out[:, tile] += jnp.sum((dyf * xf).reshape(SPAN // 8, 8, 2 * TILE), axis=0)
        dx = total + skip_ref[:, both] * dyf
        for part in (0, 1):
            at = (2 * quad + part) * TILE
            one = pl.ds(pl.multiple_of(group_at + at, TILE), TILE)
            out, conv_sums = conv_back(
                dx[:, part * TILE : (part + 1) * TILE], slope_ref[:, at : at + TILE], pc_ref[:, at : at + TILE],
                same, cw_ref[:, at : at + TILE], carry.at[:, :, one],
            )
            dproj_out[:, pl.ds(pl.multiple_of(first_x + group_at + at, TILE), TILE)] = out.astype(BF16)
            for k, value in enumerate(conv_sums):
                dcw_out[k, :, one] += value

    in_place = (lane >= group_head) & (lane < group_head + GROUP)
    for kind in range(3):
        moved = pltpu.roll(sums, lax.rem(group_head + TILE - GROUP * kind, TILE), 1)
        per_row[kind] += jnp.where(in_place, moved, 0.0)
    moved = pltpu.roll(jnp.broadcast_to(last_sum, (8, TILE)), group_head, 1)
    dlast[...] += jnp.where(in_place[0:8], moved, 0.0)

    @pl.when(group == groups - 1)
    def _():
        state_part = per_row[1]
        dcum = dcum_rows[...].T + per_row[2] - state_part
        dlast_all = dlast[0:1] + jnp.sum(state_part, axis=0, keepdims=True)
        if not last_call:
            after_out[0][...] = dscores[...]
            after_out[1][...] = d_bc[...]
            after_out[2][:, :TILE] = per_row[0]
            after_out[2][:, TILE:] = dcum
            after_out[3][...] = jnp.broadcast_to(dlast_all, (8, TILE))
            return
        ds_b = dscores[...].astype(BF16)
        grad_b = d_bc[:, :N] + mm(ds_b, query)
        grad_c = d_bc[:, N:] + mm(dscores[...].T.astype(BF16), keys)
        out, conv_sums = conv_back(
            wide([grad_b, grad_c]), bc_slope_ref[...], bc_ref[...], same, bcw_ref[...], carry_bc
        )
        dproj_out[:, : 2 * N] = out.astype(BF16)
        for k, value in enumerate(conv_sums):
            dbcw_out[k] += value
        heads = heads_ref[...]
        shifted = raw_ref[...] + heads[0:1]
        step = step_sizes(raw_ref[...], heads)
        slope = jax.nn.sigmoid(shifted)
        row = lax.broadcasted_iota(jnp.int32, (SPAN, SPAN), 0)
        col = lax.broadcasted_iota(jnp.int32, (SPAN, SPAN), 1)
        tri = (row <= col).astype(F32)
        da = dot_f32(tri, dcum, ((1,), (0,)), HIGHEST) + dlast_all
        small = shifted < -16.0
        ratio = jnp.where(small, 1.0, slope / jnp.where(small, 1.0, step))
        live = lane < H
        draw = jnp.where(live, per_row[0] * ratio + da * heads[2:3] * slope, 0.0)
        dproj_out[:, 2 * N : 3 * N] = draw.astype(BF16)
        dproj_out[:, 3 * N : 4 * N] = jnp.zeros((SPAN, N), BF16)
        dhead_out[0] += jnp.sum(draw.reshape(SPAN // 8, 8, TILE), axis=0)
        dhead_out[1] += jnp.sum(jnp.where(live, da * step, 0.0).reshape(SPAN // 8, 8, TILE), axis=0)


def run_backward(
    dy, x, bcv, states, slope, bc_slope, pc, first_x, pc_bc, conv_x, conv_bc, same, seg_col, seg_row, heads, skip,
    cums, start, count, last, before,
):
    tokens, di = dy.shape
    spans = tokens // SPAN
    width = GROUP * P_SIZE
    turn = lambda s: spans - 1 - s
    own = count * width
    out_width = own + (4 * N if last else 0)
    sums_specs = [
        pl.BlockSpec((SPAN, SPAN), lambda s, g: (turn(s), 0)),
        pl.BlockSpec((SPAN, 2 * N), lambda s, g: (turn(s), 0)),
        pl.BlockSpec((SPAN, 2 * TILE), lambda s, g: (turn(s), 0)),
        pl.BlockSpec((8, TILE), lambda s, g: (turn(s), 0)),
    ]
    sums_shapes = [
        jax.ShapeDtypeStruct((tokens, SPAN), F32),
        jax.ShapeDtypeStruct((tokens, 2 * N), F32),
        jax.ShapeDtypeStruct((tokens, 2 * TILE), F32),
        jax.ShapeDtypeStruct((spans * 8, TILE), F32),
    ]
    out_specs = [
        pl.BlockSpec((SPAN, out_width), lambda s, g: (turn(s), 0)),
        pl.BlockSpec((5, 8, own), lambda s, g: (0, 0, 0)),
        pl.BlockSpec((8, own), lambda s, g: (0, 0)),
    ]
    out_shape = [
        jax.ShapeDtypeStruct((tokens, out_width), BF16),
        jax.ShapeDtypeStruct((5, 8, own), F32),
        jax.ShapeDtypeStruct((8, own), F32),
    ]
    wide = pl.BlockSpec((SPAN, width), lambda s, g: (turn(s), start + g))
    in_specs = [
        wide,
        wide,
        pl.BlockSpec((SPAN, 2 * N), lambda s, g: (turn(s), 0)),
        pl.BlockSpec((N, width), lambda s, g: (turn(s), start + g)),
        wide,
        pl.BlockSpec((SPAN, width), lambda s, g: (turn(s), first_x + g)),
        pl.BlockSpec((8, width), lambda s, g: (0, start + g)),
        pl.BlockSpec((5, SPAN, TILE), lambda s, g: (0, turn(s), 0)),
        pl.BlockSpec((SPAN, 1), lambda s, g: (turn(s), 0)),
        pl.BlockSpec((1, SPAN), lambda s, g: (0, turn(s))),
        pl.BlockSpec((1, width), lambda s, g: (0, start + g)),
        pl.BlockSpec((SPAN, TILE), lambda s, g: (turn(s), 0)),
        pl.BlockSpec((SPAN, TILE), lambda s, g: (turn(s), 0)),
        pl.BlockSpec((TILE, SPAN), lambda s, g: (turn(s), 0)),
    ]
    args = [dy, x, bcv, states, slope, pc, conv_x, same, seg_col, seg_row, skip, *cums]
    if before is not None:
        in_specs += sums_specs
        args += before
    if last:
        in_specs += [
            pl.BlockSpec((SPAN, TILE), lambda s, g: (turn(s), 2)),
            pl.BlockSpec((8, TILE), lambda s, g: (0, 0)),
            pl.BlockSpec((SPAN, 2 * N), lambda s, g: (turn(s), 0)),
            pl.BlockSpec((SPAN, 2 * N), lambda s, g: (turn(s), 0)),
            pl.BlockSpec((8, 2 * N), lambda s, g: (0, 0)),
        ]
        args += [pc_bc, heads, pc_bc, bc_slope, conv_bc]
        out_specs += [
            pl.BlockSpec((5, 8, 2 * N), lambda s, g: (0, 0, 0)),
            pl.BlockSpec((2, 8, TILE), lambda s, g: (0, 0, 0)),
        ]
        out_shape += [
            jax.ShapeDtypeStruct((5, 8, 2 * N), F32),
            jax.ShapeDtypeStruct((2, 8, TILE), F32),
        ]
    else:
        out_specs += sums_specs
        out_shape += sums_shapes
    return pl.pallas_call(
        functools.partial(backward_kernel, before is None, last, start * GROUP),
        grid_spec=pltpu.PrefetchScalarGridSpec(
            num_scalar_prefetch=0,
            grid=(spans, count),
            in_specs=in_specs,
            out_specs=out_specs,
            scratch_shapes=[
                pltpu.VMEM((N, own), F32),
                pltpu.VMEM((SPAN, SPAN), F32),
                pltpu.VMEM((SPAN, SPAN), F32),
                pltpu.VMEM((SPAN, SPAN), F32),
                pltpu.VMEM((SPAN, TILE), F32),
                pltpu.VMEM((N, SPAN), BF16),
                pltpu.VMEM((3, 8, own), F32),
                pltpu.VMEM((3, 8, 2 * N), F32),
                pltpu.VMEM((SPAN, 2 * N), F32),
                pltpu.VMEM((3, SPAN, TILE), F32),
                pltpu.VMEM((TILE, SPAN), F32),
                pltpu.VMEM((8, TILE), F32),
            ],
        ),
        out_shape=out_shape,
        compiler_params=pltpu.CompilerParams(dimension_semantics=("arbitrary", "arbitrary")),
        cost_estimate=pl.CostEstimate(
            flops=int(1.2e10 * count), bytes_accessed=12 * tokens * own, transcendentals=0
        ),
        name="scan_backward",
    )(*args)


def seg_facts(seg):
    length = seg.shape[0]
    cols = []
    for offset in (1, 2, 3):
        moved = jnp.concatenate([jnp.full((offset,), -1, jnp.int32), seg[:-offset]])
        cols.append((moved == seg).astype(F32))
    spans = length // SPAN
    ends = seg[SPAN - 1 :: SPAN]
    before = jnp.concatenate([seg[:1], ends[:-1]])
    cols.append((seg == jnp.repeat(before, SPAN)).astype(F32))
    cols.append((seg == jnp.repeat(ends, SPAN)).astype(F32))
    value = seg.astype(F32)
    same = jnp.broadcast_to(jnp.stack(cols, axis=0)[:, :, None], (5, length, TILE))
    return same, value[:, None], value[None, :]


def head_rows(dt_bias, a_log):
    rate = -jnp.exp(a_log)
    rows = jnp.stack([dt_bias, rate * LOG2E, rate] + [jnp.zeros_like(rate)] * 5, axis=0)
    return jnp.pad(rows, ((0, 0), (0, TILE - H)))


BLOCKS = 32
ORDERS = ((8, 1, 4, 2), (8, 2, 4, 1))


def reach(masks):
    out = [0]
    for mask in masks:
        out = out + [mask ^ place for place in out]
    return out


def exchange(values, stage):
    pairs = []
    for shard in range(16):
        for core in range(2):
            pairs.append((shard * 2 + core, (shard ^ ORDERS[core][stage]) * 2 + core))
    return lax.ppermute(values, ("shard", "rep"), pairs)


def swap_cores(values):
    return lax.ppermute(values, "rep", [(0, 1), (1, 0)])


def after(values, *others):
    return lax.optimization_barrier((values, *others))[0]


class Gather:
    def __init__(self, local):
        self.held = local
        self.seen = []
        self.swapped = []

    def step(self, *ahead):
        stage = len(self.seen)
        if stage > 0:
            self.held = jnp.concatenate([self.held, after(self.seen[-1], *ahead)], axis=0)
        elif ahead:
            self.held = after(self.held, *ahead)
        got = exchange(self.held, stage)
        self.seen.append(got)
        return self.held, got

    def swap(self, *ahead):
        send = after(self.held if not self.swapped else self.seen[3], *ahead)
        self.swapped.append(swap_cores(send))
        return send, self.swapped[-1]

    def pieces(self):
        return self.held, self.seen[3], *self.swapped


def gather_small(local):
    held = local[None]
    ahead = yield None
    for stage in range(4):
        send = after(held, *ahead)
        got = exchange(send, stage)
        ahead = yield send, got
        held = jnp.concatenate([send, got], axis=0)
    core = lax.axis_index("rep")
    places = jnp.asarray([reach(order) for order in ORDERS], jnp.int32)[core] ^ lax.axis_index("shard")
    hot = (places[None, :] == jnp.arange(16, dtype=jnp.int32)[:, None]).astype(local.dtype)
    yield dot_f32(hot, held, ((1,), (0,)), HIGHEST).astype(local.dtype)


class Scatter:
    def __init__(self, partial, block):
        mine, self.other = partial
        self.terms = [mine]
        self.block = block
        self.left = [3, 2, 1, 0]

    def rows(self, start, stop):
        total = self.terms[0][start:stop].astype(F32)
        for term in self.terms[1:]:
            total = total + term[start:stop].astype(F32)
        return total

    def step(self, *ahead):
        if len(self.terms) == 1:
            self.other = after(self.other, *ahead)
            self.terms.append(swap_cores(self.other))
            return self.other, self.terms[-1]
        if self.left:
            stage = self.left.pop(0)
            cut = self.block << stage
            self.terms[-1] = after(self.terms[-1], *ahead)
            send = self.rows(cut, 2 * cut).astype(BF16)
            self.terms.append(exchange(send, stage))
            return send, self.terms[-1]
        return self.terms[-1], self.terms[-1]

    def finish(self, *ahead):
        while self.left:
            self.step()
        if ahead:
            self.terms[-1] = after(self.terms[-1], *ahead)
        return self.rows(0, self.block)


def block_order(core):
    shard = lax.axis_index("shard")
    tables = jnp.asarray([reach(order) for order in ORDERS], jnp.int32)
    inverse = jnp.asarray(
        [[reach(order).index(mask) for mask in range(16)] for order in ORDERS], jnp.int32
    )
    own = 2 * (tables[core] ^ shard) + core
    partner = 2 * (tables[1 - core] ^ shard) + (1 - core)
    order = jnp.concatenate([own, partner])
    natural = jnp.arange(BLOCKS, dtype=jnp.int32)
    which = natural % 2
    place = inverse[which, (natural // 2) ^ shard] + 16 * (which != core).astype(jnp.int32)
    return order, place


def fetch_tile(order_ref, pieces, buffer, sems, tile, slot, block, width):
    for q in range(BLOCKS):
        pltpu.make_async_copy(
            pieces[q // 8].at[pl.ds((q % 8) * block, block), pl.ds(pl.multiple_of(tile * width, width), width)],
            buffer.at[slot, pl.ds(pl.multiple_of(order_ref[q] * block, block), block), :],
            sems.at[slot],
        ).start()


def next_tile(order_ref, pieces, buffer, sems, block, width):
    tile = pl.program_id(0)
    slot = lax.rem(tile, 2)

    @pl.when(tile == 0)
    def _():
        fetch_tile(order_ref, pieces, buffer, sems, tile, slot, block, width)

    @pl.when(tile + 1 < pl.num_programs(0))
    def _():
        fetch_tile(order_ref, pieces, buffer, sems, tile + 1, 1 - slot, block, width)

    pltpu.make_async_copy(buffer.at[slot], buffer.at[slot], sems.at[slot]).wait()
    return slot


def project_kernel(block, width, order_ref, x_ref, p0, p1, p2, p3, *rest):
    out_ref, w_ref, buffer, sems = rest[-4:]
    slot = next_tile(order_ref, (p0, p1, p2, p3), buffer, sems, block, width)
    w = buffer[slot]
    w_ref[...] = w
    for i in range(x_ref.shape[0] // SPAN):
        rows = slice(i * SPAN, (i + 1) * SPAN)
        out_ref[rows] = mm(x_ref[rows], w)


def project(x, pieces, order, so_far, start, full, width=512):
    tokens, depth = x.shape
    columns = pieces[0].shape[1]
    block = depth // BLOCKS
    at = start // width
    any_spec = pl.BlockSpec(memory_space=pl.ANY)
    extra = [] if so_far is None else list(so_far)
    return pl.pallas_call(
        functools.partial(project_kernel, block, width),
        grid_spec=pltpu.PrefetchScalarGridSpec(
            num_scalar_prefetch=1,
            grid=(columns // width,),
            in_specs=[pl.BlockSpec((tokens, depth), lambda j, o: (0, 0))] + [any_spec] * (4 + len(extra)),
            out_specs=[
                pl.BlockSpec((tokens, width), lambda j, o: (0, at + j)),
                pl.BlockSpec((depth, width), lambda j, o: (0, at + j)),
            ],
            scratch_shapes=[pltpu.VMEM((2, depth, width), BF16), pltpu.SemaphoreType.DMA((2,))],
        ),
        out_shape=[jax.ShapeDtypeStruct((tokens, full), F32), jax.ShapeDtypeStruct((depth, full), BF16)],
        input_output_aliases={} if so_far is None else {6: 0, 7: 1},
        cost_estimate=pl.CostEstimate(
            flops=2 * tokens * depth * columns,
            bytes_accessed=4 * depth * columns + 4 * tokens * columns + 2 * tokens * depth,
            transcendentals=0,
        ),
        name="project",
    )(order, x, *pieces, *extra)


def gate_kernel(block, width, order_ref, x_ref, p0, p1, p2, p3, y_ref, gain_ref, *rest):
    gate_ref, w_ref, zg_ref, square_ref, buffer, sems = rest[-6:]
    slot = next_tile(order_ref, (p0, p1, p2, p3), buffer, sems, block, width)
    w = buffer[slot]
    w_ref[...] = w

    @pl.when(pl.program_id(0) == 0)
    def _():
        square_ref[...] = jnp.zeros_like(square_ref)

    for i in range(x_ref.shape[0] // SPAN):
        rows = slice(i * SPAN, (i + 1) * SPAN)
        gate = mm(x_ref[rows], w)
        gate_ref[rows] = gate.astype(BF16)
        gated = y_ref[rows].astype(F32) * (gate * jax.nn.sigmoid(gate))
        zg_ref[rows] = (gated * gain_ref[...]).astype(BF16)
        square = gated * gated
        total = square[:, :TILE]
        for k in range(1, width // TILE):
            total = total + square[:, k * TILE : (k + 1) * TILE]
        square_ref[rows] += total


def gate_project(x, pieces, order, y, gain, so_far, start, full, width=512):
    tokens, depth = x.shape
    columns = pieces[0].shape[1]
    block = depth // BLOCKS
    at = start // width
    any_spec = pl.BlockSpec(memory_space=pl.ANY)
    extra = [] if so_far is None else list(so_far)
    wide = pl.BlockSpec((tokens, width), lambda j, o: (0, at + j))
    return pl.pallas_call(
        functools.partial(gate_kernel, block, width),
        grid_spec=pltpu.PrefetchScalarGridSpec(
            num_scalar_prefetch=1,
            grid=(columns // width,),
            in_specs=[pl.BlockSpec((tokens, depth), lambda j, o: (0, 0))]
            + [any_spec] * 4
            + [wide, pl.BlockSpec((1, width), lambda j, o: (0, at + j))]
            + [any_spec] * len(extra),
            out_specs=[
                wide,
                pl.BlockSpec((depth, width), lambda j, o: (0, at + j)),
                wide,
                pl.BlockSpec((tokens, TILE), lambda j, o: (0, 0)),
            ],
            scratch_shapes=[pltpu.VMEM((2, depth, width), BF16), pltpu.SemaphoreType.DMA((2,))],
        ),
        out_shape=[
            jax.ShapeDtypeStruct((tokens, full), BF16),
            jax.ShapeDtypeStruct((depth, full), BF16),
            jax.ShapeDtypeStruct((tokens, full), BF16),
            jax.ShapeDtypeStruct((tokens, TILE), F32),
        ],
        input_output_aliases={} if so_far is None else {8: 0, 9: 1, 10: 2},
        cost_estimate=pl.CostEstimate(
            flops=2 * tokens * depth * columns,
            bytes_accessed=4 * depth * columns + 10 * tokens * columns + 2 * tokens * depth,
            transcendentals=tokens * columns,
        ),
        name="project_gate",
    )(order, x, *pieces, y, gain, *extra)


def restore_kernel(block, width, order_ref, p0, p1, p2, p3, *rest):
    w_ref, buffer, sems = rest[-3:]
    slot = next_tile(order_ref, (p0, p1, p2, p3), buffer, sems, block, width)
    w_ref[...] = buffer[slot]


def restore(pieces, order, so_far, start, full, width=256):
    columns = pieces[0].shape[1]
    block = pieces[0].shape[0] // 8
    depth = block * BLOCKS
    at = start // width
    any_spec = pl.BlockSpec(memory_space=pl.ANY)
    extra = [] if so_far is None else [so_far]
    return pl.pallas_call(
        functools.partial(restore_kernel, block, width),
        grid_spec=pltpu.PrefetchScalarGridSpec(
            num_scalar_prefetch=1,
            grid=(columns // width,),
            in_specs=[any_spec] * (4 + len(extra)),
            out_specs=pl.BlockSpec((depth, width), lambda j, o: (0, at + j)),
            scratch_shapes=[pltpu.VMEM((2, depth, width), BF16), pltpu.SemaphoreType.DMA((2,))],
        ),
        out_shape=jax.ShapeDtypeStruct((depth, full), BF16),
        input_output_aliases={} if so_far is None else {5: 0},
        cost_estimate=pl.CostEstimate(flops=0, bytes_accessed=4 * depth * columns, transcendentals=0),
        name="restore",
    )(order, *pieces, *extra)


def output_kernel(block, width, order_ref, zg_ref, inverse_ref, tokens_ref, cot_ref, p0, p1, p2, p3, w_ref, out_ref, dots_ref, buffer, sems):
    slot = next_tile(order_ref, (p0, p1, p2, p3), buffer, sems, block, width)
    w = buffer[slot]
    w_ref[...] = w

    @pl.when(pl.program_id(0) == 0)
    def _():
        dots_ref[...] = jnp.zeros_like(dots_ref)

    for i in range(zg_ref.shape[0] // SPAN):
        rows = slice(i * SPAN, (i + 1) * SPAN)
        projected = inverse_ref[rows] * mm(zg_ref[rows], w)
        out_ref[rows] = (tokens_ref[rows].astype(F32) + projected).astype(BF16)
        dots_ref[rows] += jnp.sum(cot_ref[rows].astype(F32) * projected, axis=1, keepdims=True)


def output_project(zg, inverse, tokens, cot, pieces, order, width=512):
    count, depth = zg.shape
    model = tokens.shape[1]
    block = depth // BLOCKS
    any_spec = pl.BlockSpec(memory_space=pl.ANY)
    whole = lambda i, o: (0, 0)
    part = pl.BlockSpec((count, width), lambda i, o: (0, i))
    return pl.pallas_call(
        functools.partial(output_kernel, block, width),
        grid_spec=pltpu.PrefetchScalarGridSpec(
            num_scalar_prefetch=1,
            grid=(model // width,),
            in_specs=[pl.BlockSpec((count, depth), whole), pl.BlockSpec((count, 1), whole), part, part]
            + [any_spec] * 4,
            out_specs=[
                pl.BlockSpec((depth, width), lambda i, o: (0, i)),
                part,
                pl.BlockSpec((count, 1), whole),
            ],
            scratch_shapes=[pltpu.VMEM((2, depth, width), BF16), pltpu.SemaphoreType.DMA((2,))],
        ),
        out_shape=[
            jax.ShapeDtypeStruct((depth, model), BF16),
            jax.ShapeDtypeStruct((count, model), BF16),
            jax.ShapeDtypeStruct((count, 1), F32),
        ],
        cost_estimate=pl.CostEstimate(
            flops=2 * count * depth * model,
            bytes_accessed=4 * depth * model + 2 * count * (depth + 3 * model),
            transcendentals=0,
        ),
        name="project_out",
    )(order, zg, inverse, tokens, cot, *pieces)


def weight_grad_kernel(block, place_ref, lhs_ref, rhs_ref, mine, other, buffer, sems):
    step = pl.program_id(0)
    slot = lax.rem(step, 2)

    def settle(which):
        pltpu.make_async_copy(buffer.at[which], buffer.at[which], sems.at[which]).wait()

    @pl.when(step >= 2)
    def _():
        settle(slot)

    buffer[slot] = dot_f32(lhs_ref[...], rhs_ref[...], ((0,), (0,))).astype(BF16)
    for t in range(8):
        q = place_ref[step * 8 + t]
        source = buffer.at[slot, pl.ds(t * block, block), :]

        @pl.when(q < 16)
        def _():
            pltpu.make_async_copy(
                source, mine.at[pl.ds(pl.multiple_of(q * block, block), block), :], sems.at[slot]
            ).start()

        @pl.when(q >= 16)
        def _():
            pltpu.make_async_copy(
                source, other.at[pl.ds(pl.multiple_of((q - 16) * block, block), block), :], sems.at[slot]
            ).start()

    @pl.when(step == pl.num_programs(0) - 1)
    def _():
        settle(1 - slot)
        settle(slot)


def weight_grad(lhs, rhs, place, column, columns):
    tokens, rows = lhs.shape
    block = rows // BLOCKS
    any_spec = pl.BlockSpec(memory_space=pl.ANY)
    out = jax.ShapeDtypeStruct((16 * block, columns), BF16)
    return pl.pallas_call(
        functools.partial(weight_grad_kernel, block),
        grid_spec=pltpu.PrefetchScalarGridSpec(
            num_scalar_prefetch=1,
            grid=(4,),
            in_specs=[
                pl.BlockSpec((tokens, 8 * block), lambda i, o: (0, i)),
                pl.BlockSpec((tokens, columns), lambda i, o: (0, column)),
            ],
            out_specs=[any_spec, any_spec],
            scratch_shapes=[pltpu.VMEM((2, 8 * block, columns), BF16), pltpu.SemaphoreType.DMA((2,))],
        ),
        out_shape=[out, out],
        cost_estimate=pl.CostEstimate(
            flops=2 * tokens * rows * columns,
            bytes_accessed=2 * (tokens * rows + tokens * columns + rows * columns),
            transcendentals=0,
        ),
        name="weight_grad",
    )(place, lhs, rhs)


def rows_of(packed, start, count):
    return packed[:, start : start + count]


def on_device(
    hypercube,
    tokens,
    seg_ids,
    gain_in,
    w_in,
    conv_weight,
    conv_bias,
    dt_bias,
    a_log,
    d_skip,
    gain_out,
    w_out,
    cotangent,
):
    shards = lax.psum(1, "shard")
    taps, conv_local = conv_weight.shape
    model = tokens.shape[1]
    di = gain_out.shape[0] * shards
    conv_dim = conv_local * shards
    calls = ((0, 1), (1, 2), (3, 3))
    width = GROUP * P_SIZE

    def columns(w, call):
        start, count = call
        own = w[:, di + start * width : di + (start + count) * width]
        if start > 0:
            return own
        head = w[:, 2 * di :]
        return jnp.concatenate([jnp.pad(head, ((0, 0), (0, 4 * N - head.shape[1]))), own], axis=1)

    small = jnp.concatenate([conv_weight.reshape(-1), conv_bias, gain_in, gain_out])
    if hypercube:
        core = lax.axis_index("rep")
        w_half = lax.dynamic_slice_in_dim(w_in, core * (w_in.shape[0] // 2), w_in.shape[0] // 2, 0)
        o_half = lax.dynamic_slice_in_dim(w_out, core * (w_out.shape[0] // 2), w_out.shape[0] // 2, 0)
        near, middle, far = [Gather(columns(w_half, call)) for call in calls]
        gate_gather, out_gather = Gather(w_half[:, :di]), Gather(o_half)
        small_flow = gather_small(small)
        next(small_flow)
        got = []
        for starts in ((near,), (near, middle), (near, middle, far), (near, middle, far)):
            pairs = [each.step(*got) for each in starts] + [small_flow.send(got)]
            got = [pair[1] for pair in pairs]
            if len(starts) == 1:
                later = (far.held, gate_gather.held, out_gather.held), (tokens, seg_ids, dt_bias, a_log, d_skip, core)
                helds, (tokens, seg_ids, dt_bias, a_log, d_skip, core) = after(later, *got)
                far.held, gate_gather.held, out_gather.held = helds
        small_all = small_flow.send(got)
        order, place = block_order(core)
        sent, got = zip(
            middle.step(*got), far.step(*got), near.swap(*got), near.swap(*got), gate_gather.step(*got)
        )
        normed_tie = sent
        conv_tie = sent
        last_pair = got[0], got[1], got[4]
    else:
        small_all = lax.all_gather(small, "shard", axis=0, tiled=False)
        full_w_in = lax.all_gather(w_in, "shard", axis=0, tiled=True)
        full_w_out = lax.all_gather(w_out, "shard", axis=0, tiled=True)
    cut = taps * conv_local
    small_conv = after(small_all, *conv_tie) if hypercube else small_all
    conv_w = small_conv[:, :cut].reshape(shards, taps, conv_local).transpose(1, 0, 2).reshape(taps, -1)
    conv_b = rows_of(small_conv, cut, conv_local).reshape(1, -1)
    cut += conv_local
    full_gain_in = rows_of(small_all, cut, gain_in.shape[0]).reshape(1, -1).astype(F32)
    full_gain_out = rows_of(small_conv, cut + gain_in.shape[0], gain_out.shape[0]).reshape(1, -1).astype(F32)
    conv_all = jnp.concatenate(
        [conv_w.astype(F32), conv_b.astype(F32), jnp.zeros((3, conv_dim), F32)], axis=0
    )
    conv_x, conv_bc = conv_all[:, :di], conv_all[:, di:]
    inputs = tokens.astype(F32)
    rscale = lax.rsqrt(jnp.mean(inputs * inputs, axis=1, keepdims=True) + EPSILON)
    unit = inputs * rscale
    normed = (unit * full_gain_in).astype(BF16)
    if hypercube:
        normed = after(normed, *normed_tie)
    same, seg_col, seg_row = seg_facts(seg_ids[0])
    heads = head_rows(dt_bias, a_log)
    skip = jnp.repeat(d_skip, P_SIZE)[None]

    pcs, w_parts = [], []
    shared = written = mark = None
    project_tie = ()
    for index, call in enumerate(calls):
        if hypercube:
            pieces = (near, middle, far)[index].pieces()
            pc, w_part = project(after(normed, *project_tie), pieces, order, None, 0, pieces[0].shape[1])
            if index == 0:
                done = last_pair[0], last_pair[2], pc
                sent, got = zip(
                    middle.swap(*done), middle.swap(*done), gate_gather.step(*done), out_gather.step(*done)
                )
                pc = after(pc, *sent)
            if index == 1:
                done = got[0], pc
                sent, _ = zip(far.swap(*done), far.swap(*done))
                pc = after(pc, *sent)
        else:
            w_part = columns(full_w_in, call)
            pc = mm(normed, w_part)
        pcs.append((pc, 1 if index == 0 else 0))
        w_parts.append(w_part)
        written = run_forward(
            pc, pcs[-1][1], pcs[0][0], conv_x, conv_bc, same, seg_col, seg_row, heads, skip, *call, shared, written
        )
        mark = written[4]
        if index == 0:
            bcv, bc_slope, cum, shifted, cum_lines, shifted_lines, weight_lines = written[5:]
            shared = bcv, cum, shifted_lines, weight_lines
        written = written[:5]
        if hypercube and index == 0:
            done = last_pair[1], got[2], got[3], mark
            sent, got = zip(far.step(*done), gate_gather.step(*done), out_gather.step(*done))
            project_tie = sent
        if hypercube and index == 1:
            done = got[1], got[2], mark
            sent, got = zip(gate_gather.step(*done), gate_gather.swap(*done), out_gather.step(*done))
            project_tie = sent
    if hypercube:
        done = got[0], got[1], got[2], mark
        sent, got = zip(gate_gather.swap(*done), out_gather.step(*done), out_gather.swap(*done))
        gate_tie = sent
    x, y, states, slope, mark = written
    if hypercube:
        gate, w_gate, zg, squares = gate_project(
            after(normed, *gate_tie), gate_gather.pieces(), order, y, full_gain_out + mark[0, 0], None, 0, di
        )
    else:
        w_gate = full_w_in[:, :di]
        gate = mm(normed, w_gate)
        gated = y.astype(F32) * (gate * jax.nn.sigmoid(gate))
        squares = gated * gated
        zg = (gated * full_gain_out).astype(BF16)
    inverse = lax.rsqrt(jnp.sum(squares, axis=1, keepdims=True) / di + EPSILON)
    cot = cotangent.astype(F32)
    cot_scaled = (inverse * cot).astype(BF16)
    y, gate = y.astype(F32), gate.astype(F32)
    sig = jax.nn.sigmoid(gate)
    sums = None
    parts = {}
    if hypercube:
        in_block = w_in.shape[0] // 2
        out_tie, out_got = out_gather.swap(out_gather.seen[3], zg)
        out_grad = weight_grad(zg, after(cot_scaled, out_tie), place, 0, model)
        out_sum = Scatter(out_grad, w_out.shape[0] // 2)
        sent, got = out_sum.step(*out_gather.swapped)
        full_w_out, output, dots = output_project(
            after(zg, sent), inverse, tokens, cotangent, out_gather.pieces(), order
        )
        sent, got = out_sum.step(got, dots)
        grad_ynorm = mm_nt(after(cotangent, sent), full_w_out)
    else:
        projected = inverse * mm(zg, full_w_out)
        output = (inputs + projected).astype(BF16)
        dots = jnp.sum(cot * projected, axis=1, keepdims=True)
        grad_ynorm = mm_nt(cotangent, full_w_out)
    dz = inverse * (full_gain_out * grad_ynorm) - (y * (gate * sig)) * (inverse * inverse * dots / di)
    dy = (dz * (gate * sig)).astype(BF16)
    dgate = (dz * y * (sig * (1.0 + gate * (1.0 - sig)))).astype(BF16)
    if hypercube:
        gate_grad = weight_grad(normed, after(dgate, got), place, 0, di)
        gate_sum = Scatter(gate_grad, in_block)
        sent, gate_got = gate_sum.step()
        scaled = mm_nt(after(dgate, sent), w_gate)
        sent, got = zip(out_sum.step(got, scaled), gate_sum.step(gate_got, scaled))
        dy = after(dy, *sent, gate_got, scaled)
    else:
        scaled = mm_nt(dgate, w_gate)
    grad_sums = {}
    for index, call in reversed(list(enumerate(calls))):
        pc, first_x = pcs[index]
        dpart, dcw, dskip, *sums = run_backward(
            dy, x, bcv, states, slope, bc_slope, pc, first_x, pcs[0][0], conv_x, conv_bc,
            same, seg_col, seg_row, heads, skip, (cum, shifted, cum_lines), *call, index == 0, sums,
        )
        parts[index] = (dpart, dcw, dskip)
        if not hypercube:
            scaled = scaled + mm_nt(dpart, w_parts[index])
            continue
        done = *got, dpart
        if index == 2:
            sent, out_got = out_sum.step(*done)
            early = (sent, *done)
        elif index == 1:
            sent, gate_got = gate_sum.step(*done)
            early = (sent, *done)
        else:
            sent, late = grad_sums[1].step(*got)
            early = (sent, *got)
        grad = weight_grad(normed, after(dpart, *early), place, 0, dpart.shape[1])
        grad_sums[index] = Scatter(grad, in_block)
        swap_sent, swap_got = grad_sums[index].step()
        if index == 2:
            scaled = scaled + mm_nt(after(dpart, swap_sent), w_parts[index])
            done = swap_got, scaled
            sent, got = zip(out_sum.step(out_got, *done), gate_sum.step(got[1], *done), grad_sums[2].step(*done))
            dy = after(dy, *sent, *done)
        elif index == 1:
            sent, got = zip(gate_sum.step(gate_got, swap_sent), grad_sums[2].step(got[2], swap_sent))
            got = got + (swap_got,)
            dy = after(dy, *sent, swap_sent)
        else:
            sent, late = zip(grad_sums[1].step(late, swap_sent), grad_sums[2].step(swap_sent))
            sent, got = grad_sums[0].step(swap_got, *sent)
            scaled = scaled + mm_nt(after(dpart, sent), w_parts[index])
    dbcw, dhead = after(tuple(sums), swap_sent) if hypercube else sums
    dbcw, dhead = after(tuple(sums), swap_sent) if hypercube else sums
    dcw = jnp.concatenate([parts[index][1] for index in range(len(calls))] + [dbcw], axis=2)
    dskip = jnp.concatenate([parts[index][2] for index in range(len(calls))], axis=1)
    if hypercube:
        ties = [swap_sent, swap_got, got]
        sent, got = grad_sums[0].step(got, scaled)
        ties.append(got)
        sent, late = zip(grad_sums[1].step(*late, sent), grad_sums[2].step(*late, sent))
        late = late[0]
        scaled = scaled + mm_nt(after(parts[1][0], *sent), w_parts[1])
    scaled = scaled * full_gain_in
    inner = jnp.mean(unit * scaled, axis=1, keepdims=True)
    grad_tokens = (cot + rscale * (scaled - unit * inner)).astype(BF16)

    conv_sums = dcw.sum(1)
    conv_sums = jnp.concatenate([conv_sums[4:5], conv_sums[3:4], conv_sums[2:3], conv_sums[1:2], conv_sums[0:1]])
    per_head = jnp.concatenate(
        [
            dhead[0].sum(0)[:H],
            dhead[1].sum(0)[:H] * -jnp.exp(a_log),
            dskip.sum(0).reshape(H, P_SIZE).sum(1),
        ]
    )
    conv_part = conv_sums.reshape(taps + 1, shards, conv_local).transpose(1, 0, 2).reshape(shards, -1)
    small_grad = jnp.concatenate([conv_part, jnp.broadcast_to(per_head[None], (shards, 3 * H))], axis=1)
    real = w_in.shape[1] - 2 * di
    if hypercube:
        last_sent, got = grad_sums[0].step(got, grad_tokens)
        ties.append(got)
        grad_sums[1].step(late, last_sent)
        grad_sums[0].step(got)
        small_sum = reduce_small(small_grad, ties)[0]
        whole = [gate_sum.finish(last_sent), grad_sums[2].finish(last_sent)]
        whole = [both_cores(part) for part in whole + [grad_sums[1].finish(), grad_sums[0].finish()]]
        head = whole.pop()
        whole = [whole[0], head[:, 4 * N :], whole[2], whole[1], head[:, :real]]
        sum_w_in = jnp.concatenate(whole, axis=1)
        edges = [0, di, di + width, di + 3 * width, 2 * di, w_in.shape[1]]
        gain_sum = 0.0
        for part, a, b in zip(whole, edges, edges[1:]):
            gain_sum = gain_sum + jnp.sum(part * w_in[:, a:b].astype(F32), axis=1)
        sum_w_out = both_cores(out_sum.finish())
    else:
        grad_w_out = dot_f32(zg, cot_scaled, ((0,), (0,)))
        rest = [parts[index][0] for index in range(len(calls))]
        grads = jnp.concatenate([dgate, rest[0][:, 4 * N :], *rest[1:], rest[0][:, :real]], axis=1)
        grad_w_in = dot_f32(normed, grads, ((0,), (0,)))
        small_sum = lax.psum(
            lax.psum_scatter(small_grad, "shard", scatter_dimension=0, tiled=True), "rep"
        )[0]
        sum_w_in = lax.psum_scatter(grad_w_in, "shard", scatter_dimension=0, tiled=True)
        sum_w_out = lax.psum_scatter(grad_w_out, "shard", scatter_dimension=0, tiled=True)
        sum_w_in, sum_w_out = lax.psum((sum_w_in, sum_w_out), "rep")
        gain_sum = jnp.sum(sum_w_in * w_in.astype(F32), axis=1)
    grad_gain_in = gain_sum / gain_in.astype(F32)
    grad_gain_out = jnp.sum(sum_w_out * w_out.astype(F32), axis=1) / gain_out.astype(F32)
    cut = taps * conv_local
    head_at = cut + conv_local
    return (
        output,
        grad_tokens,
        grad_gain_in,
        sum_w_in,
        small_sum[:cut].reshape(taps, conv_local),
        small_sum[cut:head_at],
        small_sum[head_at : head_at + H],
        small_sum[head_at + H : head_at + 2 * H],
        small_sum[head_at + 2 * H :],
        grad_gain_out,
        sum_w_out,
    )


def both_cores(own):
    partner = swap_cores(own)
    first = lax.axis_index("rep") == 0
    return jnp.concatenate([jnp.where(first, own, partner), jnp.where(first, partner, own)], axis=0)


def reduce_small(rows, ties):
    core = lax.axis_index("rep")
    places = jnp.asarray([reach(order) for order in ORDERS], jnp.int32)[core] ^ lax.axis_index("shard")
    hot = (places[:, None] == jnp.arange(16, dtype=jnp.int32)[None, :]).astype(F32)
    total = dot_f32(hot, rows, ((1,), (0,)), HIGHEST)
    for stage, tie in zip((3, 2, 1, 0), ties[:4]):
        cut = 1 << stage
        total = after(total, tie)
        total = total[:cut] + exchange(total[cut:], stage)
    total = after(total, ties[4])
    return total + swap_cores(total)


def solution(mesh):
    rows = P(("shard", "rep"), None)
    in_specs = (
        rows, rows, P("shard"), P("shard", None), P(None, "shard"), P("shard"), P(), P(), P(), P("shard"),
        P("shard", None), rows,
    )
    out_specs = (
        rows, rows, P("shard"), P("shard", None), P(None, "shard"), P("shard"), P(), P(), P(), P("shard"),
        P("shard", None),
    )
    hypercube = mesh.shape["shard"] == 16 and mesh.shape["rep"] == 2
    return jax.shard_map(
        functools.partial(on_device, hypercube),
        mesh=mesh,
        in_specs=in_specs,
        out_specs=out_specs,
        check_vma=False,
    )
```

```python
import functools

import jax
import jax.numpy as jnp
from jax import lax
from jax.experimental import pallas as pl
from jax.experimental.pallas import tpu as pltpu
from jax.sharding import PartitionSpec as P
from jax.sharding import PartitionSpec as P

H = 48
P_SIZE = 64
N = 128
SPAN = 256
HALF = 128
GROUP = 8
TILE = 128
EPSILON = 1e-05
HIGHEST = lax.Precision.HIGHEST
LOG2E = 1.4426950408889634
NEG = -1e30
F32 = jnp.float32
BF16 = jnp.bfloat16


def dot_f32(a, b, contract, precision=None):
    return lax.dot_general(
        a, b, ((contract[0], contract[1]), ((), ())), preferred_element_type=F32, precision=precision
    )


def mm(a, b):
    return dot_f32(a, b, ((1,), (0,)))


def mm_nt(a, b):
    return dot_f32(a, b, ((1,), (1,)))


def lanes_of(column, rows):
    return jnp.broadcast_to(column, (rows, TILE))


def step_sizes(raw, heads):
    shifted = raw + heads[0:1]
    return jnp.maximum(shifted, 0.0) + jnp.log1p(jnp.exp(-jnp.abs(shifted)))


def conv_taps(ext, same, start, width, rows=SPAN):
    out = [ext[8 : 8 + rows, start : start + width]]
    for offset in (1, 2, 3):
        moved = ext[8 - offset : 8 - offset + rows, start : start + width]
        mask = same[offset - 1]
        if width > TILE:
            mask = jnp.concatenate([mask] * (width // TILE), axis=1)
        out.append(moved * mask)
    return out


def conv_sum(taps, weights):
    total = weights[4:5] + weights[3:4] * taps[0]
    for offset in (1, 2, 3):
        total = total + weights[3 - offset : 4 - offset] * taps[offset]
    return total


def prepare(raw_ref, heads_ref):
    heads = heads_ref[...]
    step = step_sizes(raw_ref[...], heads)
    row = lax.broadcasted_iota(jnp.int32, (SPAN, SPAN), 0)
    col = lax.broadcasted_iota(jnp.int32, (SPAN, SPAN), 1)
    tri = (row >= col).astype(F32)
    cum = dot_f32(tri, step * heads[1:2], ((1,), (0,)), HIGHEST)
    return cum, cum - jnp.log2(step)


def pick(first, columns, at):
    return jnp.where(first, lanes_of(columns[:, at : at + 1], first.shape[0]), lanes_of(columns[:, at + 1 : at + 2], first.shape[0]))


def forward_kernel(first_call, base, pc_ref, halo_ref, cw_ref, same, seg_col_ref, seg_ref, skip_ref, *rest):
    rest = list(rest)
    if first_call:
        raw_ref, heads_ref, bc_ref, bc_halo_ref, bcw_ref = [rest.pop(0) for _ in range(5)]
        x_out, y_out, st_out, slope_out, mark, bc_out, bc_slope_out = [rest.pop(0) for _ in range(7)]
        pack, shifted_out, cum_out, cum_rows, w_rows = [rest.pop(0) for _ in range(5)]
    else:
        bc_out, pack, cum_rows, w_rows = [rest.pop(0) for _ in range(4)]
        mark_ref = rest[4]
        rest = rest[5:]
        x_out, y_out, st_out, slope_out, mark = [rest.pop(0) for _ in range(5)]
    state, scores, block, keep_row, b_t, ext, ext_bc = rest
    span = pl.program_id(0)
    group = pl.program_id(1)
    group_head = base + GROUP * group

    @pl.when((span == 0) & (group == 0))
    def _():
        state[...] = jnp.zeros_like(state)
        mark[...] = jnp.zeros_like(mark) if first_call else mark_ref[...]

    @pl.when(group == 0)
    def _():
        if first_call:
            cum, shifted = prepare(raw_ref, heads_ref)
            pack[...] = cum
            shifted_out[...] = shifted
            cum_out[...] = cum.T
            cum_rows[...] = shifted.T
            w_rows[...] = (jnp.exp2(cum[SPAN - 1 : SPAN] - shifted) * same[4]).T
        last = pack[SPAN - 1 : SPAN]
        keep_row[...] = jnp.broadcast_to(jnp.exp2(last) * same[3, SPAN - 1 : SPAN], (8, TILE))
        if first_call:
            ext_bc[0:8] = bc_halo_ref[...]
            ext_bc[8:] = bc_ref[...]
            total = conv_sum(conv_taps(ext_bc, same, 0, 2 * N), bcw_ref[...])
            gate = jax.nn.sigmoid(total)
            both = total * gate
            bc_out[...] = both.astype(BF16)
            bc_slope_out[...] = (gate + both * (1.0 - gate)).astype(BF16)
        row = lax.broadcasted_iota(jnp.int32, (SPAN, SPAN), 0)
        col = lax.broadcasted_iota(jnp.int32, (SPAN, SPAN), 1)
        linked = (row >= col) & (seg_col_ref[...] == seg_ref[...])
        block[...] = jnp.where(linked, 0.0, NEG)
        scores[...] = mm_nt(bc_out[:, N:], bc_out[:, :N])
        b_t[...] = bc_out[:, :N].astype(F32).T

    ext[0:8] = halo_ref[...]
    ext[8:] = pc_ref[...]
    shift = lax.rem(TILE - group_head, TILE)
    cums = pltpu.roll(pack[...], shift, 1)
    keep = jnp.broadcast_to(pltpu.roll(keep_row[...], shift, 1)[0:1], (N, TILE))
    first = lax.broadcasted_iota(jnp.int32, (SPAN, TILE), 1) < P_SIZE
    query = bc_out[:, N:]
    empty = jnp.zeros((HALF, HALF), BF16)
    wide = lambda parts: jnp.concatenate(parts, axis=1)
    for quad in range(GROUP // 4):
        xbs, outs, entries, keeps, fresh = [], [], [], [], []
        for pair in (2 * quad, 2 * quad + 1):
            at = pair * TILE
            total = conv_sum(conv_taps(ext, same, at, TILE), cw_ref[:, at : at + TILE])
            gate = jax.nn.sigmoid(total)
            x = total * gate
            xb = x.astype(BF16)
            x_out[:, at : at + TILE] = xb
            slope_out[:, at : at + TILE] = (gate + x * (1.0 - gate)).astype(BF16)
            mixes, weighted, cum_cols = [], [], []
            for head in (2 * pair, 2 * pair + 1):
                cum_col = lanes_of(cums[:, head : head + 1], SPAN)
                cum_cols.append(cum_col)
                cum_row = cum_rows[pl.ds(group_head + head, 1), :]
                blocks = []
                for i, j in ((0, 0), (1, 0), (1, 1)):
                    rows = slice(i * HALF, (i + 1) * HALF)
                    cols = slice(j * HALF, (j + 1) * HALF)
                    gap = cum_col[rows] - cum_row[:, cols] + block[rows, cols]
                    blocks.append((jnp.exp2(gap) * scores[rows, cols]).astype(BF16))
                mixes.append(wide([blocks[0], empty]))
                mixes.append(wide(blocks[1:]))
                weighted.append((b_t[...] * w_rows[pl.ds(group_head + head, 1), :]).astype(BF16))
            inner = mm(jnp.concatenate(mixes + weighted, axis=0), xb)
            outs.append(jnp.where(first, inner[:SPAN], inner[SPAN : 2 * SPAN]))
            fresh.append(jnp.where(first[:N], inner[2 * SPAN : 2 * SPAN + N], inner[2 * SPAN + N :]))
            xbs.append(xb)
            entries.append(jnp.exp2(jnp.where(first, cum_cols[0], cum_cols[1])) * same[3])
            keeps.append(pick(first[:N], keep, 2 * pair))
        both = slice(quad * 2 * TILE, (quad + 1) * 2 * TILE)
        tile = pl.ds(pl.multiple_of(group * GROUP * P_SIZE + quad * 2 * TILE, 2 * TILE), 2 * TILE)
        old = state[:, tile]
        old_b = old.astype(BF16)
        st_out[:, both] = old_b
        carried = mm(query, old_b)
        y = wide(outs) + wide(entries) * carried + skip_ref[:, both] * wide(xbs).astype(F32)
        y_out[:, both] = y.astype(BF16)
        state[:, tile] = old * wide(keeps) + wide(fresh)


def run_forward(pc, first_x, pc_bc, conv_x, conv_bc, same, seg_col, seg_row, heads, skip, start, count, shared, before):
    tokens = pc.shape[0]
    spans = tokens // SPAN
    di = skip.shape[1]
    width = GROUP * P_SIZE
    own = count * width
    first_call = before is None
    any_spec = pl.BlockSpec(memory_space=pl.ANY)
    halo = lambda s: jnp.maximum(s * (SPAN // 8) - 1, 0)
    wide = pl.BlockSpec((SPAN, width), lambda s, g: (s, start + g))
    bcv_spec = pl.BlockSpec((SPAN, 2 * N), lambda s, g: (s, 0))
    in_specs = [
        pl.BlockSpec((SPAN, width), lambda s, g: (s, first_x + g)),
        pl.BlockSpec((8, width), lambda s, g: (halo(s), first_x + g)),
        pl.BlockSpec((8, width), lambda s, g: (0, start + g)),
        pl.BlockSpec((5, SPAN, TILE), lambda s, g: (0, s, 0)),
        pl.BlockSpec((SPAN, 1), lambda s, g: (s, 0)),
        pl.BlockSpec((1, SPAN), lambda s, g: (0, s)),
        pl.BlockSpec((1, width), lambda s, g: (0, start + g)),
    ]
    args = [pc, pc, conv_x, same, seg_col, seg_row, skip]
    column_spec = pl.BlockSpec((SPAN, TILE), lambda s, g: (s, 0))
    row_spec = pl.BlockSpec((TILE, SPAN), lambda s, g: (s, 0))
    columns_shape = jax.ShapeDtypeStruct((tokens, TILE), F32)
    rows_shape = jax.ShapeDtypeStruct((spans * TILE, SPAN), F32)
    mark_spec = pl.BlockSpec((8, TILE), lambda s, g: (0, 0))
    out_specs = [wide, wide, pl.BlockSpec((N, width), lambda s, g: (s, start + g)), wide, mark_spec]
    out_shape = [
        jax.ShapeDtypeStruct((tokens, di), BF16),
        jax.ShapeDtypeStruct((tokens, di), BF16),
        jax.ShapeDtypeStruct((spans * N, di), BF16),
        jax.ShapeDtypeStruct((tokens, di), BF16),
        jax.ShapeDtypeStruct((8, TILE), F32),
    ]
    if first_call:
        in_specs += [
            pl.BlockSpec((SPAN, TILE), lambda s, g: (s, 2)),
            pl.BlockSpec((8, TILE), lambda s, g: (0, 0)),
            pl.BlockSpec((SPAN, 2 * N), lambda s, g: (s, 0)),
            pl.BlockSpec((8, 2 * N), lambda s, g: (halo(s), 0)),
            pl.BlockSpec((8, 2 * N), lambda s, g: (0, 0)),
        ]
        args += [pc_bc, heads, pc_bc, pc_bc, conv_bc]
        out_specs += [bcv_spec, bcv_spec, column_spec, column_spec, row_spec, row_spec, row_spec]
        out_shape += [jax.ShapeDtypeStruct((tokens, 2 * N), BF16)] * 2
        out_shape += [columns_shape] * 2 + [rows_shape] * 3
        aliases = {}
    else:
        in_specs += [bcv_spec, column_spec, row_spec, row_spec, any_spec, any_spec, any_spec, any_spec, mark_spec]
        args += [*shared, *before]
        aliases = {11: 0, 12: 1, 13: 2, 14: 3}
    return pl.pallas_call(
        functools.partial(forward_kernel, first_call, start * GROUP),
        grid_spec=pltpu.PrefetchScalarGridSpec(
            num_scalar_prefetch=0,
            grid=(spans, count),
            in_specs=in_specs,
            out_specs=out_specs,
            scratch_shapes=[
                pltpu.VMEM((N, own), F32),
                pltpu.VMEM((SPAN, SPAN), F32),
                pltpu.VMEM((SPAN, SPAN), F32),
                pltpu.VMEM((8, TILE), F32),
                pltpu.VMEM((N, SPAN), F32),
                pltpu.VMEM((SPAN + 8, width), F32),
                pltpu.VMEM((SPAN + 8, 2 * N), F32),
            ],
        ),
        out_shape=out_shape,
        input_output_aliases=aliases,
        compiler_params=pltpu.CompilerParams(dimension_semantics=("arbitrary", "arbitrary")),
        cost_estimate=pl.CostEstimate(flops=int(5e9 * count), bytes_accessed=14 * tokens * own, transcendentals=0),
        name="scan_forward",
    )(*args)


def conv_back(grad, slope, signal, same, weights, carry):
    width = grad.shape[1]
    du = grad * slope.astype(F32)

    def add_rows(values):
        return jnp.sum(values.reshape(SPAN // 8, 8, width), axis=0)

    out = weights[3:4] * du
    sums = [add_rows(du), add_rows(du * signal)]
    for offset in (1, 2, 3):
        mask = same[offset - 1]
        if width > TILE:
            mask = jnp.concatenate([mask] * (width // TILE), axis=1)
        masked = du * mask
        moved = jnp.concatenate([masked, carry[offset - 1]], axis=0)[offset : offset + SPAN]
        carry[offset - 1] = masked[0:8]
        out = out + weights[3 - offset : 4 - offset] * moved
        sums.append(add_rows(moved * signal))
    return out, sums


def backward_kernel(
    first_call, last_call, base,
    dy_ref, x_ref, bcv_ref, st_ref, slope_ref, pc_ref, cw_ref, same, seg_col_ref, seg_ref, skip_ref,
    cum_ref, shifted_ref, cum_rows, *rest,
):
    rest = list(rest)
    before = None if first_call else [rest.pop(0) for _ in range(4)]
    if last_call:
        raw_ref, heads_ref, bc_ref, bc_slope_ref, bcw_ref = [rest.pop(0) for _ in range(5)]
    dproj_out, dcw_out, dskip_out = [rest.pop(0) for _ in range(3)]
    if last_call:
        dbcw_out, dhead_out = [rest.pop(0) for _ in range(2)]
    else:
        after_out = [rest.pop(0) for _ in range(4)]
    (
        dstate, scores, block, dscores, pack, c_t,
        carry, carry_bc, d_bc, per_row, dcum_rows, dlast,
    ) = rest
    back = pl.program_id(0)
    group = pl.program_id(1)
    groups = pl.num_programs(1)
    width = GROUP * P_SIZE
    group_head = base + GROUP * group
    first_x = 4 * N if last_call else 0

    @pl.when((back == 0) & (group == 0))
    def _():
        dstate[...] = jnp.zeros_like(dstate)
        carry[...] = jnp.zeros_like(carry)
        dcw_out[...] = jnp.zeros_like(dcw_out)
        dskip_out[...] = jnp.zeros_like(dskip_out)
        dcum_rows[...] = jnp.zeros_like(dcum_rows)
        if last_call:
            carry_bc[...] = jnp.zeros_like(carry_bc)
            dbcw_out[...] = jnp.zeros_like(dbcw_out)
            dhead_out[...] = jnp.zeros_like(dhead_out)

    keys = bcv_ref[:, :N]
    query = bcv_ref[:, N:]
    lane = lax.broadcasted_iota(jnp.int32, (SPAN, TILE), 1)

    @pl.when(group == 0)
    def _():
        entry = jnp.exp2(cum_ref[...]) * same[3]
        pack[...] = jnp.where(lane < 64, shifted_ref[...], pltpu.roll(entry, 64, 1))
        row = lax.broadcasted_iota(jnp.int32, (SPAN, SPAN), 0)
        col = lax.broadcasted_iota(jnp.int32, (SPAN, SPAN), 1)
        linked = (row <= col) & (seg_col_ref[...] == seg_ref[...])
        block[...] = jnp.where(linked, 0.0, NEG)
        scores[...] = mm_nt(keys, query)
        c_t[...] = query.T
        per_row[...] = jnp.zeros_like(per_row)
        if first_call:
            dscores[...] = jnp.zeros_like(dscores)
            d_bc[...] = jnp.zeros_like(d_bc)
            dlast[...] = jnp.zeros_like(dlast)
        else:
            dscores[...] = before[0][...]
            d_bc[...] = before[1][...]
            per_row[0] = before[2][:, :TILE]
            per_row[2] = before[2][:, TILE:]
            dlast[...] = before[3][...]

    shift = lax.rem(TILE - group_head, TILE)
    cols = pltpu.roll(pack[...], shift, 1)
    last_cum = pltpu.roll(jnp.broadcast_to(cum_ref[SPAN - 1 : SPAN], (8, TILE)), shift, 1)[0:1]
    keep_mask = same[3, SPAN - 1 : SPAN]
    first = lane < P_SIZE
    lane_row = lax.broadcasted_iota(jnp.int32, (2 * TILE, TILE), 0) // P_SIZE
    lane_col = lax.broadcasted_iota(jnp.int32, (2 * TILE, TILE), 1)
    sums = jnp.zeros((SPAN, TILE), F32)
    last_sum = jnp.zeros((1, TILE), F32)
    group_at = group * width
    empty = jnp.zeros((HALF, HALF), BF16)
    wide = lambda parts: jnp.concatenate(parts, axis=1)
    for quad in range(GROUP // 4):
        both = slice(quad * 2 * TILE, (quad + 1) * 2 * TILE)
        tile = pl.ds(pl.multiple_of(group_at + quad * 2 * TILE, 2 * TILE), 2 * TILE)
        entries, tails, keeps, inners = [], [], [], []
        for pair in (2 * quad, 2 * quad + 1):
            at = pair * TILE
            heads = (2 * pair, 2 * pair + 1)
            dy_pair = dy_ref[:, at : at + TILE]
            xb = x_ref[:, at : at + TILE]
            nothing = jnp.zeros_like(xb)
            split = jnp.concatenate([jnp.where(first, xb, nothing), jnp.where(first, nothing, xb)], axis=0)
            g_both = mm_nt(split, dy_pair)
            cum_cols = [lanes_of(cols[:, head : head + 1], SPAN) for head in heads]
            cum_lines = [cum_rows[pl.ds(group_head + head, 1), :] for head in heads]
            mixes = [[], []]
            across = [[], []]
            down = [[], []]
            for j, i in ((0, 0), (0, 1), (1, 1)):
                rows = slice(j * HALF, (j + 1) * HALF)
                cells = slice(i * HALF, (i + 1) * HALF)
                spread = jnp.zeros((HALF, HALF), F32)
                for which in (0, 1):
                    decay = jnp.exp2(cum_lines[which][:, cells] - cum_cols[which][rows] + block[rows, cells])
                    mix = decay * scores[rows, cells]
                    g = g_both[which * SPAN + j * HALF : which * SPAN + (j + 1) * HALF, cells]
                    spread = spread + decay * g
                    w = mix * g
                    mixes[which].append(mix.astype(BF16))
                    across[which].append(w)
                    down[which].append(jnp.sum(w, axis=0, keepdims=True))
                dscores[rows, cells] += spread
            lefts = []
            for which in (0, 1):
                row_sum = jnp.concatenate(
                    [
                        jnp.sum(across[which][0] + across[which][1], axis=1, keepdims=True),
                        jnp.sum(across[which][2], axis=1, keepdims=True),
                    ],
                    axis=0,
                )
                sums = sums - jnp.where(lane == 2 * GROUP + heads[which], row_sum, 0.0)
                dcum_rows[pl.ds(group_head + heads[which], 1), :] = wide(
                    [down[which][0], down[which][1] + down[which][2]]
                )
                lefts += [wide(mixes[which][:2]), wide([empty, mixes[which][2]])]
            inner = mm(jnp.concatenate(lefts, axis=0), dy_pair)
            inners.append(jnp.where(first, inner[:SPAN], inner[SPAN:]))
            last_pair = jnp.where(
                first[0:1],
                jnp.broadcast_to(last_cum[:, heads[0] : heads[0] + 1], (1, TILE)),
                jnp.broadcast_to(last_cum[:, heads[1] : heads[1] + 1], (1, TILE)),
            )
            tails.append(jnp.exp2(last_pair - jnp.where(first, cum_cols[0], cum_cols[1])) * same[4])
            keeps.append(jnp.exp2(last_pair) * keep_mask)
            entries.append(pick(first, cols, 64 + 2 * pair))
        dyf = dy_ref[:, both].astype(F32)
        xf = x_ref[:, both].astype(F32)
        tail = wide(tails)
        stb = st_ref[:, both]
        ds = dstate[:, tile]
        dsb = ds.astype(BF16)
        dye_f = dyf * wide(entries)
        dye = dye_f.astype(BF16)
        fresh = mm(keys, dsb) * tail
        total = wide(inners) + fresh
        d_bc[:, N:] += mm_nt(dye, stb)
        d_bc[:, :N] += mm_nt((xf * tail).astype(BF16), dsb)

        def head_sum(values, kind):
            spread = (lane_col == kind * GROUP + 4 * quad + lane_row).astype(BF16)
            return mm(values.astype(BF16), spread)

        sums = sums + head_sum(xf * total, 0) + head_sum(xf * fresh, 1) + head_sum(dye_f * mm(query, stb), 2)
        kept = ds * wide(keeps)
        kept_sum = jnp.sum(kept * stb.astype(F32), axis=0, keepdims=True)
        lane_pair = lax.broadcasted_iota(jnp.int32, (1, 2 * TILE), 1) // P_SIZE
        for head in range(4):
            one = jnp.sum(jnp.where(lane_pair == head, kept_sum, 0.0), axis=1, keepdims=True)
            last_sum = last_sum + jnp.where(lane[0:1] == 4 * quad + head, one, 0.0)
        dstate[:, tile] = kept + mm(c_t[...], dye)
        dskip_out[:, tile] += jnp.sum((dyf * xf).reshape(SPAN // 8, 8, 2 * TILE), axis=0)
        dx = total + skip_ref[:, both] * dyf
        for part in (0, 1):
            at = (2 * quad + part) * TILE
            one = pl.ds(pl.multiple_of(group_at + at, TILE), TILE)
            out, conv_sums = conv_back(
                dx[:, part * TILE : (part + 1) * TILE], slope_ref[:, at : at + TILE], pc_ref[:, at : at + TILE],
                same, cw_ref[:, at : at + TILE], carry.at[:, :, one],
            )
            dproj_out[:, pl.ds(pl.multiple_of(first_x + group_at + at, TILE), TILE)] = out.astype(BF16)
            for k, value in enumerate(conv_sums):
                dcw_out[k, :, one] += value

    in_place = (lane >= group_head) & (lane < group_head + GROUP)
    for kind in range(3):
        moved = pltpu.roll(sums, lax.rem(group_head + TILE - GROUP * kind, TILE), 1)
        per_row[kind] += jnp.where(in_place, moved, 0.0)
    moved = pltpu.roll(jnp.broadcast_to(last_sum, (8, TILE)), group_head, 1)
    dlast[...] += jnp.where(in_place[0:8], moved, 0.0)

    @pl.when(group == groups - 1)
    def _():
        state_part = per_row[1]
        dcum = dcum_rows[...].T + per_row[2] - state_part
        dlast_all = dlast[0:1] + jnp.sum(state_part, axis=0, keepdims=True)
        if not last_call:
            after_out[0][...] = dscores[...]
            after_out[1][...] = d_bc[...]
            after_out[2][:, :TILE] = per_row[0]
            after_out[2][:, TILE:] = dcum
            after_out[3][...] = jnp.broadcast_to(dlast_all, (8, TILE))
            return
        ds_b = dscores[...].astype(BF16)
        grad_b = d_bc[:, :N] + mm(ds_b, query)
        grad_c = d_bc[:, N:] + mm(dscores[...].T.astype(BF16), keys)
        out, conv_sums = conv_back(
            wide([grad_b, grad_c]), bc_slope_ref[...], bc_ref[...], same, bcw_ref[...], carry_bc
        )
        dproj_out[:, : 2 * N] = out.astype(BF16)
        for k, value in enumerate(conv_sums):
            dbcw_out[k] += value
        heads = heads_ref[...]
        shifted = raw_ref[...] + heads[0:1]
        step = step_sizes(raw_ref[...], heads)
        slope = jax.nn.sigmoid(shifted)
        row = lax.broadcasted_iota(jnp.int32, (SPAN, SPAN), 0)
        col = lax.broadcasted_iota(jnp.int32, (SPAN, SPAN), 1)
        tri = (row <= col).astype(F32)
        da = dot_f32(tri, dcum, ((1,), (0,)), HIGHEST) + dlast_all
        small = shifted < -16.0
        ratio = jnp.where(small, 1.0, slope / jnp.where(small, 1.0, step))
        live = lane < H
        draw = jnp.where(live, per_row[0] * ratio + da * heads[2:3] * slope, 0.0)
        dproj_out[:, 2 * N : 3 * N] = draw.astype(BF16)
        dproj_out[:, 3 * N : 4 * N] = jnp.zeros((SPAN, N), BF16)
        dhead_out[0] += jnp.sum(draw.reshape(SPAN // 8, 8, TILE), axis=0)
        dhead_out[1] += jnp.sum(jnp.where(live, da * step, 0.0).reshape(SPAN // 8, 8, TILE), axis=0)


def run_backward(
    dy, x, bcv, states, slope, bc_slope, pc, first_x, pc_bc, conv_x, conv_bc, same, seg_col, seg_row, heads, skip,
    cums, start, count, last, before,
):
    tokens, di = dy.shape
    spans = tokens // SPAN
    width = GROUP * P_SIZE
    turn = lambda s: spans - 1 - s
    own = count * width
    out_width = own + (4 * N if last else 0)
    sums_specs = [
        pl.BlockSpec((SPAN, SPAN), lambda s, g: (turn(s), 0)),
        pl.BlockSpec((SPAN, 2 * N), lambda s, g: (turn(s), 0)),
        pl.BlockSpec((SPAN, 2 * TILE), lambda s, g: (turn(s), 0)),
        pl.BlockSpec((8, TILE), lambda s, g: (turn(s), 0)),
    ]
    sums_shapes = [
        jax.ShapeDtypeStruct((tokens, SPAN), F32),
        jax.ShapeDtypeStruct((tokens, 2 * N), F32),
        jax.ShapeDtypeStruct((tokens, 2 * TILE), F32),
        jax.ShapeDtypeStruct((spans * 8, TILE), F32),
    ]
    out_specs = [
        pl.BlockSpec((SPAN, out_width), lambda s, g: (turn(s), 0)),
        pl.BlockSpec((5, 8, own), lambda s, g: (0, 0, 0)),
        pl.BlockSpec((8, own), lambda s, g: (0, 0)),
    ]
    out_shape = [
        jax.ShapeDtypeStruct((tokens, out_width), BF16),
        jax.ShapeDtypeStruct((5, 8, own), F32),
        jax.ShapeDtypeStruct((8, own), F32),
    ]
    wide = pl.BlockSpec((SPAN, width), lambda s, g: (turn(s), start + g))
    in_specs = [
        wide,
        wide,
        pl.BlockSpec((SPAN, 2 * N), lambda s, g: (turn(s), 0)),
        pl.BlockSpec((N, width), lambda s, g: (turn(s), start + g)),
        wide,
        pl.BlockSpec((SPAN, width), lambda s, g: (turn(s), first_x + g)),
        pl.BlockSpec((8, width), lambda s, g: (0, start + g)),
        pl.BlockSpec((5, SPAN, TILE), lambda s, g: (0, turn(s), 0)),
        pl.BlockSpec((SPAN, 1), lambda s, g: (turn(s), 0)),
        pl.BlockSpec((1, SPAN), lambda s, g: (0, turn(s))),
        pl.BlockSpec((1, width), lambda s, g: (0, start + g)),
        pl.BlockSpec((SPAN, TILE), lambda s, g: (turn(s), 0)),
        pl.BlockSpec((SPAN, TILE), lambda s, g: (turn(s), 0)),
        pl.BlockSpec((TILE, SPAN), lambda s, g: (turn(s), 0)),
    ]
    args = [dy, x, bcv, states, slope, pc, conv_x, same, seg_col, seg_row, skip, *cums]
    if before is not None:
        in_specs += sums_specs
        args += before
    if last:
        in_specs += [
            pl.BlockSpec((SPAN, TILE), lambda s, g: (turn(s), 2)),
            pl.BlockSpec((8, TILE), lambda s, g: (0, 0)),
            pl.BlockSpec((SPAN, 2 * N), lambda s, g: (turn(s), 0)),
            pl.BlockSpec((SPAN, 2 * N), lambda s, g: (turn(s), 0)),
            pl.BlockSpec((8, 2 * N), lambda s, g: (0, 0)),
        ]
        args += [pc_bc, heads, pc_bc, bc_slope, conv_bc]
        out_specs += [
            pl.BlockSpec((5, 8, 2 * N), lambda s, g: (0, 0, 0)),
            pl.BlockSpec((2, 8, TILE), lambda s, g: (0, 0, 0)),
        ]
        out_shape += [
            jax.ShapeDtypeStruct((5, 8, 2 * N), F32),
            jax.ShapeDtypeStruct((2, 8, TILE), F32),
        ]
    else:
        out_specs += sums_specs
        out_shape += sums_shapes
    return pl.pallas_call(
        functools.partial(backward_kernel, before is None, last, start * GROUP),
        grid_spec=pltpu.PrefetchScalarGridSpec(
            num_scalar_prefetch=0,
            grid=(spans, count),
            in_specs=in_specs,
            out_specs=out_specs,
            scratch_shapes=[
                pltpu.VMEM((N, own), F32),
                pltpu.VMEM((SPAN, SPAN), F32),
                pltpu.VMEM((SPAN, SPAN), F32),
                pltpu.VMEM((SPAN, SPAN), F32),
                pltpu.VMEM((SPAN, TILE), F32),
                pltpu.VMEM((N, SPAN), BF16),
                pltpu.VMEM((3, 8, own), F32),
                pltpu.VMEM((3, 8, 2 * N), F32),
                pltpu.VMEM((SPAN, 2 * N), F32),
                pltpu.VMEM((3, SPAN, TILE), F32),
                pltpu.VMEM((TILE, SPAN), F32),
                pltpu.VMEM((8, TILE), F32),
            ],
        ),
        out_shape=out_shape,
        compiler_params=pltpu.CompilerParams(dimension_semantics=("arbitrary", "arbitrary")),
        cost_estimate=pl.CostEstimate(
            flops=int(1.2e10 * count), bytes_accessed=12 * tokens * own, transcendentals=0
        ),
        name="scan_backward",
    )(*args)


def seg_facts(seg):
    length = seg.shape[0]
    cols = []
    for offset in (1, 2, 3):
        moved = jnp.concatenate([jnp.full((offset,), -1, jnp.int32), seg[:-offset]])
        cols.append((moved == seg).astype(F32))
    spans = length // SPAN
    ends = seg[SPAN - 1 :: SPAN]
    before = jnp.concatenate([seg[:1], ends[:-1]])
    cols.append((seg == jnp.repeat(before, SPAN)).astype(F32))
    cols.append((seg == jnp.repeat(ends, SPAN)).astype(F32))
    value = seg.astype(F32)
    same = jnp.broadcast_to(jnp.stack(cols, axis=0)[:, :, None], (5, length, TILE))
    return same, value[:, None], value[None, :]


def head_rows(dt_bias, a_log):
    rate = -jnp.exp(a_log)
    rows = jnp.stack([dt_bias, rate * LOG2E, rate] + [jnp.zeros_like(rate)] * 5, axis=0)
    return jnp.pad(rows, ((0, 0), (0, TILE - H)))


BLOCKS = 32
ORDERS = ((8, 1, 4, 2), (8, 2, 4, 1))


def reach(masks):
    out = [0]
    for mask in masks:
        out = out + [mask ^ place for place in out]
    return out


def exchange(values, stage):
    pairs = []
    for shard in range(16):
        for core in range(2):
            pairs.append((shard * 2 + core, (shard ^ ORDERS[core][stage]) * 2 + core))
    return lax.ppermute(values, ("shard", "rep"), pairs)


def swap_cores(values):
    return lax.ppermute(values, "rep", [(0, 1), (1, 0)])


def after(values, *others):
    return lax.optimization_barrier((values, *others))[0]


class Gather:
    def __init__(self, local):
        self.held = local
        self.seen = []
        self.swapped = []

    def step(self, *ahead):
        stage = len(self.seen)
        if stage > 0:
            self.held = jnp.concatenate([self.held, after(self.seen[-1], *ahead)], axis=0)
        elif ahead:
            self.held = after(self.held, *ahead)
        got = exchange(self.held, stage)
        self.seen.append(got)
        return self.held, got

    def swap(self, *ahead):
        send = after(self.held if not self.swapped else self.seen[3], *ahead)
        self.swapped.append(swap_cores(send))
        return send, self.swapped[-1]

    def pieces(self):
        return self.held, self.seen[3], *self.swapped


def gather_small(local):
    held = local[None]
    ahead = yield None
    for stage in range(4):
        send = after(held, *ahead)
        got = exchange(send, stage)
        ahead = yield send, got
        held = jnp.concatenate([send, got], axis=0)
    core = lax.axis_index("rep")
    places = jnp.asarray([reach(order) for order in ORDERS], jnp.int32)[core] ^ lax.axis_index("shard")
    hot = (places[None, :] == jnp.arange(16, dtype=jnp.int32)[:, None]).astype(local.dtype)
    yield dot_f32(hot, held, ((1,), (0,)), HIGHEST).astype(local.dtype)


class Scatter:
    def __init__(self, partial, block):
        mine, self.other = partial
        self.terms = [mine]
        self.block = block
        self.left = [3, 2, 1, 0]

    def rows(self, start, stop):
        total = self.terms[0][start:stop].astype(F32)
        for term in self.terms[1:]:
            total = total + term[start:stop].astype(F32)
        return total

    def step(self, *ahead):
        if len(self.terms) == 1:
            self.other = after(self.other, *ahead)
            self.terms.append(swap_cores(self.other))
            return self.other, self.terms[-1]
        if self.left:
            stage = self.left.pop(0)
            cut = self.block << stage
            self.terms[-1] = after(self.terms[-1], *ahead)
            send = self.rows(cut, 2 * cut).astype(BF16)
            self.terms.append(exchange(send, stage))
            return send, self.terms[-1]
        return self.terms[-1], self.terms[-1]

    def finish(self, *ahead):
        while self.left:
            self.step()
        if ahead:
            self.terms[-1] = after(self.terms[-1], *ahead)
        return self.rows(0, self.block)


def block_order(core):
    shard = lax.axis_index("shard")
    tables = jnp.asarray([reach(order) for order in ORDERS], jnp.int32)
    inverse = jnp.asarray(
        [[reach(order).index(mask) for mask in range(16)] for order in ORDERS], jnp.int32
    )
    own = 2 * (tables[core] ^ shard) + core
    partner = 2 * (tables[1 - core] ^ shard) + (1 - core)
    order = jnp.concatenate([own, partner])
    natural = jnp.arange(BLOCKS, dtype=jnp.int32)
    which = natural % 2
    place = inverse[which, (natural // 2) ^ shard] + 16 * (which != core).astype(jnp.int32)
    return order, place


def fetch_tile(order_ref, pieces, buffer, sems, tile, slot, block, width):
    for q in range(BLOCKS):
        pltpu.make_async_copy(
            pieces[q // 8].at[pl.ds((q % 8) * block, block), pl.ds(pl.multiple_of(tile * width, width), width)],
            buffer.at[slot, pl.ds(pl.multiple_of(order_ref[q] * block, block), block), :],
            sems.at[slot],
        ).start()


def next_tile(order_ref, pieces, buffer, sems, block, width):
    tile = pl.program_id(0)
    slot = lax.rem(tile, 2)

    @pl.when(tile == 0)
    def _():
        fetch_tile(order_ref, pieces, buffer, sems, tile, slot, block, width)

    @pl.when(tile + 1 < pl.num_programs(0))
    def _():
        fetch_tile(order_ref, pieces, buffer, sems, tile + 1, 1 - slot, block, width)

    pltpu.make_async_copy(buffer.at[slot], buffer.at[slot], sems.at[slot]).wait()
    return slot


def project_kernel(block, width, order_ref, x_ref, p0, p1, p2, p3, *rest):
    out_ref, w_ref, buffer, sems = rest[-4:]
    slot = next_tile(order_ref, (p0, p1, p2, p3), buffer, sems, block, width)
    w = buffer[slot]
    w_ref[...] = w
    for i in range(x_ref.shape[0] // SPAN):
        rows = slice(i * SPAN, (i + 1) * SPAN)
        out_ref[rows] = mm(x_ref[rows], w)


def project(x, pieces, order, so_far, start, full, width=512):
    tokens, depth = x.shape
    columns = pieces[0].shape[1]
    block = depth // BLOCKS
    at = start // width
    any_spec = pl.BlockSpec(memory_space=pl.ANY)
    extra = [] if so_far is None else list(so_far)
    return pl.pallas_call(
        functools.partial(project_kernel, block, width),
        grid_spec=pltpu.PrefetchScalarGridSpec(
            num_scalar_prefetch=1,
            grid=(columns // width,),
            in_specs=[pl.BlockSpec((tokens, depth), lambda j, o: (0, 0))] + [any_spec] * (4 + len(extra)),
            out_specs=[
                pl.BlockSpec((tokens, width), lambda j, o: (0, at + j)),
                pl.BlockSpec((depth, width), lambda j, o: (0, at + j)),
            ],
            scratch_shapes=[pltpu.VMEM((2, depth, width), BF16), pltpu.SemaphoreType.DMA((2,))],
        ),
        out_shape=[jax.ShapeDtypeStruct((tokens, full), F32), jax.ShapeDtypeStruct((depth, full), BF16)],
        input_output_aliases={} if so_far is None else {6: 0, 7: 1},
        cost_estimate=pl.CostEstimate(
            flops=2 * tokens * depth * columns,
            bytes_accessed=4 * depth * columns + 4 * tokens * columns + 2 * tokens * depth,
            transcendentals=0,
        ),
        name="project",
    )(order, x, *pieces, *extra)


def gate_kernel(block, width, order_ref, x_ref, p0, p1, p2, p3, y_ref, gain_ref, mark_ref, *rest):
    gate_ref, w_ref, zg_ref, square_ref, buffer, sems = rest[-6:]
    slot = next_tile(order_ref, (p0, p1, p2, p3), buffer, sems, block, width)
    w = buffer[slot]
    w_ref[...] = w

    @pl.when(pl.program_id(0) == 0)
    def _():
        square_ref[...] = jnp.zeros_like(square_ref)

    for i in range(x_ref.shape[0] // SPAN):
        rows = slice(i * SPAN, (i + 1) * SPAN)
        gate = mm(x_ref[rows], w)
        gate_ref[rows] = gate.astype(BF16)
        gated = y_ref[rows].astype(F32) * (gate * jax.nn.sigmoid(gate))
        zg_ref[rows] = (gated * gain_ref[...]).astype(BF16)
        square = gated * gated
        total = square[:, :TILE]
        for k in range(1, width // TILE):
            total = total + square[:, k * TILE : (k + 1) * TILE]
        square_ref[rows] += total


def gate_project(x, pieces, order, y, gain, mark, so_far, start, full, width=512):
    tokens, depth = x.shape
    columns = pieces[0].shape[1]
    block = depth // BLOCKS
    at = start // width
    any_spec = pl.BlockSpec(memory_space=pl.ANY)
    extra = [] if so_far is None else list(so_far)
    wide = pl.BlockSpec((tokens, width), lambda j, o: (0, at + j))
    return pl.pallas_call(
        functools.partial(gate_kernel, block, width),
        grid_spec=pltpu.PrefetchScalarGridSpec(
            num_scalar_prefetch=1,
            grid=(columns // width,),
            in_specs=[pl.BlockSpec((tokens, depth), lambda j, o: (0, 0))]
            + [any_spec] * 4
            + [wide, pl.BlockSpec((1, width), lambda j, o: (0, at + j)), pl.BlockSpec((8, TILE), lambda j, o: (0, 0))]
            + [any_spec] * len(extra),
            out_specs=[
                wide,
                pl.BlockSpec((depth, width), lambda j, o: (0, at + j)),
                wide,
                pl.BlockSpec((tokens, TILE), lambda j, o: (0, 0)),
            ],
            scratch_shapes=[pltpu.VMEM((2, depth, width), BF16), pltpu.SemaphoreType.DMA((2,))],
        ),
        out_shape=[
            jax.ShapeDtypeStruct((tokens, full), BF16),
            jax.ShapeDtypeStruct((depth, full), BF16),
            jax.ShapeDtypeStruct((tokens, full), BF16),
            jax.ShapeDtypeStruct((tokens, TILE), F32),
        ],
        input_output_aliases={} if so_far is None else {9: 0, 10: 1, 11: 2},
        cost_estimate=pl.CostEstimate(
            flops=2 * tokens * depth * columns,
            bytes_accessed=4 * depth * columns + 10 * tokens * columns + 2 * tokens * depth,
            transcendentals=tokens * columns,
        ),
        name="project_gate",
    )(order, x, *pieces, y, gain, mark, *extra)


def restore_kernel(block, width, order_ref, p0, p1, p2, p3, *rest):
    w_ref, buffer, sems = rest[-3:]
    slot = next_tile(order_ref, (p0, p1, p2, p3), buffer, sems, block, width)
    w_ref[...] = buffer[slot]


def restore(pieces, order, so_far, start, full, width=256):
    columns = pieces[0].shape[1]
    block = pieces[0].shape[0] // 8
    depth = block * BLOCKS
    at = start // width
    any_spec = pl.BlockSpec(memory_space=pl.ANY)
    extra = [] if so_far is None else [so_far]
    return pl.pallas_call(
        functools.partial(restore_kernel, block, width),
        grid_spec=pltpu.PrefetchScalarGridSpec(
            num_scalar_prefetch=1,
            grid=(columns // width,),
            in_specs=[any_spec] * (4 + len(extra)),
            out_specs=pl.BlockSpec((depth, width), lambda j, o: (0, at + j)),
            scratch_shapes=[pltpu.VMEM((2, depth, width), BF16), pltpu.SemaphoreType.DMA((2,))],
        ),
        out_shape=jax.ShapeDtypeStruct((depth, full), BF16),
        input_output_aliases={} if so_far is None else {5: 0},
        cost_estimate=pl.CostEstimate(flops=0, bytes_accessed=4 * depth * columns, transcendentals=0),
        name="restore",
    )(order, *pieces, *extra)


def output_kernel(block, width, order_ref, zg_ref, inverse_ref, tokens_ref, cot_ref, p0, p1, p2, p3, w_ref, out_ref, dots_ref, buffer, sems):
    slot = next_tile(order_ref, (p0, p1, p2, p3), buffer, sems, block, width)
    w = buffer[slot]
    w_ref[...] = w

    @pl.when(pl.program_id(0) == 0)
    def _():
        dots_ref[...] = jnp.zeros_like(dots_ref)

    for i in range(zg_ref.shape[0] // SPAN):
        rows = slice(i * SPAN, (i + 1) * SPAN)
        projected = inverse_ref[rows] * mm(zg_ref[rows], w)
        out_ref[rows] = (tokens_ref[rows].astype(F32) + projected).astype(BF16)
        dots_ref[rows] += jnp.sum(cot_ref[rows].astype(F32) * projected, axis=1, keepdims=True)


def output_project(zg, inverse, tokens, cot, pieces, order, width=512):
    count, depth = zg.shape
    model = tokens.shape[1]
    block = depth // BLOCKS
    any_spec = pl.BlockSpec(memory_space=pl.ANY)
    whole = lambda i, o: (0, 0)
    part = pl.BlockSpec((count, width), lambda i, o: (0, i))
    return pl.pallas_call(
        functools.partial(output_kernel, block, width),
        grid_spec=pltpu.PrefetchScalarGridSpec(
            num_scalar_prefetch=1,
            grid=(model // width,),
            in_specs=[pl.BlockSpec((count, depth), whole), pl.BlockSpec((count, 1), whole), part, part]
            + [any_spec] * 4,
            out_specs=[
                pl.BlockSpec((depth, width), lambda i, o: (0, i)),
                part,
                pl.BlockSpec((count, 1), whole),
            ],
            scratch_shapes=[pltpu.VMEM((2, depth, width), BF16), pltpu.SemaphoreType.DMA((2,))],
        ),
        out_shape=[
            jax.ShapeDtypeStruct((depth, model), BF16),
            jax.ShapeDtypeStruct((count, model), BF16),
            jax.ShapeDtypeStruct((count, 1), F32),
        ],
        cost_estimate=pl.CostEstimate(
            flops=2 * count * depth * model,
            bytes_accessed=4 * depth * model + 2 * count * (depth + 3 * model),
            transcendentals=0,
        ),
        name="project_out",
    )(order, zg, inverse, tokens, cot, *pieces)


def gate_back_kernel(cot_ref, w_ref, gate_ref, y_ref, gain_ref, inverse_ref, less_ref, dy_ref, dgate_ref):
    w = w_ref[...]
    for i in range(cot_ref.shape[0] // SPAN):
        rows = slice(i * SPAN, (i + 1) * SPAN)
        gate = gate_ref[rows].astype(F32)
        y = y_ref[rows].astype(F32)
        part = jax.nn.sigmoid(gate)
        opened = gate * part
        dz = inverse_ref[rows] * (gain_ref[...] * mm_nt(cot_ref[rows], w)) - (y * opened) * less_ref[rows]
        dy_ref[rows] = (dz * opened).astype(BF16)
        dgate_ref[rows] = (dz * y * (part + opened * (1.0 - part))).astype(BF16)


def gate_back(cot, w, gate, y, gain, inverse, less, width=512):
    count, model = cot.shape
    di = w.shape[0]
    part = pl.BlockSpec((count, width), lambda i: (0, i))
    column = pl.BlockSpec((count, 1), lambda i: (0, 0))
    shape = jax.ShapeDtypeStruct((count, di), BF16)
    return pl.pallas_call(
        gate_back_kernel,
        grid_spec=pltpu.PrefetchScalarGridSpec(
            num_scalar_prefetch=0,
            grid=(di // width,),
            in_specs=[
                pl.BlockSpec((count, model), lambda i: (0, 0)),
                pl.BlockSpec((width, model), lambda i: (i, 0)),
                part,
                part,
                pl.BlockSpec((1, width), lambda i: (0, i)),
                column,
                column,
            ],
            out_specs=[part, part],
        ),
        out_shape=[shape, shape],
        cost_estimate=pl.CostEstimate(
            flops=2 * count * di * model, bytes_accessed=2 * (di * model + 4 * count * di), transcendentals=count * di
        ),
        name="gate_back",
    )(cot, w, gate, y, gain, inverse, less)


def weight_grad_kernel(block, place_ref, lhs_ref, rhs_ref, mine, other, buffer, sems):
    step = pl.program_id(0)
    slot = lax.rem(step, 2)

    def settle(which):
        pltpu.make_async_copy(buffer.at[which], buffer.at[which], sems.at[which]).wait()

    @pl.when(step >= 2)
    def _():
        settle(slot)

    buffer[slot] = dot_f32(lhs_ref[...], rhs_ref[...], ((0,), (0,))).astype(BF16)
    for t in range(8):
        q = place_ref[step * 8 + t]
        source = buffer.at[slot, pl.ds(t * block, block), :]

        @pl.when(q < 16)
        def _():
            pltpu.make_async_copy(
                source, mine.at[pl.ds(pl.multiple_of(q * block, block), block), :], sems.at[slot]
            ).start()

        @pl.when(q >= 16)
        def _():
            pltpu.make_async_copy(
                source, other.at[pl.ds(pl.multiple_of((q - 16) * block, block), block), :], sems.at[slot]
            ).start()

    @pl.when(step == pl.num_programs(0) - 1)
    def _():
        settle(1 - slot)
        settle(slot)


def weight_grad(lhs, rhs, place, column, columns):
    tokens, rows = lhs.shape
    block = rows // BLOCKS
    any_spec = pl.BlockSpec(memory_space=pl.ANY)
    out = jax.ShapeDtypeStruct((16 * block, columns), BF16)
    return pl.pallas_call(
        functools.partial(weight_grad_kernel, block),
        grid_spec=pltpu.PrefetchScalarGridSpec(
            num_scalar_prefetch=1,
            grid=(4,),
            in_specs=[
                pl.BlockSpec((tokens, 8 * block), lambda i, o: (0, i)),
                pl.BlockSpec((tokens, columns), lambda i, o: (0, column)),
            ],
            out_specs=[any_spec, any_spec],
            scratch_shapes=[pltpu.VMEM((2, 8 * block, columns), BF16), pltpu.SemaphoreType.DMA((2,))],
        ),
        out_shape=[out, out],
        cost_estimate=pl.CostEstimate(
            flops=2 * tokens * rows * columns,
            bytes_accessed=2 * (tokens * rows + tokens * columns + rows * columns),
            transcendentals=0,
        ),
        name="weight_grad",
    )(place, lhs, rhs)


def rows_of(packed, start, count):
    return packed[:, start : start + count]


def on_device(
    hypercube,
    tokens,
    seg_ids,
    gain_in,
    w_in,
    conv_weight,
    conv_bias,
    dt_bias,
    a_log,
    d_skip,
    gain_out,
    w_out,
    cotangent,
):
    shards = lax.psum(1, "shard")
    taps, conv_local = conv_weight.shape
    model = tokens.shape[1]
    di = gain_out.shape[0] * shards
    conv_dim = conv_local * shards
    calls = ((0, 1), (1, 2), (3, 3))
    width = GROUP * P_SIZE

    def columns(w, call):
        start, count = call
        own = w[:, di + start * width : di + (start + count) * width]
        if start > 0:
            return own
        head = w[:, 2 * di :]
        return jnp.concatenate([jnp.pad(head, ((0, 0), (0, 4 * N - head.shape[1]))), own], axis=1)

    small = jnp.concatenate([conv_weight.reshape(-1), conv_bias, gain_in, gain_out])
    if hypercube:
        core = lax.axis_index("rep")
        w_half = lax.dynamic_slice_in_dim(w_in, core * (w_in.shape[0] // 2), w_in.shape[0] // 2, 0)
        o_half = lax.dynamic_slice_in_dim(w_out, core * (w_out.shape[0] // 2), w_out.shape[0] // 2, 0)
        near, middle, far = [Gather(columns(w_half, call)) for call in calls]
        gate_gather, out_gather = Gather(w_half[:, :di]), Gather(o_half)
        small_flow = gather_small(small)
        next(small_flow)
        got = []
        for starts in ((near,), (near, middle), (near, middle, far), (near, middle, far)):
            pairs = [each.step(*got) for each in starts] + [small_flow.send(got)]
            got = [pair[1] for pair in pairs]
            if len(starts) == 1:
                later = (far.held, gate_gather.held, out_gather.held), (tokens, seg_ids, dt_bias, a_log, d_skip, core)
                helds, (tokens, seg_ids, dt_bias, a_log, d_skip, core) = after(later, *got)
                far.held, gate_gather.held, out_gather.held = helds
        small_all = small_flow.send(got)
        order, place = block_order(core)
        sent, got = zip(
            middle.step(*got), far.step(*got), near.swap(*got), near.swap(*got), gate_gather.step(*got)
        )
        normed_tie = sent
        conv_tie = sent
        last_pair = got[0], got[1], got[4]
    else:
        small_all = lax.all_gather(small, "shard", axis=0, tiled=False)
        full_w_in = lax.all_gather(w_in, "shard", axis=0, tiled=True)
        full_w_out = lax.all_gather(w_out, "shard", axis=0, tiled=True)
    cut = taps * conv_local
    small_conv = after(small_all, *conv_tie) if hypercube else small_all
    conv_w = small_conv[:, :cut].reshape(shards, taps, conv_local).transpose(1, 0, 2).reshape(taps, -1)
    conv_b = rows_of(small_conv, cut, conv_local).reshape(1, -1)
    cut += conv_local
    full_gain_in = rows_of(small_all, cut, gain_in.shape[0]).reshape(1, -1).astype(F32)
    full_gain_out = rows_of(small_conv, cut + gain_in.shape[0], gain_out.shape[0]).reshape(1, -1).astype(F32)
    conv_all = jnp.concatenate(
        [conv_w.astype(F32), conv_b.astype(F32), jnp.zeros((3, conv_dim), F32)], axis=0
    )
    conv_x, conv_bc = conv_all[:, :di], conv_all[:, di:]
    inputs = tokens.astype(F32)
    rscale = lax.rsqrt(jnp.mean(inputs * inputs, axis=1, keepdims=True) + EPSILON)
    unit = inputs * rscale
    normed = (unit * full_gain_in).astype(BF16)
    same, seg_col, seg_row = seg_facts(seg_ids[0])
    if hypercube:
        normed, same = after((normed, same), *normed_tie)
    heads = head_rows(dt_bias, a_log)
    skip = jnp.repeat(d_skip, P_SIZE)[None]

    pcs, w_parts = [], []
    shared = written = mark = None
    project_tie = ()
    for index, call in enumerate(calls):
        if hypercube:
            pieces = (near, middle, far)[index].pieces()
            pc, w_part = project(after(normed, *project_tie), pieces, order, None, 0, pieces[0].shape[1])
            if index == 0:
                done = last_pair[0], last_pair[2], pc
                sent, got = zip(
                    middle.swap(*done), middle.swap(*done), gate_gather.step(*done), out_gather.step(*done)
                )
                pc = after(pc, *sent)
            if index == 1:
                sent, _ = far.swap(pc)
                pc = after(pc, sent)
        else:
            w_part = columns(full_w_in, call)
            pc = mm(normed, w_part)
        pcs.append((pc, 1 if index == 0 else 0))
        w_parts.append(w_part)
        written = run_forward(
            pc, pcs[-1][1], pcs[0][0], conv_x, conv_bc, same, seg_col, seg_row, heads, skip, *call, shared, written
        )
        mark = written[4]
        if index == 0:
            bcv, bc_slope, cum, shifted, cum_lines, shifted_lines, weight_lines = written[5:]
            shared = bcv, cum, shifted_lines, weight_lines
        written = written[:5]
        if hypercube and index == 0:
            done = last_pair[1], got[2], got[3], mark
            sent, got = zip(far.step(*done), gate_gather.step(*done), out_gather.step(*done))
            project_tie = sent
        if hypercube and index == 1:
            far.swap(got[0], mark)
            done = got[1], got[2], mark
            sent, got = zip(gate_gather.step(*done), gate_gather.swap(*done), out_gather.step(*done))
            project_tie = sent
    if hypercube:
        done = got[0], got[1], got[2], mark
        sent, got = zip(gate_gather.swap(*done), out_gather.step(*done), out_gather.swap(*done))
        gate_tie = sent
    x, y, states, slope, mark = written
    if hypercube:
        gate, w_gate, zg, squares = gate_project(
            after(normed, *gate_tie), gate_gather.pieces(), order, y, full_gain_out, mark, None, 0, di
        )
    else:
        w_gate = full_w_in[:, :di]
        gate = mm(normed, w_gate)
        gated = y.astype(F32) * (gate * jax.nn.sigmoid(gate))
        squares = gated * gated
        zg = (gated * full_gain_out).astype(BF16)
    inverse = lax.rsqrt(jnp.sum(squares, axis=1, keepdims=True) / di + EPSILON)
    cot = cotangent.astype(F32)
    cot_scaled = (inverse * cot).astype(BF16)
    sums = None
    parts = {}
    if hypercube:
        in_block = w_in.shape[0] // 2
        out_tie, out_got = out_gather.swap(cot_scaled)
        out_grad = weight_grad(zg, after(cot_scaled, out_tie), place, 0, model)
        out_sum = Scatter(out_grad, w_out.shape[0] // 2)
        sent, got = out_sum.step(*out_gather.swapped)
        full_w_out, output, dots = output_project(
            after(zg, sent), inverse, tokens, cotangent, out_gather.pieces(), order
        )
        sent, got = out_sum.step(got, dots)
        less = inverse * inverse * dots / di
        dy, dgate = gate_back(
            after(cotangent, sent), full_w_out, gate, y, full_gain_out, inverse, less
        )
    else:
        projected = inverse * mm(zg, full_w_out)
        output = (inputs + projected).astype(BF16)
        dots = jnp.sum(cot * projected, axis=1, keepdims=True)
        grad_ynorm = mm_nt(cotangent, full_w_out)
        y, gate = y.astype(F32), gate.astype(F32)
        sig = jax.nn.sigmoid(gate)
        dz = inverse * (full_gain_out * grad_ynorm) - (y * (gate * sig)) * (inverse * inverse * dots / di)
        dy = (dz * (gate * sig)).astype(BF16)
        dgate = (dz * y * (sig * (1.0 + gate * (1.0 - sig)))).astype(BF16)
    if hypercube:
        gate_grad = weight_grad(normed, after(dgate, got), place, 0, di)
        gate_sum = Scatter(gate_grad, in_block)
        sent, gate_got = gate_sum.step()
        scaled = mm_nt(after(dgate, sent), w_gate)
        sent, got = zip(out_sum.step(got, scaled), gate_sum.step(gate_got, scaled))
        dy = after(dy, *sent, gate_got, scaled)
    else:
        scaled = mm_nt(dgate, w_gate)
    grad_sums = {}
    for index, call in reversed(list(enumerate(calls))):
        pc, first_x = pcs[index]
        dpart, dcw, dskip, *sums = run_backward(
            dy, x, bcv, states, slope, bc_slope, pc, first_x, pcs[0][0], conv_x, conv_bc,
            same, seg_col, seg_row, heads, skip, (cum, shifted, cum_lines), *call, index == 0, sums,
        )
        parts[index] = (dpart, dcw, dskip)
        if not hypercube:
            scaled = scaled + mm_nt(dpart, w_parts[index])
            continue
        done = *got, dpart
        if index == 2:
            sent, out_got = out_sum.step(*done)
            early = (sent, *done)
        elif index == 1:
            sent, gate_got = gate_sum.step(*done)
            early = (sent, *done)
        else:
            sent, late = grad_sums[1].step(*got)
            early = (sent, *got)
        grad = weight_grad(normed, after(dpart, *early), place, 0, dpart.shape[1])
        grad_sums[index] = Scatter(grad, in_block)
        swap_sent, swap_got = grad_sums[index].step()
        if index == 2:
            scaled = scaled + mm_nt(after(dpart, swap_sent), w_parts[index])
            done = swap_got, scaled
            sent, got = zip(out_sum.step(out_got, *done), gate_sum.step(got[1], *done), grad_sums[2].step(*done))
            dy = after(dy, *sent, *done)
        elif index == 1:
            sent, got = zip(gate_sum.step(gate_got, swap_sent), grad_sums[2].step(got[2], swap_sent))
            got = got + (swap_got,)
            dy = after(dy, *sent, swap_sent)
        else:
            sent, late = zip(grad_sums[1].step(late, swap_sent), grad_sums[2].step(swap_sent))
            sent, got = grad_sums[0].step(swap_got, *sent)
            scaled = scaled + mm_nt(after(dpart, sent), w_parts[index])
    dbcw, dhead = after(tuple(sums), swap_sent) if hypercube else sums
    dbcw, dhead = after(tuple(sums), swap_sent) if hypercube else sums
    dcw = jnp.concatenate([parts[index][1] for index in range(len(calls))] + [dbcw], axis=2)
    dskip = jnp.concatenate([parts[index][2] for index in range(len(calls))], axis=1)
    if hypercube:
        ties = [swap_sent, sent]
        sent, got = grad_sums[0].step(got, scaled)
        ties.append(sent)
        sent, late = zip(grad_sums[1].step(*late, sent), grad_sums[2].step(*late, sent))
        late = late[0]
        scaled = scaled + mm_nt(after(parts[1][0], *sent), w_parts[1])
    scaled = scaled * full_gain_in
    inner = jnp.mean(unit * scaled, axis=1, keepdims=True)
    grad_tokens = (cot + rscale * (scaled - unit * inner)).astype(BF16)

    conv_sums = dcw.sum(1)
    conv_sums = jnp.concatenate([conv_sums[4:5], conv_sums[3:4], conv_sums[2:3], conv_sums[1:2], conv_sums[0:1]])
    per_head = jnp.concatenate(
        [
            dhead[0].sum(0)[:H],
            dhead[1].sum(0)[:H] * -jnp.exp(a_log),
            dskip.sum(0).reshape(H, P_SIZE).sum(1),
        ]
    )
    conv_part = conv_sums.reshape(taps + 1, shards, conv_local).transpose(1, 0, 2).reshape(shards, -1)
    small_grad = jnp.concatenate([conv_part, jnp.broadcast_to(per_head[None], (shards, 3 * H))], axis=1)
    real = w_in.shape[1] - 2 * di
    if hypercube:
        last_sent, got = grad_sums[0].step(got, grad_tokens)
        ties.append(last_sent)
        grad_sums[1].step(late, last_sent)
        end_sent, _ = grad_sums[0].step(got)
        ties.append(end_sent)
        small_sum = reduce_small(small_grad, ties)[0]
        whole = [each.finish(end_sent) for each in (gate_sum, grad_sums[2], grad_sums[1])]
        whole = [both_cores(part) for part in whole + [grad_sums[0].finish()]]
        head = whole.pop()
        whole = [whole[0], head[:, 4 * N :], whole[2], whole[1], head[:, :real]]
        sum_w_in = jnp.concatenate(whole, axis=1)
        edges = [0, di, di + width, di + 3 * width, 2 * di, w_in.shape[1]]
        gain_sum = 0.0
        for part, a, b in zip(whole, edges, edges[1:]):
            gain_sum = gain_sum + jnp.sum(part * w_in[:, a:b].astype(F32), axis=1)
        sum_w_out = both_cores(out_sum.finish())
    else:
        grad_w_out = dot_f32(zg, cot_scaled, ((0,), (0,)))
        rest = [parts[index][0] for index in range(len(calls))]
        grads = jnp.concatenate([dgate, rest[0][:, 4 * N :], *rest[1:], rest[0][:, :real]], axis=1)
        grad_w_in = dot_f32(normed, grads, ((0,), (0,)))
        small_sum = lax.psum(
            lax.psum_scatter(small_grad, "shard", scatter_dimension=0, tiled=True), "rep"
        )[0]
        sum_w_in = lax.psum_scatter(grad_w_in, "shard", scatter_dimension=0, tiled=True)
        sum_w_out = lax.psum_scatter(grad_w_out, "shard", scatter_dimension=0, tiled=True)
        sum_w_in, sum_w_out = lax.psum((sum_w_in, sum_w_out), "rep")
        gain_sum = jnp.sum(sum_w_in * w_in.astype(F32), axis=1)
    grad_gain_in = gain_sum / gain_in.astype(F32)
    grad_gain_out = jnp.sum(sum_w_out * w_out.astype(F32), axis=1) / gain_out.astype(F32)
    cut = taps * conv_local
    head_at = cut + conv_local
    return (
        output,
        grad_tokens,
        grad_gain_in,
        sum_w_in,
        small_sum[:cut].reshape(taps, conv_local),
        small_sum[cut:head_at],
        small_sum[head_at : head_at + H],
        small_sum[head_at + H : head_at + 2 * H],
        small_sum[head_at + 2 * H :],
        grad_gain_out,
        sum_w_out,
    )


def both_cores(own):
    partner = swap_cores(own)
    first = lax.axis_index("rep") == 0
    return jnp.concatenate([jnp.where(first, own, partner), jnp.where(first, partner, own)], axis=0)


def reduce_small(rows, ties):
    core = lax.axis_index("rep")
    places = jnp.asarray([reach(order) for order in ORDERS], jnp.int32)[core] ^ lax.axis_index("shard")
    hot = (places[:, None] == jnp.arange(16, dtype=jnp.int32)[None, :]).astype(F32)
    total = dot_f32(hot, rows, ((1,), (0,)), HIGHEST)
    for stage, tie in zip((3, 2, 1, 0), ties[:4]):
        cut = 1 << stage
        total = after(total, tie)
        total = total[:cut] + exchange(total[cut:], stage)
    total = after(total, ties[4])
    return total + swap_cores(total)


def solution(mesh):
    rows = P(("shard", "rep"), None)
    in_specs = (
        rows, rows, P("shard"), P("shard", None), P(None, "shard"), P("shard"), P(), P(), P(), P("shard"),
        P("shard", None), rows,
    )
    out_specs = (
        rows, rows, P("shard"), P("shard", None), P(None, "shard"), P("shard"), P(), P(), P(), P("shard"),
        P("shard", None),
    )
    hypercube = mesh.shape["shard"] == 16 and mesh.shape["rep"] == 2
    return jax.shard_map(
        functools.partial(on_device, hypercube),
        mesh=mesh,
        in_specs=in_specs,
        out_specs=out_specs,
        check_vma=False,
    )
```

```python
import functools

import jax
import jax.numpy as jnp
from jax import lax
from jax.experimental import pallas as pl
from jax.experimental.pallas import tpu as pltpu
from jax.sharding import PartitionSpec as P
from jax.sharding import PartitionSpec as P

H = 48
P_SIZE = 64
N = 128
SPAN = 256
HALF = 128
GROUP = 8
TILE = 128
EPSILON = 1e-05
HIGHEST = lax.Precision.HIGHEST
LOG2E = 1.4426950408889634
NEG = -1e30
F32 = jnp.float32
BF16 = jnp.bfloat16


def dot_f32(a, b, contract, precision=None):
    return lax.dot_general(
        a, b, ((contract[0], contract[1]), ((), ())), preferred_element_type=F32, precision=precision
    )


def mm(a, b):
    return dot_f32(a, b, ((1,), (0,)))


def mm_nt(a, b):
    return dot_f32(a, b, ((1,), (1,)))


def lanes_of(column, rows):
    return jnp.broadcast_to(column, (rows, TILE))


def step_sizes(raw, heads):
    shifted = raw + heads[0:1]
    return jnp.maximum(shifted, 0.0) + jnp.log1p(jnp.exp(-jnp.abs(shifted)))


def conv_taps(ext, same, start, width, rows=SPAN):
    out = [ext[8 : 8 + rows, start : start + width]]
    for offset in (1, 2, 3):
        moved = ext[8 - offset : 8 - offset + rows, start : start + width]
        mask = same[offset - 1]
        if width > TILE:
            mask = jnp.concatenate([mask] * (width // TILE), axis=1)
        out.append(moved * mask)
    return out


def conv_sum(taps, weights):
    total = weights[4:5] + weights[3:4] * taps[0]
    for offset in (1, 2, 3):
        total = total + weights[3 - offset : 4 - offset] * taps[offset]
    return total


def prepare(raw_ref, heads_ref):
    heads = heads_ref[...]
    step = step_sizes(raw_ref[...], heads)
    row = lax.broadcasted_iota(jnp.int32, (SPAN, SPAN), 0)
    col = lax.broadcasted_iota(jnp.int32, (SPAN, SPAN), 1)
    tri = (row >= col).astype(F32)
    cum = dot_f32(tri, step * heads[1:2], ((1,), (0,)), HIGHEST)
    return cum, cum - jnp.log2(step)


def pick(first, columns, at):
    return jnp.where(first, lanes_of(columns[:, at : at + 1], first.shape[0]), lanes_of(columns[:, at + 1 : at + 2], first.shape[0]))


def forward_kernel(first_call, base, pc_ref, halo_ref, cw_ref, same, seg_col_ref, seg_ref, skip_ref, *rest):
    rest = list(rest)
    if first_call:
        raw_ref, heads_ref, bc_ref, bc_halo_ref, bcw_ref = [rest.pop(0) for _ in range(5)]
        x_out, y_out, st_out, slope_out, mark, bc_out, bc_slope_out = [rest.pop(0) for _ in range(7)]
        pack, shifted_out, cum_out, cum_rows, w_rows = [rest.pop(0) for _ in range(5)]
    else:
        bc_out, pack, cum_rows, w_rows = [rest.pop(0) for _ in range(4)]
        mark_ref = rest[4]
        rest = rest[5:]
        x_out, y_out, st_out, slope_out, mark = [rest.pop(0) for _ in range(5)]
    state, scores, block, keep_row, b_t, ext, ext_bc = rest
    span = pl.program_id(0)
    group = pl.program_id(1)
    group_head = base + GROUP * group

    @pl.when((span == 0) & (group == 0))
    def _():
        state[...] = jnp.zeros_like(state)
        mark[...] = jnp.zeros_like(mark) if first_call else mark_ref[...]

    @pl.when(group == 0)
    def _():
        if first_call:
            cum, shifted = prepare(raw_ref, heads_ref)
            pack[...] = cum
            shifted_out[...] = shifted
            cum_out[...] = cum.T
            cum_rows[...] = shifted.T
            w_rows[...] = (jnp.exp2(cum[SPAN - 1 : SPAN] - shifted) * same[4]).T
        last = pack[SPAN - 1 : SPAN]
        keep_row[...] = jnp.broadcast_to(jnp.exp2(last) * same[3, SPAN - 1 : SPAN], (8, TILE))
        if first_call:
            ext_bc[0:8] = bc_halo_ref[...]
            ext_bc[8:] = bc_ref[...]
            total = conv_sum(conv_taps(ext_bc, same, 0, 2 * N), bcw_ref[...])
            gate = jax.nn.sigmoid(total)
            both = total * gate
            bc_out[...] = both.astype(BF16)
            bc_slope_out[...] = (gate + both * (1.0 - gate)).astype(BF16)
        row = lax.broadcasted_iota(jnp.int32, (SPAN, SPAN), 0)
        col = lax.broadcasted_iota(jnp.int32, (SPAN, SPAN), 1)
        linked = (row >= col) & (seg_col_ref[...] == seg_ref[...])
        block[...] = jnp.where(linked, 0.0, NEG)
        scores[...] = mm_nt(bc_out[:, N:], bc_out[:, :N])
        b_t[...] = bc_out[:, :N].astype(F32).T

    ext[0:8] = halo_ref[...]
    ext[8:] = pc_ref[...]
    shift = lax.rem(TILE - group_head, TILE)
    cums = pltpu.roll(pack[...], shift, 1)
    keep = jnp.broadcast_to(pltpu.roll(keep_row[...], shift, 1)[0:1], (N, TILE))
    first = lax.broadcasted_iota(jnp.int32, (SPAN, TILE), 1) < P_SIZE
    query = bc_out[:, N:]
    empty = jnp.zeros((HALF, HALF), BF16)
    wide = lambda parts: jnp.concatenate(parts, axis=1)
    for quad in range(GROUP // 4):
        xbs, outs, entries, keeps, fresh = [], [], [], [], []
        for pair in (2 * quad, 2 * quad + 1):
            at = pair * TILE
            total = conv_sum(conv_taps(ext, same, at, TILE), cw_ref[:, at : at + TILE])
            gate = jax.nn.sigmoid(total)
            x = total * gate
            xb = x.astype(BF16)
            x_out[:, at : at + TILE] = xb
            slope_out[:, at : at + TILE] = (gate + x * (1.0 - gate)).astype(BF16)
            mixes, weighted, cum_cols = [], [], []
            for head in (2 * pair, 2 * pair + 1):
                cum_col = lanes_of(cums[:, head : head + 1], SPAN)
                cum_cols.append(cum_col)
                cum_row = cum_rows[pl.ds(group_head + head, 1), :]
                blocks = []
                for i, j in ((0, 0), (1, 0), (1, 1)):
                    rows = slice(i * HALF, (i + 1) * HALF)
                    cols = slice(j * HALF, (j + 1) * HALF)
                    gap = cum_col[rows] - cum_row[:, cols] + block[rows, cols]
                    blocks.append((jnp.exp2(gap) * scores[rows, cols]).astype(BF16))
                mixes.append(wide([blocks[0], empty]))
                mixes.append(wide(blocks[1:]))
                weighted.append((b_t[...] * w_rows[pl.ds(group_head + head, 1), :]).astype(BF16))
            inner = mm(jnp.concatenate(mixes + weighted, axis=0), xb)
            outs.append(jnp.where(first, inner[:SPAN], inner[SPAN : 2 * SPAN]))
            fresh.append(jnp.where(first[:N], inner[2 * SPAN : 2 * SPAN + N], inner[2 * SPAN + N :]))
            xbs.append(xb)
            entries.append(jnp.exp2(jnp.where(first, cum_cols[0], cum_cols[1])) * same[3])
            keeps.append(pick(first[:N], keep, 2 * pair))
        both = slice(quad * 2 * TILE, (quad + 1) * 2 * TILE)
        tile = pl.ds(pl.multiple_of(group * GROUP * P_SIZE + quad * 2 * TILE, 2 * TILE), 2 * TILE)
        old = state[:, tile]
        old_b = old.astype(BF16)
        st_out[:, both] = old_b
        carried = mm(query, old_b)
        y = wide(outs) + wide(entries) * carried + skip_ref[:, both] * wide(xbs).astype(F32)
        y_out[:, both] = y.astype(BF16)
        state[:, tile] = old * wide(keeps) + wide(fresh)


def run_forward(pc, first_x, pc_bc, conv_x, conv_bc, same, seg_col, seg_row, heads, skip, start, count, shared, before):
    tokens = pc.shape[0]
    spans = tokens // SPAN
    di = skip.shape[1]
    width = GROUP * P_SIZE
    own = count * width
    first_call = before is None
    any_spec = pl.BlockSpec(memory_space=pl.ANY)
    halo = lambda s: jnp.maximum(s * (SPAN // 8) - 1, 0)
    wide = pl.BlockSpec((SPAN, width), lambda s, g: (s, start + g))
    bcv_spec = pl.BlockSpec((SPAN, 2 * N), lambda s, g: (s, 0))
    in_specs = [
        pl.BlockSpec((SPAN, width), lambda s, g: (s, first_x + g)),
        pl.BlockSpec((8, width), lambda s, g: (halo(s), first_x + g)),
        pl.BlockSpec((8, width), lambda s, g: (0, start + g)),
        pl.BlockSpec((5, SPAN, TILE), lambda s, g: (0, s, 0)),
        pl.BlockSpec((SPAN, 1), lambda s, g: (s, 0)),
        pl.BlockSpec((1, SPAN), lambda s, g: (0, s)),
        pl.BlockSpec((1, width), lambda s, g: (0, start + g)),
    ]
    args = [pc, pc, conv_x, same, seg_col, seg_row, skip]
    column_spec = pl.BlockSpec((SPAN, TILE), lambda s, g: (s, 0))
    row_spec = pl.BlockSpec((TILE, SPAN), lambda s, g: (s, 0))
    columns_shape = jax.ShapeDtypeStruct((tokens, TILE), F32)
    rows_shape = jax.ShapeDtypeStruct((spans * TILE, SPAN), F32)
    mark_spec = pl.BlockSpec((8, TILE), lambda s, g: (0, 0))
    out_specs = [wide, wide, pl.BlockSpec((N, width), lambda s, g: (s, start + g)), wide, mark_spec]
    out_shape = [
        jax.ShapeDtypeStruct((tokens, di), BF16),
        jax.ShapeDtypeStruct((tokens, di), BF16),
        jax.ShapeDtypeStruct((spans * N, di), BF16),
        jax.ShapeDtypeStruct((tokens, di), BF16),
        jax.ShapeDtypeStruct((8, TILE), F32),
    ]
    if first_call:
        in_specs += [
            pl.BlockSpec((SPAN, TILE), lambda s, g: (s, 2)),
            pl.BlockSpec((8, TILE), lambda s, g: (0, 0)),
            pl.BlockSpec((SPAN, 2 * N), lambda s, g: (s, 0)),
            pl.BlockSpec((8, 2 * N), lambda s, g: (halo(s), 0)),
            pl.BlockSpec((8, 2 * N), lambda s, g: (0, 0)),
        ]
        args += [pc_bc, heads, pc_bc, pc_bc, conv_bc]
        out_specs += [bcv_spec, bcv_spec, column_spec, column_spec, row_spec, row_spec, row_spec]
        out_shape += [jax.ShapeDtypeStruct((tokens, 2 * N), BF16)] * 2
        out_shape += [columns_shape] * 2 + [rows_shape] * 3
        aliases = {}
    else:
        in_specs += [bcv_spec, column_spec, row_spec, row_spec, any_spec, any_spec, any_spec, any_spec, mark_spec]
        args += [*shared, *before]
        aliases = {11: 0, 12: 1, 13: 2, 14: 3}
    return pl.pallas_call(
        functools.partial(forward_kernel, first_call, start * GROUP),
        grid_spec=pltpu.PrefetchScalarGridSpec(
            num_scalar_prefetch=0,
            grid=(spans, count),
            in_specs=in_specs,
            out_specs=out_specs,
            scratch_shapes=[
                pltpu.VMEM((N, own), F32),
                pltpu.VMEM((SPAN, SPAN), F32),
                pltpu.VMEM((SPAN, SPAN), F32),
                pltpu.VMEM((8, TILE), F32),
                pltpu.VMEM((N, SPAN), F32),
                pltpu.VMEM((SPAN + 8, width), F32),
                pltpu.VMEM((SPAN + 8, 2 * N), F32),
            ],
        ),
        out_shape=out_shape,
        input_output_aliases=aliases,
        compiler_params=pltpu.CompilerParams(dimension_semantics=("arbitrary", "arbitrary")),
        cost_estimate=pl.CostEstimate(flops=int(5e9 * count), bytes_accessed=14 * tokens * own, transcendentals=0),
        name="scan_forward",
    )(*args)


def conv_back(grad, slope, signal, same, weights, carry):
    width = grad.shape[1]
    du = grad * slope.astype(F32)

    def add_rows(values):
        return jnp.sum(values.reshape(SPAN // 8, 8, width), axis=0)

    out = weights[3:4] * du
    sums = [add_rows(du), add_rows(du * signal)]
    for offset in (1, 2, 3):
        mask = same[offset - 1]
        if width > TILE:
            mask = jnp.concatenate([mask] * (width // TILE), axis=1)
        masked = du * mask
        moved = jnp.concatenate([masked, carry[offset - 1]], axis=0)[offset : offset + SPAN]
        carry[offset - 1] = masked[0:8]
        out = out + weights[3 - offset : 4 - offset] * moved
        sums.append(add_rows(moved * signal))
    return out, sums


def backward_kernel(
    first_call, last_call, base,
    dy_ref, x_ref, bcv_ref, st_ref, slope_ref, pc_ref, cw_ref, same, seg_col_ref, seg_ref, skip_ref,
    cum_ref, shifted_ref, cum_rows, *rest,
):
    rest = list(rest)
    before = None if first_call else [rest.pop(0) for _ in range(4)]
    if last_call:
        raw_ref, heads_ref, bc_ref, bc_slope_ref, bcw_ref = [rest.pop(0) for _ in range(5)]
    dproj_out, dcw_out, dskip_out = [rest.pop(0) for _ in range(3)]
    if last_call:
        dbcw_out, dhead_out = [rest.pop(0) for _ in range(2)]
    else:
        after_out = [rest.pop(0) for _ in range(4)]
    (
        dstate, scores, block, dscores, pack, c_t,
        carry, carry_bc, d_bc, per_row, dcum_rows, dlast,
    ) = rest
    back = pl.program_id(0)
    group = pl.program_id(1)
    groups = pl.num_programs(1)
    width = GROUP * P_SIZE
    group_head = base + GROUP * group
    first_x = 4 * N if last_call else 0

    @pl.when((back == 0) & (group == 0))
    def _():
        dstate[...] = jnp.zeros_like(dstate)
        carry[...] = jnp.zeros_like(carry)
        dcw_out[...] = jnp.zeros_like(dcw_out)
        dskip_out[...] = jnp.zeros_like(dskip_out)
        dcum_rows[...] = jnp.zeros_like(dcum_rows)
        if last_call:
            carry_bc[...] = jnp.zeros_like(carry_bc)
            dbcw_out[...] = jnp.zeros_like(dbcw_out)
            dhead_out[...] = jnp.zeros_like(dhead_out)

    keys = bcv_ref[:, :N]
    query = bcv_ref[:, N:]
    lane = lax.broadcasted_iota(jnp.int32, (SPAN, TILE), 1)

    @pl.when(group == 0)
    def _():
        entry = jnp.exp2(cum_ref[...]) * same[3]
        pack[...] = jnp.where(lane < 64, shifted_ref[...], pltpu.roll(entry, 64, 1))
        row = lax.broadcasted_iota(jnp.int32, (SPAN, SPAN), 0)
        col = lax.broadcasted_iota(jnp.int32, (SPAN, SPAN), 1)
        linked = (row <= col) & (seg_col_ref[...] == seg_ref[...])
        block[...] = jnp.where(linked, 0.0, NEG)
        scores[...] = mm_nt(keys, query)
        c_t[...] = query.T
        per_row[...] = jnp.zeros_like(per_row)
        if first_call:
            dscores[...] = jnp.zeros_like(dscores)
            d_bc[...] = jnp.zeros_like(d_bc)
            dlast[...] = jnp.zeros_like(dlast)
        else:
            dscores[...] = before[0][...]
            d_bc[...] = before[1][...]
            per_row[0] = before[2][:, :TILE]
            per_row[2] = before[2][:, TILE:]
            dlast[...] = before[3][...]

    shift = lax.rem(TILE - group_head, TILE)
    cols = pltpu.roll(pack[...], shift, 1)
    last_cum = pltpu.roll(jnp.broadcast_to(cum_ref[SPAN - 1 : SPAN], (8, TILE)), shift, 1)[0:1]
    keep_mask = same[3, SPAN - 1 : SPAN]
    first = lane < P_SIZE
    lane_row = lax.broadcasted_iota(jnp.int32, (2 * TILE, TILE), 0) // P_SIZE
    lane_col = lax.broadcasted_iota(jnp.int32, (2 * TILE, TILE), 1)
    sums = jnp.zeros((SPAN, TILE), F32)
    last_sum = jnp.zeros((1, TILE), F32)
    group_at = group * width
    empty = jnp.zeros((HALF, HALF), BF16)
    wide = lambda parts: jnp.concatenate(parts, axis=1)
    for quad in range(GROUP // 4):
        both = slice(quad * 2 * TILE, (quad + 1) * 2 * TILE)
        tile = pl.ds(pl.multiple_of(group_at + quad * 2 * TILE, 2 * TILE), 2 * TILE)
        entries, tails, keeps, inners = [], [], [], []
        for pair in (2 * quad, 2 * quad + 1):
            at = pair * TILE
            heads = (2 * pair, 2 * pair + 1)
            dy_pair = dy_ref[:, at : at + TILE]
            xb = x_ref[:, at : at + TILE]
            nothing = jnp.zeros_like(xb)
            split = jnp.concatenate([jnp.where(first, xb, nothing), jnp.where(first, nothing, xb)], axis=0)
            g_both = mm_nt(split, dy_pair)
            cum_cols = [lanes_of(cols[:, head : head + 1], SPAN) for head in heads]
            cum_lines = [cum_rows[pl.ds(group_head + head, 1), :] for head in heads]
            mixes = [[], []]
            across = [[], []]
            down = [[], []]
            for j, i in ((0, 0), (0, 1), (1, 1)):
                rows = slice(j * HALF, (j + 1) * HALF)
                cells = slice(i * HALF, (i + 1) * HALF)
                spread = jnp.zeros((HALF, HALF), F32)
                for which in (0, 1):
                    decay = jnp.exp2(cum_lines[which][:, cells] - cum_cols[which][rows] + block[rows, cells])
                    mix = decay * scores[rows, cells]
                    g = g_both[which * SPAN + j * HALF : which * SPAN + (j + 1) * HALF, cells]
                    spread = spread + decay * g
                    w = mix * g
                    mixes[which].append(mix.astype(BF16))
                    across[which].append(w)
                    down[which].append(jnp.sum(w, axis=0, keepdims=True))
                dscores[rows, cells] += spread
            lefts = []
            for which in (0, 1):
                row_sum = jnp.concatenate(
                    [
                        jnp.sum(across[which][0] + across[which][1], axis=1, keepdims=True),
                        jnp.sum(across[which][2], axis=1, keepdims=True),
                    ],
                    axis=0,
                )
                sums = sums - jnp.where(lane == 2 * GROUP + heads[which], row_sum, 0.0)
                dcum_rows[pl.ds(group_head + heads[which], 1), :] = wide(
                    [down[which][0], down[which][1] + down[which][2]]
                )
                lefts += [wide(mixes[which][:2]), wide([empty, mixes[which][2]])]
            inner = mm(jnp.concatenate(lefts, axis=0), dy_pair)
            inners.append(jnp.where(first, inner[:SPAN], inner[SPAN:]))
            last_pair = jnp.where(
                first[0:1],
                jnp.broadcast_to(last_cum[:, heads[0] : heads[0] + 1], (1, TILE)),
                jnp.broadcast_to(last_cum[:, heads[1] : heads[1] + 1], (1, TILE)),
            )
            tails.append(jnp.exp2(last_pair - jnp.where(first, cum_cols[0], cum_cols[1])) * same[4])
            keeps.append(jnp.exp2(last_pair) * keep_mask)
            entries.append(pick(first, cols, 64 + 2 * pair))
        dyf = dy_ref[:, both].astype(F32)
        xf = x_ref[:, both].astype(F32)
        tail = wide(tails)
        stb = st_ref[:, both]
        ds = dstate[:, tile]
        dsb = ds.astype(BF16)
        dye_f = dyf * wide(entries)
        dye = dye_f.astype(BF16)
        fresh = mm(keys, dsb) * tail
        total = wide(inners) + fresh
        d_bc[:, N:] += mm_nt(dye, stb)
        d_bc[:, :N] += mm_nt((xf * tail).astype(BF16), dsb)

        def head_sum(values, kind):
            spread = (lane_col == kind * GROUP + 4 * quad + lane_row).astype(BF16)
            return mm(values.astype(BF16), spread)

        sums = sums + head_sum(xf * total, 0) + head_sum(xf * fresh, 1) + head_sum(dye_f * mm(query, stb), 2)
        kept = ds * wide(keeps)
        kept_sum = jnp.sum(kept * stb.astype(F32), axis=0, keepdims=True)
        lane_pair = lax.broadcasted_iota(jnp.int32, (1, 2 * TILE), 1) // P_SIZE
        for head in range(4):
            one = jnp.sum(jnp.where(lane_pair == head, kept_sum, 0.0), axis=1, keepdims=True)
            last_sum = last_sum + jnp.where(lane[0:1] == 4 * quad + head, one, 0.0)
        dstate[:, tile] = kept + mm(c_t[...], dye)
        dskip_out[:, tile] += jnp.sum((dyf * xf).reshape(SPAN // 8, 8, 2 * TILE), axis=0)
        dx = total + skip_ref[:, both] * dyf
        for part in (0, 1):
            at = (2 * quad + part) * TILE
            one = pl.ds(pl.multiple_of(group_at + at, TILE), TILE)
            out, conv_sums = conv_back(
                dx[:, part * TILE : (part + 1) * TILE], slope_ref[:, at : at + TILE], pc_ref[:, at : at + TILE],
                same, cw_ref[:, at : at + TILE], carry.at[:, :, one],
            )
            dproj_out[:, pl.ds(pl.multiple_of(first_x + group_at + at, TILE), TILE)] = out.astype(BF16)
            for k, value in enumerate(conv_sums):
                dcw_out[k, :, one] += value

    in_place = (lane >= group_head) & (lane < group_head + GROUP)
    for kind in range(3):
        moved = pltpu.roll(sums, lax.rem(group_head + TILE - GROUP * kind, TILE), 1)
        per_row[kind] += jnp.where(in_place, moved, 0.0)
    moved = pltpu.roll(jnp.broadcast_to(last_sum, (8, TILE)), group_head, 1)
    dlast[...] += jnp.where(in_place[0:8], moved, 0.0)

    @pl.when(group == groups - 1)
    def _():
        state_part = per_row[1]
        dcum = dcum_rows[...].T + per_row[2] - state_part
        dlast_all = dlast[0:1] + jnp.sum(state_part, axis=0, keepdims=True)
        if not last_call:
            after_out[0][...] = dscores[...]
            after_out[1][...] = d_bc[...]
            after_out[2][:, :TILE] = per_row[0]
            after_out[2][:, TILE:] = dcum
            after_out[3][...] = jnp.broadcast_to(dlast_all, (8, TILE))
            return
        ds_b = dscores[...].astype(BF16)
        grad_b = d_bc[:, :N] + mm(ds_b, query)
        grad_c = d_bc[:, N:] + mm(dscores[...].T.astype(BF16), keys)
        out, conv_sums = conv_back(
            wide([grad_b, grad_c]), bc_slope_ref[...], bc_ref[...], same, bcw_ref[...], carry_bc
        )
        dproj_out[:, : 2 * N] = out.astype(BF16)
        for k, value in enumerate(conv_sums):
            dbcw_out[k] += value
        heads = heads_ref[...]
        shifted = raw_ref[...] + heads[0:1]
        step = step_sizes(raw_ref[...], heads)
        slope = jax.nn.sigmoid(shifted)
        row = lax.broadcasted_iota(jnp.int32, (SPAN, SPAN), 0)
        col = lax.broadcasted_iota(jnp.int32, (SPAN, SPAN), 1)
        tri = (row <= col).astype(F32)
        da = dot_f32(tri, dcum, ((1,), (0,)), HIGHEST) + dlast_all
        small = shifted < -16.0
        ratio = jnp.where(small, 1.0, slope / jnp.where(small, 1.0, step))
        live = lane < H
        draw = jnp.where(live, per_row[0] * ratio + da * heads[2:3] * slope, 0.0)
        dproj_out[:, 2 * N : 3 * N] = draw.astype(BF16)
        dproj_out[:, 3 * N : 4 * N] = jnp.zeros((SPAN, N), BF16)
        dhead_out[0] += jnp.sum(draw.reshape(SPAN // 8, 8, TILE), axis=0)
        dhead_out[1] += jnp.sum(jnp.where(live, da * step, 0.0).reshape(SPAN // 8, 8, TILE), axis=0)


def run_backward(
    dy, x, bcv, states, slope, bc_slope, pc, first_x, pc_bc, conv_x, conv_bc, same, seg_col, seg_row, heads, skip,
    cums, start, count, last, before,
):
    tokens, di = dy.shape
    spans = tokens // SPAN
    width = GROUP * P_SIZE
    turn = lambda s: spans - 1 - s
    own = count * width
    out_width = own + (4 * N if last else 0)
    sums_specs = [
        pl.BlockSpec((SPAN, SPAN), lambda s, g: (turn(s), 0)),
        pl.BlockSpec((SPAN, 2 * N), lambda s, g: (turn(s), 0)),
        pl.BlockSpec((SPAN, 2 * TILE), lambda s, g: (turn(s), 0)),
        pl.BlockSpec((8, TILE), lambda s, g: (turn(s), 0)),
    ]
    sums_shapes = [
        jax.ShapeDtypeStruct((tokens, SPAN), F32),
        jax.ShapeDtypeStruct((tokens, 2 * N), F32),
        jax.ShapeDtypeStruct((tokens, 2 * TILE), F32),
        jax.ShapeDtypeStruct((spans * 8, TILE), F32),
    ]
    out_specs = [
        pl.BlockSpec((SPAN, out_width), lambda s, g: (turn(s), 0)),
        pl.BlockSpec((5, 8, own), lambda s, g: (0, 0, 0)),
        pl.BlockSpec((8, own), lambda s, g: (0, 0)),
    ]
    out_shape = [
        jax.ShapeDtypeStruct((tokens, out_width), BF16),
        jax.ShapeDtypeStruct((5, 8, own), F32),
        jax.ShapeDtypeStruct((8, own), F32),
    ]
    wide = pl.BlockSpec((SPAN, width), lambda s, g: (turn(s), start + g))
    in_specs = [
        wide,
        wide,
        pl.BlockSpec((SPAN, 2 * N), lambda s, g: (turn(s), 0)),
        pl.BlockSpec((N, width), lambda s, g: (turn(s), start + g)),
        wide,
        pl.BlockSpec((SPAN, width), lambda s, g: (turn(s), first_x + g)),
        pl.BlockSpec((8, width), lambda s, g: (0, start + g)),
        pl.BlockSpec((5, SPAN, TILE), lambda s, g: (0, turn(s), 0)),
        pl.BlockSpec((SPAN, 1), lambda s, g: (turn(s), 0)),
        pl.BlockSpec((1, SPAN), lambda s, g: (0, turn(s))),
        pl.BlockSpec((1, width), lambda s, g: (0, start + g)),
        pl.BlockSpec((SPAN, TILE), lambda s, g: (turn(s), 0)),
        pl.BlockSpec((SPAN, TILE), lambda s, g: (turn(s), 0)),
        pl.BlockSpec((TILE, SPAN), lambda s, g: (turn(s), 0)),
    ]
    args = [dy, x, bcv, states, slope, pc, conv_x, same, seg_col, seg_row, skip, *cums]
    if before is not None:
        in_specs += sums_specs
        args += before
    if last:
        in_specs += [
            pl.BlockSpec((SPAN, TILE), lambda s, g: (turn(s), 2)),
            pl.BlockSpec((8, TILE), lambda s, g: (0, 0)),
            pl.BlockSpec((SPAN, 2 * N), lambda s, g: (turn(s), 0)),
            pl.BlockSpec((SPAN, 2 * N), lambda s, g: (turn(s), 0)),
            pl.BlockSpec((8, 2 * N), lambda s, g: (0, 0)),
        ]
        args += [pc_bc, heads, pc_bc, bc_slope, conv_bc]
        out_specs += [
            pl.BlockSpec((5, 8, 2 * N), lambda s, g: (0, 0, 0)),
            pl.BlockSpec((2, 8, TILE), lambda s, g: (0, 0, 0)),
        ]
        out_shape += [
            jax.ShapeDtypeStruct((5, 8, 2 * N), F32),
            jax.ShapeDtypeStruct((2, 8, TILE), F32),
        ]
    else:
        out_specs += sums_specs
        out_shape += sums_shapes
    return pl.pallas_call(
        functools.partial(backward_kernel, before is None, last, start * GROUP),
        grid_spec=pltpu.PrefetchScalarGridSpec(
            num_scalar_prefetch=0,
            grid=(spans, count),
            in_specs=in_specs,
            out_specs=out_specs,
            scratch_shapes=[
                pltpu.VMEM((N, own), F32),
                pltpu.VMEM((SPAN, SPAN), F32),
                pltpu.VMEM((SPAN, SPAN), F32),
                pltpu.VMEM((SPAN, SPAN), F32),
                pltpu.VMEM((SPAN, TILE), F32),
                pltpu.VMEM((N, SPAN), BF16),
                pltpu.VMEM((3, 8, own), F32),
                pltpu.VMEM((3, 8, 2 * N), F32),
                pltpu.VMEM((SPAN, 2 * N), F32),
                pltpu.VMEM((3, SPAN, TILE), F32),
                pltpu.VMEM((TILE, SPAN), F32),
                pltpu.VMEM((8, TILE), F32),
            ],
        ),
        out_shape=out_shape,
        compiler_params=pltpu.CompilerParams(dimension_semantics=("arbitrary", "arbitrary")),
        cost_estimate=pl.CostEstimate(
            flops=int(1.2e10 * count), bytes_accessed=12 * tokens * own, transcendentals=0
        ),
        name="scan_backward",
    )(*args)


def seg_facts(seg):
    length = seg.shape[0]
    cols = []
    for offset in (1, 2, 3):
        moved = jnp.concatenate([jnp.full((offset,), -1, jnp.int32), seg[:-offset]])
        cols.append((moved == seg).astype(F32))
    spans = length // SPAN
    ends = seg[SPAN - 1 :: SPAN]
    before = jnp.concatenate([seg[:1], ends[:-1]])
    cols.append((seg == jnp.repeat(before, SPAN)).astype(F32))
    cols.append((seg == jnp.repeat(ends, SPAN)).astype(F32))
    value = seg.astype(F32)
    same = jnp.broadcast_to(jnp.stack(cols, axis=0)[:, :, None], (5, length, TILE))
    return same, value[:, None], value[None, :]


def head_rows(dt_bias, a_log):
    rate = -jnp.exp(a_log)
    rows = jnp.stack([dt_bias, rate * LOG2E, rate] + [jnp.zeros_like(rate)] * 5, axis=0)
    return jnp.pad(rows, ((0, 0), (0, TILE - H)))


BLOCKS = 32
ORDERS = ((8, 1, 4, 2), (8, 2, 4, 1))


def reach(masks):
    out = [0]
    for mask in masks:
        out = out + [mask ^ place for place in out]
    return out


def exchange(values, stage):
    pairs = []
    for shard in range(16):
        for core in range(2):
            pairs.append((shard * 2 + core, (shard ^ ORDERS[core][stage]) * 2 + core))
    return lax.ppermute(values, ("shard", "rep"), pairs)


def swap_cores(values):
    return lax.ppermute(values, "rep", [(0, 1), (1, 0)])


def after(values, *others):
    return lax.optimization_barrier((values, *others))[0]


class Gather:
    def __init__(self, local):
        self.held = local
        self.seen = []
        self.swapped = []

    def step(self, *ahead):
        stage = len(self.seen)
        if stage > 0:
            self.held = jnp.concatenate([self.held, after(self.seen[-1], *ahead)], axis=0)
        elif ahead:
            self.held = after(self.held, *ahead)
        got = exchange(self.held, stage)
        self.seen.append(got)
        return self.held, got

    def swap(self, *ahead):
        send = after(self.held if not self.swapped else self.seen[3], *ahead)
        self.swapped.append(swap_cores(send))
        return send, self.swapped[-1]

    def pieces(self):
        return self.held, self.seen[3], *self.swapped


def gather_small(local):
    held = local[None]
    ahead = yield None
    for stage in range(4):
        send = after(held, *ahead)
        got = exchange(send, stage)
        ahead = yield send, got
        held = jnp.concatenate([send, got], axis=0)
    core = lax.axis_index("rep")
    places = jnp.asarray([reach(order) for order in ORDERS], jnp.int32)[core] ^ lax.axis_index("shard")
    hot = (places[None, :] == jnp.arange(16, dtype=jnp.int32)[:, None]).astype(local.dtype)
    yield dot_f32(hot, held, ((1,), (0,)), HIGHEST).astype(local.dtype)


class Scatter:
    def __init__(self, partial, block):
        mine, self.other = partial
        self.terms = [mine]
        self.block = block
        self.left = [3, 2, 1, 0]

    def rows(self, start, stop):
        total = self.terms[0][start:stop].astype(F32)
        for term in self.terms[1:]:
            total = total + term[start:stop].astype(F32)
        return total

    def step(self, *ahead):
        if len(self.terms) == 1:
            self.other = after(self.other, *ahead)
            self.terms.append(swap_cores(self.other))
            return self.other, self.terms[-1]
        if self.left:
            stage = self.left.pop(0)
            cut = self.block << stage
            self.terms[-1] = after(self.terms[-1], *ahead)
            send = self.rows(cut, 2 * cut).astype(BF16)
            self.terms.append(exchange(send, stage))
            return send, self.terms[-1]
        return self.terms[-1], self.terms[-1]

    def finish(self, *ahead):
        while self.left:
            self.step()
        if ahead:
            self.terms[-1] = after(self.terms[-1], *ahead)
        return self.rows(0, self.block)


def block_order(core):
    shard = lax.axis_index("shard")
    tables = jnp.asarray([reach(order) for order in ORDERS], jnp.int32)
    inverse = jnp.asarray(
        [[reach(order).index(mask) for mask in range(16)] for order in ORDERS], jnp.int32
    )
    own = 2 * (tables[core] ^ shard) + core
    partner = 2 * (tables[1 - core] ^ shard) + (1 - core)
    order = jnp.concatenate([own, partner])
    natural = jnp.arange(BLOCKS, dtype=jnp.int32)
    which = natural % 2
    place = inverse[which, (natural // 2) ^ shard] + 16 * (which != core).astype(jnp.int32)
    return order, place


def fetch_tile(order_ref, pieces, buffer, sems, tile, slot, block, width):
    for q in range(BLOCKS):
        pltpu.make_async_copy(
            pieces[q // 8].at[pl.ds((q % 8) * block, block), pl.ds(pl.multiple_of(tile * width, width), width)],
            buffer.at[slot, pl.ds(pl.multiple_of(order_ref[q] * block, block), block), :],
            sems.at[slot],
        ).start()


def next_tile(order_ref, pieces, buffer, sems, block, width):
    tile = pl.program_id(0)
    slot = lax.rem(tile, 2)

    @pl.when(tile == 0)
    def _():
        fetch_tile(order_ref, pieces, buffer, sems, tile, slot, block, width)

    @pl.when(tile + 1 < pl.num_programs(0))
    def _():
        fetch_tile(order_ref, pieces, buffer, sems, tile + 1, 1 - slot, block, width)

    pltpu.make_async_copy(buffer.at[slot], buffer.at[slot], sems.at[slot]).wait()
    return slot


def project_kernel(block, width, order_ref, x_ref, p0, p1, p2, p3, *rest):
    out_ref, w_ref, buffer, sems = rest[-4:]
    slot = next_tile(order_ref, (p0, p1, p2, p3), buffer, sems, block, width)
    w = buffer[slot]
    w_ref[...] = w
    for i in range(x_ref.shape[0] // SPAN):
        rows = slice(i * SPAN, (i + 1) * SPAN)
        out_ref[rows] = mm(x_ref[rows], w)


def project(x, pieces, order, so_far, start, full, width=512):
    tokens, depth = x.shape
    columns = pieces[0].shape[1]
    block = depth // BLOCKS
    at = start // width
    any_spec = pl.BlockSpec(memory_space=pl.ANY)
    extra = [] if so_far is None else list(so_far)
    return pl.pallas_call(
        functools.partial(project_kernel, block, width),
        grid_spec=pltpu.PrefetchScalarGridSpec(
            num_scalar_prefetch=1,
            grid=(columns // width,),
            in_specs=[pl.BlockSpec((tokens, depth), lambda j, o: (0, 0))] + [any_spec] * (4 + len(extra)),
            out_specs=[
                pl.BlockSpec((tokens, width), lambda j, o: (0, at + j)),
                pl.BlockSpec((depth, width), lambda j, o: (0, at + j)),
            ],
            scratch_shapes=[pltpu.VMEM((2, depth, width), BF16), pltpu.SemaphoreType.DMA((2,))],
        ),
        out_shape=[jax.ShapeDtypeStruct((tokens, full), F32), jax.ShapeDtypeStruct((depth, full), BF16)],
        input_output_aliases={} if so_far is None else {6: 0, 7: 1},
        cost_estimate=pl.CostEstimate(
            flops=2 * tokens * depth * columns,
            bytes_accessed=4 * depth * columns + 4 * tokens * columns + 2 * tokens * depth,
            transcendentals=0,
        ),
        name="project",
    )(order, x, *pieces, *extra)


def gate_kernel(block, width, order_ref, x_ref, p0, p1, p2, p3, y_ref, gain_ref, mark_ref, *rest):
    gate_ref, w_ref, zg_ref, square_ref, buffer, sems = rest[-6:]
    slot = next_tile(order_ref, (p0, p1, p2, p3), buffer, sems, block, width)
    w = buffer[slot]
    w_ref[...] = w

    @pl.when(pl.program_id(0) == 0)
    def _():
        square_ref[...] = jnp.zeros_like(square_ref)

    for i in range(x_ref.shape[0] // SPAN):
        rows = slice(i * SPAN, (i + 1) * SPAN)
        gate = mm(x_ref[rows], w)
        gate_ref[rows] = gate.astype(BF16)
        gated = y_ref[rows].astype(F32) * (gate * jax.nn.sigmoid(gate))
        zg_ref[rows] = (gated * gain_ref[...]).astype(BF16)
        square = gated * gated
        total = square[:, :TILE]
        for k in range(1, width // TILE):
            total = total + square[:, k * TILE : (k + 1) * TILE]
        square_ref[rows] += total


def gate_project(x, pieces, order, y, gain, mark, so_far, start, full, width=512):
    tokens, depth = x.shape
    columns = pieces[0].shape[1]
    block = depth // BLOCKS
    at = start // width
    any_spec = pl.BlockSpec(memory_space=pl.ANY)
    extra = [] if so_far is None else list(so_far)
    wide = pl.BlockSpec((tokens, width), lambda j, o: (0, at + j))
    return pl.pallas_call(
        functools.partial(gate_kernel, block, width),
        grid_spec=pltpu.PrefetchScalarGridSpec(
            num_scalar_prefetch=1,
            grid=(columns // width,),
            in_specs=[pl.BlockSpec((tokens, depth), lambda j, o: (0, 0))]
            + [any_spec] * 4
            + [wide, pl.BlockSpec((1, width), lambda j, o: (0, at + j)), pl.BlockSpec((8, TILE), lambda j, o: (0, 0))]
            + [any_spec] * len(extra),
            out_specs=[
                wide,
                pl.BlockSpec((depth, width), lambda j, o: (0, at + j)),
                wide,
                pl.BlockSpec((tokens, TILE), lambda j, o: (0, 0)),
            ],
            scratch_shapes=[pltpu.VMEM((2, depth, width), BF16), pltpu.SemaphoreType.DMA((2,))],
        ),
        out_shape=[
            jax.ShapeDtypeStruct((tokens, full), BF16),
            jax.ShapeDtypeStruct((depth, full), BF16),
            jax.ShapeDtypeStruct((tokens, full), BF16),
            jax.ShapeDtypeStruct((tokens, TILE), F32),
        ],
        input_output_aliases={} if so_far is None else {9: 0, 10: 1, 11: 2},
        cost_estimate=pl.CostEstimate(
            flops=2 * tokens * depth * columns,
            bytes_accessed=4 * depth * columns + 10 * tokens * columns + 2 * tokens * depth,
            transcendentals=tokens * columns,
        ),
        name="project_gate",
    )(order, x, *pieces, y, gain, mark, *extra)


def restore_kernel(block, width, order_ref, p0, p1, p2, p3, *rest):
    w_ref, buffer, sems = rest[-3:]
    slot = next_tile(order_ref, (p0, p1, p2, p3), buffer, sems, block, width)
    w_ref[...] = buffer[slot]


def restore(pieces, order, so_far, start, full, width=256):
    columns = pieces[0].shape[1]
    block = pieces[0].shape[0] // 8
    depth = block * BLOCKS
    at = start // width
    any_spec = pl.BlockSpec(memory_space=pl.ANY)
    extra = [] if so_far is None else [so_far]
    return pl.pallas_call(
        functools.partial(restore_kernel, block, width),
        grid_spec=pltpu.PrefetchScalarGridSpec(
            num_scalar_prefetch=1,
            grid=(columns // width,),
            in_specs=[any_spec] * (4 + len(extra)),
            out_specs=pl.BlockSpec((depth, width), lambda j, o: (0, at + j)),
            scratch_shapes=[pltpu.VMEM((2, depth, width), BF16), pltpu.SemaphoreType.DMA((2,))],
        ),
        out_shape=jax.ShapeDtypeStruct((depth, full), BF16),
        input_output_aliases={} if so_far is None else {5: 0},
        cost_estimate=pl.CostEstimate(flops=0, bytes_accessed=4 * depth * columns, transcendentals=0),
        name="restore",
    )(order, *pieces, *extra)


def output_kernel(block, width, order_ref, zg_ref, inverse_ref, tokens_ref, cot_ref, p0, p1, p2, p3, w_ref, out_ref, dots_ref, buffer, sems):
    slot = next_tile(order_ref, (p0, p1, p2, p3), buffer, sems, block, width)
    w = buffer[slot]
    w_ref[...] = w

    @pl.when(pl.program_id(0) == 0)
    def _():
        dots_ref[...] = jnp.zeros_like(dots_ref)

    for i in range(zg_ref.shape[0] // SPAN):
        rows = slice(i * SPAN, (i + 1) * SPAN)
        projected = inverse_ref[rows] * mm(zg_ref[rows], w)
        out_ref[rows] = (tokens_ref[rows].astype(F32) + projected).astype(BF16)
        dots_ref[rows] += jnp.sum(cot_ref[rows].astype(F32) * projected, axis=1, keepdims=True)


def output_project(zg, inverse, tokens, cot, pieces, order, width=512):
    count, depth = zg.shape
    model = tokens.shape[1]
    block = depth // BLOCKS
    any_spec = pl.BlockSpec(memory_space=pl.ANY)
    whole = lambda i, o: (0, 0)
    part = pl.BlockSpec((count, width), lambda i, o: (0, i))
    return pl.pallas_call(
        functools.partial(output_kernel, block, width),
        grid_spec=pltpu.PrefetchScalarGridSpec(
            num_scalar_prefetch=1,
            grid=(model // width,),
            in_specs=[pl.BlockSpec((count, depth), whole), pl.BlockSpec((count, 1), whole), part, part]
            + [any_spec] * 4,
            out_specs=[
                pl.BlockSpec((depth, width), lambda i, o: (0, i)),
                part,
                pl.BlockSpec((count, 1), whole),
            ],
            scratch_shapes=[pltpu.VMEM((2, depth, width), BF16), pltpu.SemaphoreType.DMA((2,))],
        ),
        out_shape=[
            jax.ShapeDtypeStruct((depth, model), BF16),
            jax.ShapeDtypeStruct((count, model), BF16),
            jax.ShapeDtypeStruct((count, 1), F32),
        ],
        cost_estimate=pl.CostEstimate(
            flops=2 * count * depth * model,
            bytes_accessed=4 * depth * model + 2 * count * (depth + 3 * model),
            transcendentals=0,
        ),
        name="project_out",
    )(order, zg, inverse, tokens, cot, *pieces)


def gate_back_kernel(cot_ref, w_ref, gate_ref, y_ref, gain_ref, inverse_ref, less_ref, dy_ref, dgate_ref):
    w = w_ref[...]
    for i in range(cot_ref.shape[0] // SPAN):
        rows = slice(i * SPAN, (i + 1) * SPAN)
        gate = gate_ref[rows].astype(F32)
        y = y_ref[rows].astype(F32)
        part = jax.nn.sigmoid(gate)
        opened = gate * part
        dz = inverse_ref[rows] * (gain_ref[...] * mm_nt(cot_ref[rows], w)) - (y * opened) * less_ref[rows]
        dy_ref[rows] = (dz * opened).astype(BF16)
        dgate_ref[rows] = (dz * y * (part + opened * (1.0 - part))).astype(BF16)


def gate_back(cot, w, gate, y, gain, inverse, less, width=512):
    count, model = cot.shape
    di = w.shape[0]
    part = pl.BlockSpec((count, width), lambda i: (0, i))
    column = pl.BlockSpec((count, 1), lambda i: (0, 0))
    shape = jax.ShapeDtypeStruct((count, di), BF16)
    return pl.pallas_call(
        gate_back_kernel,
        grid_spec=pltpu.PrefetchScalarGridSpec(
            num_scalar_prefetch=0,
            grid=(di // width,),
            in_specs=[
                pl.BlockSpec((count, model), lambda i: (0, 0)),
                pl.BlockSpec((width, model), lambda i: (i, 0)),
                part,
                part,
                pl.BlockSpec((1, width), lambda i: (0, i)),
                column,
                column,
            ],
            out_specs=[part, part],
        ),
        out_shape=[shape, shape],
        cost_estimate=pl.CostEstimate(
            flops=2 * count * di * model, bytes_accessed=2 * (di * model + 4 * count * di), transcendentals=count * di
        ),
        name="gate_back",
    )(cot, w, gate, y, gain, inverse, less)


def weight_grad_kernel(block, place_ref, lhs_ref, rhs_ref, mine, other, buffer, sems):
    step = pl.program_id(0)
    slot = lax.rem(step, 2)

    def settle(which):
        pltpu.make_async_copy(buffer.at[which], buffer.at[which], sems.at[which]).wait()

    @pl.when(step >= 2)
    def _():
        settle(slot)

    buffer[slot] = dot_f32(lhs_ref[...], rhs_ref[...], ((0,), (0,))).astype(BF16)
    for t in range(8):
        q = place_ref[step * 8 + t]
        source = buffer.at[slot, pl.ds(t * block, block), :]

        @pl.when(q < 16)
        def _():
            pltpu.make_async_copy(
                source, mine.at[pl.ds(pl.multiple_of(q * block, block), block), :], sems.at[slot]
            ).start()

        @pl.when(q >= 16)
        def _():
            pltpu.make_async_copy(
                source, other.at[pl.ds(pl.multiple_of((q - 16) * block, block), block), :], sems.at[slot]
            ).start()

    @pl.when(step == pl.num_programs(0) - 1)
    def _():
        settle(1 - slot)
        settle(slot)


def weight_grad(lhs, rhs, place, column, columns):
    tokens, rows = lhs.shape
    block = rows // BLOCKS
    any_spec = pl.BlockSpec(memory_space=pl.ANY)
    out = jax.ShapeDtypeStruct((16 * block, columns), BF16)
    return pl.pallas_call(
        functools.partial(weight_grad_kernel, block),
        grid_spec=pltpu.PrefetchScalarGridSpec(
            num_scalar_prefetch=1,
            grid=(4,),
            in_specs=[
                pl.BlockSpec((tokens, 8 * block), lambda i, o: (0, i)),
                pl.BlockSpec((tokens, columns), lambda i, o: (0, column)),
            ],
            out_specs=[any_spec, any_spec],
            scratch_shapes=[pltpu.VMEM((2, 8 * block, columns), BF16), pltpu.SemaphoreType.DMA((2,))],
        ),
        out_shape=[out, out],
        cost_estimate=pl.CostEstimate(
            flops=2 * tokens * rows * columns,
            bytes_accessed=2 * (tokens * rows + tokens * columns + rows * columns),
            transcendentals=0,
        ),
        name="weight_grad",
    )(place, lhs, rhs)


def rows_of(packed, start, count):
    return packed[:, start : start + count]


def on_device(
    hypercube,
    tokens,
    seg_ids,
    gain_in,
    w_in,
    conv_weight,
    conv_bias,
    dt_bias,
    a_log,
    d_skip,
    gain_out,
    w_out,
    cotangent,
):
    shards = lax.psum(1, "shard")
    taps, conv_local = conv_weight.shape
    model = tokens.shape[1]
    di = gain_out.shape[0] * shards
    conv_dim = conv_local * shards
    calls = ((0, 1), (1, 2), (3, 3))
    width = GROUP * P_SIZE

    def columns(w, call):
        start, count = call
        own = w[:, di + start * width : di + (start + count) * width]
        if start > 0:
            return own
        head = w[:, 2 * di :]
        return jnp.concatenate([jnp.pad(head, ((0, 0), (0, 4 * N - head.shape[1]))), own], axis=1)

    small = jnp.concatenate([conv_weight.reshape(-1), conv_bias, gain_in, gain_out])
    if hypercube:
        core = lax.axis_index("rep")
        w_half = lax.dynamic_slice_in_dim(w_in, core * (w_in.shape[0] // 2), w_in.shape[0] // 2, 0)
        o_half = lax.dynamic_slice_in_dim(w_out, core * (w_out.shape[0] // 2), w_out.shape[0] // 2, 0)
        near, middle, far = [Gather(columns(w_half, call)) for call in calls]
        gate_gather, out_gather = Gather(w_half[:, :di]), Gather(o_half)
        small_flow = gather_small(small)
        next(small_flow)
        got = []
        for starts in ((near,), (near, middle), (near, middle, far), (near, middle, far)):
            pairs = [near.step(*got)]
            ahead = [*got, pairs[0][0]]
            pairs += [each.step(*ahead) for each in starts[1:]] + [small_flow.send(ahead)]
            got = [pair[1] for pair in pairs]
            if len(starts) == 1:
                later = (far.held, gate_gather.held, out_gather.held), (tokens, seg_ids, dt_bias, a_log, d_skip, core)
                helds, (tokens, seg_ids, dt_bias, a_log, d_skip, core) = after(later, *got)
                far.held, gate_gather.held, out_gather.held = helds
        small_all = small_flow.send(got)
        order, place = block_order(core)
        swaps = [near.swap(near.seen[3]), near.swap()]
        got = [*got[1:], swaps[1][0]]
        sent, got = zip(middle.step(*got), far.step(*got), *swaps, gate_gather.step(*got))
        normed_tie = sent
        conv_tie = sent
        last_pair = got[0], got[1], got[4]
    else:
        small_all = lax.all_gather(small, "shard", axis=0, tiled=False)
        full_w_in = lax.all_gather(w_in, "shard", axis=0, tiled=True)
        full_w_out = lax.all_gather(w_out, "shard", axis=0, tiled=True)
    cut = taps * conv_local
    small_conv = after(small_all, *conv_tie) if hypercube else small_all
    conv_w = small_conv[:, :cut].reshape(shards, taps, conv_local).transpose(1, 0, 2).reshape(taps, -1)
    conv_b = rows_of(small_conv, cut, conv_local).reshape(1, -1)
    cut += conv_local
    full_gain_in = rows_of(small_all, cut, gain_in.shape[0]).reshape(1, -1).astype(F32)
    full_gain_out = rows_of(small_conv, cut + gain_in.shape[0], gain_out.shape[0]).reshape(1, -1).astype(F32)
    conv_all = jnp.concatenate(
        [conv_w.astype(F32), conv_b.astype(F32), jnp.zeros((3, conv_dim), F32)], axis=0
    )
    conv_x, conv_bc = conv_all[:, :di], conv_all[:, di:]
    inputs = tokens.astype(F32)
    rscale = lax.rsqrt(jnp.mean(inputs * inputs, axis=1, keepdims=True) + EPSILON)
    unit = inputs * rscale
    normed = (unit * full_gain_in).astype(BF16)
    same, seg_col, seg_row = seg_facts(seg_ids[0])
    if hypercube:
        normed, same = after((normed, same), *normed_tie)
    heads = head_rows(dt_bias, a_log)
    skip = jnp.repeat(d_skip, P_SIZE)[None]

    pcs, w_parts = [], []
    shared = written = mark = None
    project_tie = ()
    for index, call in enumerate(calls):
        if hypercube:
            pieces = (near, middle, far)[index].pieces()
            pc, w_part = project(after(normed, *project_tie), pieces, order, None, 0, pieces[0].shape[1])
            if index == 0:
                done = last_pair[0], last_pair[2], pc
                sent, got = zip(
                    middle.swap(*done), middle.swap(*done), gate_gather.step(*done), out_gather.step(*done)
                )
                pc = after(pc, *sent)
            if index == 1:
                sent, _ = far.swap(pc)
                pc = after(pc, sent)
        else:
            w_part = columns(full_w_in, call)
            pc = mm(normed, w_part)
        pcs.append((pc, 1 if index == 0 else 0))
        w_parts.append(w_part)
        written = run_forward(
            pc, pcs[-1][1], pcs[0][0], conv_x, conv_bc, same, seg_col, seg_row, heads, skip, *call, shared, written
        )
        mark = written[4]
        if index == 0:
            bcv, bc_slope, cum, shifted, cum_lines, shifted_lines, weight_lines = written[5:]
            shared = bcv, cum, shifted_lines, weight_lines
        written = written[:5]
        if hypercube and index == 0:
            done = last_pair[1], got[2], got[3], mark
            sent, got = zip(far.step(*done), gate_gather.step(*done), out_gather.step(*done))
            project_tie = sent
        if hypercube and index == 1:
            far.swap(got[0], mark)
            done = got[1], got[2], mark
            sent, got = zip(gate_gather.step(*done), gate_gather.swap(*done), out_gather.step(*done))
            project_tie = sent
    if hypercube:
        done = got[0], got[1], got[2], mark
        sent, got = zip(gate_gather.swap(*done), out_gather.step(*done), out_gather.swap(*done))
        gate_tie = sent
    x, y, states, slope, mark = written
    if hypercube:
        gate, w_gate, zg, squares = gate_project(
            after(normed, *gate_tie), gate_gather.pieces(), order, y, full_gain_out, mark, None, 0, di
        )
    else:
        w_gate = full_w_in[:, :di]
        gate = mm(normed, w_gate)
        gated = y.astype(F32) * (gate * jax.nn.sigmoid(gate))
        squares = gated * gated
        zg = (gated * full_gain_out).astype(BF16)
    inverse = lax.rsqrt(jnp.sum(squares, axis=1, keepdims=True) / di + EPSILON)
    cot = cotangent.astype(F32)
    cot_scaled = (inverse * cot).astype(BF16)
    sums = None
    parts = {}
    if hypercube:
        in_block = w_in.shape[0] // 2
        out_tie, out_got = out_gather.swap(cot_scaled)
        out_grad = weight_grad(zg, after(cot_scaled, out_tie), place, 0, model)
        out_sum = Scatter(out_grad, w_out.shape[0] // 2)
        sent, got = out_sum.step(*out_gather.swapped)
        full_w_out, output, dots = output_project(
            after(zg, sent), inverse, tokens, cotangent, out_gather.pieces(), order
        )
        sent, got = out_sum.step(got, dots)
        less = inverse * inverse * dots / di
        dy, dgate = gate_back(
            after(cotangent, sent), full_w_out, gate, y, full_gain_out, inverse, less
        )
    else:
        projected = inverse * mm(zg, full_w_out)
        output = (inputs + projected).astype(BF16)
        dots = jnp.sum(cot * projected, axis=1, keepdims=True)
        grad_ynorm = mm_nt(cotangent, full_w_out)
        y, gate = y.astype(F32), gate.astype(F32)
        sig = jax.nn.sigmoid(gate)
        dz = inverse * (full_gain_out * grad_ynorm) - (y * (gate * sig)) * (inverse * inverse * dots / di)
        dy = (dz * (gate * sig)).astype(BF16)
        dgate = (dz * y * (sig * (1.0 + gate * (1.0 - sig)))).astype(BF16)
    if hypercube:
        gate_grad = weight_grad(normed, after(dgate, got), place, 0, di)
        gate_sum = Scatter(gate_grad, in_block)
        sent, gate_got = gate_sum.step()
        scaled = mm_nt(after(dgate, sent), w_gate)
        sent, got = zip(out_sum.step(got, scaled), gate_sum.step(gate_got, scaled))
        dy = after(dy, *sent, gate_got, scaled)
    else:
        scaled = mm_nt(dgate, w_gate)
    grad_sums = {}
    for index, call in reversed(list(enumerate(calls))):
        pc, first_x = pcs[index]
        dpart, dcw, dskip, *sums = run_backward(
            dy, x, bcv, states, slope, bc_slope, pc, first_x, pcs[0][0], conv_x, conv_bc,
            same, seg_col, seg_row, heads, skip, (cum, shifted, cum_lines), *call, index == 0, sums,
        )
        parts[index] = (dpart, dcw, dskip)
        if not hypercube:
            scaled = scaled + mm_nt(dpart, w_parts[index])
            continue
        done = *got, dpart
        if index == 2:
            sent, out_got = out_sum.step(*done)
            early = (sent, *done)
        elif index == 1:
            sent, gate_got = gate_sum.step(*done)
            early = (sent, *done)
        else:
            sent, late = grad_sums[1].step(*got)
            early = (sent, *got)
        grad = weight_grad(normed, after(dpart, *early), place, 0, dpart.shape[1])
        grad_sums[index] = Scatter(grad, in_block)
        swap_sent, swap_got = grad_sums[index].step()
        if index == 2:
            scaled = scaled + mm_nt(after(dpart, swap_sent), w_parts[index])
            done = swap_got, scaled
            sent, got = zip(out_sum.step(out_got, *done), gate_sum.step(got[1], *done), grad_sums[2].step(*done))
            dy = after(dy, *sent, *done)
        elif index == 1:
            sent, got = zip(gate_sum.step(gate_got, swap_sent), grad_sums[2].step(got[2], swap_sent))
            got = got + (swap_got,)
            dy = after(dy, *sent, swap_sent)
        else:
            sent, late = zip(grad_sums[1].step(late, swap_sent), grad_sums[2].step(swap_sent))
            sent, got = grad_sums[0].step(swap_got, *sent)
            scaled = scaled + mm_nt(after(dpart, sent), w_parts[index])
    dbcw, dhead = after(tuple(sums), swap_sent) if hypercube else sums
    dbcw, dhead = after(tuple(sums), swap_sent) if hypercube else sums
    dcw = jnp.concatenate([parts[index][1] for index in range(len(calls))] + [dbcw], axis=2)
    dskip = jnp.concatenate([parts[index][2] for index in range(len(calls))], axis=1)
    if hypercube:
        ties = [swap_sent, sent]
        sent, got = grad_sums[0].step(got, scaled)
        ties.append(sent)
        sent, late = zip(grad_sums[1].step(*late, sent), grad_sums[2].step(*late, sent))
        late = late[0]
        scaled = scaled + mm_nt(after(parts[1][0], *sent), w_parts[1])
    scaled = scaled * full_gain_in
    inner = jnp.mean(unit * scaled, axis=1, keepdims=True)
    grad_tokens = (cot + rscale * (scaled - unit * inner)).astype(BF16)

    conv_sums = dcw.sum(1)
    conv_sums = jnp.concatenate([conv_sums[4:5], conv_sums[3:4], conv_sums[2:3], conv_sums[1:2], conv_sums[0:1]])
    per_head = jnp.concatenate(
        [
            dhead[0].sum(0)[:H],
            dhead[1].sum(0)[:H] * -jnp.exp(a_log),
            dskip.sum(0).reshape(H, P_SIZE).sum(1),
        ]
    )
    conv_part = conv_sums.reshape(taps + 1, shards, conv_local).transpose(1, 0, 2).reshape(shards, -1)
    small_grad = jnp.concatenate([conv_part, jnp.broadcast_to(per_head[None], (shards, 3 * H))], axis=1)
    real = w_in.shape[1] - 2 * di
    if hypercube:
        last_sent, got = grad_sums[0].step(got, grad_tokens)
        ties.append(last_sent)
        grad_sums[1].step(late, last_sent)
        end_sent, _ = grad_sums[0].step(got)
        ties.append(end_sent)
        small_sum = reduce_small(small_grad, ties)[0]
        whole = [each.finish(end_sent) for each in (gate_sum, grad_sums[2], grad_sums[1])]
        whole = [both_cores(part) for part in whole + [grad_sums[0].finish()]]
        head = whole.pop()
        whole = [whole[0], head[:, 4 * N :], whole[2], whole[1], head[:, :real]]
        sum_w_in = jnp.concatenate(whole, axis=1)
        edges = [0, di, di + width, di + 3 * width, 2 * di, w_in.shape[1]]
        gain_sum = 0.0
        for part, a, b in zip(whole, edges, edges[1:]):
            gain_sum = gain_sum + jnp.sum(part * w_in[:, a:b].astype(F32), axis=1)
        sum_w_out = both_cores(out_sum.finish())
    else:
        grad_w_out = dot_f32(zg, cot_scaled, ((0,), (0,)))
        rest = [parts[index][0] for index in range(len(calls))]
        grads = jnp.concatenate([dgate, rest[0][:, 4 * N :], *rest[1:], rest[0][:, :real]], axis=1)
        grad_w_in = dot_f32(normed, grads, ((0,), (0,)))
        small_sum = lax.psum(
            lax.psum_scatter(small_grad, "shard", scatter_dimension=0, tiled=True), "rep"
        )[0]
        sum_w_in = lax.psum_scatter(grad_w_in, "shard", scatter_dimension=0, tiled=True)
        sum_w_out = lax.psum_scatter(grad_w_out, "shard", scatter_dimension=0, tiled=True)
        sum_w_in, sum_w_out = lax.psum((sum_w_in, sum_w_out), "rep")
        gain_sum = jnp.sum(sum_w_in * w_in.astype(F32), axis=1)
    grad_gain_in = gain_sum / gain_in.astype(F32)
    grad_gain_out = jnp.sum(sum_w_out * w_out.astype(F32), axis=1) / gain_out.astype(F32)
    cut = taps * conv_local
    head_at = cut + conv_local
    return (
        output,
        grad_tokens,
        grad_gain_in,
        sum_w_in,
        small_sum[:cut].reshape(taps, conv_local),
        small_sum[cut:head_at],
        small_sum[head_at : head_at + H],
        small_sum[head_at + H : head_at + 2 * H],
        small_sum[head_at + 2 * H :],
        grad_gain_out,
        sum_w_out,
    )


def both_cores(own):
    partner = swap_cores(own)
    first = lax.axis_index("rep") == 0
    return jnp.concatenate([jnp.where(first, own, partner), jnp.where(first, partner, own)], axis=0)


def reduce_small(rows, ties):
    core = lax.axis_index("rep")
    places = jnp.asarray([reach(order) for order in ORDERS], jnp.int32)[core] ^ lax.axis_index("shard")
    hot = (places[:, None] == jnp.arange(16, dtype=jnp.int32)[None, :]).astype(F32)
    total = dot_f32(hot, rows, ((1,), (0,)), HIGHEST)
    for stage, tie in zip((3, 2, 1, 0), ties[:4]):
        cut = 1 << stage
        total = after(total, tie)
        total = total[:cut] + exchange(total[cut:], stage)
    total = after(total, ties[4])
    return total + swap_cores(total)


def solution(mesh):
    rows = P(("shard", "rep"), None)
    in_specs = (
        rows, rows, P("shard"), P("shard", None), P(None, "shard"), P("shard"), P(), P(), P(), P("shard"),
        P("shard", None), rows,
    )
    out_specs = (
        rows, rows, P("shard"), P("shard", None), P(None, "shard"), P("shard"), P(), P(), P(), P("shard"),
        P("shard", None),
    )
    hypercube = mesh.shape["shard"] == 16 and mesh.shape["rep"] == 2
    return jax.shard_map(
        functools.partial(on_device, hypercube),
        mesh=mesh,
        in_specs=in_specs,
        out_specs=out_specs,
        check_vma=False,
    )
```

```python
import functools

import jax
import jax.numpy as jnp
from jax import lax
from jax.experimental import pallas as pl
from jax.experimental.pallas import tpu as pltpu
from jax.sharding import PartitionSpec as P
from jax.sharding import PartitionSpec as P

H = 48
P_SIZE = 64
N = 128
SPAN = 256
HALF = 128
GROUP = 8
TILE = 128
EPSILON = 1e-05
HIGHEST = lax.Precision.HIGHEST
LOG2E = 1.4426950408889634
NEG = -1e30
F32 = jnp.float32
BF16 = jnp.bfloat16


def dot_f32(a, b, contract, precision=None):
    return lax.dot_general(
        a, b, ((contract[0], contract[1]), ((), ())), preferred_element_type=F32, precision=precision
    )


def mm(a, b):
    return dot_f32(a, b, ((1,), (0,)))


def mm_nt(a, b):
    return dot_f32(a, b, ((1,), (1,)))


def lanes_of(column, rows):
    return jnp.broadcast_to(column, (rows, TILE))


def step_sizes(raw, heads):
    shifted = raw + heads[0:1]
    return jnp.maximum(shifted, 0.0) + jnp.log1p(jnp.exp(-jnp.abs(shifted)))


def conv_taps(ext, same, start, width, rows=SPAN):
    out = [ext[8 : 8 + rows, start : start + width]]
    for offset in (1, 2, 3):
        moved = ext[8 - offset : 8 - offset + rows, start : start + width]
        mask = same[offset - 1]
        if width > TILE:
            mask = jnp.concatenate([mask] * (width // TILE), axis=1)
        out.append(moved * mask)
    return out


def conv_sum(taps, weights):
    total = weights[4:5] + weights[3:4] * taps[0]
    for offset in (1, 2, 3):
        total = total + weights[3 - offset : 4 - offset] * taps[offset]
    return total


def prepare(raw_ref, heads_ref):
    heads = heads_ref[...]
    step = step_sizes(raw_ref[...], heads)
    row = lax.broadcasted_iota(jnp.int32, (SPAN, SPAN), 0)
    col = lax.broadcasted_iota(jnp.int32, (SPAN, SPAN), 1)
    tri = (row >= col).astype(F32)
    cum = dot_f32(tri, step * heads[1:2], ((1,), (0,)), HIGHEST)
    return cum, cum - jnp.log2(step)


def pick(first, columns, at):
    return jnp.where(first, lanes_of(columns[:, at : at + 1], first.shape[0]), lanes_of(columns[:, at + 1 : at + 2], first.shape[0]))


def forward_kernel(first_call, base, pc_ref, halo_ref, cw_ref, same, seg_col_ref, seg_ref, skip_ref, *rest):
    rest = list(rest)
    if first_call:
        raw_ref, heads_ref, bc_ref, bc_halo_ref, bcw_ref = [rest.pop(0) for _ in range(5)]
        x_out, y_out, st_out, slope_out, mark, bc_out, bc_slope_out = [rest.pop(0) for _ in range(7)]
        pack, shifted_out, cum_out, cum_rows, w_rows = [rest.pop(0) for _ in range(5)]
    else:
        bc_out, pack, cum_rows, w_rows = [rest.pop(0) for _ in range(4)]
        mark_ref = rest[4]
        rest = rest[5:]
        x_out, y_out, st_out, slope_out, mark = [rest.pop(0) for _ in range(5)]
    state, scores, block, keep_row, b_t, ext, ext_bc = rest
    span = pl.program_id(0)
    group = pl.program_id(1)
    group_head = base + GROUP * group

    @pl.when((span == 0) & (group == 0))
    def _():
        state[...] = jnp.zeros_like(state)
        mark[...] = jnp.zeros_like(mark) if first_call else mark_ref[...]

    @pl.when(group == 0)
    def _():
        if first_call:
            cum, shifted = prepare(raw_ref, heads_ref)
            pack[...] = cum
            shifted_out[...] = shifted
            cum_out[...] = cum.T
            cum_rows[...] = shifted.T
            w_rows[...] = (jnp.exp2(cum[SPAN - 1 : SPAN] - shifted) * same[4]).T
        last = pack[SPAN - 1 : SPAN]
        keep_row[...] = jnp.broadcast_to(jnp.exp2(last) * same[3, SPAN - 1 : SPAN], (8, TILE))
        if first_call:
            ext_bc[0:8] = bc_halo_ref[...]
            ext_bc[8:] = bc_ref[...]
            total = conv_sum(conv_taps(ext_bc, same, 0, 2 * N), bcw_ref[...])
            gate = jax.nn.sigmoid(total)
            both = total * gate
            bc_out[...] = both.astype(BF16)
            bc_slope_out[...] = (gate + both * (1.0 - gate)).astype(BF16)
        row = lax.broadcasted_iota(jnp.int32, (SPAN, SPAN), 0)
        col = lax.broadcasted_iota(jnp.int32, (SPAN, SPAN), 1)
        linked = (row >= col) & (seg_col_ref[...] == seg_ref[...])
        block[...] = jnp.where(linked, 0.0, NEG)
        scores[...] = mm_nt(bc_out[:, N:], bc_out[:, :N])
        b_t[...] = bc_out[:, :N].astype(F32).T

    ext[0:8] = halo_ref[...]
    ext[8:] = pc_ref[...]
    shift = lax.rem(TILE - group_head, TILE)
    cums = pltpu.roll(pack[...], shift, 1)
    keep = jnp.broadcast_to(pltpu.roll(keep_row[...], shift, 1)[0:1], (N, TILE))
    first = lax.broadcasted_iota(jnp.int32, (SPAN, TILE), 1) < P_SIZE
    query = bc_out[:, N:]
    empty = jnp.zeros((HALF, HALF), BF16)
    wide = lambda parts: jnp.concatenate(parts, axis=1)
    for quad in range(GROUP // 4):
        xbs, outs, entries, keeps, fresh = [], [], [], [], []
        for pair in (2 * quad, 2 * quad + 1):
            at = pair * TILE
            total = conv_sum(conv_taps(ext, same, at, TILE), cw_ref[:, at : at + TILE])
            gate = jax.nn.sigmoid(total)
            x = total * gate
            xb = x.astype(BF16)
            x_out[:, at : at + TILE] = xb
            slope_out[:, at : at + TILE] = (gate + x * (1.0 - gate)).astype(BF16)
            mixes, weighted, cum_cols = [], [], []
            for head in (2 * pair, 2 * pair + 1):
                cum_col = lanes_of(cums[:, head : head + 1], SPAN)
                cum_cols.append(cum_col)
                cum_row = cum_rows[pl.ds(group_head + head, 1), :]
                blocks = []
                for i, j in ((0, 0), (1, 0), (1, 1)):
                    rows = slice(i * HALF, (i + 1) * HALF)
                    cols = slice(j * HALF, (j + 1) * HALF)
                    gap = cum_col[rows] - cum_row[:, cols] + block[rows, cols]
                    blocks.append((jnp.exp2(gap) * scores[rows, cols]).astype(BF16))
                mixes.append(wide([blocks[0], empty]))
                mixes.append(wide(blocks[1:]))
                weighted.append((b_t[...] * w_rows[pl.ds(group_head + head, 1), :]).astype(BF16))
            inner = mm(jnp.concatenate(mixes + weighted, axis=0), xb)
            outs.append(jnp.where(first, inner[:SPAN], inner[SPAN : 2 * SPAN]))
            fresh.append(jnp.where(first[:N], inner[2 * SPAN : 2 * SPAN + N], inner[2 * SPAN + N :]))
            xbs.append(xb)
            entries.append(jnp.exp2(jnp.where(first, cum_cols[0], cum_cols[1])) * same[3])
            keeps.append(pick(first[:N], keep, 2 * pair))
        both = slice(quad * 2 * TILE, (quad + 1) * 2 * TILE)
        tile = pl.ds(pl.multiple_of(group * GROUP * P_SIZE + quad * 2 * TILE, 2 * TILE), 2 * TILE)
        old = state[:, tile]
        old_b = old.astype(BF16)
        st_out[:, both] = old_b
        carried = mm(query, old_b)
        y = wide(outs) + wide(entries) * carried + skip_ref[:, both] * wide(xbs).astype(F32)
        y_out[:, both] = y.astype(BF16)
        state[:, tile] = old * wide(keeps) + wide(fresh)


def run_forward(pc, first_x, pc_bc, conv_x, conv_bc, same, seg_col, seg_row, heads, skip, start, count, shared, before):
    tokens = pc.shape[0]
    spans = tokens // SPAN
    di = skip.shape[1]
    width = GROUP * P_SIZE
    own = count * width
    first_call = before is None
    any_spec = pl.BlockSpec(memory_space=pl.ANY)
    halo = lambda s: jnp.maximum(s * (SPAN // 8) - 1, 0)
    wide = pl.BlockSpec((SPAN, width), lambda s, g: (s, start + g))
    bcv_spec = pl.BlockSpec((SPAN, 2 * N), lambda s, g: (s, 0))
    in_specs = [
        pl.BlockSpec((SPAN, width), lambda s, g: (s, first_x + g)),
        pl.BlockSpec((8, width), lambda s, g: (halo(s), first_x + g)),
        pl.BlockSpec((8, width), lambda s, g: (0, start + g)),
        pl.BlockSpec((5, SPAN, TILE), lambda s, g: (0, s, 0)),
        pl.BlockSpec((SPAN, 1), lambda s, g: (s, 0)),
        pl.BlockSpec((1, SPAN), lambda s, g: (0, s)),
        pl.BlockSpec((1, width), lambda s, g: (0, start + g)),
    ]
    args = [pc, pc, conv_x, same, seg_col, seg_row, skip]
    column_spec = pl.BlockSpec((SPAN, TILE), lambda s, g: (s, 0))
    row_spec = pl.BlockSpec((TILE, SPAN), lambda s, g: (s, 0))
    columns_shape = jax.ShapeDtypeStruct((tokens, TILE), F32)
    rows_shape = jax.ShapeDtypeStruct((spans * TILE, SPAN), F32)
    mark_spec = pl.BlockSpec((8, TILE), lambda s, g: (0, 0))
    out_specs = [wide, wide, pl.BlockSpec((N, width), lambda s, g: (s, start + g)), wide, mark_spec]
    out_shape = [
        jax.ShapeDtypeStruct((tokens, di), BF16),
        jax.ShapeDtypeStruct((tokens, di), BF16),
        jax.ShapeDtypeStruct((spans * N, di), BF16),
        jax.ShapeDtypeStruct((tokens, di), BF16),
        jax.ShapeDtypeStruct((8, TILE), F32),
    ]
    if first_call:
        in_specs += [
            pl.BlockSpec((SPAN, TILE), lambda s, g: (s, 2)),
            pl.BlockSpec((8, TILE), lambda s, g: (0, 0)),
            pl.BlockSpec((SPAN, 2 * N), lambda s, g: (s, 0)),
            pl.BlockSpec((8, 2 * N), lambda s, g: (halo(s), 0)),
            pl.BlockSpec((8, 2 * N), lambda s, g: (0, 0)),
        ]
        args += [pc_bc, heads, pc_bc, pc_bc, conv_bc]
        out_specs += [bcv_spec, bcv_spec, column_spec, column_spec, row_spec, row_spec, row_spec]
        out_shape += [jax.ShapeDtypeStruct((tokens, 2 * N), BF16)] * 2
        out_shape += [columns_shape] * 2 + [rows_shape] * 3
        aliases = {}
    else:
        in_specs += [bcv_spec, column_spec, row_spec, row_spec, any_spec, any_spec, any_spec, any_spec, mark_spec]
        args += [*shared, *before]
        aliases = {11: 0, 12: 1, 13: 2, 14: 3}
    return pl.pallas_call(
        functools.partial(forward_kernel, first_call, start * GROUP),
        grid_spec=pltpu.PrefetchScalarGridSpec(
            num_scalar_prefetch=0,
            grid=(spans, count),
            in_specs=in_specs,
            out_specs=out_specs,
            scratch_shapes=[
                pltpu.VMEM((N, own), F32),
                pltpu.VMEM((SPAN, SPAN), F32),
                pltpu.VMEM((SPAN, SPAN), F32),
                pltpu.VMEM((8, TILE), F32),
                pltpu.VMEM((N, SPAN), F32),
                pltpu.VMEM((SPAN + 8, width), F32),
                pltpu.VMEM((SPAN + 8, 2 * N), F32),
            ],
        ),
        out_shape=out_shape,
        input_output_aliases=aliases,
        compiler_params=pltpu.CompilerParams(dimension_semantics=("arbitrary", "arbitrary")),
        cost_estimate=pl.CostEstimate(flops=int(5e9 * count), bytes_accessed=14 * tokens * own, transcendentals=0),
        name="scan_forward",
    )(*args)


def conv_back(grad, slope, signal, same, weights, carry):
    width = grad.shape[1]
    du = grad * slope.astype(F32)

    def add_rows(values):
        return jnp.sum(values.reshape(SPAN // 8, 8, width), axis=0)

    out = weights[3:4] * du
    sums = [add_rows(du), add_rows(du * signal)]
    for offset in (1, 2, 3):
        mask = same[offset - 1]
        if width > TILE:
            mask = jnp.concatenate([mask] * (width // TILE), axis=1)
        masked = du * mask
        moved = jnp.concatenate([masked, carry[offset - 1]], axis=0)[offset : offset + SPAN]
        carry[offset - 1] = masked[0:8]
        out = out + weights[3 - offset : 4 - offset] * moved
        sums.append(add_rows(moved * signal))
    return out, sums


def backward_kernel(
    first_call, last_call, base,
    dy_ref, x_ref, bcv_ref, st_ref, slope_ref, pc_ref, cw_ref, same, seg_col_ref, seg_ref, skip_ref,
    cum_ref, shifted_ref, cum_rows, *rest,
):
    rest = list(rest)
    before = None if first_call else [rest.pop(0) for _ in range(4)]
    if last_call:
        raw_ref, heads_ref, bc_ref, bc_slope_ref, bcw_ref = [rest.pop(0) for _ in range(5)]
    dproj_out, dcw_out, dskip_out = [rest.pop(0) for _ in range(3)]
    if last_call:
        dbcw_out, dhead_out = [rest.pop(0) for _ in range(2)]
    else:
        after_out = [rest.pop(0) for _ in range(4)]
    (
        dstate, scores, block, dscores, pack, c_t,
        carry, carry_bc, d_bc, per_row, dcum_rows, dlast,
    ) = rest
    back = pl.program_id(0)
    group = pl.program_id(1)
    groups = pl.num_programs(1)
    width = GROUP * P_SIZE
    group_head = base + GROUP * group
    first_x = 4 * N if last_call else 0

    @pl.when((back == 0) & (group == 0))
    def _():
        dstate[...] = jnp.zeros_like(dstate)
        carry[...] = jnp.zeros_like(carry)
        dcw_out[...] = jnp.zeros_like(dcw_out)
        dskip_out[...] = jnp.zeros_like(dskip_out)
        dcum_rows[...] = jnp.zeros_like(dcum_rows)
        if last_call:
            carry_bc[...] = jnp.zeros_like(carry_bc)
            dbcw_out[...] = jnp.zeros_like(dbcw_out)
            dhead_out[...] = jnp.zeros_like(dhead_out)

    keys = bcv_ref[:, :N]
    query = bcv_ref[:, N:]
    lane = lax.broadcasted_iota(jnp.int32, (SPAN, TILE), 1)

    @pl.when(group == 0)
    def _():
        entry = jnp.exp2(cum_ref[...]) * same[3]
        pack[...] = jnp.where(lane < 64, shifted_ref[...], pltpu.roll(entry, 64, 1))
        row = lax.broadcasted_iota(jnp.int32, (SPAN, SPAN), 0)
        col = lax.broadcasted_iota(jnp.int32, (SPAN, SPAN), 1)
        linked = (row <= col) & (seg_col_ref[...] == seg_ref[...])
        block[...] = jnp.where(linked, 0.0, NEG)
        scores[...] = mm_nt(keys, query)
        c_t[...] = query.T
        per_row[...] = jnp.zeros_like(per_row)
        if first_call:
            dscores[...] = jnp.zeros_like(dscores)
            d_bc[...] = jnp.zeros_like(d_bc)
            dlast[...] = jnp.zeros_like(dlast)
        else:
            dscores[...] = before[0][...]
            d_bc[...] = before[1][...]
            per_row[0] = before[2][:, :TILE]
            per_row[2] = before[2][:, TILE:]
            dlast[...] = before[3][...]

    shift = lax.rem(TILE - group_head, TILE)
    cols = pltpu.roll(pack[...], shift, 1)
    last_cum = pltpu.roll(jnp.broadcast_to(cum_ref[SPAN - 1 : SPAN], (8, TILE)), shift, 1)[0:1]
    keep_mask = same[3, SPAN - 1 : SPAN]
    first = lane < P_SIZE
    lane_row = lax.broadcasted_iota(jnp.int32, (2 * TILE, TILE), 0) // P_SIZE
    lane_col = lax.broadcasted_iota(jnp.int32, (2 * TILE, TILE), 1)
    sums = jnp.zeros((SPAN, TILE), F32)
    last_sum = jnp.zeros((1, TILE), F32)
    group_at = group * width
    empty = jnp.zeros((HALF, HALF), BF16)
    wide = lambda parts: jnp.concatenate(parts, axis=1)
    for quad in range(GROUP // 4):
        both = slice(quad * 2 * TILE, (quad + 1) * 2 * TILE)
        tile = pl.ds(pl.multiple_of(group_at + quad * 2 * TILE, 2 * TILE), 2 * TILE)
        entries, tails, keeps, inners = [], [], [], []
        for pair in (2 * quad, 2 * quad + 1):
            at = pair * TILE
            heads = (2 * pair, 2 * pair + 1)
            dy_pair = dy_ref[:, at : at + TILE]
            xb = x_ref[:, at : at + TILE]
            nothing = jnp.zeros_like(xb)
            split = jnp.concatenate([jnp.where(first, xb, nothing), jnp.where(first, nothing, xb)], axis=0)
            g_both = mm_nt(split, dy_pair)
            cum_cols = [lanes_of(cols[:, head : head + 1], SPAN) for head in heads]
            cum_lines = [cum_rows[pl.ds(group_head + head, 1), :] for head in heads]
            mixes = [[], []]
            across = [[], []]
            down = [[], []]
            for j, i in ((0, 0), (0, 1), (1, 1)):
                rows = slice(j * HALF, (j + 1) * HALF)
                cells = slice(i * HALF, (i + 1) * HALF)
                spread = jnp.zeros((HALF, HALF), F32)
                for which in (0, 1):
                    decay = jnp.exp2(cum_lines[which][:, cells] - cum_cols[which][rows] + block[rows, cells])
                    mix = decay * scores[rows, cells]
                    g = g_both[which * SPAN + j * HALF : which * SPAN + (j + 1) * HALF, cells]
                    spread = spread + decay * g
                    w = mix * g
                    mixes[which].append(mix.astype(BF16))
                    across[which].append(w)
                    down[which].append(jnp.sum(w, axis=0, keepdims=True))
                dscores[rows, cells] += spread
            lefts = []
            for which in (0, 1):
                row_sum = jnp.concatenate(
                    [
                        jnp.sum(across[which][0] + across[which][1], axis=1, keepdims=True),
                        jnp.sum(across[which][2], axis=1, keepdims=True),
                    ],
                    axis=0,
                )
                sums = sums - jnp.where(lane == 2 * GROUP + heads[which], row_sum, 0.0)
                dcum_rows[pl.ds(group_head + heads[which], 1), :] = wide(
                    [down[which][0], down[which][1] + down[which][2]]
                )
                lefts += [wide(mixes[which][:2]), wide([empty, mixes[which][2]])]
            inner = mm(jnp.concatenate(lefts, axis=0), dy_pair)
            inners.append(jnp.where(first, inner[:SPAN], inner[SPAN:]))
            last_pair = jnp.where(
                first[0:1],
                jnp.broadcast_to(last_cum[:, heads[0] : heads[0] + 1], (1, TILE)),
                jnp.broadcast_to(last_cum[:, heads[1] : heads[1] + 1], (1, TILE)),
            )
            tails.append(jnp.exp2(last_pair - jnp.where(first, cum_cols[0], cum_cols[1])) * same[4])
            keeps.append(jnp.exp2(last_pair) * keep_mask)
            entries.append(pick(first, cols, 64 + 2 * pair))
        dyf = dy_ref[:, both].astype(F32)
        xf = x_ref[:, both].astype(F32)
        tail = wide(tails)
        stb = st_ref[:, both]
        ds = dstate[:, tile]
        dsb = ds.astype(BF16)
        dye_f = dyf * wide(entries)
        dye = dye_f.astype(BF16)
        fresh = mm(keys, dsb) * tail
        total = wide(inners) + fresh
        d_bc[:, N:] += mm_nt(dye, stb)
        d_bc[:, :N] += mm_nt((xf * tail).astype(BF16), dsb)

        def head_sum(values, kind):
            spread = (lane_col == kind * GROUP + 4 * quad + lane_row).astype(BF16)
            return mm(values.astype(BF16), spread)

        sums = sums + head_sum(xf * total, 0) + head_sum(xf * fresh, 1) + head_sum(dye_f * mm(query, stb), 2)
        kept = ds * wide(keeps)
        kept_sum = jnp.sum(kept * stb.astype(F32), axis=0, keepdims=True)
        lane_pair = lax.broadcasted_iota(jnp.int32, (1, 2 * TILE), 1) // P_SIZE
        for head in range(4):
            one = jnp.sum(jnp.where(lane_pair == head, kept_sum, 0.0), axis=1, keepdims=True)
            last_sum = last_sum + jnp.where(lane[0:1] == 4 * quad + head, one, 0.0)
        dstate[:, tile] = kept + mm(c_t[...], dye)
        dskip_out[:, tile] += jnp.sum((dyf * xf).reshape(SPAN // 8, 8, 2 * TILE), axis=0)
        dx = total + skip_ref[:, both] * dyf
        for part in (0, 1):
            at = (2 * quad + part) * TILE
            one = pl.ds(pl.multiple_of(group_at + at, TILE), TILE)
            out, conv_sums = conv_back(
                dx[:, part * TILE : (part + 1) * TILE], slope_ref[:, at : at + TILE], pc_ref[:, at : at + TILE],
                same, cw_ref[:, at : at + TILE], carry.at[:, :, one],
            )
            dproj_out[:, pl.ds(pl.multiple_of(first_x + group_at + at, TILE), TILE)] = out.astype(BF16)
            for k, value in enumerate(conv_sums):
                dcw_out[k, :, one] += value

    in_place = (lane >= group_head) & (lane < group_head + GROUP)
    for kind in range(3):
        moved = pltpu.roll(sums, lax.rem(group_head + TILE - GROUP * kind, TILE), 1)
        per_row[kind] += jnp.where(in_place, moved, 0.0)
    moved = pltpu.roll(jnp.broadcast_to(last_sum, (8, TILE)), group_head, 1)
    dlast[...] += jnp.where(in_place[0:8], moved, 0.0)

    @pl.when(group == groups - 1)
    def _():
        state_part = per_row[1]
        dcum = dcum_rows[...].T + per_row[2] - state_part
        dlast_all = dlast[0:1] + jnp.sum(state_part, axis=0, keepdims=True)
        if not last_call:
            after_out[0][...] = dscores[...]
            after_out[1][...] = d_bc[...]
            after_out[2][:, :TILE] = per_row[0]
            after_out[2][:, TILE:] = dcum
            after_out[3][...] = jnp.broadcast_to(dlast_all, (8, TILE))
            return
        ds_b = dscores[...].astype(BF16)
        grad_b = d_bc[:, :N] + mm(ds_b, query)
        grad_c = d_bc[:, N:] + mm(dscores[...].T.astype(BF16), keys)
        out, conv_sums = conv_back(
            wide([grad_b, grad_c]), bc_slope_ref[...], bc_ref[...], same, bcw_ref[...], carry_bc
        )
        dproj_out[:, : 2 * N] = out.astype(BF16)
        for k, value in enumerate(conv_sums):
            dbcw_out[k] += value
        heads = heads_ref[...]
        shifted = raw_ref[...] + heads[0:1]
        step = step_sizes(raw_ref[...], heads)
        slope = jax.nn.sigmoid(shifted)
        row = lax.broadcasted_iota(jnp.int32, (SPAN, SPAN), 0)
        col = lax.broadcasted_iota(jnp.int32, (SPAN, SPAN), 1)
        tri = (row <= col).astype(F32)
        da = dot_f32(tri, dcum, ((1,), (0,)), HIGHEST) + dlast_all
        small = shifted < -16.0
        ratio = jnp.where(small, 1.0, slope / jnp.where(small, 1.0, step))
        live = lane < H
        draw = jnp.where(live, per_row[0] * ratio + da * heads[2:3] * slope, 0.0)
        dproj_out[:, 2 * N : 3 * N] = draw.astype(BF16)
        dproj_out[:, 3 * N : 4 * N] = jnp.zeros((SPAN, N), BF16)
        dhead_out[0] += jnp.sum(draw.reshape(SPAN // 8, 8, TILE), axis=0)
        dhead_out[1] += jnp.sum(jnp.where(live, da * step, 0.0).reshape(SPAN // 8, 8, TILE), axis=0)


def run_backward(
    dy, x, bcv, states, slope, bc_slope, pc, first_x, pc_bc, conv_x, conv_bc, same, seg_col, seg_row, heads, skip,
    cums, start, count, last, before,
):
    tokens, di = dy.shape
    spans = tokens // SPAN
    width = GROUP * P_SIZE
    turn = lambda s: spans - 1 - s
    own = count * width
    out_width = own + (4 * N if last else 0)
    sums_specs = [
        pl.BlockSpec((SPAN, SPAN), lambda s, g: (turn(s), 0)),
        pl.BlockSpec((SPAN, 2 * N), lambda s, g: (turn(s), 0)),
        pl.BlockSpec((SPAN, 2 * TILE), lambda s, g: (turn(s), 0)),
        pl.BlockSpec((8, TILE), lambda s, g: (turn(s), 0)),
    ]
    sums_shapes = [
        jax.ShapeDtypeStruct((tokens, SPAN), F32),
        jax.ShapeDtypeStruct((tokens, 2 * N), F32),
        jax.ShapeDtypeStruct((tokens, 2 * TILE), F32),
        jax.ShapeDtypeStruct((spans * 8, TILE), F32),
    ]
    out_specs = [
        pl.BlockSpec((SPAN, out_width), lambda s, g: (turn(s), 0)),
        pl.BlockSpec((5, 8, own), lambda s, g: (0, 0, 0)),
        pl.BlockSpec((8, own), lambda s, g: (0, 0)),
    ]
    out_shape = [
        jax.ShapeDtypeStruct((tokens, out_width), BF16),
        jax.ShapeDtypeStruct((5, 8, own), F32),
        jax.ShapeDtypeStruct((8, own), F32),
    ]
    wide = pl.BlockSpec((SPAN, width), lambda s, g: (turn(s), start + g))
    in_specs = [
        wide,
        wide,
        pl.BlockSpec((SPAN, 2 * N), lambda s, g: (turn(s), 0)),
        pl.BlockSpec((N, width), lambda s, g: (turn(s), start + g)),
        wide,
        pl.BlockSpec((SPAN, width), lambda s, g: (turn(s), first_x + g)),
        pl.BlockSpec((8, width), lambda s, g: (0, start + g)),
        pl.BlockSpec((5, SPAN, TILE), lambda s, g: (0, turn(s), 0)),
        pl.BlockSpec((SPAN, 1), lambda s, g: (turn(s), 0)),
        pl.BlockSpec((1, SPAN), lambda s, g: (0, turn(s))),
        pl.BlockSpec((1, width), lambda s, g: (0, start + g)),
        pl.BlockSpec((SPAN, TILE), lambda s, g: (turn(s), 0)),
        pl.BlockSpec((SPAN, TILE), lambda s, g: (turn(s), 0)),
        pl.BlockSpec((TILE, SPAN), lambda s, g: (turn(s), 0)),
    ]
    args = [dy, x, bcv, states, slope, pc, conv_x, same, seg_col, seg_row, skip, *cums]
    if before is not None:
        in_specs += sums_specs
        args += before
    if last:
        in_specs += [
            pl.BlockSpec((SPAN, TILE), lambda s, g: (turn(s), 2)),
            pl.BlockSpec((8, TILE), lambda s, g: (0, 0)),
            pl.BlockSpec((SPAN, 2 * N), lambda s, g: (turn(s), 0)),
            pl.BlockSpec((SPAN, 2 * N), lambda s, g: (turn(s), 0)),
            pl.BlockSpec((8, 2 * N), lambda s, g: (0, 0)),
        ]
        args += [pc_bc, heads, pc_bc, bc_slope, conv_bc]
        out_specs += [
            pl.BlockSpec((5, 8, 2 * N), lambda s, g: (0, 0, 0)),
            pl.BlockSpec((2, 8, TILE), lambda s, g: (0, 0, 0)),
        ]
        out_shape += [
            jax.ShapeDtypeStruct((5, 8, 2 * N), F32),
            jax.ShapeDtypeStruct((2, 8, TILE), F32),
        ]
    else:
        out_specs += sums_specs
        out_shape += sums_shapes
    return pl.pallas_call(
        functools.partial(backward_kernel, before is None, last, start * GROUP),
        grid_spec=pltpu.PrefetchScalarGridSpec(
            num_scalar_prefetch=0,
            grid=(spans, count),
            in_specs=in_specs,
            out_specs=out_specs,
            scratch_shapes=[
                pltpu.VMEM((N, own), F32),
                pltpu.VMEM((SPAN, SPAN), F32),
                pltpu.VMEM((SPAN, SPAN), F32),
                pltpu.VMEM((SPAN, SPAN), F32),
                pltpu.VMEM((SPAN, TILE), F32),
                pltpu.VMEM((N, SPAN), BF16),
                pltpu.VMEM((3, 8, own), F32),
                pltpu.VMEM((3, 8, 2 * N), F32),
                pltpu.VMEM((SPAN, 2 * N), F32),
                pltpu.VMEM((3, SPAN, TILE), F32),
                pltpu.VMEM((TILE, SPAN), F32),
                pltpu.VMEM((8, TILE), F32),
            ],
        ),
        out_shape=out_shape,
        compiler_params=pltpu.CompilerParams(dimension_semantics=("arbitrary", "arbitrary")),
        cost_estimate=pl.CostEstimate(
            flops=int(1.2e10 * count), bytes_accessed=12 * tokens * own, transcendentals=0
        ),
        name="scan_backward",
    )(*args)


def seg_facts(seg):
    length = seg.shape[0]
    cols = []
    for offset in (1, 2, 3):
        moved = jnp.concatenate([jnp.full((offset,), -1, jnp.int32), seg[:-offset]])
        cols.append((moved == seg).astype(F32))
    spans = length // SPAN
    ends = seg[SPAN - 1 :: SPAN]
    before = jnp.concatenate([seg[:1], ends[:-1]])
    cols.append((seg == jnp.repeat(before, SPAN)).astype(F32))
    cols.append((seg == jnp.repeat(ends, SPAN)).astype(F32))
    value = seg.astype(F32)
    same = jnp.broadcast_to(jnp.stack(cols, axis=0)[:, :, None], (5, length, TILE))
    return same, value[:, None], value[None, :]


def head_rows(dt_bias, a_log):
    rate = -jnp.exp(a_log)
    rows = jnp.stack([dt_bias, rate * LOG2E, rate] + [jnp.zeros_like(rate)] * 5, axis=0)
    return jnp.pad(rows, ((0, 0), (0, TILE - H)))


BLOCKS = 32
ORDERS = ((8, 1, 4, 2), (8, 2, 4, 1))


def reach(masks):
    out = [0]
    for mask in masks:
        out = out + [mask ^ place for place in out]
    return out


def exchange(values, stage):
    pairs = []
    for shard in range(16):
        for core in range(2):
            pairs.append((shard * 2 + core, (shard ^ ORDERS[core][stage]) * 2 + core))
    return lax.ppermute(values, ("shard", "rep"), pairs)


def swap_cores(values):
    return lax.ppermute(values, "rep", [(0, 1), (1, 0)])


def after(values, *others):
    return lax.optimization_barrier((values, *others))[0]


class Gather:
    def __init__(self, local):
        self.held = local
        self.seen = []
        self.swapped = []

    def step(self, *ahead):
        stage = len(self.seen)
        if stage > 0:
            self.held = jnp.concatenate([self.held, after(self.seen[-1], *ahead)], axis=0)
        elif ahead:
            self.held = after(self.held, *ahead)
        got = exchange(self.held, stage)
        self.seen.append(got)
        return self.held, got

    def swap(self, *ahead):
        send = after(self.held if not self.swapped else self.seen[3], *ahead)
        self.swapped.append(swap_cores(send))
        return send, self.swapped[-1]

    def pieces(self):
        return self.held, self.seen[3], *self.swapped


def gather_small(local):
    held = local[None]
    ahead = yield None
    for stage in range(4):
        send = after(held, *ahead)
        got = exchange(send, stage)
        ahead = yield send, got
        held = jnp.concatenate([send, got], axis=0)
    core = lax.axis_index("rep")
    places = jnp.asarray([reach(order) for order in ORDERS], jnp.int32)[core] ^ lax.axis_index("shard")
    hot = (places[None, :] == jnp.arange(16, dtype=jnp.int32)[:, None]).astype(local.dtype)
    yield dot_f32(hot, held, ((1,), (0,)), HIGHEST).astype(local.dtype)


class Scatter:
    def __init__(self, partial, block):
        mine, self.other = partial
        self.terms = [mine]
        self.block = block
        self.left = [3, 2, 1, 0]

    def rows(self, start, stop):
        total = self.terms[0][start:stop].astype(F32)
        for term in self.terms[1:]:
            total = total + term[start:stop].astype(F32)
        return total

    def step(self, *ahead):
        if len(self.terms) == 1:
            self.other = after(self.other, *ahead)
            self.terms.append(swap_cores(self.other))
            return self.other, self.terms[-1]
        if self.left:
            stage = self.left.pop(0)
            cut = self.block << stage
            self.terms[-1] = after(self.terms[-1], *ahead)
            send = self.rows(cut, 2 * cut).astype(BF16)
            self.terms.append(exchange(send, stage))
            return send, self.terms[-1]
        return self.terms[-1], self.terms[-1]

    def finish(self, *ahead):
        while self.left:
            self.step()
        if ahead:
            self.terms[-1] = after(self.terms[-1], *ahead)
        return self.rows(0, self.block)


def block_order(core):
    shard = lax.axis_index("shard")
    tables = jnp.asarray([reach(order) for order in ORDERS], jnp.int32)
    inverse = jnp.asarray(
        [[reach(order).index(mask) for mask in range(16)] for order in ORDERS], jnp.int32
    )
    own = 2 * (tables[core] ^ shard) + core
    partner = 2 * (tables[1 - core] ^ shard) + (1 - core)
    order = jnp.concatenate([own, partner])
    natural = jnp.arange(BLOCKS, dtype=jnp.int32)
    which = natural % 2
    place = inverse[which, (natural // 2) ^ shard] + 16 * (which != core).astype(jnp.int32)
    return order, place


def fetch_tile(order_ref, pieces, buffer, sems, tile, slot, block, width):
    for q in range(BLOCKS):
        pltpu.make_async_copy(
            pieces[q // 8].at[pl.ds((q % 8) * block, block), pl.ds(pl.multiple_of(tile * width, width), width)],
            buffer.at[slot, pl.ds(pl.multiple_of(order_ref[q] * block, block), block), :],
            sems.at[slot],
        ).start()


def next_tile(order_ref, pieces, buffer, sems, block, width):
    tile = pl.program_id(0)
    slot = lax.rem(tile, 2)

    @pl.when(tile == 0)
    def _():
        fetch_tile(order_ref, pieces, buffer, sems, tile, slot, block, width)

    @pl.when(tile + 1 < pl.num_programs(0))
    def _():
        fetch_tile(order_ref, pieces, buffer, sems, tile + 1, 1 - slot, block, width)

    pltpu.make_async_copy(buffer.at[slot], buffer.at[slot], sems.at[slot]).wait()
    return slot


def project_kernel(block, width, order_ref, x_ref, p0, p1, p2, p3, *rest):
    out_ref, w_ref, buffer, sems = rest[-4:]
    slot = next_tile(order_ref, (p0, p1, p2, p3), buffer, sems, block, width)
    w = buffer[slot]
    w_ref[...] = w
    for i in range(x_ref.shape[0] // SPAN):
        rows = slice(i * SPAN, (i + 1) * SPAN)
        out_ref[rows] = mm(x_ref[rows], w)


def project(x, pieces, order, so_far, start, full, width=512):
    tokens, depth = x.shape
    columns = pieces[0].shape[1]
    block = depth // BLOCKS
    at = start // width
    any_spec = pl.BlockSpec(memory_space=pl.ANY)
    extra = [] if so_far is None else list(so_far)
    return pl.pallas_call(
        functools.partial(project_kernel, block, width),
        grid_spec=pltpu.PrefetchScalarGridSpec(
            num_scalar_prefetch=1,
            grid=(columns // width,),
            in_specs=[pl.BlockSpec((tokens, depth), lambda j, o: (0, 0))] + [any_spec] * (4 + len(extra)),
            out_specs=[
                pl.BlockSpec((tokens, width), lambda j, o: (0, at + j)),
                pl.BlockSpec((depth, width), lambda j, o: (0, at + j)),
            ],
            scratch_shapes=[pltpu.VMEM((2, depth, width), BF16), pltpu.SemaphoreType.DMA((2,))],
        ),
        out_shape=[jax.ShapeDtypeStruct((tokens, full), F32), jax.ShapeDtypeStruct((depth, full), BF16)],
        input_output_aliases={} if so_far is None else {6: 0, 7: 1},
        cost_estimate=pl.CostEstimate(
            flops=2 * tokens * depth * columns,
            bytes_accessed=4 * depth * columns + 4 * tokens * columns + 2 * tokens * depth,
            transcendentals=0,
        ),
        name="project",
    )(order, x, *pieces, *extra)


def gate_kernel(block, width, order_ref, x_ref, p0, p1, p2, p3, y_ref, gain_ref, mark_ref, *rest):
    gate_ref, w_ref, zg_ref, square_ref, buffer, sems = rest[-6:]
    slot = next_tile(order_ref, (p0, p1, p2, p3), buffer, sems, block, width)
    w = buffer[slot]
    w_ref[...] = w

    @pl.when(pl.program_id(0) == 0)
    def _():
        square_ref[...] = jnp.zeros_like(square_ref)

    for i in range(x_ref.shape[0] // SPAN):
        rows = slice(i * SPAN, (i + 1) * SPAN)
        gate = mm(x_ref[rows], w)
        gate_ref[rows] = gate.astype(BF16)
        gated = y_ref[rows].astype(F32) * (gate * jax.nn.sigmoid(gate))
        zg_ref[rows] = (gated * gain_ref[...]).astype(BF16)
        square = gated * gated
        total = square[:, :TILE]
        for k in range(1, width // TILE):
            total = total + square[:, k * TILE : (k + 1) * TILE]
        square_ref[rows] += total


def gate_project(x, pieces, order, y, gain, mark, so_far, start, full, width=512):
    tokens, depth = x.shape
    columns = pieces[0].shape[1]
    block = depth // BLOCKS
    at = start // width
    any_spec = pl.BlockSpec(memory_space=pl.ANY)
    extra = [] if so_far is None else list(so_far)
    wide = pl.BlockSpec((tokens, width), lambda j, o: (0, at + j))
    return pl.pallas_call(
        functools.partial(gate_kernel, block, width),
        grid_spec=pltpu.PrefetchScalarGridSpec(
            num_scalar_prefetch=1,
            grid=(columns // width,),
            in_specs=[pl.BlockSpec((tokens, depth), lambda j, o: (0, 0))]
            + [any_spec] * 4
            + [wide, pl.BlockSpec((1, width), lambda j, o: (0, at + j)), pl.BlockSpec((8, TILE), lambda j, o: (0, 0))]
            + [any_spec] * len(extra),
            out_specs=[
                wide,
                pl.BlockSpec((depth, width), lambda j, o: (0, at + j)),
                wide,
                pl.BlockSpec((tokens, TILE), lambda j, o: (0, 0)),
            ],
            scratch_shapes=[pltpu.VMEM((2, depth, width), BF16), pltpu.SemaphoreType.DMA((2,))],
        ),
        out_shape=[
            jax.ShapeDtypeStruct((tokens, full), BF16),
            jax.ShapeDtypeStruct((depth, full), BF16),
            jax.ShapeDtypeStruct((tokens, full), BF16),
            jax.ShapeDtypeStruct((tokens, TILE), F32),
        ],
        input_output_aliases={} if so_far is None else {9: 0, 10: 1, 11: 2},
        cost_estimate=pl.CostEstimate(
            flops=2 * tokens * depth * columns,
            bytes_accessed=4 * depth * columns + 10 * tokens * columns + 2 * tokens * depth,
            transcendentals=tokens * columns,
        ),
        name="project_gate",
    )(order, x, *pieces, y, gain, mark, *extra)


def restore_kernel(block, width, order_ref, p0, p1, p2, p3, *rest):
    w_ref, buffer, sems = rest[-3:]
    slot = next_tile(order_ref, (p0, p1, p2, p3), buffer, sems, block, width)
    w_ref[...] = buffer[slot]


def restore(pieces, order, so_far, start, full, width=256):
    columns = pieces[0].shape[1]
    block = pieces[0].shape[0] // 8
    depth = block * BLOCKS
    at = start // width
    any_spec = pl.BlockSpec(memory_space=pl.ANY)
    extra = [] if so_far is None else [so_far]
    return pl.pallas_call(
        functools.partial(restore_kernel, block, width),
        grid_spec=pltpu.PrefetchScalarGridSpec(
            num_scalar_prefetch=1,
            grid=(columns // width,),
            in_specs=[any_spec] * (4 + len(extra)),
            out_specs=pl.BlockSpec((depth, width), lambda j, o: (0, at + j)),
            scratch_shapes=[pltpu.VMEM((2, depth, width), BF16), pltpu.SemaphoreType.DMA((2,))],
        ),
        out_shape=jax.ShapeDtypeStruct((depth, full), BF16),
        input_output_aliases={} if so_far is None else {5: 0},
        cost_estimate=pl.CostEstimate(flops=0, bytes_accessed=4 * depth * columns, transcendentals=0),
        name="restore",
    )(order, *pieces, *extra)


def output_kernel(block, width, order_ref, zg_ref, inverse_ref, tokens_ref, cot_ref, p0, p1, p2, p3, w_ref, out_ref, dots_ref, buffer, sems):
    slot = next_tile(order_ref, (p0, p1, p2, p3), buffer, sems, block, width)
    w = buffer[slot]
    w_ref[...] = w

    @pl.when(pl.program_id(0) == 0)
    def _():
        dots_ref[...] = jnp.zeros_like(dots_ref)

    for i in range(zg_ref.shape[0] // SPAN):
        rows = slice(i * SPAN, (i + 1) * SPAN)
        projected = inverse_ref[rows] * mm(zg_ref[rows], w)
        out_ref[rows] = (tokens_ref[rows].astype(F32) + projected).astype(BF16)
        dots_ref[rows] += jnp.sum(cot_ref[rows].astype(F32) * projected, axis=1, keepdims=True)


def output_project(zg, inverse, tokens, cot, pieces, order, width=512):
    count, depth = zg.shape
    model = tokens.shape[1]
    block = depth // BLOCKS
    any_spec = pl.BlockSpec(memory_space=pl.ANY)
    whole = lambda i, o: (0, 0)
    part = pl.BlockSpec((count, width), lambda i, o: (0, i))
    return pl.pallas_call(
        functools.partial(output_kernel, block, width),
        grid_spec=pltpu.PrefetchScalarGridSpec(
            num_scalar_prefetch=1,
            grid=(model // width,),
            in_specs=[pl.BlockSpec((count, depth), whole), pl.BlockSpec((count, 1), whole), part, part]
            + [any_spec] * 4,
            out_specs=[
                pl.BlockSpec((depth, width), lambda i, o: (0, i)),
                part,
                pl.BlockSpec((count, 1), whole),
            ],
            scratch_shapes=[pltpu.VMEM((2, depth, width), BF16), pltpu.SemaphoreType.DMA((2,))],
        ),
        out_shape=[
            jax.ShapeDtypeStruct((depth, model), BF16),
            jax.ShapeDtypeStruct((count, model), BF16),
            jax.ShapeDtypeStruct((count, 1), F32),
        ],
        cost_estimate=pl.CostEstimate(
            flops=2 * count * depth * model,
            bytes_accessed=4 * depth * model + 2 * count * (depth + 3 * model),
            transcendentals=0,
        ),
        name="project_out",
    )(order, zg, inverse, tokens, cot, *pieces)


def gate_back_kernel(cot_ref, w_ref, gate_ref, y_ref, gain_ref, inverse_ref, less_ref, dy_ref, dgate_ref):
    w = w_ref[...]
    for i in range(cot_ref.shape[0] // SPAN):
        rows = slice(i * SPAN, (i + 1) * SPAN)
        gate = gate_ref[rows].astype(F32)
        y = y_ref[rows].astype(F32)
        part = jax.nn.sigmoid(gate)
        opened = gate * part
        dz = inverse_ref[rows] * (gain_ref[...] * mm_nt(cot_ref[rows], w)) - (y * opened) * less_ref[rows]
        dy_ref[rows] = (dz * opened).astype(BF16)
        dgate_ref[rows] = (dz * y * (part + opened * (1.0 - part))).astype(BF16)


def gate_back(cot, w, gate, y, gain, inverse, less, width=512):
    count, model = cot.shape
    di = w.shape[0]
    part = pl.BlockSpec((count, width), lambda i: (0, i))
    column = pl.BlockSpec((count, 1), lambda i: (0, 0))
    shape = jax.ShapeDtypeStruct((count, di), BF16)
    return pl.pallas_call(
        gate_back_kernel,
        grid_spec=pltpu.PrefetchScalarGridSpec(
            num_scalar_prefetch=0,
            grid=(di // width,),
            in_specs=[
                pl.BlockSpec((count, model), lambda i: (0, 0)),
                pl.BlockSpec((width, model), lambda i: (i, 0)),
                part,
                part,
                pl.BlockSpec((1, width), lambda i: (0, i)),
                column,
                column,
            ],
            out_specs=[part, part],
        ),
        out_shape=[shape, shape],
        cost_estimate=pl.CostEstimate(
            flops=2 * count * di * model, bytes_accessed=2 * (di * model + 4 * count * di), transcendentals=count * di
        ),
        name="gate_back",
    )(cot, w, gate, y, gain, inverse, less)


def weight_grad_kernel(block, place_ref, lhs_ref, rhs_ref, mine, other, buffer, sems):
    step = pl.program_id(0)
    slot = lax.rem(step, 2)

    def settle(which):
        pltpu.make_async_copy(buffer.at[which], buffer.at[which], sems.at[which]).wait()

    @pl.when(step >= 2)
    def _():
        settle(slot)

    buffer[slot] = dot_f32(lhs_ref[...], rhs_ref[...], ((0,), (0,))).astype(BF16)
    for t in range(8):
        q = place_ref[step * 8 + t]
        source = buffer.at[slot, pl.ds(t * block, block), :]

        @pl.when(q < 16)
        def _():
            pltpu.make_async_copy(
                source, mine.at[pl.ds(pl.multiple_of(q * block, block), block), :], sems.at[slot]
            ).start()

        @pl.when(q >= 16)
        def _():
            pltpu.make_async_copy(
                source, other.at[pl.ds(pl.multiple_of((q - 16) * block, block), block), :], sems.at[slot]
            ).start()

    @pl.when(step == pl.num_programs(0) - 1)
    def _():
        settle(1 - slot)
        settle(slot)


def weight_grad(lhs, rhs, place, column, columns):
    tokens, rows = lhs.shape
    block = rows // BLOCKS
    any_spec = pl.BlockSpec(memory_space=pl.ANY)
    out = jax.ShapeDtypeStruct((16 * block, columns), BF16)
    return pl.pallas_call(
        functools.partial(weight_grad_kernel, block),
        grid_spec=pltpu.PrefetchScalarGridSpec(
            num_scalar_prefetch=1,
            grid=(4,),
            in_specs=[
                pl.BlockSpec((tokens, 8 * block), lambda i, o: (0, i)),
                pl.BlockSpec((tokens, columns), lambda i, o: (0, column)),
            ],
            out_specs=[any_spec, any_spec],
            scratch_shapes=[pltpu.VMEM((2, 8 * block, columns), BF16), pltpu.SemaphoreType.DMA((2,))],
        ),
        out_shape=[out, out],
        cost_estimate=pl.CostEstimate(
            flops=2 * tokens * rows * columns,
            bytes_accessed=2 * (tokens * rows + tokens * columns + rows * columns),
            transcendentals=0,
        ),
        name="weight_grad",
    )(place, lhs, rhs)


def rows_of(packed, start, count):
    return packed[:, start : start + count]


def on_device(
    hypercube,
    tokens,
    seg_ids,
    gain_in,
    w_in,
    conv_weight,
    conv_bias,
    dt_bias,
    a_log,
    d_skip,
    gain_out,
    w_out,
    cotangent,
):
    shards = lax.psum(1, "shard")
    taps, conv_local = conv_weight.shape
    model = tokens.shape[1]
    di = gain_out.shape[0] * shards
    conv_dim = conv_local * shards
    calls = ((0, 1), (1, 2), (3, 3))
    width = GROUP * P_SIZE

    def columns(w, call):
        start, count = call
        own = w[:, di + start * width : di + (start + count) * width]
        if start > 0:
            return own
        head = w[:, 2 * di :]
        return jnp.concatenate([jnp.pad(head, ((0, 0), (0, 4 * N - head.shape[1]))), own], axis=1)

    small = jnp.concatenate([conv_weight.reshape(-1), conv_bias, gain_in, gain_out])
    if hypercube:
        core = lax.axis_index("rep")
        w_half = lax.dynamic_slice_in_dim(w_in, core * (w_in.shape[0] // 2), w_in.shape[0] // 2, 0)
        o_half = lax.dynamic_slice_in_dim(w_out, core * (w_out.shape[0] // 2), w_out.shape[0] // 2, 0)
        near, middle, far = [Gather(columns(w_half, call)) for call in calls]
        gate_gather, out_gather = Gather(w_half[:, :di]), Gather(o_half)
        small_flow = gather_small(small)
        next(small_flow)
        got = []
        for starts in ((near,), (near, middle), (near, middle, far), (near, middle, far)):
            pairs = [near.step(*got)]
            ahead = [*got, pairs[0][0]]
            pairs += [each.step(*ahead) for each in starts[1:]] + [small_flow.send(ahead)]
            got = [pair[1] for pair in pairs]
            if len(starts) == 1:
                later = (far.held, gate_gather.held, out_gather.held), (tokens, seg_ids, dt_bias, a_log, d_skip, core)
                helds, (tokens, seg_ids, dt_bias, a_log, d_skip, core) = after(later, *got)
                far.held, gate_gather.held, out_gather.held = helds
        small_all = small_flow.send(got)
        order, place = block_order(core)
        swaps = [near.swap(near.seen[3]), near.swap()]
        got = [*got[1:], swaps[1][0]]
        sent, got = zip(middle.step(*got), far.step(*got), *swaps, gate_gather.step(*got))
        normed_tie = sent
        conv_tie = sent
        last_pair = got[0], got[1], got[4]
    else:
        small_all = lax.all_gather(small, "shard", axis=0, tiled=False)
        full_w_in = lax.all_gather(w_in, "shard", axis=0, tiled=True)
        full_w_out = lax.all_gather(w_out, "shard", axis=0, tiled=True)
    cut = taps * conv_local
    small_conv = after(small_all, *conv_tie) if hypercube else small_all
    conv_w = small_conv[:, :cut].reshape(shards, taps, conv_local).transpose(1, 0, 2).reshape(taps, -1)
    conv_b = rows_of(small_conv, cut, conv_local).reshape(1, -1)
    cut += conv_local
    full_gain_in = rows_of(small_all, cut, gain_in.shape[0]).reshape(1, -1).astype(F32)
    full_gain_out = rows_of(small_conv, cut + gain_in.shape[0], gain_out.shape[0]).reshape(1, -1).astype(F32)
    conv_all = jnp.concatenate(
        [conv_w.astype(F32), conv_b.astype(F32), jnp.zeros((3, conv_dim), F32)], axis=0
    )
    conv_x, conv_bc = conv_all[:, :di], conv_all[:, di:]
    inputs = tokens.astype(F32)
    rscale = lax.rsqrt(jnp.mean(inputs * inputs, axis=1, keepdims=True) + EPSILON)
    unit = inputs * rscale
    normed = (unit * full_gain_in).astype(BF16)
    same, seg_col, seg_row = seg_facts(seg_ids[0])
    if hypercube:
        normed, same = after((normed, same), *normed_tie)
    heads = head_rows(dt_bias, a_log)
    skip = jnp.repeat(d_skip, P_SIZE)[None]

    pcs, w_parts = [], []
    shared = written = mark = None
    project_tie = ()
    for index, call in enumerate(calls):
        if hypercube:
            pieces = (near, middle, far)[index].pieces()
            pc, w_part = project(after(normed, *project_tie), pieces, order, None, 0, pieces[0].shape[1])
            if index == 0:
                done = last_pair[0], last_pair[2], pc
                sent, got = zip(
                    middle.swap(*done), middle.swap(*done), gate_gather.step(*done), out_gather.step(*done)
                )
                pc = after(pc, *sent)
            if index == 1:
                sent, _ = far.swap(pc)
                pc = after(pc, sent)
        else:
            w_part = columns(full_w_in, call)
            pc = mm(normed, w_part)
        pcs.append((pc, 1 if index == 0 else 0))
        w_parts.append(w_part)
        written = run_forward(
            pc, pcs[-1][1], pcs[0][0], conv_x, conv_bc, same, seg_col, seg_row, heads, skip, *call, shared, written
        )
        mark = written[4]
        if index == 0:
            bcv, bc_slope, cum, shifted, cum_lines, shifted_lines, weight_lines = written[5:]
            shared = bcv, cum, shifted_lines, weight_lines
        written = written[:5]
        if hypercube and index == 0:
            done = last_pair[1], got[2], got[3], mark
            sent, got = zip(far.step(*done), gate_gather.step(*done), out_gather.step(*done))
            project_tie = sent
        if hypercube and index == 1:
            far.swap(got[0], mark)
            done = got[1], got[2], mark
            sent, got = zip(gate_gather.step(*done), gate_gather.swap(*done), out_gather.step(*done))
            project_tie = sent
    if hypercube:
        done = got[0], got[1], got[2], mark
        sent, got = zip(gate_gather.swap(*done), out_gather.step(*done), out_gather.swap(*done))
        gate_tie = sent
    x, y, states, slope, mark = written
    if hypercube:
        gate, w_gate, zg, squares = gate_project(
            after(normed, *gate_tie), gate_gather.pieces(), order, y, full_gain_out, mark, None, 0, di
        )
    else:
        w_gate = full_w_in[:, :di]
        gate = mm(normed, w_gate)
        gated = y.astype(F32) * (gate * jax.nn.sigmoid(gate))
        squares = gated * gated
        zg = (gated * full_gain_out).astype(BF16)
    inverse = lax.rsqrt(jnp.sum(squares, axis=1, keepdims=True) / di + EPSILON)
    cot = cotangent.astype(F32)
    cot_scaled = (inverse * cot).astype(BF16)
    sums = None
    parts = {}
    if hypercube:
        in_block = w_in.shape[0] // 2
        out_tie, out_got = out_gather.swap(cot_scaled)
        out_grad = weight_grad(zg, after(cot_scaled, out_tie), place, 0, model)
        out_sum = Scatter(out_grad, w_out.shape[0] // 2)
        sent, got = out_sum.step(*out_gather.swapped)
        full_w_out, output, dots = output_project(
            after(zg, sent), inverse, tokens, cotangent, out_gather.pieces(), order
        )
        sent, got = out_sum.step(got, dots)
        less = inverse * inverse * dots / di
        dy, dgate = gate_back(
            after(cotangent, sent), full_w_out, gate, y, full_gain_out, inverse, less
        )
    else:
        projected = inverse * mm(zg, full_w_out)
        output = (inputs + projected).astype(BF16)
        dots = jnp.sum(cot * projected, axis=1, keepdims=True)
        grad_ynorm = mm_nt(cotangent, full_w_out)
        y, gate = y.astype(F32), gate.astype(F32)
        sig = jax.nn.sigmoid(gate)
        dz = inverse * (full_gain_out * grad_ynorm) - (y * (gate * sig)) * (inverse * inverse * dots / di)
        dy = (dz * (gate * sig)).astype(BF16)
        dgate = (dz * y * (sig * (1.0 + gate * (1.0 - sig)))).astype(BF16)
    if hypercube:
        gate_grad = weight_grad(normed, after(dgate, got), place, 0, di)
        gate_sum = Scatter(gate_grad, in_block)
        sent, gate_got = gate_sum.step()
        scaled = mm_nt(after(dgate, sent), w_gate)
        sent, got = zip(out_sum.step(got, scaled), gate_sum.step(gate_got, scaled))
        dy = after(dy, *sent, gate_got, scaled)
    else:
        scaled = mm_nt(dgate, w_gate)
    grad_sums = {}
    for index, call in reversed(list(enumerate(calls))):
        pc, first_x = pcs[index]
        dpart, dcw, dskip, *sums = run_backward(
            dy, x, bcv, states, slope, bc_slope, pc, first_x, pcs[0][0], conv_x, conv_bc,
            same, seg_col, seg_row, heads, skip, (cum, shifted, cum_lines), *call, index == 0, sums,
        )
        parts[index] = (dpart, dcw, dskip)
        if not hypercube:
            scaled = scaled + mm_nt(dpart, w_parts[index])
            continue
        done = *got, dpart
        if index == 2:
            sent, out_got = out_sum.step(*done)
            early = (sent, *done)
        elif index == 1:
            sent, gate_got = gate_sum.step(*done)
            early = (sent, *done)
        else:
            sent, late = grad_sums[1].step(*got)
            early = (sent, *got)
        grad = weight_grad(normed, after(dpart, *early), place, 0, dpart.shape[1])
        grad_sums[index] = Scatter(grad, in_block)
        swap_sent, swap_got = grad_sums[index].step()
        if index == 2:
            scaled = scaled + mm_nt(after(dpart, swap_sent), w_parts[index])
            done = swap_got, scaled
            sent, got = zip(out_sum.step(out_got, *done), gate_sum.step(got[1], *done), grad_sums[2].step(*done))
            dy = after(dy, *sent, *done)
        elif index == 1:
            sent, got = zip(gate_sum.step(gate_got, swap_sent), grad_sums[2].step(got[2], swap_sent))
            got = got + (swap_got,)
            dy = after(dy, *sent, swap_sent)
        else:
            sent, late = zip(grad_sums[1].step(late, swap_sent), grad_sums[2].step(swap_sent))
            sent, got = grad_sums[0].step(swap_got, *sent)
            scaled = scaled + mm_nt(after(dpart, sent), w_parts[index])
    dbcw, dhead = after(tuple(sums), swap_sent) if hypercube else sums
    dbcw, dhead = after(tuple(sums), swap_sent) if hypercube else sums
    dcw = jnp.concatenate([parts[index][1] for index in range(len(calls))] + [dbcw], axis=2)
    dskip = jnp.concatenate([parts[index][2] for index in range(len(calls))], axis=1)
    if hypercube:
        ties = [swap_sent, sent]
        sent, got = grad_sums[0].step(got, scaled)
        ties.append(sent)
        sent, late = zip(grad_sums[1].step(*late, sent), grad_sums[2].step(*late, sent))
        late = late[0]
        scaled = scaled + mm_nt(after(parts[1][0], *sent), w_parts[1])
    scaled = scaled * full_gain_in
    inner = jnp.mean(unit * scaled, axis=1, keepdims=True)
    grad_tokens = (cot + rscale * (scaled - unit * inner)).astype(BF16)

    conv_sums = dcw.sum(1)
    conv_sums = jnp.concatenate([conv_sums[4:5], conv_sums[3:4], conv_sums[2:3], conv_sums[1:2], conv_sums[0:1]])
    per_head = jnp.concatenate(
        [
            dhead[0].sum(0)[:H],
            dhead[1].sum(0)[:H] * -jnp.exp(a_log),
            dskip.sum(0).reshape(H, P_SIZE).sum(1),
        ]
    )
    conv_part = conv_sums.reshape(taps + 1, shards, conv_local).transpose(1, 0, 2).reshape(shards, -1)
    small_grad = jnp.concatenate([conv_part, jnp.broadcast_to(per_head[None], (shards, 3 * H))], axis=1)
    real = w_in.shape[1] - 2 * di
    if hypercube:
        last_sent, got = grad_sums[0].step(got, grad_tokens)
        ties.append(last_sent)
        grad_sums[1].step(late, last_sent)
        end_sent, _ = grad_sums[0].step(got)
        ties.append(end_sent)
        small_sum = reduce_small(small_grad, ties)[0]
        whole = [each.finish(end_sent) for each in (gate_sum, grad_sums[2], grad_sums[1])]
        whole = [both_cores(part) for part in whole + [grad_sums[0].finish()]]
        head = whole.pop()
        whole = [whole[0], head[:, 4 * N :], whole[2], whole[1], head[:, :real]]
        sum_w_in = jnp.concatenate(whole, axis=1)
        edges = [0, di, di + width, di + 3 * width, 2 * di, w_in.shape[1]]
        gain_sum = 0.0
        for part, a, b in zip(whole, edges, edges[1:]):
            gain_sum = gain_sum + jnp.sum(part * w_in[:, a:b].astype(F32), axis=1)
        sum_w_out = both_cores(out_sum.finish(grad_sums[1].terms[0]))
    else:
        grad_w_out = dot_f32(zg, cot_scaled, ((0,), (0,)))
        rest = [parts[index][0] for index in range(len(calls))]
        grads = jnp.concatenate([dgate, rest[0][:, 4 * N :], *rest[1:], rest[0][:, :real]], axis=1)
        grad_w_in = dot_f32(normed, grads, ((0,), (0,)))
        small_sum = lax.psum(
            lax.psum_scatter(small_grad, "shard", scatter_dimension=0, tiled=True), "rep"
        )[0]
        sum_w_in = lax.psum_scatter(grad_w_in, "shard", scatter_dimension=0, tiled=True)
        sum_w_out = lax.psum_scatter(grad_w_out, "shard", scatter_dimension=0, tiled=True)
        sum_w_in, sum_w_out = lax.psum((sum_w_in, sum_w_out), "rep")
        gain_sum = jnp.sum(sum_w_in * w_in.astype(F32), axis=1)
    grad_gain_in = gain_sum / gain_in.astype(F32)
    grad_gain_out = jnp.sum(sum_w_out * w_out.astype(F32), axis=1) / gain_out.astype(F32)
    cut = taps * conv_local
    head_at = cut + conv_local
    return (
        output,
        grad_tokens,
        grad_gain_in,
        sum_w_in,
        small_sum[:cut].reshape(taps, conv_local),
        small_sum[cut:head_at],
        small_sum[head_at : head_at + H],
        small_sum[head_at + H : head_at + 2 * H],
        small_sum[head_at + 2 * H :],
        grad_gain_out,
        sum_w_out,
    )


def both_cores(own):
    partner = swap_cores(own)
    first = lax.axis_index("rep") == 0
    return jnp.concatenate([jnp.where(first, own, partner), jnp.where(first, partner, own)], axis=0)


def reduce_small(rows, ties):
    core = lax.axis_index("rep")
    places = jnp.asarray([reach(order) for order in ORDERS], jnp.int32)[core] ^ lax.axis_index("shard")
    hot = (places[:, None] == jnp.arange(16, dtype=jnp.int32)[None, :]).astype(F32)
    total = dot_f32(hot, rows, ((1,), (0,)), HIGHEST)
    for stage, tie in zip((3, 2, 1, 0), ties[:4]):
        cut = 1 << stage
        total = after(total, tie)
        total = total[:cut] + exchange(total[cut:], stage)
    total = after(total, ties[4])
    return total + swap_cores(total)


def solution(mesh):
    rows = P(("shard", "rep"), None)
    in_specs = (
        rows, rows, P("shard"), P("shard", None), P(None, "shard"), P("shard"), P(), P(), P(), P("shard"),
        P("shard", None), rows,
    )
    out_specs = (
        rows, rows, P("shard"), P("shard", None), P(None, "shard"), P("shard"), P(), P(), P(), P("shard"),
        P("shard", None),
    )
    hypercube = mesh.shape["shard"] == 16 and mesh.shape["rep"] == 2
    return jax.shard_map(
        functools.partial(on_device, hypercube),
        mesh=mesh,
        in_specs=in_specs,
        out_specs=out_specs,
        check_vma=False,
    )
```

```python
import functools

import jax
import jax.numpy as jnp
from jax import lax
from jax.experimental import pallas as pl
from jax.experimental.pallas import tpu as pltpu
from jax.sharding import PartitionSpec as P
from jax.sharding import PartitionSpec as P

H = 48
P_SIZE = 64
N = 128
SPAN = 256
HALF = 128
GROUP = 8
TILE = 128
EPSILON = 1e-05
HIGHEST = lax.Precision.HIGHEST
LOG2E = 1.4426950408889634
NEG = -1e30
F32 = jnp.float32
BF16 = jnp.bfloat16


def dot_f32(a, b, contract, precision=None):
    return lax.dot_general(
        a, b, ((contract[0], contract[1]), ((), ())), preferred_element_type=F32, precision=precision
    )


def mm(a, b):
    return dot_f32(a, b, ((1,), (0,)))


def mm_nt(a, b):
    return dot_f32(a, b, ((1,), (1,)))


def lanes_of(column, rows):
    return jnp.broadcast_to(column, (rows, TILE))


def step_sizes(raw, heads):
    shifted = raw + heads[0:1]
    return jnp.maximum(shifted, 0.0) + jnp.log1p(jnp.exp(-jnp.abs(shifted)))


def conv_taps(ext, same, start, width, rows=SPAN):
    out = [ext[8 : 8 + rows, start : start + width]]
    for offset in (1, 2, 3):
        moved = ext[8 - offset : 8 - offset + rows, start : start + width]
        mask = same[offset - 1]
        if width > TILE:
            mask = jnp.concatenate([mask] * (width // TILE), axis=1)
        out.append(moved * mask)
    return out


def conv_sum(taps, weights):
    total = weights[4:5] + weights[3:4] * taps[0]
    for offset in (1, 2, 3):
        total = total + weights[3 - offset : 4 - offset] * taps[offset]
    return total


def prepare(raw_ref, heads_ref):
    heads = heads_ref[...]
    step = step_sizes(raw_ref[...], heads)
    row = lax.broadcasted_iota(jnp.int32, (SPAN, SPAN), 0)
    col = lax.broadcasted_iota(jnp.int32, (SPAN, SPAN), 1)
    tri = (row >= col).astype(F32)
    cum = dot_f32(tri, step * heads[1:2], ((1,), (0,)), HIGHEST)
    return cum, cum - jnp.log2(step)


def pick(first, columns, at):
    return jnp.where(first, lanes_of(columns[:, at : at + 1], first.shape[0]), lanes_of(columns[:, at + 1 : at + 2], first.shape[0]))


def forward_kernel(first_call, base, pc_ref, halo_ref, cw_ref, same, seg_col_ref, seg_ref, skip_ref, *rest):
    rest = list(rest)
    if first_call:
        raw_ref, heads_ref, bc_ref, bc_halo_ref, bcw_ref = [rest.pop(0) for _ in range(5)]
        x_out, y_out, st_out, slope_out, mark, bc_out, bc_slope_out = [rest.pop(0) for _ in range(7)]
        pack, shifted_out, cum_out, cum_rows, w_rows = [rest.pop(0) for _ in range(5)]
    else:
        bc_out, pack, cum_rows, w_rows = [rest.pop(0) for _ in range(4)]
        mark_ref = rest[4]
        rest = rest[5:]
        x_out, y_out, st_out, slope_out, mark = [rest.pop(0) for _ in range(5)]
    state, scores, block, keep_row, b_t, ext, ext_bc = rest
    span = pl.program_id(0)
    group = pl.program_id(1)
    group_head = base + GROUP * group

    @pl.when((span == 0) & (group == 0))
    def _():
        state[...] = jnp.zeros_like(state)
        mark[...] = jnp.zeros_like(mark) if first_call else mark_ref[...]

    @pl.when(group == 0)
    def _():
        if first_call:
            cum, shifted = prepare(raw_ref, heads_ref)
            pack[...] = cum
            shifted_out[...] = shifted
            cum_out[...] = cum.T
            cum_rows[...] = shifted.T
            w_rows[...] = (jnp.exp2(cum[SPAN - 1 : SPAN] - shifted) * same[4]).T
        last = pack[SPAN - 1 : SPAN]
        keep_row[...] = jnp.broadcast_to(jnp.exp2(last) * same[3, SPAN - 1 : SPAN], (8, TILE))
        if first_call:
            ext_bc[0:8] = bc_halo_ref[...]
            ext_bc[8:] = bc_ref[...]
            total = conv_sum(conv_taps(ext_bc, same, 0, 2 * N), bcw_ref[...])
            gate = jax.nn.sigmoid(total)
            both = total * gate
            bc_out[...] = both.astype(BF16)
            bc_slope_out[...] = (gate + both * (1.0 - gate)).astype(BF16)
        row = lax.broadcasted_iota(jnp.int32, (SPAN, SPAN), 0)
        col = lax.broadcasted_iota(jnp.int32, (SPAN, SPAN), 1)
        linked = (row >= col) & (seg_col_ref[...] == seg_ref[...])
        block[...] = jnp.where(linked, 0.0, NEG)
        scores[...] = mm_nt(bc_out[:, N:], bc_out[:, :N])
        b_t[...] = bc_out[:, :N].astype(F32).T

    ext[0:8] = halo_ref[...]
    ext[8:] = pc_ref[...]
    shift = lax.rem(TILE - group_head, TILE)
    cums = pltpu.roll(pack[...], shift, 1)
    keep = jnp.broadcast_to(pltpu.roll(keep_row[...], shift, 1)[0:1], (N, TILE))
    first = lax.broadcasted_iota(jnp.int32, (SPAN, TILE), 1) < P_SIZE
    query = bc_out[:, N:]
    empty = jnp.zeros((HALF, HALF), BF16)
    wide = lambda parts: jnp.concatenate(parts, axis=1)
    for quad in range(GROUP // 4):
        xbs, outs, entries, keeps, fresh = [], [], [], [], []
        for pair in (2 * quad, 2 * quad + 1):
            at = pair * TILE
            total = conv_sum(conv_taps(ext, same, at, TILE), cw_ref[:, at : at + TILE])
            gate = jax.nn.sigmoid(total)
            x = total * gate
            xb = x.astype(BF16)
            x_out[:, at : at + TILE] = xb
            slope_out[:, at : at + TILE] = (gate + x * (1.0 - gate)).astype(BF16)
            mixes, weighted, cum_cols = [], [], []
            for head in (2 * pair, 2 * pair + 1):
                cum_col = lanes_of(cums[:, head : head + 1], SPAN)
                cum_cols.append(cum_col)
                cum_row = cum_rows[pl.ds(group_head + head, 1), :]
                blocks = []
                for i, j in ((0, 0), (1, 0), (1, 1)):
                    rows = slice(i * HALF, (i + 1) * HALF)
                    cols = slice(j * HALF, (j + 1) * HALF)
                    gap = cum_col[rows] - cum_row[:, cols] + block[rows, cols]
                    blocks.append((jnp.exp2(gap) * scores[rows, cols]).astype(BF16))
                mixes.append(wide([blocks[0], empty]))
                mixes.append(wide(blocks[1:]))
                weighted.append((b_t[...] * w_rows[pl.ds(group_head + head, 1), :]).astype(BF16))
            inner = mm(jnp.concatenate(mixes + weighted, axis=0), xb)
            outs.append(jnp.where(first, inner[:SPAN], inner[SPAN : 2 * SPAN]))
            fresh.append(jnp.where(first[:N], inner[2 * SPAN : 2 * SPAN + N], inner[2 * SPAN + N :]))
            xbs.append(xb)
            entries.append(jnp.exp2(jnp.where(first, cum_cols[0], cum_cols[1])) * same[3])
            keeps.append(pick(first[:N], keep, 2 * pair))
        both = slice(quad * 2 * TILE, (quad + 1) * 2 * TILE)
        tile = pl.ds(pl.multiple_of(group * GROUP * P_SIZE + quad * 2 * TILE, 2 * TILE), 2 * TILE)
        old = state[:, tile]
        old_b = old.astype(BF16)
        st_out[:, both] = old_b
        carried = mm(query, old_b)
        y = wide(outs) + wide(entries) * carried + skip_ref[:, both] * wide(xbs).astype(F32)
        y_out[:, both] = y.astype(BF16)
        state[:, tile] = old * wide(keeps) + wide(fresh)


def run_forward(pc, first_x, pc_bc, conv_x, conv_bc, same, seg_col, seg_row, heads, skip, start, count, shared, before):
    tokens = pc.shape[0]
    spans = tokens // SPAN
    di = skip.shape[1]
    width = GROUP * P_SIZE
    own = count * width
    first_call = before is None
    any_spec = pl.BlockSpec(memory_space=pl.ANY)
    halo = lambda s: jnp.maximum(s * (SPAN // 8) - 1, 0)
    wide = pl.BlockSpec((SPAN, width), lambda s, g: (s, start + g))
    bcv_spec = pl.BlockSpec((SPAN, 2 * N), lambda s, g: (s, 0))
    in_specs = [
        pl.BlockSpec((SPAN, width), lambda s, g: (s, first_x + g)),
        pl.BlockSpec((8, width), lambda s, g: (halo(s), first_x + g)),
        pl.BlockSpec((8, width), lambda s, g: (0, start + g)),
        pl.BlockSpec((5, SPAN, TILE), lambda s, g: (0, s, 0)),
        pl.BlockSpec((SPAN, 1), lambda s, g: (s, 0)),
        pl.BlockSpec((1, SPAN), lambda s, g: (0, s)),
        pl.BlockSpec((1, width), lambda s, g: (0, start + g)),
    ]
    args = [pc, pc, conv_x, same, seg_col, seg_row, skip]
    column_spec = pl.BlockSpec((SPAN, TILE), lambda s, g: (s, 0))
    row_spec = pl.BlockSpec((TILE, SPAN), lambda s, g: (s, 0))
    columns_shape = jax.ShapeDtypeStruct((tokens, TILE), F32)
    rows_shape = jax.ShapeDtypeStruct((spans * TILE, SPAN), F32)
    mark_spec = pl.BlockSpec((8, TILE), lambda s, g: (0, 0))
    out_specs = [wide, wide, pl.BlockSpec((N, width), lambda s, g: (s, start + g)), wide, mark_spec]
    out_shape = [
        jax.ShapeDtypeStruct((tokens, di), BF16),
        jax.ShapeDtypeStruct((tokens, di), BF16),
        jax.ShapeDtypeStruct((spans * N, di), BF16),
        jax.ShapeDtypeStruct((tokens, di), BF16),
        jax.ShapeDtypeStruct((8, TILE), F32),
    ]
    if first_call:
        in_specs += [
            pl.BlockSpec((SPAN, TILE), lambda s, g: (s, 2)),
            pl.BlockSpec((8, TILE), lambda s, g: (0, 0)),
            pl.BlockSpec((SPAN, 2 * N), lambda s, g: (s, 0)),
            pl.BlockSpec((8, 2 * N), lambda s, g: (halo(s), 0)),
            pl.BlockSpec((8, 2 * N), lambda s, g: (0, 0)),
        ]
        args += [pc_bc, heads, pc_bc, pc_bc, conv_bc]
        out_specs += [bcv_spec, bcv_spec, column_spec, column_spec, row_spec, row_spec, row_spec]
        out_shape += [jax.ShapeDtypeStruct((tokens, 2 * N), BF16)] * 2
        out_shape += [columns_shape] * 2 + [rows_shape] * 3
        aliases = {}
    else:
        in_specs += [bcv_spec, column_spec, row_spec, row_spec, any_spec, any_spec, any_spec, any_spec, mark_spec]
        args += [*shared, *before]
        aliases = {11: 0, 12: 1, 13: 2, 14: 3}
    return pl.pallas_call(
        functools.partial(forward_kernel, first_call, start * GROUP),
        grid_spec=pltpu.PrefetchScalarGridSpec(
            num_scalar_prefetch=0,
            grid=(spans, count),
            in_specs=in_specs,
            out_specs=out_specs,
            scratch_shapes=[
                pltpu.VMEM((N, own), F32),
                pltpu.VMEM((SPAN, SPAN), F32),
                pltpu.VMEM((SPAN, SPAN), F32),
                pltpu.VMEM((8, TILE), F32),
                pltpu.VMEM((N, SPAN), F32),
                pltpu.VMEM((SPAN + 8, width), F32),
                pltpu.VMEM((SPAN + 8, 2 * N), F32),
            ],
        ),
        out_shape=out_shape,
        input_output_aliases=aliases,
        compiler_params=pltpu.CompilerParams(dimension_semantics=("arbitrary", "arbitrary")),
        cost_estimate=pl.CostEstimate(flops=int(5e9 * count), bytes_accessed=14 * tokens * own, transcendentals=0),
        name="scan_forward",
    )(*args)


def conv_back(grad, slope, signal, same, weights, carry):
    width = grad.shape[1]
    du = grad * slope.astype(F32)

    def add_rows(values):
        return jnp.sum(values.reshape(SPAN // 8, 8, width), axis=0)

    out = weights[3:4] * du
    sums = [add_rows(du), add_rows(du * signal)]
    for offset in (1, 2, 3):
        mask = same[offset - 1]
        if width > TILE:
            mask = jnp.concatenate([mask] * (width // TILE), axis=1)
        masked = du * mask
        moved = jnp.concatenate([masked, carry[offset - 1]], axis=0)[offset : offset + SPAN]
        carry[offset - 1] = masked[0:8]
        out = out + weights[3 - offset : 4 - offset] * moved
        sums.append(add_rows(moved * signal))
    return out, sums


def backward_kernel(
    first_call, last_call, base,
    dy_ref, x_ref, bcv_ref, st_ref, slope_ref, pc_ref, cw_ref, same, seg_col_ref, seg_ref, skip_ref,
    cum_ref, shifted_ref, cum_rows, *rest,
):
    rest = list(rest)
    before = None if first_call else [rest.pop(0) for _ in range(4)]
    if last_call:
        raw_ref, heads_ref, bc_ref, bc_slope_ref, bcw_ref = [rest.pop(0) for _ in range(5)]
    dproj_out, dcw_out, dskip_out = [rest.pop(0) for _ in range(3)]
    if last_call:
        dbcw_out, dhead_out = [rest.pop(0) for _ in range(2)]
    else:
        after_out = [rest.pop(0) for _ in range(4)]
    (
        dstate, scores, block, dscores, pack, c_t,
        carry, carry_bc, d_bc, per_row, dcum_rows, dlast,
    ) = rest
    back = pl.program_id(0)
    group = pl.program_id(1)
    groups = pl.num_programs(1)
    width = GROUP * P_SIZE
    group_head = base + GROUP * group
    first_x = 4 * N if last_call else 0

    @pl.when((back == 0) & (group == 0))
    def _():
        dstate[...] = jnp.zeros_like(dstate)
        carry[...] = jnp.zeros_like(carry)
        dcw_out[...] = jnp.zeros_like(dcw_out)
        dskip_out[...] = jnp.zeros_like(dskip_out)
        dcum_rows[...] = jnp.zeros_like(dcum_rows)
        if last_call:
            carry_bc[...] = jnp.zeros_like(carry_bc)
            dbcw_out[...] = jnp.zeros_like(dbcw_out)
            dhead_out[...] = jnp.zeros_like(dhead_out)

    keys = bcv_ref[:, :N]
    query = bcv_ref[:, N:]
    lane = lax.broadcasted_iota(jnp.int32, (SPAN, TILE), 1)

    @pl.when(group == 0)
    def _():
        entry = jnp.exp2(cum_ref[...]) * same[3]
        pack[...] = jnp.where(lane < 64, shifted_ref[...], pltpu.roll(entry, 64, 1))
        row = lax.broadcasted_iota(jnp.int32, (SPAN, SPAN), 0)
        col = lax.broadcasted_iota(jnp.int32, (SPAN, SPAN), 1)
        linked = (row <= col) & (seg_col_ref[...] == seg_ref[...])
        block[...] = jnp.where(linked, 0.0, NEG)
        scores[...] = mm_nt(keys, query)
        c_t[...] = query.T
        per_row[...] = jnp.zeros_like(per_row)
        if first_call:
            dscores[...] = jnp.zeros_like(dscores)
            d_bc[...] = jnp.zeros_like(d_bc)
            dlast[...] = jnp.zeros_like(dlast)
        else:
            dscores[...] = before[0][...]
            d_bc[...] = before[1][...]
            per_row[0] = before[2][:, :TILE]
            per_row[2] = before[2][:, TILE:]
            dlast[...] = before[3][...]

    shift = lax.rem(TILE - group_head, TILE)
    cols = pltpu.roll(pack[...], shift, 1)
    last_cum = pltpu.roll(jnp.broadcast_to(cum_ref[SPAN - 1 : SPAN], (8, TILE)), shift, 1)[0:1]
    keep_mask = same[3, SPAN - 1 : SPAN]
    first = lane < P_SIZE
    lane_row = lax.broadcasted_iota(jnp.int32, (2 * TILE, TILE), 0) // P_SIZE
    lane_col = lax.broadcasted_iota(jnp.int32, (2 * TILE, TILE), 1)
    sums = jnp.zeros((SPAN, TILE), F32)
    last_sum = jnp.zeros((1, TILE), F32)
    group_at = group * width
    empty = jnp.zeros((HALF, HALF), BF16)
    wide = lambda parts: jnp.concatenate(parts, axis=1)
    for quad in range(GROUP // 4):
        both = slice(quad * 2 * TILE, (quad + 1) * 2 * TILE)
        tile = pl.ds(pl.multiple_of(group_at + quad * 2 * TILE, 2 * TILE), 2 * TILE)
        entries, tails, keeps, inners = [], [], [], []
        for pair in (2 * quad, 2 * quad + 1):
            at = pair * TILE
            heads = (2 * pair, 2 * pair + 1)
            dy_pair = dy_ref[:, at : at + TILE]
            xb = x_ref[:, at : at + TILE]
            nothing = jnp.zeros_like(xb)
            split = jnp.concatenate([jnp.where(first, xb, nothing), jnp.where(first, nothing, xb)], axis=0)
            g_both = mm_nt(split, dy_pair)
            cum_cols = [lanes_of(cols[:, head : head + 1], SPAN) for head in heads]
            cum_lines = [cum_rows[pl.ds(group_head + head, 1), :] for head in heads]
            mixes = [[], []]
            across = [[], []]
            down = [[], []]
            for j, i in ((0, 0), (0, 1), (1, 1)):
                rows = slice(j * HALF, (j + 1) * HALF)
                cells = slice(i * HALF, (i + 1) * HALF)
                spread = jnp.zeros((HALF, HALF), F32)
                for which in (0, 1):
                    decay = jnp.exp2(cum_lines[which][:, cells] - cum_cols[which][rows] + block[rows, cells])
                    mix = decay * scores[rows, cells]
                    g = g_both[which * SPAN + j * HALF : which * SPAN + (j + 1) * HALF, cells]
                    spread = spread + decay * g
                    w = mix * g
                    mixes[which].append(mix.astype(BF16))
                    across[which].append(w)
                    down[which].append(jnp.sum(w, axis=0, keepdims=True))
                dscores[rows, cells] += spread
            lefts = []
            for which in (0, 1):
                row_sum = jnp.concatenate(
                    [
                        jnp.sum(across[which][0] + across[which][1], axis=1, keepdims=True),
                        jnp.sum(across[which][2], axis=1, keepdims=True),
                    ],
                    axis=0,
                )
                sums = sums - jnp.where(lane == 2 * GROUP + heads[which], row_sum, 0.0)
                dcum_rows[pl.ds(group_head + heads[which], 1), :] = wide(
                    [down[which][0], down[which][1] + down[which][2]]
                )
                lefts += [wide(mixes[which][:2]), wide([empty, mixes[which][2]])]
            inner = mm(jnp.concatenate(lefts, axis=0), dy_pair)
            inners.append(jnp.where(first, inner[:SPAN], inner[SPAN:]))
            last_pair = jnp.where(
                first[0:1],
                jnp.broadcast_to(last_cum[:, heads[0] : heads[0] + 1], (1, TILE)),
                jnp.broadcast_to(last_cum[:, heads[1] : heads[1] + 1], (1, TILE)),
            )
            tails.append(jnp.exp2(last_pair - jnp.where(first, cum_cols[0], cum_cols[1])) * same[4])
            keeps.append(jnp.exp2(last_pair) * keep_mask)
            entries.append(pick(first, cols, 64 + 2 * pair))
        dyf = dy_ref[:, both].astype(F32)
        xf = x_ref[:, both].astype(F32)
        tail = wide(tails)
        stb = st_ref[:, both]
        ds = dstate[:, tile]
        dsb = ds.astype(BF16)
        dye_f = dyf * wide(entries)
        dye = dye_f.astype(BF16)
        fresh = mm(keys, dsb) * tail
        total = wide(inners) + fresh
        d_bc[:, N:] += mm_nt(dye, stb)
        d_bc[:, :N] += mm_nt((xf * tail).astype(BF16), dsb)

        def head_sum(values, kind):
            spread = (lane_col == kind * GROUP + 4 * quad + lane_row).astype(BF16)
            return mm(values.astype(BF16), spread)

        sums = sums + head_sum(xf * total, 0) + head_sum(xf * fresh, 1) + head_sum(dye_f * mm(query, stb), 2)
        kept = ds * wide(keeps)
        kept_sum = jnp.sum(kept * stb.astype(F32), axis=0, keepdims=True)
        lane_pair = lax.broadcasted_iota(jnp.int32, (1, 2 * TILE), 1) // P_SIZE
        for head in range(4):
            one = jnp.sum(jnp.where(lane_pair == head, kept_sum, 0.0), axis=1, keepdims=True)
            last_sum = last_sum + jnp.where(lane[0:1] == 4 * quad + head, one, 0.0)
        dstate[:, tile] = kept + mm(c_t[...], dye)
        dskip_out[:, tile] += jnp.sum((dyf * xf).reshape(SPAN // 8, 8, 2 * TILE), axis=0)
        dx = total + skip_ref[:, both] * dyf
        for part in (0, 1):
            at = (2 * quad + part) * TILE
            one = pl.ds(pl.multiple_of(group_at + at, TILE), TILE)
            out, conv_sums = conv_back(
                dx[:, part * TILE : (part + 1) * TILE], slope_ref[:, at : at + TILE], pc_ref[:, at : at + TILE],
                same, cw_ref[:, at : at + TILE], carry.at[:, :, one],
            )
            dproj_out[:, pl.ds(pl.multiple_of(first_x + group_at + at, TILE), TILE)] = out.astype(BF16)
            for k, value in enumerate(conv_sums):
                dcw_out[k, :, one] += value

    in_place = (lane >= group_head) & (lane < group_head + GROUP)
    for kind in range(3):
        moved = pltpu.roll(sums, lax.rem(group_head + TILE - GROUP * kind, TILE), 1)
        per_row[kind] += jnp.where(in_place, moved, 0.0)
    moved = pltpu.roll(jnp.broadcast_to(last_sum, (8, TILE)), group_head, 1)
    dlast[...] += jnp.where(in_place[0:8], moved, 0.0)

    @pl.when(group == groups - 1)
    def _():
        state_part = per_row[1]
        dcum = dcum_rows[...].T + per_row[2] - state_part
        dlast_all = dlast[0:1] + jnp.sum(state_part, axis=0, keepdims=True)
        if not last_call:
            after_out[0][...] = dscores[...]
            after_out[1][...] = d_bc[...]
            after_out[2][:, :TILE] = per_row[0]
            after_out[2][:, TILE:] = dcum
            after_out[3][...] = jnp.broadcast_to(dlast_all, (8, TILE))
            return
        ds_b = dscores[...].astype(BF16)
        grad_b = d_bc[:, :N] + mm(ds_b, query)
        grad_c = d_bc[:, N:] + mm(dscores[...].T.astype(BF16), keys)
        out, conv_sums = conv_back(
            wide([grad_b, grad_c]), bc_slope_ref[...], bc_ref[...], same, bcw_ref[...], carry_bc
        )
        dproj_out[:, : 2 * N] = out.astype(BF16)
        for k, value in enumerate(conv_sums):
            dbcw_out[k] += value
        heads = heads_ref[...]
        shifted = raw_ref[...] + heads[0:1]
        step = step_sizes(raw_ref[...], heads)
        slope = jax.nn.sigmoid(shifted)
        row = lax.broadcasted_iota(jnp.int32, (SPAN, SPAN), 0)
        col = lax.broadcasted_iota(jnp.int32, (SPAN, SPAN), 1)
        tri = (row <= col).astype(F32)
        da = dot_f32(tri, dcum, ((1,), (0,)), HIGHEST) + dlast_all
        small = shifted < -16.0
        ratio = jnp.where(small, 1.0, slope / jnp.where(small, 1.0, step))
        live = lane < H
        draw = jnp.where(live, per_row[0] * ratio + da * heads[2:3] * slope, 0.0)
        dproj_out[:, 2 * N : 3 * N] = draw.astype(BF16)
        dproj_out[:, 3 * N : 4 * N] = jnp.zeros((SPAN, N), BF16)
        dhead_out[0] += jnp.sum(draw.reshape(SPAN // 8, 8, TILE), axis=0)
        dhead_out[1] += jnp.sum(jnp.where(live, da * step, 0.0).reshape(SPAN // 8, 8, TILE), axis=0)


def run_backward(
    dy, x, bcv, states, slope, bc_slope, pc, first_x, pc_bc, conv_x, conv_bc, same, seg_col, seg_row, heads, skip,
    cums, start, count, last, before,
):
    tokens, di = dy.shape
    spans = tokens // SPAN
    width = GROUP * P_SIZE
    turn = lambda s: spans - 1 - s
    own = count * width
    out_width = own + (4 * N if last else 0)
    sums_specs = [
        pl.BlockSpec((SPAN, SPAN), lambda s, g: (turn(s), 0)),
        pl.BlockSpec((SPAN, 2 * N), lambda s, g: (turn(s), 0)),
        pl.BlockSpec((SPAN, 2 * TILE), lambda s, g: (turn(s), 0)),
        pl.BlockSpec((8, TILE), lambda s, g: (turn(s), 0)),
    ]
    sums_shapes = [
        jax.ShapeDtypeStruct((tokens, SPAN), F32),
        jax.ShapeDtypeStruct((tokens, 2 * N), F32),
        jax.ShapeDtypeStruct((tokens, 2 * TILE), F32),
        jax.ShapeDtypeStruct((spans * 8, TILE), F32),
    ]
    out_specs = [
        pl.BlockSpec((SPAN, out_width), lambda s, g: (turn(s), 0)),
        pl.BlockSpec((5, 8, own), lambda s, g: (0, 0, 0)),
        pl.BlockSpec((8, own), lambda s, g: (0, 0)),
    ]
    out_shape = [
        jax.ShapeDtypeStruct((tokens, out_width), BF16),
        jax.ShapeDtypeStruct((5, 8, own), F32),
        jax.ShapeDtypeStruct((8, own), F32),
    ]
    wide = pl.BlockSpec((SPAN, width), lambda s, g: (turn(s), start + g))
    in_specs = [
        wide,
        wide,
        pl.BlockSpec((SPAN, 2 * N), lambda s, g: (turn(s), 0)),
        pl.BlockSpec((N, width), lambda s, g: (turn(s), start + g)),
        wide,
        pl.BlockSpec((SPAN, width), lambda s, g: (turn(s), first_x + g)),
        pl.BlockSpec((8, width), lambda s, g: (0, start + g)),
        pl.BlockSpec((5, SPAN, TILE), lambda s, g: (0, turn(s), 0)),
        pl.BlockSpec((SPAN, 1), lambda s, g: (turn(s), 0)),
        pl.BlockSpec((1, SPAN), lambda s, g: (0, turn(s))),
        pl.BlockSpec((1, width), lambda s, g: (0, start + g)),
        pl.BlockSpec((SPAN, TILE), lambda s, g: (turn(s), 0)),
        pl.BlockSpec((SPAN, TILE), lambda s, g: (turn(s), 0)),
        pl.BlockSpec((TILE, SPAN), lambda s, g: (turn(s), 0)),
    ]
    args = [dy, x, bcv, states, slope, pc, conv_x, same, seg_col, seg_row, skip, *cums]
    if before is not None:
        in_specs += sums_specs
        args += before
    if last:
        in_specs += [
            pl.BlockSpec((SPAN, TILE), lambda s, g: (turn(s), 2)),
            pl.BlockSpec((8, TILE), lambda s, g: (0, 0)),
            pl.BlockSpec((SPAN, 2 * N), lambda s, g: (turn(s), 0)),
            pl.BlockSpec((SPAN, 2 * N), lambda s, g: (turn(s), 0)),
            pl.BlockSpec((8, 2 * N), lambda s, g: (0, 0)),
        ]
        args += [pc_bc, heads, pc_bc, bc_slope, conv_bc]
        out_specs += [
            pl.BlockSpec((5, 8, 2 * N), lambda s, g: (0, 0, 0)),
            pl.BlockSpec((2, 8, TILE), lambda s, g: (0, 0, 0)),
        ]
        out_shape += [
            jax.ShapeDtypeStruct((5, 8, 2 * N), F32),
            jax.ShapeDtypeStruct((2, 8, TILE), F32),
        ]
    else:
        out_specs += sums_specs
        out_shape += sums_shapes
    return pl.pallas_call(
        functools.partial(backward_kernel, before is None, last, start * GROUP),
        grid_spec=pltpu.PrefetchScalarGridSpec(
            num_scalar_prefetch=0,
            grid=(spans, count),
            in_specs=in_specs,
            out_specs=out_specs,
            scratch_shapes=[
                pltpu.VMEM((N, own), F32),
                pltpu.VMEM((SPAN, SPAN), F32),
                pltpu.VMEM((SPAN, SPAN), F32),
                pltpu.VMEM((SPAN, SPAN), F32),
                pltpu.VMEM((SPAN, TILE), F32),
                pltpu.VMEM((N, SPAN), BF16),
                pltpu.VMEM((3, 8, own), F32),
                pltpu.VMEM((3, 8, 2 * N), F32),
                pltpu.VMEM((SPAN, 2 * N), F32),
                pltpu.VMEM((3, SPAN, TILE), F32),
                pltpu.VMEM((TILE, SPAN), F32),
                pltpu.VMEM((8, TILE), F32),
            ],
        ),
        out_shape=out_shape,
        compiler_params=pltpu.CompilerParams(dimension_semantics=("arbitrary", "arbitrary")),
        cost_estimate=pl.CostEstimate(
            flops=int(1.2e10 * count), bytes_accessed=12 * tokens * own, transcendentals=0
        ),
        name="scan_backward",
    )(*args)


def seg_facts(seg):
    length = seg.shape[0]
    cols = []
    for offset in (1, 2, 3):
        moved = jnp.concatenate([jnp.full((offset,), -1, jnp.int32), seg[:-offset]])
        cols.append((moved == seg).astype(F32))
    spans = length // SPAN
    ends = seg[SPAN - 1 :: SPAN]
    before = jnp.concatenate([seg[:1], ends[:-1]])
    cols.append((seg == jnp.repeat(before, SPAN)).astype(F32))
    cols.append((seg == jnp.repeat(ends, SPAN)).astype(F32))
    value = seg.astype(F32)
    same = jnp.broadcast_to(jnp.stack(cols, axis=0)[:, :, None], (5, length, TILE))
    return same, value[:, None], value[None, :]


def head_rows(dt_bias, a_log):
    rate = -jnp.exp(a_log)
    rows = jnp.stack([dt_bias, rate * LOG2E, rate] + [jnp.zeros_like(rate)] * 5, axis=0)
    return jnp.pad(rows, ((0, 0), (0, TILE - H)))


BLOCKS = 32
ORDERS = ((8, 1, 4, 2), (8, 2, 4, 1))


def reach(masks):
    out = [0]
    for mask in masks:
        out = out + [mask ^ place for place in out]
    return out


def exchange(values, stage):
    pairs = []
    for shard in range(16):
        for core in range(2):
            pairs.append((shard * 2 + core, (shard ^ ORDERS[core][stage]) * 2 + core))
    return lax.ppermute(values, ("shard", "rep"), pairs)


def swap_cores(values):
    return lax.ppermute(values, "rep", [(0, 1), (1, 0)])


def after(values, *others):
    return lax.optimization_barrier((values, *others))[0]


class Gather:
    def __init__(self, local):
        self.held = local
        self.seen = []
        self.swapped = []

    def step(self, *ahead):
        stage = len(self.seen)
        if stage > 0:
            self.held = jnp.concatenate([self.held, after(self.seen[-1], *ahead)], axis=0)
        elif ahead:
            self.held = after(self.held, *ahead)
        got = exchange(self.held, stage)
        self.seen.append(got)
        return self.held, got

    def swap(self, *ahead):
        send = after(self.held if not self.swapped else self.seen[3], *ahead)
        self.swapped.append(swap_cores(send))
        return send, self.swapped[-1]

    def pieces(self):
        return self.held, self.seen[3], *self.swapped


def gather_small(local):
    held = local[None]
    ahead = yield None
    for stage in range(4):
        send = after(held, *ahead)
        got = exchange(send, stage)
        ahead = yield send, got
        held = jnp.concatenate([send, got], axis=0)
    core = lax.axis_index("rep")
    places = jnp.asarray([reach(order) for order in ORDERS], jnp.int32)[core] ^ lax.axis_index("shard")
    hot = (places[None, :] == jnp.arange(16, dtype=jnp.int32)[:, None]).astype(local.dtype)
    yield dot_f32(hot, held, ((1,), (0,)), HIGHEST).astype(local.dtype)


class Scatter:
    def __init__(self, partial, block):
        mine, self.other = partial
        self.terms = [mine]
        self.block = block
        self.left = [3, 2, 1, 0]

    def rows(self, start, stop):
        total = self.terms[0][start:stop].astype(F32)
        for term in self.terms[1:]:
            total = total + term[start:stop].astype(F32)
        return total

    def step(self, *ahead):
        if len(self.terms) == 1:
            self.other = after(self.other, *ahead)
            self.terms.append(swap_cores(self.other))
            return self.other, self.terms[-1]
        if self.left:
            stage = self.left.pop(0)
            cut = self.block << stage
            self.terms[-1] = after(self.terms[-1], *ahead)
            send = self.rows(cut, 2 * cut).astype(BF16)
            self.terms.append(exchange(send, stage))
            return send, self.terms[-1]
        return self.terms[-1], self.terms[-1]

    def finish(self, *ahead):
        while self.left:
            self.step()
        if ahead:
            self.terms[-1] = after(self.terms[-1], *ahead)
        return self.rows(0, self.block)


def block_order(core):
    shard = lax.axis_index("shard")
    tables = jnp.asarray([reach(order) for order in ORDERS], jnp.int32)
    inverse = jnp.asarray(
        [[reach(order).index(mask) for mask in range(16)] for order in ORDERS], jnp.int32
    )
    own = 2 * (tables[core] ^ shard) + core
    partner = 2 * (tables[1 - core] ^ shard) + (1 - core)
    order = jnp.concatenate([own, partner])
    natural = jnp.arange(BLOCKS, dtype=jnp.int32)
    which = natural % 2
    place = inverse[which, (natural // 2) ^ shard] + 16 * (which != core).astype(jnp.int32)
    return order, place


def fetch_tile(order_ref, pieces, buffer, sems, tile, slot, block, width):
    for q in range(BLOCKS):
        pltpu.make_async_copy(
            pieces[q // 8].at[pl.ds((q % 8) * block, block), pl.ds(pl.multiple_of(tile * width, width), width)],
            buffer.at[slot, pl.ds(pl.multiple_of(order_ref[q] * block, block), block), :],
            sems.at[slot],
        ).start()


def next_tile(order_ref, pieces, buffer, sems, block, width):
    tile = pl.program_id(0)
    slot = lax.rem(tile, 2)

    @pl.when(tile == 0)
    def _():
        fetch_tile(order_ref, pieces, buffer, sems, tile, slot, block, width)

    @pl.when(tile + 1 < pl.num_programs(0))
    def _():
        fetch_tile(order_ref, pieces, buffer, sems, tile + 1, 1 - slot, block, width)

    pltpu.make_async_copy(buffer.at[slot], buffer.at[slot], sems.at[slot]).wait()
    return slot


def project_kernel(block, width, order_ref, x_ref, p0, p1, p2, p3, *rest):
    out_ref, w_ref, buffer, sems = rest[-4:]
    slot = next_tile(order_ref, (p0, p1, p2, p3), buffer, sems, block, width)
    w = buffer[slot]
    w_ref[...] = w
    for i in range(x_ref.shape[0] // SPAN):
        rows = slice(i * SPAN, (i + 1) * SPAN)
        out_ref[rows] = mm(x_ref[rows], w)


def project(x, pieces, order, so_far, start, full, width=512):
    tokens, depth = x.shape
    columns = pieces[0].shape[1]
    block = depth // BLOCKS
    at = start // width
    any_spec = pl.BlockSpec(memory_space=pl.ANY)
    extra = [] if so_far is None else list(so_far)
    return pl.pallas_call(
        functools.partial(project_kernel, block, width),
        grid_spec=pltpu.PrefetchScalarGridSpec(
            num_scalar_prefetch=1,
            grid=(columns // width,),
            in_specs=[pl.BlockSpec((tokens, depth), lambda j, o: (0, 0))] + [any_spec] * (4 + len(extra)),
            out_specs=[
                pl.BlockSpec((tokens, width), lambda j, o: (0, at + j)),
                pl.BlockSpec((depth, width), lambda j, o: (0, at + j)),
            ],
            scratch_shapes=[pltpu.VMEM((2, depth, width), BF16), pltpu.SemaphoreType.DMA((2,))],
        ),
        out_shape=[jax.ShapeDtypeStruct((tokens, full), F32), jax.ShapeDtypeStruct((depth, full), BF16)],
        input_output_aliases={} if so_far is None else {6: 0, 7: 1},
        cost_estimate=pl.CostEstimate(
            flops=2 * tokens * depth * columns,
            bytes_accessed=4 * depth * columns + 4 * tokens * columns + 2 * tokens * depth,
            transcendentals=0,
        ),
        name="project",
    )(order, x, *pieces, *extra)


def gate_kernel(block, width, order_ref, x_ref, p0, p1, p2, p3, y_ref, gain_ref, mark_ref, *rest):
    gate_ref, w_ref, zg_ref, square_ref, buffer, sems = rest[-6:]
    slot = next_tile(order_ref, (p0, p1, p2, p3), buffer, sems, block, width)
    w = buffer[slot]
    w_ref[...] = w

    @pl.when(pl.program_id(0) == 0)
    def _():
        square_ref[...] = jnp.zeros_like(square_ref)

    for i in range(x_ref.shape[0] // SPAN):
        rows = slice(i * SPAN, (i + 1) * SPAN)
        gate = mm(x_ref[rows], w)
        gate_ref[rows] = gate.astype(BF16)
        gated = y_ref[rows].astype(F32) * (gate * jax.nn.sigmoid(gate))
        zg_ref[rows] = (gated * gain_ref[...]).astype(BF16)
        square = gated * gated
        total = square[:, :TILE]
        for k in range(1, width // TILE):
            total = total + square[:, k * TILE : (k + 1) * TILE]
        square_ref[rows] += total


def gate_project(x, pieces, order, y, gain, mark, so_far, start, full, width=512):
    tokens, depth = x.shape
    columns = pieces[0].shape[1]
    block = depth // BLOCKS
    at = start // width
    any_spec = pl.BlockSpec(memory_space=pl.ANY)
    extra = [] if so_far is None else list(so_far)
    wide = pl.BlockSpec((tokens, width), lambda j, o: (0, at + j))
    return pl.pallas_call(
        functools.partial(gate_kernel, block, width),
        grid_spec=pltpu.PrefetchScalarGridSpec(
            num_scalar_prefetch=1,
            grid=(columns // width,),
            in_specs=[pl.BlockSpec((tokens, depth), lambda j, o: (0, 0))]
            + [any_spec] * 4
            + [wide, pl.BlockSpec((1, width), lambda j, o: (0, at + j)), pl.BlockSpec((8, TILE), lambda j, o: (0, 0))]
            + [any_spec] * len(extra),
            out_specs=[
                wide,
                pl.BlockSpec((depth, width), lambda j, o: (0, at + j)),
                wide,
                pl.BlockSpec((tokens, TILE), lambda j, o: (0, 0)),
            ],
            scratch_shapes=[pltpu.VMEM((2, depth, width), BF16), pltpu.SemaphoreType.DMA((2,))],
        ),
        out_shape=[
            jax.ShapeDtypeStruct((tokens, full), BF16),
            jax.ShapeDtypeStruct((depth, full), BF16),
            jax.ShapeDtypeStruct((tokens, full), BF16),
            jax.ShapeDtypeStruct((tokens, TILE), F32),
        ],
        input_output_aliases={} if so_far is None else {9: 0, 10: 1, 11: 2},
        cost_estimate=pl.CostEstimate(
            flops=2 * tokens * depth * columns,
            bytes_accessed=4 * depth * columns + 10 * tokens * columns + 2 * tokens * depth,
            transcendentals=tokens * columns,
        ),
        name="project_gate",
    )(order, x, *pieces, y, gain, mark, *extra)


def restore_kernel(block, width, order_ref, p0, p1, p2, p3, *rest):
    w_ref, buffer, sems = rest[-3:]
    slot = next_tile(order_ref, (p0, p1, p2, p3), buffer, sems, block, width)
    w_ref[...] = buffer[slot]


def restore(pieces, order, so_far, start, full, width=256):
    columns = pieces[0].shape[1]
    block = pieces[0].shape[0] // 8
    depth = block * BLOCKS
    at = start // width
    any_spec = pl.BlockSpec(memory_space=pl.ANY)
    extra = [] if so_far is None else [so_far]
    return pl.pallas_call(
        functools.partial(restore_kernel, block, width),
        grid_spec=pltpu.PrefetchScalarGridSpec(
            num_scalar_prefetch=1,
            grid=(columns // width,),
            in_specs=[any_spec] * (4 + len(extra)),
            out_specs=pl.BlockSpec((depth, width), lambda j, o: (0, at + j)),
            scratch_shapes=[pltpu.VMEM((2, depth, width), BF16), pltpu.SemaphoreType.DMA((2,))],
        ),
        out_shape=jax.ShapeDtypeStruct((depth, full), BF16),
        input_output_aliases={} if so_far is None else {5: 0},
        cost_estimate=pl.CostEstimate(flops=0, bytes_accessed=4 * depth * columns, transcendentals=0),
        name="restore",
    )(order, *pieces, *extra)


def output_kernel(block, width, order_ref, zg_ref, inverse_ref, tokens_ref, cot_ref, p0, p1, p2, p3, w_ref, out_ref, dots_ref, buffer, sems):
    slot = next_tile(order_ref, (p0, p1, p2, p3), buffer, sems, block, width)
    w = buffer[slot]
    w_ref[...] = w

    @pl.when(pl.program_id(0) == 0)
    def _():
        dots_ref[...] = jnp.zeros_like(dots_ref)

    for i in range(zg_ref.shape[0] // SPAN):
        rows = slice(i * SPAN, (i + 1) * SPAN)
        projected = inverse_ref[rows] * mm(zg_ref[rows], w)
        out_ref[rows] = (tokens_ref[rows].astype(F32) + projected).astype(BF16)
        dots_ref[rows] += jnp.sum(cot_ref[rows].astype(F32) * projected, axis=1, keepdims=True)


def output_project(zg, inverse, tokens, cot, pieces, order, width=512):
    count, depth = zg.shape
    model = tokens.shape[1]
    block = depth // BLOCKS
    any_spec = pl.BlockSpec(memory_space=pl.ANY)
    whole = lambda i, o: (0, 0)
    part = pl.BlockSpec((count, width), lambda i, o: (0, i))
    return pl.pallas_call(
        functools.partial(output_kernel, block, width),
        grid_spec=pltpu.PrefetchScalarGridSpec(
            num_scalar_prefetch=1,
            grid=(model // width,),
            in_specs=[pl.BlockSpec((count, depth), whole), pl.BlockSpec((count, 1), whole), part, part]
            + [any_spec] * 4,
            out_specs=[
                pl.BlockSpec((depth, width), lambda i, o: (0, i)),
                part,
                pl.BlockSpec((count, 1), whole),
            ],
            scratch_shapes=[pltpu.VMEM((2, depth, width), BF16), pltpu.SemaphoreType.DMA((2,))],
        ),
        out_shape=[
            jax.ShapeDtypeStruct((depth, model), BF16),
            jax.ShapeDtypeStruct((count, model), BF16),
            jax.ShapeDtypeStruct((count, 1), F32),
        ],
        cost_estimate=pl.CostEstimate(
            flops=2 * count * depth * model,
            bytes_accessed=4 * depth * model + 2 * count * (depth + 3 * model),
            transcendentals=0,
        ),
        name="project_out",
    )(order, zg, inverse, tokens, cot, *pieces)


def gate_back_kernel(cot_ref, w_ref, gate_ref, y_ref, gain_ref, inverse_ref, less_ref, dy_ref, dgate_ref):
    w = w_ref[...]
    for i in range(cot_ref.shape[0] // SPAN):
        rows = slice(i * SPAN, (i + 1) * SPAN)
        gate = gate_ref[rows].astype(F32)
        y = y_ref[rows].astype(F32)
        part = jax.nn.sigmoid(gate)
        opened = gate * part
        dz = inverse_ref[rows] * (gain_ref[...] * mm_nt(cot_ref[rows], w)) - (y * opened) * less_ref[rows]
        dy_ref[rows] = (dz * opened).astype(BF16)
        dgate_ref[rows] = (dz * y * (part + opened * (1.0 - part))).astype(BF16)


def gate_back(cot, w, gate, y, gain, inverse, less, width=256):
    count, model = cot.shape
    di = w.shape[0]
    part = pl.BlockSpec((count, width), lambda i: (0, i))
    column = pl.BlockSpec((count, 1), lambda i: (0, 0))
    shape = jax.ShapeDtypeStruct((count, di), BF16)
    return pl.pallas_call(
        gate_back_kernel,
        grid_spec=pltpu.PrefetchScalarGridSpec(
            num_scalar_prefetch=0,
            grid=(di // width,),
            in_specs=[
                pl.BlockSpec((count, model), lambda i: (0, 0)),
                pl.BlockSpec((width, model), lambda i: (i, 0)),
                part,
                part,
                pl.BlockSpec((1, width), lambda i: (0, i)),
                column,
                column,
            ],
            out_specs=[part, part],
        ),
        out_shape=[shape, shape],
        cost_estimate=pl.CostEstimate(
            flops=2 * count * di * model, bytes_accessed=2 * (di * model + 4 * count * di), transcendentals=count * di
        ),
        name="gate_back",
    )(cot, w, gate, y, gain, inverse, less)


def weight_grad_kernel(block, place_ref, lhs_ref, rhs_ref, mine, other, buffer, sems):
    step = pl.program_id(0)
    slot = lax.rem(step, 2)

    def settle(which):
        pltpu.make_async_copy(buffer.at[which], buffer.at[which], sems.at[which]).wait()

    @pl.when(step >= 2)
    def _():
        settle(slot)

    buffer[slot] = dot_f32(lhs_ref[...], rhs_ref[...], ((0,), (0,))).astype(BF16)
    for t in range(8):
        q = place_ref[step * 8 + t]
        source = buffer.at[slot, pl.ds(t * block, block), :]

        @pl.when(q < 16)
        def _():
            pltpu.make_async_copy(
                source, mine.at[pl.ds(pl.multiple_of(q * block, block), block), :], sems.at[slot]
            ).start()

        @pl.when(q >= 16)
        def _():
            pltpu.make_async_copy(
                source, other.at[pl.ds(pl.multiple_of((q - 16) * block, block), block), :], sems.at[slot]
            ).start()

    @pl.when(step == pl.num_programs(0) - 1)
    def _():
        settle(1 - slot)
        settle(slot)


def weight_grad(lhs, rhs, place, column, columns):
    tokens, rows = lhs.shape
    block = rows // BLOCKS
    any_spec = pl.BlockSpec(memory_space=pl.ANY)
    out = jax.ShapeDtypeStruct((16 * block, columns), BF16)
    return pl.pallas_call(
        functools.partial(weight_grad_kernel, block),
        grid_spec=pltpu.PrefetchScalarGridSpec(
            num_scalar_prefetch=1,
            grid=(4,),
            in_specs=[
                pl.BlockSpec((tokens, 8 * block), lambda i, o: (0, i)),
                pl.BlockSpec((tokens, columns), lambda i, o: (0, column)),
            ],
            out_specs=[any_spec, any_spec],
            scratch_shapes=[pltpu.VMEM((2, 8 * block, columns), BF16), pltpu.SemaphoreType.DMA((2,))],
        ),
        out_shape=[out, out],
        cost_estimate=pl.CostEstimate(
            flops=2 * tokens * rows * columns,
            bytes_accessed=2 * (tokens * rows + tokens * columns + rows * columns),
            transcendentals=0,
        ),
        name="weight_grad",
    )(place, lhs, rhs)


def rows_of(packed, start, count):
    return packed[:, start : start + count]


def on_device(
    hypercube,
    tokens,
    seg_ids,
    gain_in,
    w_in,
    conv_weight,
    conv_bias,
    dt_bias,
    a_log,
    d_skip,
    gain_out,
    w_out,
    cotangent,
):
    shards = lax.psum(1, "shard")
    taps, conv_local = conv_weight.shape
    model = tokens.shape[1]
    di = gain_out.shape[0] * shards
    conv_dim = conv_local * shards
    calls = ((0, 1), (1, 2), (3, 3))
    width = GROUP * P_SIZE

    def columns(w, call):
        start, count = call
        own = w[:, di + start * width : di + (start + count) * width]
        if start > 0:
            return own
        head = w[:, 2 * di :]
        return jnp.concatenate([jnp.pad(head, ((0, 0), (0, 4 * N - head.shape[1]))), own], axis=1)

    small = jnp.concatenate([conv_weight.reshape(-1), conv_bias, gain_in, gain_out])
    if hypercube:
        core = lax.axis_index("rep")
        w_half = lax.dynamic_slice_in_dim(w_in, core * (w_in.shape[0] // 2), w_in.shape[0] // 2, 0)
        o_half = lax.dynamic_slice_in_dim(w_out, core * (w_out.shape[0] // 2), w_out.shape[0] // 2, 0)
        near, middle, far = [Gather(columns(w_half, call)) for call in calls]
        gate_gather, out_gather = Gather(w_half[:, :di]), Gather(o_half)
        small_flow = gather_small(small)
        next(small_flow)
        got = []
        for starts in ((near,), (near, middle), (near, middle, far), (near, middle, far)):
            pairs = [near.step(*got)]
            ahead = [*got, pairs[0][0]]
            pairs += [each.step(*ahead) for each in starts[1:]] + [small_flow.send(ahead)]
            got = [pair[1] for pair in pairs]
            if len(starts) == 1:
                later = (far.held, gate_gather.held, out_gather.held), (tokens, seg_ids, dt_bias, a_log, d_skip, core)
                helds, (tokens, seg_ids, dt_bias, a_log, d_skip, core) = after(later, *got)
                far.held, gate_gather.held, out_gather.held = helds
        small_all = small_flow.send(got)
        order, place = block_order(core)
        swaps = [near.swap(near.seen[3]), near.swap()]
        got = [*got[1:], swaps[1][0]]
        sent, got = zip(middle.step(*got), far.step(*got), *swaps, gate_gather.step(*got))
        normed_tie = sent
        conv_tie = sent
        last_pair = got[0], got[1], got[4]
    else:
        small_all = lax.all_gather(small, "shard", axis=0, tiled=False)
        full_w_in = lax.all_gather(w_in, "shard", axis=0, tiled=True)
        full_w_out = lax.all_gather(w_out, "shard", axis=0, tiled=True)
    cut = taps * conv_local
    small_conv = after(small_all, *conv_tie) if hypercube else small_all
    conv_w = small_conv[:, :cut].reshape(shards, taps, conv_local).transpose(1, 0, 2).reshape(taps, -1)
    conv_b = rows_of(small_conv, cut, conv_local).reshape(1, -1)
    cut += conv_local
    full_gain_in = rows_of(small_all, cut, gain_in.shape[0]).reshape(1, -1).astype(F32)
    full_gain_out = rows_of(small_conv, cut + gain_in.shape[0], gain_out.shape[0]).reshape(1, -1).astype(F32)
    conv_all = jnp.concatenate(
        [conv_w.astype(F32), conv_b.astype(F32), jnp.zeros((3, conv_dim), F32)], axis=0
    )
    conv_x, conv_bc = conv_all[:, :di], conv_all[:, di:]
    inputs = tokens.astype(F32)
    rscale = lax.rsqrt(jnp.mean(inputs * inputs, axis=1, keepdims=True) + EPSILON)
    unit = inputs * rscale
    normed = (unit * full_gain_in).astype(BF16)
    same, seg_col, seg_row = seg_facts(seg_ids[0])
    if hypercube:
        normed, same = after((normed, same), *normed_tie)
    heads = head_rows(dt_bias, a_log)
    skip = jnp.repeat(d_skip, P_SIZE)[None]

    pcs, w_parts = [], []
    shared = written = mark = None
    project_tie = ()
    for index, call in enumerate(calls):
        if hypercube:
            pieces = (near, middle, far)[index].pieces()
            pc, w_part = project(after(normed, *project_tie), pieces, order, None, 0, pieces[0].shape[1])
            if index == 0:
                done = last_pair[0], last_pair[2], pc
                sent, got = zip(
                    middle.swap(*done), middle.swap(*done), gate_gather.step(*done), out_gather.step(*done)
                )
                pc = after(pc, *sent)
            if index == 1:
                sent, _ = far.swap(pc)
                pc = after(pc, sent)
        else:
            w_part = columns(full_w_in, call)
            pc = mm(normed, w_part)
        pcs.append((pc, 1 if index == 0 else 0))
        w_parts.append(w_part)
        written = run_forward(
            pc, pcs[-1][1], pcs[0][0], conv_x, conv_bc, same, seg_col, seg_row, heads, skip, *call, shared, written
        )
        mark = written[4]
        if index == 0:
            bcv, bc_slope, cum, shifted, cum_lines, shifted_lines, weight_lines = written[5:]
            shared = bcv, cum, shifted_lines, weight_lines
        written = written[:5]
        if hypercube and index == 0:
            done = last_pair[1], got[2], got[3], mark
            sent, got = zip(far.step(*done), gate_gather.step(*done), out_gather.step(*done))
            project_tie = sent
        if hypercube and index == 1:
            far.swap(got[0], mark)
            done = got[1], got[2], mark
            sent, got = zip(gate_gather.step(*done), gate_gather.swap(*done), out_gather.step(*done))
            project_tie = sent
    if hypercube:
        done = got[0], got[1], got[2], mark
        sent, got = zip(gate_gather.swap(*done), out_gather.step(*done), out_gather.swap(*done))
        gate_tie = sent
    x, y, states, slope, mark = written
    if hypercube:
        gate, w_gate, zg, squares = gate_project(
            after(normed, *gate_tie), gate_gather.pieces(), order, y, full_gain_out, mark, None, 0, di
        )
    else:
        w_gate = full_w_in[:, :di]
        gate = mm(normed, w_gate)
        gated = y.astype(F32) * (gate * jax.nn.sigmoid(gate))
        squares = gated * gated
        zg = (gated * full_gain_out).astype(BF16)
    inverse = lax.rsqrt(jnp.sum(squares, axis=1, keepdims=True) / di + EPSILON)
    cot = cotangent.astype(F32)
    cot_scaled = (inverse * cot).astype(BF16)
    sums = None
    parts = {}
    if hypercube:
        in_block = w_in.shape[0] // 2
        out_tie, out_got = out_gather.swap(cot_scaled)
        out_grad = weight_grad(zg, after(cot_scaled, out_tie), place, 0, model)
        out_sum = Scatter(out_grad, w_out.shape[0] // 2)
        sent, got = out_sum.step(*out_gather.swapped)
        full_w_out, output, dots = output_project(
            after(zg, sent), inverse, tokens, cotangent, out_gather.pieces(), order
        )
        sent, got = out_sum.step(got, dots)
        less = inverse * inverse * dots / di
        dy, dgate = gate_back(
            after(cotangent, sent), full_w_out, gate, y, full_gain_out, inverse, less
        )
    else:
        projected = inverse * mm(zg, full_w_out)
        output = (inputs + projected).astype(BF16)
        dots = jnp.sum(cot * projected, axis=1, keepdims=True)
        grad_ynorm = mm_nt(cotangent, full_w_out)
        y, gate = y.astype(F32), gate.astype(F32)
        sig = jax.nn.sigmoid(gate)
        dz = inverse * (full_gain_out * grad_ynorm) - (y * (gate * sig)) * (inverse * inverse * dots / di)
        dy = (dz * (gate * sig)).astype(BF16)
        dgate = (dz * y * (sig * (1.0 + gate * (1.0 - sig)))).astype(BF16)
    if hypercube:
        gate_grad = weight_grad(normed, after(dgate, got), place, 0, di)
        gate_sum = Scatter(gate_grad, in_block)
        sent, gate_got = gate_sum.step()
        scaled = mm_nt(after(dgate, sent), w_gate)
        sent, got = zip(out_sum.step(got, scaled), gate_sum.step(gate_got, scaled))
        dy = after(dy, *sent, gate_got, scaled)
    else:
        scaled = mm_nt(dgate, w_gate)
    grad_sums = {}
    for index, call in reversed(list(enumerate(calls))):
        pc, first_x = pcs[index]
        dpart, dcw, dskip, *sums = run_backward(
            dy, x, bcv, states, slope, bc_slope, pc, first_x, pcs[0][0], conv_x, conv_bc,
            same, seg_col, seg_row, heads, skip, (cum, shifted, cum_lines), *call, index == 0, sums,
        )
        parts[index] = (dpart, dcw, dskip)
        if not hypercube:
            scaled = scaled + mm_nt(dpart, w_parts[index])
            continue
        done = *got, dpart
        if index == 2:
            sent, out_got = out_sum.step(*done)
            early = (sent, *done)
        elif index == 1:
            sent, gate_got = gate_sum.step(*done)
            early = (sent, *done)
        else:
            sent, late = grad_sums[1].step(*got)
            early = (sent, *got)
        grad = weight_grad(normed, after(dpart, *early), place, 0, dpart.shape[1])
        grad_sums[index] = Scatter(grad, in_block)
        swap_sent, swap_got = grad_sums[index].step()
        if index == 2:
            scaled = scaled + mm_nt(after(dpart, swap_sent), w_parts[index])
            done = swap_got, scaled
            sent, got = zip(out_sum.step(out_got, *done), gate_sum.step(got[1], *done), grad_sums[2].step(*done))
            dy = after(dy, *sent, *done)
        elif index == 1:
            sent, got = zip(gate_sum.step(gate_got, swap_sent), grad_sums[2].step(got[2], swap_sent))
            got = got + (swap_got,)
            dy = after(dy, *sent, swap_sent)
        else:
            sent, late = zip(grad_sums[1].step(late, swap_sent), grad_sums[2].step(swap_sent))
            sent, got = grad_sums[0].step(swap_got, *sent)
            scaled = scaled + mm_nt(after(dpart, sent), w_parts[index])
    dbcw, dhead = after(tuple(sums), swap_sent) if hypercube else sums
    dbcw, dhead = after(tuple(sums), swap_sent) if hypercube else sums
    dcw = jnp.concatenate([parts[index][1] for index in range(len(calls))] + [dbcw], axis=2)
    dskip = jnp.concatenate([parts[index][2] for index in range(len(calls))], axis=1)
    if hypercube:
        ties = [swap_sent, sent]
        sent, got = grad_sums[0].step(got, scaled)
        ties.append(sent)
        sent, late = zip(grad_sums[1].step(*late, sent), grad_sums[2].step(*late, sent))
        late = late[0]
        scaled = scaled + mm_nt(after(parts[1][0], *sent), w_parts[1])
    scaled = scaled * full_gain_in
    inner = jnp.mean(unit * scaled, axis=1, keepdims=True)
    grad_tokens = (cot + rscale * (scaled - unit * inner)).astype(BF16)

    conv_sums = dcw.sum(1)
    conv_sums = jnp.concatenate([conv_sums[4:5], conv_sums[3:4], conv_sums[2:3], conv_sums[1:2], conv_sums[0:1]])
    per_head = jnp.concatenate(
        [
            dhead[0].sum(0)[:H],
            dhead[1].sum(0)[:H] * -jnp.exp(a_log),
            dskip.sum(0).reshape(H, P_SIZE).sum(1),
        ]
    )
    conv_part = conv_sums.reshape(taps + 1, shards, conv_local).transpose(1, 0, 2).reshape(shards, -1)
    small_grad = jnp.concatenate([conv_part, jnp.broadcast_to(per_head[None], (shards, 3 * H))], axis=1)
    real = w_in.shape[1] - 2 * di
    if hypercube:
        last_sent, got = grad_sums[0].step(got, grad_tokens)
        ties.append(last_sent)
        grad_sums[1].step(late, last_sent)
        end_sent, _ = grad_sums[0].step(got)
        ties.append(end_sent)
        small_sum = reduce_small(small_grad, ties)[0]
        whole = [each.finish(end_sent) for each in (gate_sum, grad_sums[2], grad_sums[1])]
        whole = [both_cores(part) for part in whole + [grad_sums[0].finish()]]
        head = whole.pop()
        whole = [whole[0], head[:, 4 * N :], whole[2], whole[1], head[:, :real]]
        sum_w_in = jnp.concatenate(whole, axis=1)
        edges = [0, di, di + width, di + 3 * width, 2 * di, w_in.shape[1]]
        gain_sum = 0.0
        for part, a, b in zip(whole, edges, edges[1:]):
            gain_sum = gain_sum + jnp.sum(part * w_in[:, a:b].astype(F32), axis=1)
        sum_w_out = both_cores(out_sum.finish(grad_sums[1].terms[0]))
    else:
        grad_w_out = dot_f32(zg, cot_scaled, ((0,), (0,)))
        rest = [parts[index][0] for index in range(len(calls))]
        grads = jnp.concatenate([dgate, rest[0][:, 4 * N :], *rest[1:], rest[0][:, :real]], axis=1)
        grad_w_in = dot_f32(normed, grads, ((0,), (0,)))
        small_sum = lax.psum(
            lax.psum_scatter(small_grad, "shard", scatter_dimension=0, tiled=True), "rep"
        )[0]
        sum_w_in = lax.psum_scatter(grad_w_in, "shard", scatter_dimension=0, tiled=True)
        sum_w_out = lax.psum_scatter(grad_w_out, "shard", scatter_dimension=0, tiled=True)
        sum_w_in, sum_w_out = lax.psum((sum_w_in, sum_w_out), "rep")
        gain_sum = jnp.sum(sum_w_in * w_in.astype(F32), axis=1)
    grad_gain_in = gain_sum / gain_in.astype(F32)
    grad_gain_out = jnp.sum(sum_w_out * w_out.astype(F32), axis=1) / gain_out.astype(F32)
    cut = taps * conv_local
    head_at = cut + conv_local
    return (
        output,
        grad_tokens,
        grad_gain_in,
        sum_w_in,
        small_sum[:cut].reshape(taps, conv_local),
        small_sum[cut:head_at],
        small_sum[head_at : head_at + H],
        small_sum[head_at + H : head_at + 2 * H],
        small_sum[head_at + 2 * H :],
        grad_gain_out,
        sum_w_out,
    )


def both_cores(own):
    partner = swap_cores(own)
    first = lax.axis_index("rep") == 0
    return jnp.concatenate([jnp.where(first, own, partner), jnp.where(first, partner, own)], axis=0)


def reduce_small(rows, ties):
    core = lax.axis_index("rep")
    places = jnp.asarray([reach(order) for order in ORDERS], jnp.int32)[core] ^ lax.axis_index("shard")
    hot = (places[:, None] == jnp.arange(16, dtype=jnp.int32)[None, :]).astype(F32)
    total = dot_f32(hot, rows, ((1,), (0,)), HIGHEST)
    for stage, tie in zip((3, 2, 1, 0), ties[:4]):
        cut = 1 << stage
        total = after(total, tie)
        total = total[:cut] + exchange(total[cut:], stage)
    total = after(total, ties[4])
    return total + swap_cores(total)


def solution(mesh):
    rows = P(("shard", "rep"), None)
    in_specs = (
        rows, rows, P("shard"), P("shard", None), P(None, "shard"), P("shard"), P(), P(), P(), P("shard"),
        P("shard", None), rows,
    )
    out_specs = (
        rows, rows, P("shard"), P("shard", None), P(None, "shard"), P("shard"), P(), P(), P(), P("shard"),
        P("shard", None),
    )
    hypercube = mesh.shape["shard"] == 16 and mesh.shape["rep"] == 2
    return jax.shard_map(
        functools.partial(on_device, hypercube),
        mesh=mesh,
        in_specs=in_specs,
        out_specs=out_specs,
        check_vma=False,
    )
```
